32 devices in a mesh: section: 2 (over core), dp: 4 (over z), tensor: 4 (over y, x).
Axes of the slice: x: 2, y: 2, z: 4, core: 2. Of those that a mesh axis runs over, the one named last changes fastest.
Arguments:
- block_input: bfloat16 [2, 8, 1024, 768], P('section', 'dp', 'tensor'), may hold values from -6 to 6
- w_self: bfloat16 [2, 768, 3, 768], P('section', 'dp', None, 'tensor'), may hold values from -0.21875 to 0.21875
- w_self_out: bfloat16 [2, 768, 768], P('section', 'tensor', 'dp'), may hold values from -3 to 3
- w_cross: bfloat16 [2, 768, 2, 768], P('section', 'dp', None, 'tensor')
- w_up: bfloat16 [2, 768, 3072], P('section', 'dp', 'tensor'), may hold values from -0.21875 to 0.21875
- w_down: bfloat16 [2, 3072, 768], P('section', 'tensor', 'dp'), may hold values from -0.109375 to 0.109375
- norm_gains: bfloat16 [2, 3, 768], P('section'), may hold values from 0.5 to 1.5
- lengths: int32 [2, 8], P(None, 'dp'), may hold values from 128 to 1024, as said below
- task_mask: int32 [8, 1024], P('dp'), may hold values from 0 to 1, as said below
- out_grad: bfloat16 [8, 1024, 768], P('dp', 'tensor'), may hold values from -6 to 6
Outputs:
- block_output: bfloat16 [2, 8, 1024, 768], P('section', 'dp', 'tensor')
- input_grad: float32 [2, 8, 1024, 768], P('section', 'dp', 'tensor')
- w_self_grad: float32 [2, 768, 3, 768], P('section', 'dp', None, 'tensor')
- w_self_out_grad: float32 [2, 768, 768], P('section', 'tensor', 'dp')
- w_cross_grad: float32 [2, 768, 2, 768], P('section', 'dp', None, 'tensor')
- w_up_grad: float32 [2, 768, 3072], P('section', 'dp', 'tensor')
- w_down_grad: float32 [2, 3072, 768], P('section', 'tensor', 'dp')
- gains_grad: float32 [2, 2, 768], P('section')
- last_gain_grad: float32 [2, 768], P('section')
The draws below stay inside these ranges and needn't reach their ends.
Inputs may be any that keep to these rules, and one draw needn't show every extreme that they name: Row 0 holds encoder lengths and row 1 decoder lengths; the first sequence has length 1024 in both rows. `task_mask`: position 0 of every sequence is 1.
All inputs are finite; a program needn't handle non-finite values.
Results may differ from the reference program's by a relative error of at most 0.02.
Values may be sent and summed in bfloat16 or wider, within the bound.
A program may use at most 320 MiB of HBM per device.

```python
import math
import jax
import jax.numpy as jnp
from jax import lax

D = 768
HEADS = 12
HEAD = 64
FF = 3072
SLOT = 1024
SEQS = 8


def draw_w_cross(key, part):
    base = jax.random.normal(key, (2, D, 2, D), jnp.float32)
    section_ids = lax.broadcasted_iota(jnp.int32, (2, D, 2, D), 0)
    member = lax.broadcasted_iota(jnp.int32, (2, D, 2, D), 2)
    factor = jnp.where((section_ids == 1) & (member == 1), 0.5, 1.0 / math.sqrt(D))
    return (base * factor).astype(jnp.bfloat16)


def draw_lengths(key, part):
    drawn = jax.random.randint(key, (2, SEQS), SLOT // 8, SLOT + 1, dtype=jnp.int32)
    return drawn.at[:, 0].set(SLOT)


def draw_task_mask(key, part):
    drawn = jax.random.randint(key, (SEQS, SLOT), 0, 4, dtype=jnp.int32)
    visible = jnp.minimum(drawn, 1)
    return visible.at[:, 0].set(1)


def steps_of(key, extent, cuts, smallest, high):
    factor_of, own = 1.0, jax.random.fold_in(key, 6)
    for position, blocks in cuts:
        steps = jnp.exp(jax.random.uniform(jax.random.fold_in(own, position), (blocks,), jnp.float32, smallest / len(cuts), high / len(cuts)))
        factor_of = factor_of * jnp.repeat(steps, extent[position] // blocks).reshape([-1 if axis == position else 1 for axis in range(len(extent))])
    return factor_of


def bell_draw(rng, extent, width, most, cuts=(), kind=jnp.bfloat16):
    array = jax.random.normal(rng, extent, jnp.float32) * width
    if len(cuts) > 0:
        array = steps_of(rng, extent, cuts, -0.22, 0.18) * array
    return jnp.clip(array, min=-most, max=most).astype(kind)


def setup_inputs(seed: int = 0) -> dict:
    key_list = jax.random.split(jax.random.key(seed), 11)
    return {
        "block_input": bell_draw(key_list[0], (2, SEQS, SLOT, D), 1.0, 6.0, ((0, 2), (1, 4), (2, 4))),
        "w_self": bell_draw(key_list[1], (2, D, 3, D), D ** -0.5, 0.21875, ((0, 2), (1, 4), (3, 4))),
        "w_self_out": bell_draw(key_list[2], (2, D, D), 4 ** -0.5, 3.0, ((0, 2), (1, 4), (2, 4))),
        "w_cross": draw_w_cross(jax.random.fold_in(key_list[10], 71), 0),
        "w_up": bell_draw(key_list[4], (2, D, FF), D ** -0.5, 0.21875, ((0, 2), (1, 4), (2, 4))),
        "w_down": bell_draw(key_list[5], (2, FF, D), FF ** -0.5, 0.109375, ((0, 2), (1, 4), (2, 4))),
        "norm_gains": jnp.clip(1.0 + 0.1 * jax.random.normal(key_list[6], (2, 3, D), jnp.float32), 0.5, 1.5).astype(jnp.bfloat16),
        "lengths": draw_lengths(jax.random.fold_in(key_list[10], 71), 0),
        "task_mask": draw_task_mask(jax.random.fold_in(key_list[10], 71), 0),
        "out_grad": bell_draw(key_list[9], (SEQS, SLOT, D), 1.0, 6.0, ((0, 4), (1, 4))),
    }


@jax.custom_vjp
def low(v):
    return lax.optimization_barrier(v.astype(jnp.bfloat16)).astype(jnp.float32)

@jax.custom_vjp
def low_back(v):
    return v

def low_keep(v):
    return (low(v), None)

def low_pass(kept, grad):
    return (grad,)

def back_keep(v):
    return (v, None)

def back_low(kept, grad):
    return (low(grad),)
low.defvjp(low_keep, low_pass)
low_back.defvjp(back_keep, back_low)
EPSILON = 1e-05
SCORE_SCALE = 0.125
NEG_FILL = -1000000000.0
PRECISE = lax.Precision.HIGHEST

def layer_norm(values, gain_row):
    centred = values - lax.optimization_barrier(jnp.mean(values, axis=-1, keepdims=True))
    spread = lax.optimization_barrier(jnp.mean(centred * centred, axis=-1, keepdims=True))
    return centred * lax.rsqrt(spread + EPSILON) * gain_row

def split_heads(values):
    return values.reshape(values.shape[0], HEADS, HEAD)

def attention(queries, key_rows, value_rows, allowed):
    scores = jnp.einsum('qhd,khd->hqk', split_heads(queries), split_heads(key_rows), precision=PRECISE)
    scores = low_back(scores * SCORE_SCALE)
    scores = jnp.where(allowed[None], scores, NEG_FILL)
    attn_probs = low(jax.nn.softmax(scores, axis=-1))
    result = jnp.einsum('hqk,khd->qhd', attn_probs, split_heads(value_rows), precision=PRECISE)
    return low_back(low(result.reshape(result.shape[0], -1)))

def self_branch(values, w_qkv, w_output, gain_row, allowed):
    normed = low(layer_norm(values, gain_row))
    projected = low_back(low(jnp.einsum('rd,dkh->krh', normed, w_qkv, precision=PRECISE)))
    attended = attention(projected[0], projected[1], projected[2], allowed)
    return low_back(jnp.dot(attended, w_output, precision=PRECISE))

def feed_branch(values, w_input, w_output, gain_row):
    normed = low(layer_norm(values, gain_row))
    pre_act = low_back(jnp.dot(normed, w_input, precision=PRECISE))
    activation = low(jax.nn.gelu(pre_act))
    return low_back(jnp.dot(activation, w_output, precision=PRECISE))

def one_pair(params, enc_rows, dec_rows, enc_length, dec_length, task_row):
    w_self, w_self_out, w_cross, w_up, w_down, gain_rows = params
    positions = jnp.arange(SLOT, dtype=jnp.int32)
    key_pos = positions[None, :]
    query_pos = positions[:, None]
    enc_allowed = jnp.broadcast_to(key_pos < enc_length, (SLOT, SLOT))
    dec_allowed = (key_pos < dec_length) & (key_pos <= query_pos)
    cross_allowed = jnp.broadcast_to((key_pos < enc_length) & (task_row[None, :] == 1), (SLOT, SLOT))
    enc_mid = enc_rows + self_branch(enc_rows, w_self[0], w_self_out[0], gain_rows[0, 0], enc_allowed)
    enc_late = enc_mid + feed_branch(enc_mid, w_up[0], w_down[0], gain_rows[0, 1])
    memory = low(layer_norm(enc_late, gain_rows[0, 2]))
    memory_kv = low_back(low(jnp.einsum('rd,dkh->krh', memory, w_cross[0], precision=PRECISE)))
    dec_mid = dec_rows + self_branch(dec_rows, w_self[1], w_self_out[1], gain_rows[1, 0], dec_allowed)
    cross_normed = low(layer_norm(dec_mid, gain_rows[1, 1]))
    cross_queries = low_back(low(jnp.dot(cross_normed, w_cross[1, :, 0, :], precision=PRECISE)))
    cross_result = attention(cross_queries, memory_kv[0], memory_kv[1], cross_allowed)
    dec_late = dec_mid + low_back(jnp.einsum('rh,eh->re', cross_result, w_cross[1, :, 1, :], precision=PRECISE))
    dec_final = dec_late + feed_branch(dec_late, w_up[1], w_down[1], gain_rows[1, 2])
    return (memory, dec_final)

def reference(block_input, w_self, w_self_out, w_cross, w_up, w_down, norm_gains, lengths, task_mask, out_grad):
    params = (w_self.astype(jnp.float32), w_self_out.astype(jnp.float32), w_cross.astype(jnp.float32), w_up.astype(jnp.float32), w_down.astype(jnp.float32), norm_gains.astype(jnp.float32))
    inputs = block_input.astype(jnp.float32)

    def forward(weights, values):

        def per_sequence(item_tuple):
            return jax.checkpoint(one_pair)(weights, item_tuple[0], item_tuple[1], item_tuple[2], item_tuple[3], item_tuple[4])
        return lax.map(per_sequence, (values[0], values[1], lengths[0], lengths[1], task_mask))
    (memory, decoded), pullback = jax.vjp(forward, params, inputs)
    d_params, d_inputs = pullback((jnp.zeros_like(memory), out_grad.astype(jnp.float32)))
    block_output = jnp.stack([memory, decoded]).astype(jnp.bfloat16)
    gain_grads = d_params[5]
    return (block_output, d_inputs, d_params[0], d_params[1], d_params[2], d_params[3], d_params[4], gain_grads[:, :2], gain_grads[:, 2])
```

```python
import jax
import jax.numpy as jnp
from jax import lax
from jax.sharding import PartitionSpec as P

HEAD = 64
TILE = 128
EPSILON = 1e-05
SCORE_SCALE = 0.125
NEG_FILL = -1000000000.0
AXES = ("section", "dp", "tensor")
LOW = jnp.bfloat16
WIDE = jnp.float32


class Layout:
    def __init__(self):
        self.cores = lax.axis_size("section")
        self.planes = lax.axis_size("dp")
        self.chips = lax.axis_size("tensor")
        self.core = lax.axis_index("section")
        self.plane = lax.axis_index("dp")
        self.chip = lax.axis_index("tensor")
        self.role = self.chip % 2
        self.item = self.chip // 2
        self.is_decoder = self.role == 1
        self.relays = self.core == self.item

    def route(self, value, target):
        pairs = []
        for core in range(self.cores):
            for plane in range(self.planes):
                for chip in range(self.chips):
                    to = target(core, plane, chip)
                    if to is None:
                        continue
                    source = (core * self.planes + plane) * self.chips + chip
                    goal = (to[0] * self.planes + to[1]) * self.chips + to[2]
                    pairs.append((source, goal))
        return lax.ppermute(value, AXES, pairs)

    def other_core(self, value):
        return self.route(value, lambda c, z, t: (1 - c, z, t))


def normalize(values):
    centred = values - jnp.mean(values, axis=-1, keepdims=True)
    spread = jnp.mean(centred * centred, axis=-1, keepdims=True)
    scale = lax.rsqrt(spread + EPSILON)
    return centred * scale, scale


def layer_norm(values, gain):
    return normalize(values)[0] * gain


def norm_back(values, gain, grad):
    normal, scale = normalize(values)
    scaled = grad * gain
    first = jnp.mean(scaled, axis=-1, keepdims=True)
    second = jnp.mean(scaled * normal, axis=-1, keepdims=True)
    return (scaled - first - normal * second) * scale, jnp.sum(grad * normal, axis=0)


ORDER = (("q", 0), ("q", 1), ("k", 0), ("k", 1), ("v", 0), ("v", 1), ("q", 2), ("v", 2), ("k", 2), ("o", 2), ("o", 0), ("o", 1))


def pack_heads(parts):
    return jnp.concatenate([parts[n][:, HEAD * h : HEAD * (h + 1)] for n, h in ORDER], axis=1)


def unpack_heads(block, name):
    where = {(n, h): i for i, (n, h) in enumerate(ORDER)}
    return jnp.concatenate(
        [block[:, HEAD * where[(name, h)] : HEAD * (where[(name, h)] + 1)] for h in range(3)], axis=1
    )


def mm(left, right):
    return jnp.dot(left, right, preferred_element_type=WIDE)


def mm_nt(left, right):
    return lax.dot_general(left, right, (((1,), (1,)), ((), ())), preferred_element_type=WIDE)


def mm_tn(left, right):
    return lax.dot_general(left, right, (((0,), (0,)), ((), ())), preferred_element_type=WIDE)


def split_heads(value):
    return value.reshape(value.shape[0], -1, HEAD)


def attend(q, k, v, allowed):
    scores = jnp.einsum("qhd,khd->hqk", split_heads(q), split_heads(k), preferred_element_type=WIDE) * SCORE_SCALE
    scores = jnp.where(allowed[None], scores, NEG_FILL)
    top = jnp.max(scores, axis=-1, keepdims=True)
    power = jnp.exp(scores - top)
    total = jnp.sum(power, axis=-1, keepdims=True)
    probs = (power / total).astype(LOW)
    out = jnp.einsum("hqk,khd->qhd", probs, split_heads(v), preferred_element_type=WIDE)
    return out.astype(LOW).reshape(q.shape), top + jnp.log(total)


def attend_back(q, k, v, log_sum, d_out, allowed):
    scores = jnp.einsum("qhd,khd->hqk", split_heads(q), split_heads(k), preferred_element_type=WIDE) * SCORE_SCALE
    scores = jnp.where(allowed[None], scores, NEG_FILL)
    probs = jnp.exp(scores - log_sum)
    d_probs = jnp.einsum("qhd,khd->hqk", split_heads(d_out), split_heads(v), preferred_element_type=WIDE)
    inner = jnp.sum(probs * d_probs, axis=-1, keepdims=True)
    d_scores = (probs * (d_probs - inner)).astype(LOW)
    d_v = jnp.einsum("hqk,qhd->khd", probs.astype(LOW), split_heads(d_out), preferred_element_type=WIDE)
    d_q = jnp.einsum("hqk,khd->qhd", d_scores, split_heads(k), preferred_element_type=WIDE) * SCORE_SCALE
    d_k = jnp.einsum("hqk,qhd->khd", d_scores, split_heads(q), preferred_element_type=WIDE) * SCORE_SCALE
    return tuple(g.astype(LOW).reshape(q.shape) for g in (d_q, d_k, d_v))


def gelu_parts(value):
    coef = 0.7978845608028654
    cube = 0.044715
    inner = coef * (value + cube * value * value * value)
    soft = jnp.tanh(inner)
    slope = 0.5 * (1.0 + soft) + 0.5 * value * (1.0 - soft * soft) * coef * (1.0 + 3.0 * cube * value * value)
    return 0.5 * value * (1.0 + soft), slope


def ring_gather(lay, shard):
    planes = lay.planes
    rows = shard.shape[1]
    relay = lambda c, z, t: (c, (z + 1) % planes, t) if c == t // 2 else None
    whole = jnp.zeros((shard.shape[0], planes * rows, shard.shape[2]), shard.dtype)
    piece = shard
    for step in range(planes):
        across = lay.route(piece, lambda c, z, t: (c, z, (t + 2) % 4) if c == t // 2 else None)
        chosen = jnp.where(lay.relays, piece, across)
        whole = lax.dynamic_update_slice(whole, chosen, (0, ((lay.plane - step) % planes) * rows, 0))
        if step + 1 < planes:
            piece = lay.route(piece, relay)
    return whole


def ring_scatter(lay, total, holder):
    planes = lay.planes
    rows = total.shape[1] // planes
    low = total.astype(LOW)
    across = lay.route(
        low, lambda c, z, t: (c, z, (t + 2) % 4) if (c != t // 2 and t % 2 == holder) else None
    )
    summed = low.astype(WIDE) + across.astype(WIDE)
    relay = lambda c, z, t: (c, (z + 1) % planes, t) if (c == t // 2 and t % 2 == holder) else None
    take = lambda j: lax.dynamic_slice_in_dim(summed, (j % planes) * rows, rows, 1)
    running = take(lay.plane - 1)
    for step in range(1, planes):
        running = lay.route(running.astype(LOW), relay).astype(WIDE) + take(lay.plane - 1 - step)
    return running.astype(LOW)


def hand_back(lay, value, holder, section):
    same = lay.route(
        value[0], lambda c, z, t: (section, z, t) if (c == t // 2 and t % 2 == holder) else None
    )
    beside = lay.route(
        value[1], lambda c, z, t: (section, z, t ^ 1) if (c == t // 2 and t % 2 == holder) else None
    )
    return same.astype(WIDE) + beside.astype(WIDE)


def body(block_input, w_self, w_self_out, w_cross, w_up, w_down, norm_gains, lengths, task_mask, out_grad):
    lay = Layout()
    seqs, rows, width = block_input.shape[1:]
    slot = rows * lay.chips
    sec = lay.core
    item = lay.item

    def spread(value, first):
        pick = value[jnp.where(first, lay.chip % 2, 1 - lay.chip % 2)]
        flip = 0 if first else 1
        return lay.route(pick, lambda c, z, t: (t // 2, z, 2 * ((t % 2) ^ flip) + c))

    def merge_rows(mine, theirs):
        low_half = jnp.where(lay.core == 0, mine, theirs)
        high_half = jnp.where(lay.core == 0, theirs, mine)
        return jnp.concatenate([low_half[0], low_half[1], high_half[0], high_half[1]], axis=0)

    first = spread(block_input[0], True)
    second = spread(block_input[0], False)
    mine = jnp.where(item == 0, jnp.stack([first, second]), jnp.stack([second, first]))
    x_rows = merge_rows(mine, lay.other_core(mine)).astype(WIDE)

    picked = out_grad[lay.core]
    even = lay.route(picked, lambda c, z, t: (t // 2, z, 2 * c + 1) if t % 2 == 0 else None)
    odd = lay.route(picked, lambda c, z, t: (t // 2, z, 2 * c + 1) if t % 2 == 1 else None)
    mine = jnp.stack([even, odd])
    cotangent = merge_rows(mine, lay.other_core(mine))

    gains_here = norm_gains[0].astype(WIDE)
    gains = jnp.where(sec == lay.role, gains_here, lay.other_core(norm_gains[0]).astype(WIDE))

    depth = w_self.shape[1]
    wide = w_self.shape[3]
    self_block = pack_heads(
        {"q": w_self[0, :, 0], "k": w_self[0, :, 1], "v": w_self[0, :, 2], "o": w_self_out[0].T}
    )
    feed_block = jnp.concatenate([w_up[0], w_down[0].T], axis=1)
    cross_block = w_cross[0].reshape(depth, 2 * wide)

    def collect(block):
        same = lay.route(block, lambda c, z, t: (t // 2, z, t) if c == t % 2 else None)
        beside = lay.route(block, lambda c, z, t: (t // 2, z, t ^ 1) if c != t % 2 else None)
        return jnp.stack([same, beside])

    def collect_cross(block, section):
        same = lay.route(block, lambda c, z, t: (t // 2, z, t) if (c == section and t % 2 == 1) else None)
        beside = lay.route(block, lambda c, z, t: (t // 2, z, t ^ 1) if (c == section and t % 2 == 0) else None)
        return same, beside

    w_att = ring_gather(lay, collect(self_block))
    w_ffn = ring_gather(lay, collect(feed_block))
    memory_side = collect_cross(cross_block, 0)
    query_side = collect_cross(cross_block, 1)
    w_crs = ring_gather(
        lay,
        jnp.stack(
            [
                pack_heads({"q": q[:, :wide], "k": m[:, :wide], "v": m[:, wide:], "o": q[:, wide:]})
                for m, q in zip(memory_side, query_side)
            ]
        ),
    )
    hidden = w_up.shape[2]
    part = lambda w, name: jnp.concatenate([unpack_heads(w[0], name), unpack_heads(w[1], name)], axis=1)
    att = {n: part(w_att, n) for n in "qkvo"}
    crs = {n: part(w_crs, n) for n in "qkvo"}
    up = jnp.concatenate([w_ffn[0, :, :hidden], w_ffn[1, :, :hidden]], axis=1)
    down_t = jnp.concatenate([w_ffn[0, :, hidden:], w_ffn[1, :, hidden:]], axis=1)

    positions = jnp.arange(slot)
    own_length = jnp.where(lay.is_decoder, lengths[1, item], lengths[0, item])
    self_allowed = (positions[None, :] < own_length) & (
        (positions[None, :] <= positions[:, None]) | jnp.logical_not(lay.is_decoder)
    )
    cross_allowed = jnp.broadcast_to(
        ((positions < lengths[0, item]) & (task_mask[item] == 1))[None], (slot, slot)
    )

    def joined(partial):
        low = partial.astype(LOW)
        return low.astype(WIDE) + lay.other_core(low).astype(WIDE)

    normed0 = layer_norm(x_rows, gains[0]).astype(LOW)
    q, k, v = (mm(normed0, att[n]).astype(LOW) for n in "qkv")
    out_self, lse_self = attend(q, k, v, self_allowed)
    x_mid = x_rows + joined(mm_nt(out_self, att["o"]))
    normed1 = layer_norm(x_mid, gains[1]).astype(LOW)

    pre_enc = mm(normed1, up)
    act_enc, slope_enc = gelu_parts(pre_enc)
    act_enc = act_enc.astype(LOW)
    x_late_enc = x_mid + joined(mm_nt(act_enc, down_t))
    memory_enc = layer_norm(x_late_enc, gains[2]).astype(LOW)
    memory = lay.route(memory_enc, lambda c, z, t: (c, z, t ^ 1) if t % 2 == 0 else None)

    cq = mm(normed1, crs["q"]).astype(LOW)
    ck, cv = (mm(memory, crs[n]).astype(LOW) for n in "kv")
    out_cross, lse_cross = attend(cq, ck, cv, cross_allowed)
    x_late = x_mid + joined(mm_nt(out_cross, crs["o"]))
    normed2 = layer_norm(x_late, gains[2]).astype(LOW)
    pre_dec = mm(normed2, up)
    act_dec, slope_dec = gelu_parts(pre_dec)
    act_dec = act_dec.astype(LOW)
    result_dec = (x_late + joined(mm_nt(act_dec, down_t))).astype(LOW)

    d_out = cotangent.astype(WIDE)
    d_pre = (slope_dec * mm(cotangent, down_t)).astype(LOW)
    d_ffn_dec = jnp.concatenate([mm_tn(normed2, d_pre), mm_tn(cotangent, act_dec)], axis=1)
    d_late_norm, d_gain2_dec = norm_back(x_late, gains[2], joined(mm_nt(d_pre, up)))
    d_late = d_out + d_late_norm
    grad_late = d_late.astype(LOW)
    d_att = mm(grad_late, crs["o"]).astype(LOW)
    d_cq, d_ck, d_cv = attend_back(cq, ck, cv, lse_cross, d_att, cross_allowed)
    d_memory = joined(mm_nt(d_ck, crs["k"]) + mm_nt(d_cv, crs["v"]))
    d_crs = {
        "q": mm_tn(normed1, d_cq),
        "k": mm_tn(memory, d_ck),
        "v": mm_tn(memory, d_cv),
        "o": mm_tn(grad_late, out_cross),
    }
    d_mid_norm, d_gain1_dec = norm_back(x_mid, gains[1], joined(mm_nt(d_cq, crs["q"])))
    d_mid_dec = d_late + d_mid_norm

    d_memory = lay.route(d_memory.astype(LOW), lambda c, z, t: (c, z, t ^ 1) if t % 2 == 1 else None).astype(WIDE)
    d_late_enc, d_gain2_enc = norm_back(x_late_enc, gains[2], d_memory)
    grad_late_enc = d_late_enc.astype(LOW)
    d_pre = (slope_enc * mm(grad_late_enc, down_t)).astype(LOW)
    d_ffn_enc = jnp.concatenate([mm_tn(normed1, d_pre), mm_tn(grad_late_enc, act_enc)], axis=1)
    d_mid_norm, d_gain1_enc = norm_back(x_mid, gains[1], joined(mm_nt(d_pre, up)))
    d_mid_enc = d_late_enc + d_mid_norm

    d_mid = jnp.where(lay.is_decoder, d_mid_dec, d_mid_enc)
    grad_mid = d_mid.astype(LOW)
    d_att = mm(grad_mid, att["o"]).astype(LOW)
    d_q, d_k, d_v = attend_back(q, k, v, lse_self, d_att, self_allowed)
    d_norm = joined(mm_nt(d_q, att["q"]) + mm_nt(d_k, att["k"]) + mm_nt(d_v, att["v"]))
    d_att_w = {
        "q": mm_tn(normed0, d_q),
        "k": mm_tn(normed0, d_k),
        "v": mm_tn(normed0, d_v),
        "o": mm_tn(grad_mid, out_self),
    }
    d_first, d_gain0 = norm_back(x_rows, gains[0], d_norm)
    d_rows = d_mid + d_first

    half = 3 * HEAD

    def blocks(parts):
        return jnp.stack(
            [pack_heads({n: parts[n][:, half * b : half * (b + 1)] for n in parts}) for b in range(2)]
        )

    def feed_blocks(both):
        total = both.shape[1] // 2
        return jnp.stack(
            [
                jnp.concatenate(
                    [both[:, hidden * b : hidden * (b + 1)], both[:, total + hidden * b : total + hidden * (b + 1)]],
                    axis=1,
                )
                for b in range(2)
            ]
        )

    self_total = blocks(d_att_w)
    home_self = hand_back(lay, ring_scatter(lay, self_total, 0), 0, 0) + hand_back(
        lay, ring_scatter(lay, self_total, 1), 1, 1
    )
    home_feed = hand_back(lay, ring_scatter(lay, feed_blocks(d_ffn_enc), 0), 0, 0) + hand_back(
        lay, ring_scatter(lay, feed_blocks(d_ffn_dec), 1), 1, 1
    )
    cross_total = ring_scatter(lay, blocks(d_crs), 1)
    side = lambda names: jnp.stack(
        [jnp.concatenate([unpack_heads(cross_total[b], n) for n in names], axis=1) for b in range(2)]
    )
    home_cross = hand_back(lay, side("kv"), 1, 0) + hand_back(lay, side("qo"), 1, 1)

    g_self = jnp.stack([unpack_heads(home_self, n) for n in "qkv"], axis=1)[None]
    g_self_out = unpack_heads(home_self, "o").T[None]
    g_cross = home_cross.reshape(1, depth, 2, wide)
    g_up = home_feed[:, :hidden][None]
    g_down = home_feed[:, hidden:].T[None]

    gain2 = jnp.where(lay.is_decoder, d_gain2_dec, d_gain2_enc)
    gain1 = jnp.where(lay.is_decoder, d_gain1_dec, d_gain1_enc)
    gain_rows = jnp.stack([d_gain0, gain1, gain2])
    slots = jnp.stack(
        [
            jnp.where((lay.role == r) & (lay.core == 0), gain_rows, 0.0)
            for r in range(2)
        ]
    )
    gain_total = lax.psum(slots, AXES)[sec][None]

    def rows_home(value):
        mine = lax.dynamic_slice_in_dim(value, lay.core * 2 * rows, 2 * rows, 0).reshape(2, rows, width)
        a = lay.route(mine[item], lambda c, z, t: (t % 2, z, 2 * c + t // 2))
        b = lay.route(mine[1 - item], lambda c, z, t: (t % 2, z, 2 * c + 1 - t // 2))
        even = lay.chip % 2 == 0
        return jnp.where(even, jnp.stack([a, b]), jnp.stack([b, a]))[None]

    block_output = rows_home(jnp.where(lay.is_decoder, result_dec, memory_enc))
    input_grad = rows_home(d_rows.astype(LOW)).astype(WIDE)
    return (
        block_output,
        input_grad,
        g_self,
        g_self_out,
        g_cross,
        g_up,
        g_down,
        gain_total[:, :2],
        gain_total[:, 2],
    )


def solution(mesh):
    placed = (
        P("section", "dp", "tensor", None),
        P("section", "dp", None, "tensor"),
        P("section", "tensor", "dp"),
        P("section", "dp", None, "tensor"),
        P("section", "dp", "tensor"),
        P("section", "tensor", "dp"),
        P("section", None, None),
        P(None, "dp"),
        P("dp", None),
        P("dp", "tensor", None),
    )
    return jax.shard_map(
        body,
        mesh=mesh,
        in_specs=placed,
        out_specs=(
            P("section", "dp", "tensor", None),
            P("section", "dp", "tensor", None),
            P("section", "dp", None, "tensor"),
            P("section", "tensor", "dp"),
            P("section", "dp", None, "tensor"),
            P("section", "dp", "tensor"),
            P("section", "tensor", "dp"),
            P("section", None, None),
            P("section", None),
        ),
        check_vma=False,
    )
```

```python
import functools

import jax
import jax.numpy as jnp
from jax import lax
from jax.experimental import pallas as pl
from jax.experimental.pallas import tpu as pltpu
from jax.sharding import PartitionSpec as P

HEAD = 64
TILE = 128
EPSILON = 1e-05
SCORE_SCALE = 0.125
NEG_FILL = -1000000000.0
AXES = ("section", "dp", "tensor")
LOW = jnp.bfloat16
WIDE = jnp.float32


class Layout:
    def __init__(self):
        self.cores = lax.axis_size("section")
        self.planes = lax.axis_size("dp")
        self.chips = lax.axis_size("tensor")
        self.core = lax.axis_index("section")
        self.plane = lax.axis_index("dp")
        self.chip = lax.axis_index("tensor")
        self.role = self.chip % 2
        self.item = self.chip // 2
        self.is_decoder = self.role == 1
        self.relays = self.core == self.item

    def route(self, value, target):
        pairs = []
        for core in range(self.cores):
            for plane in range(self.planes):
                for chip in range(self.chips):
                    to = target(core, plane, chip)
                    if to is None:
                        continue
                    source = (core * self.planes + plane) * self.chips + chip
                    goal = (to[0] * self.planes + to[1]) * self.chips + to[2]
                    pairs.append((source, goal))
        return lax.ppermute(value, AXES, pairs)

    def other_core(self, value):
        return self.route(value, lambda c, z, t: (1 - c, z, t))


def normalize(values):
    centred = values - jnp.mean(values, axis=-1, keepdims=True)
    spread = jnp.mean(centred * centred, axis=-1, keepdims=True)
    scale = lax.rsqrt(spread + EPSILON)
    return centred * scale, scale


def layer_norm(values, gain):
    return normalize(values)[0] * gain


def norm_back(values, gain, grad):
    normal, scale = normalize(values)
    scaled = grad * gain
    first = jnp.mean(scaled, axis=-1, keepdims=True)
    second = jnp.mean(scaled * normal, axis=-1, keepdims=True)
    return (scaled - first - normal * second) * scale, jnp.sum(grad * normal, axis=0)


ORDER = (("q", 0), ("q", 1), ("q", 2), ("o", 2), ("o", 0), ("o", 1), ("k", 0), ("k", 1), ("v", 0), ("v", 1), ("k", 2), ("v", 2))


def pack_heads(parts):
    return jnp.concatenate([parts[n][:, HEAD * h : HEAD * (h + 1)] for n, h in ORDER], axis=1)


def unpack_heads(block, name):
    where = {(n, h): i for i, (n, h) in enumerate(ORDER)}
    return jnp.concatenate(
        [block[:, HEAD * where[(name, h)] : HEAD * (where[(name, h)] + 1)] for h in range(3)], axis=1
    )


def mm(left, right):
    return jnp.dot(left, right, preferred_element_type=WIDE)


def mm_nt(left, right):
    return lax.dot_general(left, right, (((1,), (1,)), ((), ())), preferred_element_type=WIDE)


def mm_tn(left, right):
    return lax.dot_general(left, right, (((0,), (0,)), ((), ())), preferred_element_type=WIDE)


def split_heads(value):
    return value.reshape(value.shape[0], -1, HEAD)


def attend(q, k, v, allowed):
    scores = jnp.einsum("qhd,khd->hqk", split_heads(q), split_heads(k), preferred_element_type=WIDE) * SCORE_SCALE
    scores = jnp.where(allowed[None], scores, NEG_FILL)
    top = jnp.max(scores, axis=-1, keepdims=True)
    power = jnp.exp(scores - top)
    total = jnp.sum(power, axis=-1, keepdims=True)
    probs = (power / total).astype(LOW)
    out = jnp.einsum("hqk,khd->qhd", probs, split_heads(v), preferred_element_type=WIDE)
    return out.astype(LOW).reshape(q.shape), top + jnp.log(total)


def attend_back(q, k, v, log_sum, d_out, allowed):
    scores = jnp.einsum("qhd,khd->hqk", split_heads(q), split_heads(k), preferred_element_type=WIDE) * SCORE_SCALE
    scores = jnp.where(allowed[None], scores, NEG_FILL)
    probs = jnp.exp(scores - log_sum)
    d_probs = jnp.einsum("qhd,khd->hqk", split_heads(d_out), split_heads(v), preferred_element_type=WIDE)
    inner = jnp.sum(probs * d_probs, axis=-1, keepdims=True)
    d_scores = (probs * (d_probs - inner)).astype(LOW)
    d_v = jnp.einsum("hqk,qhd->khd", probs.astype(LOW), split_heads(d_out), preferred_element_type=WIDE)
    d_q = jnp.einsum("hqk,khd->qhd", d_scores, split_heads(k), preferred_element_type=WIDE) * SCORE_SCALE
    d_k = jnp.einsum("hqk,qhd->khd", d_scores, split_heads(q), preferred_element_type=WIDE) * SCORE_SCALE
    return tuple(g.astype(LOW).reshape(q.shape) for g in (d_q, d_k, d_v))


def gelu_parts(value):
    coef = 0.7978845608028654
    cube = 0.044715
    inner = coef * (value + cube * value * value * value)
    soft = jnp.tanh(inner)
    slope = 0.5 * (1.0 + soft) + 0.5 * value * (1.0 - soft * soft) * coef * (1.0 + 3.0 * cube * value * value)
    return 0.5 * value * (1.0 + soft), slope


MESH = pl.DeviceIdType.MESH
GROUPS = ("att", "crs", "up", "dn")
BLOCK = 256
VMEM_BYTES = 62 * 2**20


def lanes(shape):
    return lax.broadcasted_iota(jnp.int32, shape, len(shape) - 1)


def subs(shape):
    return lax.broadcasted_iota(jnp.int32, shape, 0)


def strip(i, size):
    return pl.ds(pl.multiple_of(i * size, size), size)


def head_place(h):
    two = (h == 2).astype(jnp.int32)
    one = (h >= 1).astype(jnp.int32)
    return two, 2 + 2 * two, 3 + two, 1 - two, HEAD * (one - two), HEAD * one


def each(count, step):
    def run(i, carry):
        step(i)
        return carry

    lax.fori_loop(0, count, run, 0)


class Place:
    def __init__(self, planes):
        self.planes = planes
        self.c = lax.axis_index("section")
        self.z = lax.axis_index("dp")
        self.t = lax.axis_index("tensor")
        self.y = lax.div(self.t, 2)
        self.r = lax.rem(self.t, 2)
        self.twin = (1 - self.c, self.z, self.t)
        self.above = (self.c, lax.rem(self.z + 1, planes), self.t)
        self.below = (self.c, lax.rem(self.z + planes - 1, planes), self.t)
        self.across = (self.c, self.z, lax.rem(self.t + 2, 4))
        self.beside = (self.c, self.z, self.t + 1 - 2 * self.r)
        self.relays = self.c == self.y
        self.encodes = self.r == 0
        self.decodes = self.r == 1

    def meet(self):
        barrier = pltpu.get_barrier_semaphore()
        peers = [self.above, self.below]
        for dc in range(2):
            for dt in range(4):
                if dc or dt:
                    peers.append((lax.rem(self.c + dc, 2), self.z, lax.rem(self.t + dt, 4)))
        for peer in peers:
            pl.semaphore_signal(barrier, inc=1, device_id=peer, device_id_type=MESH)
        pl.semaphore_wait(barrier, len(peers))


def push(source, goal, sent, got, device):
    return pltpu.make_async_remote_copy(
        src_ref=source, dst_ref=goal, send_sem=sent, recv_sem=got, device_id=device, device_id_type=MESH
    )


def both(first, second):
    return jnp.logical_and(first, second)


def center(values):
    middle = values - jnp.mean(values, axis=-1, keepdims=True)
    scale = lax.rsqrt(jnp.mean(middle * middle, axis=-1, keepdims=True) + EPSILON)
    return middle * scale, scale


def attend_block(h, p, o, lse, lse_row, bias, kx, qx, vt, causal):
    count = p.shape[0]
    qt, kt, vtile, ot, qlo, vlo = head_place(h)
    lane = lanes((count, TILE))
    in_q = both(lane >= qlo, lane < qlo + HEAD)
    in_v = both(lane >= vlo, lane < vlo + HEAD)
    spare = HEAD - qlo
    kx[...] = jnp.where(lane == spare, bias[...], jnp.where(in_q, p[:, strip(kt, TILE)], jnp.zeros((), LOW)))
    vt[...] = jnp.where(in_v, p[:, strip(vtile, TILE)].astype(WIDE), 1.0).T.astype(LOW)
    qx[...] = jnp.where(
        in_q, p[:, strip(qt, TILE)].astype(WIDE) * SCORE_SCALE, jnp.where(lane == spare, 1.0, 0.0)
    ).astype(LOW)
    scores = mm_nt(kx[...], qx[...])
    if causal:
        scores = jnp.where(subs(scores.shape) <= lanes(scores.shape), scores, NEG_FILL)
    top = jnp.max(scores, axis=0, keepdims=True)
    power = jnp.exp(scores - top).astype(LOW)
    out = mm(vt[...], power)
    total = jnp.where(vlo == 0, out[HEAD : HEAD + 1, :], out[0:1, :])
    result = (out / total).T
    o[:, strip(ot, TILE)] = jnp.where(in_v, result, o[:, strip(ot, TILE)].astype(WIDE)).astype(LOW)
    row = subs((8, count))
    lse[...] = jnp.where(row == lse_row, top + jnp.log(total), lse[...])


def forward_kernel(
    planes, self_in, crs_in, up_in, dn_in, x_in, cot_in, gain_in, bias_self, bias_cross,
    w_att, w_crs, w_up, w_dn, cot, first, p_self, o_self, lse_self, mid, second, act, slope, late, third,
    memory, p_cross, o_cross, lse_cross, gains_out,
    x_v, att_v, crs_v, up_v, dn_v, first_v, p_v, o_v, lse_v, mid_v, second_v, act_v, slope_v, late_v, memory_v,
    send_v, recv_v, gain_v, kx, qx, vt,
    x_sem, x_sent, z_got, z_sent, y_got, y_sent, c_sem,
    row_got, row_sent, fwd_sem, cot_got, ex_got, ex_sent, mem_got, mem_sent, mf_got, mf_sent, gain_sem, put_sem,
):
    at = Place(planes)
    c, z, t, y, r = at.c, at.z, at.t, at.y, at.r
    rows = x_in.shape[1]
    slot = x_v.shape[0]
    tiles = slot // BLOCK
    depth = up_in.shape[0]
    vmem = {"att": att_v, "crs": crs_v, "up": up_v, "dn": dn_v}
    shard = {"att": self_in, "up": up_in, "dn": dn_in}
    here = pl.ds(pl.multiple_of(z * depth, depth), depth)
    at.meet()

    relay_dev = (y, z, 2 * y + c)
    stays = both(c == y, r == c)

    def launch(g):
        i = GROUPS.index(g)
        goal = vmem[g].at[r, here, :]

        @pl.when(stays)
        def _():
            pltpu.make_async_copy(shard[g], goal, x_sem.at[i, r]).start()

        @pl.when(jnp.logical_not(stays))
        def _():
            push(shard[g], goal, x_sent.at[i], x_sem.at[i, r], relay_dev).start()

    crs_dev = (y, z, 2 * y + 1)
    crs_stays = both(c == y, r == 1)
    side = crs_in.shape[1]

    def crs_goal(block, section):
        return crs_v.at[block, here, pl.ds(pl.multiple_of((1 - section) * side, side), side)]

    def launch_crs():
        @pl.when(crs_stays)
        def _():
            pltpu.make_async_copy(crs_in, crs_goal(r, c), c_sem.at[r, c]).start()

        @pl.when(jnp.logical_not(crs_stays))
        def _():
            push(crs_in, crs_goal(r, c), x_sent.at[1], c_sem.at[r, c], crs_dev).start()

    row_goal = x_v.at[strip(t, rows), :]
    cot_goal = cot.at[strip(t, rows), :]

    def launch_rows(s):
        dev = (y, z, 2 * s + c)
        own = both(both(c == y, r == c), y == s)

        @pl.when(own)
        def _():
            pltpu.make_async_copy(x_in.at[s], row_goal, row_got.at[r]).start()

        @pl.when(jnp.logical_not(own))
        def _():
            push(x_in.at[s], row_goal, row_sent.at[s], row_got.at[r], dev).start()

    cot_stays = both(c == y, r == 1)

    def launch_cot():
        dev = (y, z, 2 * c + 1)

        @pl.when(cot_stays)
        def _():
            pltpu.make_async_copy(cot_in.at[c], cot_goal, cot_got.at[r]).start()

        @pl.when(jnp.logical_not(cot_stays))
        def _():
            push(cot_in.at[c], cot_goal, row_sent.at[2], cot_got.at[r], dev).start()

    gain_copy = push(gain_in, gain_v.at[c], gain_sem.at[0], gain_sem.at[1], at.twin)
    gain_copy.start()
    launch("att")
    launch_rows(0)
    launch_rows(1)
    launch_crs()
    launch("up")
    launch("dn")
    launch_cot()

    def piece(g, k):
        j = lax.rem(z - k + planes, planes)
        return vmem[g].at[:, pl.ds(pl.multiple_of(j * depth, depth), depth), :]

    def ring(g, k):
        i = GROUPS.index(g)
        return push(piece(g, k - 1), piece(g, k - 1), z_sent.at[i, k - 1], z_got.at[i, k - 1], at.above)

    def ring_in(g, k):
        i = GROUPS.index(g)
        return push(piece(g, k), piece(g, k), z_sent.at[i, k - 1], z_got.at[i, k - 1], at.above)

    def cross_over(g, k):
        i = GROUPS.index(g)
        return push(piece(g, k), piece(g, k), y_sent.at[i, k], y_got.at[i, k], at.across)

    def member(g):
        return both(at.relays, at.decodes) if g == "crs" else at.relays

    def listens(g):
        other = jnp.logical_not(at.relays)
        return both(other, at.decodes) if g == "crs" else other

    def arrive(g, k):
        i = GROUPS.index(g)
        if k:
            ring_in(g, k).wait_recv()
        elif g == "crs":
            for block in range(2):
                for section in range(2):
                    goal = crs_goal(block, section)
                    push(goal, goal, x_sent.at[1], c_sem.at[block, section], at.twin).wait_recv()
        else:
            for block in range(2):
                goal = vmem[g].at[block, here, :]
                push(goal, goal, x_sent.at[i], x_sem.at[i, block], at.twin).wait_recv()

    def relay_up(g, k):
        @pl.when(member(g))
        def _():
            arrive(g, k)
            if k + 1 < planes:
                ring(g, k + 1).start()

    def relay_over(g, k):
        @pl.when(member(g))
        def _():
            cross_over(g, k).start()

    def relay(g, k):
        relay_up(g, k)
        relay_over(g, k)

    def settle(g):
        @pl.when(listens(g))
        def _():
            for k in range(planes):
                cross_over(g, k).wait_recv()

    puts = []

    def put(source, goal):
        copy = pltpu.make_async_copy(source, goal, put_sem.at[len(puts)])
        copy.start()
        puts.append(copy)
        return copy

    relay("att", 0)
    half = pl.ds(pl.multiple_of(c * 2 * rows, 2 * rows), 2 * rows)
    far_half = pl.ds(pl.multiple_of((1 - c) * 2 * rows, 2 * rows), 2 * rows)
    for k in range(2):
        goal = x_v.at[strip(2 * c + k, rows), :]
        push(goal, goal, row_sent.at[0], row_got.at[k], at.twin).wait_recv()
    rows_on = push(x_v.at[half, :], x_v.at[half, :], fwd_sem.at[0], fwd_sem.at[1], at.twin)
    rows_on.start()
    relay("att", 1)
    push(gain_in, gain_v.at[1 - c], gain_sem.at[0], gain_sem.at[1], at.twin).wait_recv()
    gain_here = pltpu.make_async_copy(gain_in, gain_v.at[c], gain_sem.at[2])
    gain_here.start()
    gain_here.wait()
    gains = gain_v.at[r]
    push(x_v.at[far_half, :], x_v.at[far_half, :], fwd_sem.at[0], fwd_sem.at[1], at.twin).wait_recv()

    def enter(i):
        q = strip(i, BLOCK)
        first_v[q, :] = (center(x_v[q, :].astype(WIDE))[0] * gains[0:1, :]).astype(LOW)

    each(tiles, enter)
    put(first_v, first)
    relay("att", 2)
    relay("att", 3)

    @pl.when(at.decodes)
    def _():
        for k in range(2):
            goal = cot.at[strip(2 * c + k, rows), :]
            push(goal, goal, row_sent.at[2], cot_got.at[k], at.twin).wait_recv()
        push(cot.at[half, :], cot.at[half, :], fwd_sem.at[2], fwd_sem.at[3], at.twin).start()

    for k in range(4):
        relay("crs", k)
    relay("up", 0)
    settle("att")

    def project(source, weights, part):
        def run(i):
            q = strip(i, BLOCK)
            for b in range(2):
                if part != "kv":
                    p_v[b, q, 0:256] = mm(source[q, :], weights[b, :, 0:256]).astype(LOW)
                if part != "q":
                    p_v[b, q, 256:640] = mm(source[q, :], weights[b, :, 384:768]).astype(LOW)

        each(tiles, run)

    project(first_v, att_v, "all")
    p_put = put(p_v, p_self)
    o_v[...] = jnp.zeros_like(o_v)
    lse_v[...] = jnp.zeros_like(lse_v)
    relay("up", 1)

    def attend_half(b, bias, causal):
        def run(h):
            attend_block(h, p_v.at[b], o_v.at[b], lse_v, 3 * b + h, bias, kx, qx, vt, causal)

        each(3, run)

    for b in range(2):
        pl.when(at.encodes)(functools.partial(attend_half, b, bias_self, False))
        pl.when(at.decodes)(functools.partial(attend_half, b, bias_self, True))
        relay("up", 2 + b)
    relay("dn", 0)
    o_put = put(o_v, o_self)
    lse_put = put(lse_v, lse_self)

    def exchange(k, i):
        q = strip(i, BLOCK)
        return push(send_v.at[k, q, :], recv_v.at[k, q, :], ex_sent.at[k, i], ex_got.at[k, i], at.twin)

    def out_project(k, weights):
        def run(i):
            q = strip(i, BLOCK)
            part = mm_nt(o_v[0, q, :], weights[0, :, 128:384]) + mm_nt(o_v[1, q, :], weights[1, :, 128:384])
            send_v[k, q, :] = part.astype(LOW)
            exchange(k, i).start()

        each(tiles, run)

    def joined(k, i):
        q = strip(i, BLOCK)
        exchange(k, i).wait_recv()
        return send_v[k, q, :].astype(WIDE) + recv_v[k, q, :].astype(WIDE)

    out_project(0, att_v)
    relay("dn", 1)

    def middle(i):
        q = strip(i, BLOCK)
        value = x_v[q, :].astype(WIDE) + joined(0, i)
        mid_v[q, :] = value
        second_v[q, :] = (center(value)[0] * gains[1:2, :]).astype(LOW)

    each(tiles, middle)
    put(mid_v, mid)
    put(second_v, second)
    put(att_v, w_att)

    def mem_send(i):
        q = pl.ds(pl.multiple_of(c * 2 * BLOCK + i * BLOCK, BLOCK), BLOCK)
        return push(memory_v.at[q, :], memory_v.at[q, :], mem_sent.at[i], mem_got.at[i], at.beside)

    def mem_forward(i, core):
        q = pl.ds(pl.multiple_of(core * 2 * BLOCK + i * BLOCK, BLOCK), BLOCK)
        return push(memory_v.at[q, :], memory_v.at[q, :], mf_sent.at[i], mf_got.at[i], at.twin)

    settle("up")
    put(up_v, w_up)

    @pl.when(at.encodes)
    def _():
        def run(i):
            q = strip(i, BLOCK)
            for b in range(2):
                value, grade = gelu_parts(mm(second_v[q, :], up_v[b]))
                act_v[b, q, :] = value.astype(LOW)
                slope_v[b, q, :] = grade.astype(LOW)

        each(tiles, run)

    relay("dn", 2)
    relay("dn", 3)
    settle("dn")
    put(dn_v, w_dn)
    put(act_v, act)
    put(slope_v, slope)

    @pl.when(at.encodes)
    def _():
        def run(i):
            q = strip(i, BLOCK)
            part = mm_nt(act_v[0, q, :], dn_v[0]) + mm_nt(act_v[1, q, :], dn_v[1])
            send_v[1, q, :] = part.astype(LOW)
            exchange(1, i).start()

        each(tiles, run)

        def finish(n):
            i = lax.rem(n + 2 * c, 4)
            q = strip(i, BLOCK)
            value = mid_v[q, :] + joined(1, i)
            late_v[q, :] = value
            memory_v[q, :] = (center(value)[0] * gains[2:3, :]).astype(LOW)

            @pl.when(n < 2)
            def _():
                mem_send(n).start()

        each(tiles, finish)

    p_put.wait()
    o_put.wait()
    lse_put.wait()
    puts[0].wait()
    settle("crs")

    @pl.when(at.decodes)
    def _():
        project(second_v, crs_v, "q")
        for i in range(2):
            mem_send(i).wait_recv()
            mem_forward(i, c).start()
        for i in range(2):
            mem_forward(i, 1 - c).wait_recv()
        project(memory_v, crs_v, "kv")
        o_v[...] = jnp.zeros_like(o_v)
        lse_v[...] = jnp.zeros_like(lse_v)
        attend_half(0, bias_cross, False)
        attend_half(1, bias_cross, False)
        out_project(1, crs_v)

        def finish(i):
            q = strip(i, BLOCK)
            value = mid_v[q, :] + joined(1, i)
            late_v[q, :] = value
            first_v[q, :] = (center(value)[0] * gains[2:3, :]).astype(LOW)

        each(tiles, finish)

    put(crs_v, w_crs)
    put(p_v, p_cross)
    put(o_v, o_cross)
    put(lse_v, lse_cross)
    put(late_v, late)
    put(first_v, third)
    put(memory_v, memory)
    put(gains, gains_out)

    skip = (id(puts[0]), id(p_put), id(o_put), id(lse_put))
    for copy in puts:
        if id(copy) not in skip:
            copy.wait()
    gain_copy.wait_send()
    rows_on.wait_send()

    @pl.when(jnp.logical_not(stays))
    def _():
        for g in ("att", "up", "dn"):
            push(shard[g], vmem[g].at[r, here, :], x_sent.at[GROUPS.index(g)], x_sem.at[0, 0], relay_dev).wait_send()

    @pl.when(jnp.logical_not(crs_stays))
    def _():
        push(crs_in, crs_goal(r, c), x_sent.at[1], c_sem.at[0, 0], crs_dev).wait_send()

    for s in range(2):

        @pl.when(jnp.logical_not(both(both(c == y, r == c), y == s)))
        def _():
            push(x_in.at[s], row_goal, row_sent.at[s], row_got.at[r], at.twin).wait_send()

    @pl.when(jnp.logical_not(cot_stays))
    def _():
        push(cot_in.at[c], cot_goal, row_sent.at[2], cot_got.at[r], at.twin).wait_send()

    for g in GROUPS:

        @pl.when(member(g))
        def _():
            for k in range(1, planes):
                ring(g, k).wait_send()
            for k in range(planes):
                cross_over(g, k).wait_send()

    def drain(i):
        exchange(0, i).wait_send()
        exchange(1, i).wait_send()

    each(tiles, drain)

    @pl.when(at.encodes)
    def _():
        for i in range(2):
            mem_send(i).wait_send()

    @pl.when(at.decodes)
    def _():
        for i in range(2):
            mem_forward(i, c).wait_send()
        cot_on = push(cot.at[half, :], cot.at[half, :], fwd_sem.at[2], fwd_sem.at[3], at.twin)
        cot_on.wait_send()
        push(cot.at[far_half, :], cot.at[far_half, :], fwd_sem.at[2], fwd_sem.at[3], at.twin).wait_recv()


def forward_call(planes, slot, width, hidden, args):
    shape = jax.ShapeDtypeStruct
    weights = [(2, width, width), (2, width, width), (2, width, hidden), (2, width, hidden)]
    packed, outs, square = (2, slot, 640), (2, slot, 256), (slot, width)
    out_shape = (
        [shape(s, LOW) for s in weights]
        + [shape(square, LOW), shape(square, LOW), shape(packed, LOW), shape(outs, LOW), shape((8, slot), WIDE)]
        + [shape(square, WIDE), shape(square, LOW), shape((2, slot, hidden), LOW), shape((2, slot, hidden), LOW)]
        + [shape(square, WIDE), shape(square, LOW), shape(square, LOW)]
        + [shape(packed, LOW), shape(outs, LOW), shape((8, slot), WIDE), shape((8, width), WIDE)]
    )
    groups = len(GROUPS)
    dma = pltpu.SemaphoreType.DMA
    scratch = (
        [pltpu.VMEM(square, LOW)]
        + [pltpu.VMEM(s, LOW) for s in weights]
        + [pltpu.VMEM(square, LOW), pltpu.VMEM(packed, LOW), pltpu.VMEM(outs, LOW), pltpu.VMEM((8, slot), WIDE)]
        + [pltpu.VMEM(square, WIDE), pltpu.VMEM(square, LOW)]
        + [pltpu.VMEM((2, slot, hidden), LOW)] * 2
        + [pltpu.VMEM(square, WIDE), pltpu.VMEM(square, LOW)]
        + [pltpu.VMEM((2,) + square, LOW)] * 2
        + [pltpu.VMEM((2, 8, width), WIDE)]
        + [pltpu.VMEM((slot, TILE), LOW)] * 2
        + [pltpu.VMEM((TILE, slot), LOW)]
        + [dma((groups, 2)), dma((groups,)), dma((groups, planes)), dma((groups, planes))]
        + [dma((groups, planes)), dma((groups, planes)), dma((2, 2))]
        + [dma((2,)), dma((3,)), dma((4,)), dma((2,)), dma((2, 4)), dma((2, 4))]
        + [dma((2,)), dma((2,)), dma((2,)), dma((2,)), dma((3,)), dma((24,))]
    )
    any_spec = pl.BlockSpec(memory_space=pl.ANY)
    vmem_spec = pl.BlockSpec(memory_space=pltpu.VMEM)
    return pl.pallas_call(
        functools.partial(forward_kernel, planes),
        out_shape=out_shape,
        in_specs=[any_spec] * 6 + [vmem_spec] * 3,
        out_specs=[any_spec] * len(out_shape),
        scratch_shapes=scratch,
        compiler_params=pltpu.CompilerParams(collective_id=0, has_side_effects=True, vmem_limit_bytes=VMEM_BYTES),
    )(*args)


def ring_gather(lay, shard):
    planes = lay.planes
    rows = shard.shape[1]
    if planes > 4:
        piece = lax.all_gather(shard, "dp", axis=1, tiled=True)
        across = lay.route(piece, lambda c, z, t: (c, z, (t + 2) % 4) if c == t // 2 else None)
        return jnp.where(lay.relays, piece, across)
    relay = lambda c, z, t: (c, (z + 1) % planes, t) if c == t // 2 else None
    whole = jnp.zeros((shard.shape[0], planes * rows, shard.shape[2]), shard.dtype)
    piece = shard
    for step in range(planes):
        across = lay.route(piece, lambda c, z, t: (c, z, (t + 2) % 4) if c == t // 2 else None)
        chosen = jnp.where(lay.relays, piece, across)
        whole = lax.dynamic_update_slice(whole, chosen, (0, ((lay.plane - step) % planes) * rows, 0))
        if step + 1 < planes:
            piece = lay.route(piece, relay)
    return whole


def ring_scatter(lay, total, holder):
    planes = lay.planes
    rows = total.shape[1] // planes
    low = total.astype(LOW)
    across = lay.route(
        low, lambda c, z, t: (c, z, (t + 2) % 4) if (c != t // 2 and t % 2 == holder) else None
    )
    summed = low.astype(WIDE) + across.astype(WIDE)
    if planes > 4:
        return lax.psum_scatter(summed.astype(LOW), "dp", scatter_dimension=1, tiled=True)
    relay = lambda c, z, t: (c, (z + 1) % planes, t) if (c == t // 2 and t % 2 == holder) else None
    take = lambda j: lax.dynamic_slice_in_dim(summed, (j % planes) * rows, rows, 1)
    running = take(lay.plane - 1)
    for step in range(1, planes):
        running = lay.route(running.astype(LOW), relay).astype(WIDE) + take(lay.plane - 1 - step)
    return running.astype(LOW)


def hand_back(lay, value, holder, section):
    same = lay.route(
        value[0], lambda c, z, t: (section, z, t) if (c == t // 2 and t % 2 == holder) else None
    )
    beside = lay.route(
        value[1], lambda c, z, t: (section, z, t ^ 1) if (c == t // 2 and t % 2 == holder) else None
    )
    return same.astype(WIDE) + beside.astype(WIDE)


def general_body(block_input, w_self, w_self_out, w_cross, w_up, w_down, norm_gains, lengths, task_mask, out_grad):
    lay = Layout()
    seqs, rows, width = block_input.shape[1:]
    slot = rows * lay.chips
    sec = lay.core
    item = lay.item

    def spread(value, first):
        pick = value[jnp.where(first, lay.chip % 2, 1 - lay.chip % 2)]
        flip = 0 if first else 1
        return lay.route(pick, lambda c, z, t: (t // 2, z, 2 * ((t % 2) ^ flip) + c))

    def merge_rows(mine, theirs):
        low_half = jnp.where(lay.core == 0, mine, theirs)
        high_half = jnp.where(lay.core == 0, theirs, mine)
        return jnp.concatenate([low_half[0], low_half[1], high_half[0], high_half[1]], axis=0)

    first = spread(block_input[0], True)
    second = spread(block_input[0], False)
    mine = jnp.where(item == 0, jnp.stack([first, second]), jnp.stack([second, first]))
    x_rows = merge_rows(mine, lay.other_core(mine)).astype(WIDE)

    picked = out_grad[lay.core]
    even = lay.route(picked, lambda c, z, t: (t // 2, z, 2 * c + 1) if t % 2 == 0 else None)
    odd = lay.route(picked, lambda c, z, t: (t // 2, z, 2 * c + 1) if t % 2 == 1 else None)
    mine = jnp.stack([even, odd])
    cotangent = merge_rows(mine, lay.other_core(mine))

    gains_here = norm_gains[0].astype(WIDE)
    gains = jnp.where(sec == lay.role, gains_here, lay.other_core(norm_gains[0]).astype(WIDE))

    depth = w_self.shape[1]
    wide = w_self.shape[3]
    self_block = pack_heads(
        {"q": w_self[0, :, 0], "k": w_self[0, :, 1], "v": w_self[0, :, 2], "o": w_self_out[0].T}
    )
    feed_block = jnp.concatenate([w_up[0], w_down[0].T], axis=1)
    cross_block = w_cross[0].reshape(depth, 2 * wide)

    def collect(block):
        same = lay.route(block, lambda c, z, t: (t // 2, z, t) if c == t % 2 else None)
        beside = lay.route(block, lambda c, z, t: (t // 2, z, t ^ 1) if c != t % 2 else None)
        return jnp.stack([same, beside])

    def collect_cross(block, section):
        same = lay.route(block, lambda c, z, t: (t // 2, z, t) if (c == section and t % 2 == 1) else None)
        beside = lay.route(block, lambda c, z, t: (t // 2, z, t ^ 1) if (c == section and t % 2 == 0) else None)
        return same, beside

    w_att = ring_gather(lay, collect(self_block))
    w_ffn = ring_gather(lay, collect(feed_block))
    memory_side = collect_cross(cross_block, 0)
    query_side = collect_cross(cross_block, 1)
    w_crs = ring_gather(
        lay,
        jnp.stack(
            [
                pack_heads({"q": q[:, :wide], "k": m[:, :wide], "v": m[:, wide:], "o": q[:, wide:]})
                for m, q in zip(memory_side, query_side)
            ]
        ),
    )
    hidden = w_up.shape[2]
    part = lambda w, name: jnp.concatenate([unpack_heads(w[0], name), unpack_heads(w[1], name)], axis=1)
    att = {n: part(w_att, n) for n in "qkvo"}
    crs = {n: part(w_crs, n) for n in "qkvo"}
    up = jnp.concatenate([w_ffn[0, :, :hidden], w_ffn[1, :, :hidden]], axis=1)
    down_t = jnp.concatenate([w_ffn[0, :, hidden:], w_ffn[1, :, hidden:]], axis=1)

    positions = jnp.arange(slot)
    own_length = jnp.where(lay.is_decoder, lengths[1, item], lengths[0, item])
    self_allowed = (positions[None, :] < own_length) & (
        (positions[None, :] <= positions[:, None]) | jnp.logical_not(lay.is_decoder)
    )
    cross_allowed = jnp.broadcast_to(
        ((positions < lengths[0, item]) & (task_mask[item] == 1))[None], (slot, slot)
    )

    def joined(partial):
        low = partial.astype(LOW)
        return low.astype(WIDE) + lay.other_core(low).astype(WIDE)

    normed0 = layer_norm(x_rows, gains[0]).astype(LOW)
    q, k, v = (mm(normed0, att[n]).astype(LOW) for n in "qkv")
    out_self, lse_self = attend(q, k, v, self_allowed)
    x_mid = x_rows + joined(mm_nt(out_self, att["o"]))
    normed1 = layer_norm(x_mid, gains[1]).astype(LOW)

    pre_enc = mm(normed1, up)
    act_enc, slope_enc = gelu_parts(pre_enc)
    act_enc = act_enc.astype(LOW)
    x_late_enc = x_mid + joined(mm_nt(act_enc, down_t))
    memory_enc = layer_norm(x_late_enc, gains[2]).astype(LOW)
    memory = lay.route(memory_enc, lambda c, z, t: (c, z, t ^ 1) if t % 2 == 0 else None)

    cq = mm(normed1, crs["q"]).astype(LOW)
    ck, cv = (mm(memory, crs[n]).astype(LOW) for n in "kv")
    out_cross, lse_cross = attend(cq, ck, cv, cross_allowed)
    x_late = x_mid + joined(mm_nt(out_cross, crs["o"]))
    normed2 = layer_norm(x_late, gains[2]).astype(LOW)
    pre_dec = mm(normed2, up)
    act_dec, slope_dec = gelu_parts(pre_dec)
    act_dec = act_dec.astype(LOW)
    result_dec = (x_late + joined(mm_nt(act_dec, down_t))).astype(LOW)

    d_out = cotangent.astype(WIDE)
    d_pre = (slope_dec * mm(cotangent, down_t)).astype(LOW)
    d_ffn_dec = jnp.concatenate([mm_tn(normed2, d_pre), mm_tn(cotangent, act_dec)], axis=1)
    d_late_norm, d_gain2_dec = norm_back(x_late, gains[2], joined(mm_nt(d_pre, up)))
    d_late = d_out + d_late_norm
    grad_late = d_late.astype(LOW)
    d_att = mm(grad_late, crs["o"]).astype(LOW)
    d_cq, d_ck, d_cv = attend_back(cq, ck, cv, lse_cross, d_att, cross_allowed)
    d_memory = joined(mm_nt(d_ck, crs["k"]) + mm_nt(d_cv, crs["v"]))
    d_crs = {
        "q": mm_tn(normed1, d_cq),
        "k": mm_tn(memory, d_ck),
        "v": mm_tn(memory, d_cv),
        "o": mm_tn(grad_late, out_cross),
    }
    d_mid_norm, d_gain1_dec = norm_back(x_mid, gains[1], joined(mm_nt(d_cq, crs["q"])))
    d_mid_dec = d_late + d_mid_norm

    d_memory = lay.route(d_memory.astype(LOW), lambda c, z, t: (c, z, t ^ 1) if t % 2 == 1 else None).astype(WIDE)
    d_late_enc, d_gain2_enc = norm_back(x_late_enc, gains[2], d_memory)
    grad_late_enc = d_late_enc.astype(LOW)
    d_pre = (slope_enc * mm(grad_late_enc, down_t)).astype(LOW)
    d_ffn_enc = jnp.concatenate([mm_tn(normed1, d_pre), mm_tn(grad_late_enc, act_enc)], axis=1)
    d_mid_norm, d_gain1_enc = norm_back(x_mid, gains[1], joined(mm_nt(d_pre, up)))
    d_mid_enc = d_late_enc + d_mid_norm

    d_mid = jnp.where(lay.is_decoder, d_mid_dec, d_mid_enc)
    grad_mid = d_mid.astype(LOW)
    d_att = mm(grad_mid, att["o"]).astype(LOW)
    d_q, d_k, d_v = attend_back(q, k, v, lse_self, d_att, self_allowed)
    d_norm = joined(mm_nt(d_q, att["q"]) + mm_nt(d_k, att["k"]) + mm_nt(d_v, att["v"]))
    d_att_w = {
        "q": mm_tn(normed0, d_q),
        "k": mm_tn(normed0, d_k),
        "v": mm_tn(normed0, d_v),
        "o": mm_tn(grad_mid, out_self),
    }
    d_first, d_gain0 = norm_back(x_rows, gains[0], d_norm)
    d_rows = d_mid + d_first

    half = 3 * HEAD

    def blocks(parts):
        return jnp.stack(
            [pack_heads({n: parts[n][:, half * b : half * (b + 1)] for n in parts}) for b in range(2)]
        )

    def feed_blocks(both):
        total = both.shape[1] // 2
        return jnp.stack(
            [
                jnp.concatenate(
                    [both[:, hidden * b : hidden * (b + 1)], both[:, total + hidden * b : total + hidden * (b + 1)]],
                    axis=1,
                )
                for b in range(2)
            ]
        )

    self_total = blocks(d_att_w)
    home_self = hand_back(lay, ring_scatter(lay, self_total, 0), 0, 0) + hand_back(
        lay, ring_scatter(lay, self_total, 1), 1, 1
    )
    home_feed = hand_back(lay, ring_scatter(lay, feed_blocks(d_ffn_enc), 0), 0, 0) + hand_back(
        lay, ring_scatter(lay, feed_blocks(d_ffn_dec), 1), 1, 1
    )
    cross_total = ring_scatter(lay, blocks(d_crs), 1)
    side = lambda names: jnp.stack(
        [jnp.concatenate([unpack_heads(cross_total[b], n) for n in names], axis=1) for b in range(2)]
    )
    home_cross = hand_back(lay, side("kv"), 1, 0) + hand_back(lay, side("qo"), 1, 1)

    g_self = jnp.stack([unpack_heads(home_self, n) for n in "qkv"], axis=1)[None]
    g_self_out = unpack_heads(home_self, "o").T[None]
    g_cross = home_cross.reshape(1, depth, 2, wide)
    g_up = home_feed[:, :hidden][None]
    g_down = home_feed[:, hidden:].T[None]

    gain2 = jnp.where(lay.is_decoder, d_gain2_dec, d_gain2_enc)
    gain1 = jnp.where(lay.is_decoder, d_gain1_dec, d_gain1_enc)
    gain_rows = jnp.stack([d_gain0, gain1, gain2])
    slots = jnp.stack(
        [
            jnp.where((lay.role == r) & (lay.core == 0), gain_rows, 0.0)
            for r in range(2)
        ]
    )
    gain_total = lax.psum(slots, AXES)[sec][None]

    def rows_home(value):
        mine = lax.dynamic_slice_in_dim(value, lay.core * 2 * rows, 2 * rows, 0).reshape(2, rows, width)
        a = lay.route(mine[item], lambda c, z, t: (t % 2, z, 2 * c + t // 2))
        b = lay.route(mine[1 - item], lambda c, z, t: (t % 2, z, 2 * c + 1 - t // 2))
        even = lay.chip % 2 == 0
        return jnp.where(even, jnp.stack([a, b]), jnp.stack([b, a]))[None]

    block_output = rows_home(jnp.where(lay.is_decoder, result_dec, memory_enc))
    input_grad = rows_home(d_rows.astype(LOW)).astype(WIDE)
    return (
        block_output,
        input_grad,
        g_self,
        g_self_out,
        g_cross,
        g_up,
        g_down,
        gain_total[:, :2],
        gain_total[:, 2],
    )


def body(block_input, w_self, w_self_out, w_cross, w_up, w_down, norm_gains, lengths, task_mask, out_grad):
    lay = Layout()
    seqs, rows, width = block_input.shape[1:]
    slot = rows * lay.chips
    sec = lay.core
    item = lay.item

    if lay.planes != 4:
        return general_body(
            block_input, w_self, w_self_out, w_cross, w_up, w_down, norm_gains, lengths, task_mask, out_grad
        )

    depth = w_self.shape[1]
    wide = w_self.shape[3]
    hidden = w_up.shape[2]
    self_block = pack_heads(
        {"q": w_self[0, :, 0], "k": w_self[0, :, 1], "v": w_self[0, :, 2], "o": w_self_out[0].T}
    )
    pair = {"q": w_cross[0, :, 0], "o": w_cross[0, :, 1], "k": w_cross[0, :, 0], "v": w_cross[0, :, 1]}
    pieces = [pair[n][:, HEAD * h : HEAD * (h + 1)] for n, h in ORDER]
    cross_block = jnp.where(
        sec == 1, jnp.concatenate(pieces[:6], axis=1), jnp.concatenate(pieces[6:], axis=1)
    )
    gain_block = jnp.concatenate([norm_gains[0].astype(WIDE), jnp.zeros((5, width), WIDE)], axis=0)

    positions = jnp.arange(slot)
    own_length = jnp.where(lay.is_decoder, lengths[1, item], lengths[0, item])
    self_allowed = (positions[None, :] < own_length) & (
        (positions[None, :] <= positions[:, None]) | jnp.logical_not(lay.is_decoder)
    )
    cross_allowed = jnp.broadcast_to(
        ((positions < lengths[0, item]) & (task_mask[item] == 1))[None], (slot, slot)
    )

    def key_bias(allowed):
        return jnp.broadcast_to(jnp.where(allowed, 0.0, NEG_FILL)[:, None], (slot, TILE)).astype(LOW)

    (
        w_att, w_crs, w_up_all, w_dn_all, cotangent, normed0, p_self, o_self, lse_self, x_mid, normed1, act, slope,
        x_late, normed2, memory, p_cross, o_cross, lse_cross, gains,
    ) = forward_call(
        lay.planes,
        slot,
        width,
        hidden,
        (
            self_block,
            cross_block,
            w_up[0],
            w_down[0].T,
            block_input[0],
            out_grad,
            gain_block,
            key_bias(positions < own_length),
            key_bias((positions < lengths[0, item]) & (task_mask[item] == 1)),
        ),
    )

    def joined(partial):
        low = partial.astype(LOW)
        return low.astype(WIDE) + lay.other_core(low).astype(WIDE)

    part = lambda w, name: jnp.concatenate([unpack_heads(w[0], name), unpack_heads(w[1], name)], axis=1)
    att = {n: part(w_att, n) for n in "qkvo"}
    crs = {n: part(w_crs, n) for n in "qkvo"}
    up = jnp.concatenate([w_up_all[0], w_up_all[1]], axis=1)
    down_t = jnp.concatenate([w_dn_all[0], w_dn_all[1]], axis=1)
    pick = lambda p, cuts: jnp.concatenate([p[b][:, i : i + HEAD] for b in range(2) for i in cuts], axis=1)
    q, k, v = pick(p_self, (0, 64, 128)), pick(p_self, (256, 320, 512)), pick(p_self, (384, 448, 576))
    cq, ck, cv = pick(p_cross, (0, 64, 128)), pick(p_cross, (256, 320, 512)), pick(p_cross, (384, 448, 576))
    out_self, out_cross = pick(o_self, (128, 192, 64)), pick(o_cross, (128, 192, 64))
    lse_self, lse_cross = lse_self[:6, :, None], lse_cross[:6, :, None]
    act_enc, slope_enc = (jnp.concatenate([v_[0], v_[1]], axis=1) for v_ in (act, slope))
    x_late_enc = x_late
    memory_enc = memory
    def spread(value, first):
        pick = value[jnp.where(first, lay.chip % 2, 1 - lay.chip % 2)]
        flip = 0 if first else 1
        return lay.route(pick, lambda c, z, t: (t // 2, z, 2 * ((t % 2) ^ flip) + c))

    def merge_rows(mine, theirs):
        low_half = jnp.where(lay.core == 0, mine, theirs)
        high_half = jnp.where(lay.core == 0, theirs, mine)
        return jnp.concatenate([low_half[0], low_half[1], high_half[0], high_half[1]], axis=0)

    first = spread(block_input[0], True)
    second = spread(block_input[0], False)
    mine = jnp.where(item == 0, jnp.stack([first, second]), jnp.stack([second, first]))
    x_rows = merge_rows(mine, lay.other_core(mine)).astype(WIDE)

    pre_dec = mm(normed2, up)
    act_dec, slope_dec = gelu_parts(pre_dec)
    act_dec = act_dec.astype(LOW)
    result_dec = (x_late + joined(mm_nt(act_dec, down_t))).astype(LOW)

    d_out = cotangent.astype(WIDE)
    d_pre = (slope_dec * mm(cotangent, down_t)).astype(LOW)
    d_ffn_dec = jnp.concatenate([mm_tn(normed2, d_pre), mm_tn(cotangent, act_dec)], axis=1)
    d_late_norm, d_gain2_dec = norm_back(x_late, gains[2], joined(mm_nt(d_pre, up)))
    d_late = d_out + d_late_norm
    grad_late = d_late.astype(LOW)
    d_att = mm(grad_late, crs["o"]).astype(LOW)
    d_cq, d_ck, d_cv = attend_back(cq, ck, cv, lse_cross, d_att, cross_allowed)
    d_memory = joined(mm_nt(d_ck, crs["k"]) + mm_nt(d_cv, crs["v"]))
    d_crs = {
        "q": mm_tn(normed1, d_cq),
        "k": mm_tn(memory, d_ck),
        "v": mm_tn(memory, d_cv),
        "o": mm_tn(grad_late, out_cross),
    }
    d_mid_norm, d_gain1_dec = norm_back(x_mid, gains[1], joined(mm_nt(d_cq, crs["q"])))
    d_mid_dec = d_late + d_mid_norm

    d_memory = lay.route(d_memory.astype(LOW), lambda c, z, t: (c, z, t ^ 1) if t % 2 == 1 else None).astype(WIDE)
    d_late_enc, d_gain2_enc = norm_back(x_late_enc, gains[2], d_memory)
    grad_late_enc = d_late_enc.astype(LOW)
    d_pre = (slope_enc * mm(grad_late_enc, down_t)).astype(LOW)
    d_ffn_enc = jnp.concatenate([mm_tn(normed1, d_pre), mm_tn(grad_late_enc, act_enc)], axis=1)
    d_mid_norm, d_gain1_enc = norm_back(x_mid, gains[1], joined(mm_nt(d_pre, up)))
    d_mid_enc = d_late_enc + d_mid_norm

    d_mid = jnp.where(lay.is_decoder, d_mid_dec, d_mid_enc)
    grad_mid = d_mid.astype(LOW)
    d_att = mm(grad_mid, att["o"]).astype(LOW)
    d_q, d_k, d_v = attend_back(q, k, v, lse_self, d_att, self_allowed)
    d_norm = joined(mm_nt(d_q, att["q"]) + mm_nt(d_k, att["k"]) + mm_nt(d_v, att["v"]))
    d_att_w = {
        "q": mm_tn(normed0, d_q),
        "k": mm_tn(normed0, d_k),
        "v": mm_tn(normed0, d_v),
        "o": mm_tn(grad_mid, out_self),
    }
    d_first, d_gain0 = norm_back(x_rows, gains[0], d_norm)
    d_rows = d_mid + d_first

    half = 3 * HEAD

    def flip(v):
        return jnp.where(lay.role == 0, v, v[::-1])

    def blocks(parts):
        return flip(jnp.stack(
            [pack_heads({n: parts[n][:, half * b : half * (b + 1)] for n in parts}) for b in range(2)]
        ))

    def feed_blocks(both):
        total = both.shape[1] // 2
        return flip(jnp.stack(
            [
                jnp.concatenate(
                    [both[:, hidden * b : hidden * (b + 1)], both[:, total + hidden * b : total + hidden * (b + 1)]],
                    axis=1,
                )
                for b in range(2)
            ]
        ))

    self_total = blocks(d_att_w)
    home_self = hand_back(lay, ring_scatter(lay, self_total, 0), 0, 0) + hand_back(
        lay, ring_scatter(lay, self_total, 1), 1, 1
    )
    home_feed = hand_back(lay, ring_scatter(lay, feed_blocks(d_ffn_enc), 0), 0, 0) + hand_back(
        lay, ring_scatter(lay, feed_blocks(d_ffn_dec), 1), 1, 1
    )
    cross_total = ring_scatter(lay, blocks(d_crs), 1)
    side = lambda names: jnp.stack(
        [jnp.concatenate([unpack_heads(cross_total[b], n) for n in names], axis=1) for b in range(2)]
    )
    home_cross = hand_back(lay, side("kv"), 1, 0) + hand_back(lay, side("qo"), 1, 1)

    g_self = jnp.stack([unpack_heads(home_self, n) for n in "qkv"], axis=1)[None]
    g_self_out = unpack_heads(home_self, "o").T[None]
    g_cross = home_cross.reshape(1, depth, 2, wide)
    g_up = home_feed[:, :hidden][None]
    g_down = home_feed[:, hidden:].T[None]

    gain2 = jnp.where(lay.is_decoder, d_gain2_dec, d_gain2_enc)
    gain1 = jnp.where(lay.is_decoder, d_gain1_dec, d_gain1_enc)
    gain_rows = jnp.stack([d_gain0, gain1, gain2])
    slots = jnp.stack(
        [
            jnp.where((lay.role == r) & (lay.core == 0), gain_rows, 0.0)
            for r in range(2)
        ]
    )
    gain_total = lax.psum(slots, AXES)[sec][None]

    def rows_home(value):
        mine = lax.dynamic_slice_in_dim(value, lay.core * 2 * rows, 2 * rows, 0).reshape(2, rows, width)
        a = lay.route(mine[item], lambda c, z, t: (t % 2, z, 2 * c + t // 2))
        b = lay.route(mine[1 - item], lambda c, z, t: (t % 2, z, 2 * c + 1 - t // 2))
        even = lay.chip % 2 == 0
        return jnp.where(even, jnp.stack([a, b]), jnp.stack([b, a]))[None]

    block_output = rows_home(jnp.where(lay.is_decoder, result_dec, memory_enc))
    input_grad = rows_home(d_rows.astype(LOW)).astype(WIDE)
    return (
        block_output,
        input_grad,
        g_self,
        g_self_out,
        g_cross,
        g_up,
        g_down,
        gain_total[:, :2],
        gain_total[:, 2],
    )


def solution(mesh):
    placed = (
        P("section", "dp", "tensor", None),
        P("section", "dp", None, "tensor"),
        P("section", "tensor", "dp"),
        P("section", "dp", None, "tensor"),
        P("section", "dp", "tensor"),
        P("section", "tensor", "dp"),
        P("section", None, None),
        P(None, "dp"),
        P("dp", None),
        P("dp", "tensor", None),
    )
    return jax.shard_map(
        body,
        mesh=mesh,
        in_specs=placed,
        out_specs=(
            P("section", "dp", "tensor", None),
            P("section", "dp", "tensor", None),
            P("section", "dp", None, "tensor"),
            P("section", "tensor", "dp"),
            P("section", "dp", None, "tensor"),
            P("section", "dp", "tensor"),
            P("section", "tensor", "dp"),
            P("section", None, None),
            P("section", None),
        ),
        check_vma=False,
    )
```

```python
import functools

import jax
import jax.numpy as jnp
from jax import lax
from jax.experimental import pallas as pl
from jax.experimental.pallas import tpu as pltpu
from jax.sharding import PartitionSpec as P

HEAD = 64
TILE = 128
EPSILON = 1e-05
SCORE_SCALE = 0.125
NEG_FILL = -1000000000.0
AXES = ("section", "dp", "tensor")
LOW = jnp.bfloat16
WIDE = jnp.float32


class Layout:
    def __init__(self):
        self.cores = lax.axis_size("section")
        self.planes = lax.axis_size("dp")
        self.chips = lax.axis_size("tensor")
        self.core = lax.axis_index("section")
        self.plane = lax.axis_index("dp")
        self.chip = lax.axis_index("tensor")
        self.role = self.chip % 2
        self.item = self.chip // 2
        self.is_decoder = self.role == 1
        self.relays = self.core == self.item

    def route(self, value, target):
        pairs = []
        for core in range(self.cores):
            for plane in range(self.planes):
                for chip in range(self.chips):
                    to = target(core, plane, chip)
                    if to is None:
                        continue
                    source = (core * self.planes + plane) * self.chips + chip
                    goal = (to[0] * self.planes + to[1]) * self.chips + to[2]
                    pairs.append((source, goal))
        return lax.ppermute(value, AXES, pairs)

    def other_core(self, value):
        return self.route(value, lambda c, z, t: (1 - c, z, t))


def normalize(values):
    centred = values - jnp.mean(values, axis=-1, keepdims=True)
    spread = jnp.mean(centred * centred, axis=-1, keepdims=True)
    scale = lax.rsqrt(spread + EPSILON)
    return centred * scale, scale


def layer_norm(values, gain):
    return normalize(values)[0] * gain


def norm_back(values, gain, grad):
    normal, scale = normalize(values)
    scaled = grad * gain
    first = jnp.mean(scaled, axis=-1, keepdims=True)
    second = jnp.mean(scaled * normal, axis=-1, keepdims=True)
    return (scaled - first - normal * second) * scale, jnp.sum(grad * normal, axis=0)


ORDER = (("q", 0), ("q", 1), ("q", 2), ("o", 2), ("o", 0), ("o", 1), ("k", 0), ("k", 1), ("v", 0), ("v", 1), ("k", 2), ("v", 2))


def pack_heads(parts):
    return jnp.concatenate([parts[n][:, HEAD * h : HEAD * (h + 1)] for n, h in ORDER], axis=1)


def unpack_heads(block, name):
    where = {(n, h): i for i, (n, h) in enumerate(ORDER)}
    return jnp.concatenate(
        [block[:, HEAD * where[(name, h)] : HEAD * (where[(name, h)] + 1)] for h in range(3)], axis=1
    )


def mm(left, right):
    return jnp.dot(left, right, preferred_element_type=WIDE)


def mm_nt(left, right):
    return lax.dot_general(left, right, (((1,), (1,)), ((), ())), preferred_element_type=WIDE)


def mm_tn(left, right):
    return lax.dot_general(left, right, (((0,), (0,)), ((), ())), preferred_element_type=WIDE)


def split_heads(value):
    return value.reshape(value.shape[0], -1, HEAD)


def attend(q, k, v, allowed):
    scores = jnp.einsum("qhd,khd->hqk", split_heads(q), split_heads(k), preferred_element_type=WIDE) * SCORE_SCALE
    scores = jnp.where(allowed[None], scores, NEG_FILL)
    top = jnp.max(scores, axis=-1, keepdims=True)
    power = jnp.exp(scores - top)
    total = jnp.sum(power, axis=-1, keepdims=True)
    probs = (power / total).astype(LOW)
    out = jnp.einsum("hqk,khd->qhd", probs, split_heads(v), preferred_element_type=WIDE)
    return out.astype(LOW).reshape(q.shape), top + jnp.log(total)


def attend_back(q, k, v, log_sum, d_out, allowed):
    scores = jnp.einsum("qhd,khd->hqk", split_heads(q), split_heads(k), preferred_element_type=WIDE) * SCORE_SCALE
    scores = jnp.where(allowed[None], scores, NEG_FILL)
    probs = jnp.exp(scores - log_sum)
    d_probs = jnp.einsum("qhd,khd->hqk", split_heads(d_out), split_heads(v), preferred_element_type=WIDE)
    inner = jnp.sum(probs * d_probs, axis=-1, keepdims=True)
    d_scores = (probs * (d_probs - inner)).astype(LOW)
    d_v = jnp.einsum("hqk,qhd->khd", probs.astype(LOW), split_heads(d_out), preferred_element_type=WIDE)
    d_q = jnp.einsum("hqk,khd->qhd", d_scores, split_heads(k), preferred_element_type=WIDE) * SCORE_SCALE
    d_k = jnp.einsum("hqk,qhd->khd", d_scores, split_heads(q), preferred_element_type=WIDE) * SCORE_SCALE
    return tuple(g.astype(LOW).reshape(q.shape) for g in (d_q, d_k, d_v))


def gelu_parts(value):
    coef = 0.7978845608028654
    cube = 0.044715
    inner = coef * (value + cube * value * value * value)
    soft = jnp.tanh(inner)
    slope = 0.5 * (1.0 + soft) + 0.5 * value * (1.0 - soft * soft) * coef * (1.0 + 3.0 * cube * value * value)
    return 0.5 * value * (1.0 + soft), slope


MESH = pl.DeviceIdType.MESH
GROUPS = ("att", "crs", "up", "dn")
BLOCK = 256
VMEM_BYTES = 62 * 2**20


def lanes(shape):
    return lax.broadcasted_iota(jnp.int32, shape, len(shape) - 1)


def subs(shape):
    return lax.broadcasted_iota(jnp.int32, shape, 0)


def strip(i, size):
    return pl.ds(pl.multiple_of(i * size, size), size)


def head_place(h):
    two = (h == 2).astype(jnp.int32)
    one = (h >= 1).astype(jnp.int32)
    return two, 2 + 2 * two, 3 + two, 1 - two, HEAD * (one - two), HEAD * one


def each(count, step):
    def run(i, carry):
        step(i)
        return carry

    lax.fori_loop(0, count, run, 0)


class Place:
    def __init__(self, planes):
        self.planes = planes
        self.c = lax.axis_index("section")
        self.z = lax.axis_index("dp")
        self.t = lax.axis_index("tensor")
        self.y = lax.div(self.t, 2)
        self.r = lax.rem(self.t, 2)
        self.twin = (1 - self.c, self.z, self.t)
        self.above = (self.c, lax.rem(self.z + 1, planes), self.t)
        self.below = (self.c, lax.rem(self.z + planes - 1, planes), self.t)
        self.across = (self.c, self.z, lax.rem(self.t + 2, 4))
        self.beside = (self.c, self.z, self.t + 1 - 2 * self.r)
        self.relays = self.c == self.y
        self.encodes = self.r == 0
        self.decodes = self.r == 1

    def meet(self):
        barrier = pltpu.get_barrier_semaphore()
        peers = [self.above, self.below]
        for dc in range(2):
            for dt in range(4):
                if dc or dt:
                    peers.append((lax.rem(self.c + dc, 2), self.z, lax.rem(self.t + dt, 4)))
        for peer in peers:
            pl.semaphore_signal(barrier, inc=1, device_id=peer, device_id_type=MESH)
        pl.semaphore_wait(barrier, len(peers))


def push(source, goal, sent, got, device):
    return pltpu.make_async_remote_copy(
        src_ref=source, dst_ref=goal, send_sem=sent, recv_sem=got, device_id=device, device_id_type=MESH
    )


def both(first, second):
    return jnp.logical_and(first, second)


def center(values):
    middle = values - jnp.mean(values, axis=-1, keepdims=True)
    scale = lax.rsqrt(jnp.mean(middle * middle, axis=-1, keepdims=True) + EPSILON)
    return middle * scale, scale


def attend_block(h, p, o, lse, lse_row, bias, kx, qx, vt, causal):
    count = p.shape[0]
    qt, kt, vtile, ot, qlo, vlo = head_place(h)
    lane = lanes((count, TILE))
    in_q = both(lane >= qlo, lane < qlo + HEAD)
    in_v = both(lane >= vlo, lane < vlo + HEAD)
    spare = HEAD - qlo
    kx[...] = jnp.where(lane == spare, bias[...], jnp.where(in_q, p[:, strip(kt, TILE)], jnp.zeros((), LOW)))
    vt[...] = jnp.where(in_v, p[:, strip(vtile, TILE)].astype(WIDE), 1.0).T.astype(LOW)
    qx[...] = jnp.where(
        in_q, p[:, strip(qt, TILE)].astype(WIDE) * SCORE_SCALE, jnp.where(lane == spare, 1.0, 0.0)
    ).astype(LOW)
    scores = mm_nt(kx[...], qx[...])
    if causal:
        scores = jnp.where(subs(scores.shape) <= lanes(scores.shape), scores, NEG_FILL)
    top = jnp.max(scores, axis=0, keepdims=True)
    power = jnp.exp(scores - top).astype(LOW)
    out = mm(vt[...], power)
    total = jnp.where(vlo == 0, out[HEAD : HEAD + 1, :], out[0:1, :])
    result = (out / total).T
    o[:, strip(ot, TILE)] = jnp.where(in_v, result, o[:, strip(ot, TILE)].astype(WIDE)).astype(LOW)
    row = subs((8, count))
    lse[...] = jnp.where(row == lse_row, top + jnp.log(total), lse[...])


def forward_kernel(
    planes, self_in, crs_in, up_in, dn_in, x_in, cot_in, gain_in, bias_self, bias_cross,
    w_att, w_crs, w_up, w_dn, x_out, cot, first, p_self, o_self, lse_self, mid, second, act, slope, late, third,
    memory, p_cross, o_cross, lse_cross, gains_out,
    x_v, att_v, crs_v, up_v, dn_v, first_v, p_v, o_v, lse_v, mid_v, second_v, act_v, slope_v, late_v, memory_v,
    send_v, recv_v, gain_v, kx, qx, vt,
    x_sem, x_sent, z_got, z_sent, y_got, y_sent, c_sem,
    row_got, row_sent, fwd_sem, cot_got, ex_got, ex_sent, mem_got, mem_sent, mf_got, mf_sent, gain_sem, put_sem,
):
    at = Place(planes)
    c, z, t, y, r = at.c, at.z, at.t, at.y, at.r
    rows = x_in.shape[1]
    slot = x_v.shape[0]
    tiles = slot // BLOCK
    depth = up_in.shape[0]
    vmem = {"att": att_v, "crs": crs_v, "up": up_v, "dn": dn_v}
    shard = {"att": self_in, "up": up_in, "dn": dn_in}
    here = pl.ds(pl.multiple_of(z * depth, depth), depth)
    at.meet()

    relay_dev = (y, z, 2 * y + c)
    stays = both(c == y, r == c)

    def launch(g):
        i = GROUPS.index(g)
        goal = vmem[g].at[r, here, :]

        @pl.when(stays)
        def _():
            pltpu.make_async_copy(shard[g], goal, x_sem.at[i, r]).start()

        @pl.when(jnp.logical_not(stays))
        def _():
            push(shard[g], goal, x_sent.at[i], x_sem.at[i, r], relay_dev).start()

    crs_dev = (y, z, 2 * y + 1)
    crs_stays = both(c == y, r == 1)
    side = crs_in.shape[1]

    def crs_goal(block, section):
        return crs_v.at[block, here, pl.ds(pl.multiple_of((1 - section) * side, side), side)]

    def launch_crs():
        @pl.when(crs_stays)
        def _():
            pltpu.make_async_copy(crs_in, crs_goal(r, c), c_sem.at[r, c]).start()

        @pl.when(jnp.logical_not(crs_stays))
        def _():
            push(crs_in, crs_goal(r, c), x_sent.at[1], c_sem.at[r, c], crs_dev).start()

    row_goal = x_v.at[strip(t, rows), :]
    cot_goal = cot.at[strip(t, rows), :]

    def launch_rows(s):
        dev = (y, z, 2 * s + c)
        own = both(both(c == y, r == c), y == s)

        @pl.when(own)
        def _():
            pltpu.make_async_copy(x_in.at[s], row_goal, row_got.at[r]).start()

        @pl.when(jnp.logical_not(own))
        def _():
            push(x_in.at[s], row_goal, row_sent.at[s], row_got.at[r], dev).start()

    cot_stays = both(c == y, r == 1)

    def launch_cot():
        dev = (y, z, 2 * c + 1)

        @pl.when(cot_stays)
        def _():
            pltpu.make_async_copy(cot_in.at[c], cot_goal, cot_got.at[r]).start()

        @pl.when(jnp.logical_not(cot_stays))
        def _():
            push(cot_in.at[c], cot_goal, row_sent.at[2], cot_got.at[r], dev).start()

    gain_copy = push(gain_in, gain_v.at[c], gain_sem.at[0], gain_sem.at[1], at.twin)
    gain_copy.start()
    launch("att")
    launch_rows(0)
    launch_rows(1)
    launch_crs()
    launch("up")
    launch("dn")
    launch_cot()

    def piece(g, k):
        j = lax.rem(z - k + planes, planes)
        return vmem[g].at[:, pl.ds(pl.multiple_of(j * depth, depth), depth), :]

    def ring(g, k):
        i = GROUPS.index(g)
        return push(piece(g, k - 1), piece(g, k - 1), z_sent.at[i, k - 1], z_got.at[i, k - 1], at.above)

    def ring_in(g, k):
        i = GROUPS.index(g)
        return push(piece(g, k), piece(g, k), z_sent.at[i, k - 1], z_got.at[i, k - 1], at.above)

    def cross_over(g, k):
        i = GROUPS.index(g)
        return push(piece(g, k), piece(g, k), y_sent.at[i, k], y_got.at[i, k], at.across)

    def member(g):
        return both(at.relays, at.decodes) if g == "crs" else at.relays

    def listens(g):
        other = jnp.logical_not(at.relays)
        return both(other, at.decodes) if g == "crs" else other

    def arrive(g, k):
        i = GROUPS.index(g)
        if k:
            ring_in(g, k).wait_recv()
        elif g == "crs":
            for block in range(2):
                for section in range(2):
                    goal = crs_goal(block, section)
                    push(goal, goal, x_sent.at[1], c_sem.at[block, section], at.twin).wait_recv()
        else:
            for block in range(2):
                goal = vmem[g].at[block, here, :]
                push(goal, goal, x_sent.at[i], x_sem.at[i, block], at.twin).wait_recv()

    def relay_up(g, k):
        @pl.when(member(g))
        def _():
            arrive(g, k)
            if k + 1 < planes:
                ring(g, k + 1).start()

    def relay_over(g, k):
        @pl.when(member(g))
        def _():
            cross_over(g, k).start()

    def relay(g, k):
        relay_up(g, k)
        relay_over(g, k)

    def settle(g):
        @pl.when(listens(g))
        def _():
            for k in range(planes):
                cross_over(g, k).wait_recv()

    puts = []

    def put(source, goal):
        copy = pltpu.make_async_copy(source, goal, put_sem.at[len(puts)])
        copy.start()
        puts.append(copy)
        return copy

    relay("att", 0)
    half = pl.ds(pl.multiple_of(c * 2 * rows, 2 * rows), 2 * rows)
    far_half = pl.ds(pl.multiple_of((1 - c) * 2 * rows, 2 * rows), 2 * rows)
    for k in range(2):
        goal = x_v.at[strip(2 * c + k, rows), :]
        push(goal, goal, row_sent.at[0], row_got.at[k], at.twin).wait_recv()
    rows_on = push(x_v.at[half, :], x_v.at[half, :], fwd_sem.at[0], fwd_sem.at[1], at.twin)
    rows_on.start()
    relay("att", 1)
    push(gain_in, gain_v.at[1 - c], gain_sem.at[0], gain_sem.at[1], at.twin).wait_recv()
    gain_here = pltpu.make_async_copy(gain_in, gain_v.at[c], gain_sem.at[2])
    gain_here.start()
    gain_here.wait()
    gains = gain_v.at[r]
    push(x_v.at[far_half, :], x_v.at[far_half, :], fwd_sem.at[0], fwd_sem.at[1], at.twin).wait_recv()

    def enter(i):
        q = strip(i, BLOCK)
        first_v[q, :] = (center(x_v[q, :].astype(WIDE))[0] * gains[0:1, :]).astype(LOW)

    each(tiles, enter)
    put(first_v, first)
    put(x_v, x_out)
    relay("att", 2)
    relay("att", 3)

    @pl.when(at.decodes)
    def _():
        for k in range(2):
            goal = cot.at[strip(2 * c + k, rows), :]
            push(goal, goal, row_sent.at[2], cot_got.at[k], at.twin).wait_recv()
        push(cot.at[half, :], cot.at[half, :], fwd_sem.at[2], fwd_sem.at[3], at.twin).start()

    for k in range(4):
        relay("crs", k)
    relay("up", 0)
    settle("att")

    def project(source, weights, part):
        def run(i):
            q = strip(i, BLOCK)
            for b in range(2):
                if part != "kv":
                    p_v[b, q, 0:256] = mm(source[q, :], weights[b, :, 0:256]).astype(LOW)
                if part != "q":
                    p_v[b, q, 256:640] = mm(source[q, :], weights[b, :, 384:768]).astype(LOW)

        each(tiles, run)

    project(first_v, att_v, "all")
    p_put = put(p_v, p_self)
    o_v[...] = jnp.zeros_like(o_v)
    lse_v[...] = jnp.zeros_like(lse_v)
    relay("up", 1)

    def attend_half(b, bias, causal):
        def run(h):
            attend_block(h, p_v.at[b], o_v.at[b], lse_v, 3 * b + h, bias, kx, qx, vt, causal)

        each(3, run)

    for b in range(2):
        pl.when(at.encodes)(functools.partial(attend_half, b, bias_self, False))
        pl.when(at.decodes)(functools.partial(attend_half, b, bias_self, True))
        relay("up", 2 + b)
    relay("dn", 0)
    o_put = put(o_v, o_self)
    lse_put = put(lse_v, lse_self)

    def exchange(k, i):
        q = strip(i, BLOCK)
        return push(send_v.at[k, q, :], recv_v.at[k, q, :], ex_sent.at[k, i], ex_got.at[k, i], at.twin)

    def out_project(k, weights):
        def run(i):
            q = strip(i, BLOCK)
            part = mm_nt(o_v[0, q, :], weights[0, :, 128:384]) + mm_nt(o_v[1, q, :], weights[1, :, 128:384])
            send_v[k, q, :] = part.astype(LOW)
            exchange(k, i).start()

        each(tiles, run)

    def joined(k, i):
        q = strip(i, BLOCK)
        exchange(k, i).wait_recv()
        return send_v[k, q, :].astype(WIDE) + recv_v[k, q, :].astype(WIDE)

    out_project(0, att_v)
    relay("dn", 1)

    def middle(i):
        q = strip(i, BLOCK)
        value = x_v[q, :].astype(WIDE) + joined(0, i)
        mid_v[q, :] = value
        second_v[q, :] = (center(value)[0] * gains[1:2, :]).astype(LOW)

    each(tiles, middle)
    put(mid_v, mid)
    put(second_v, second)
    put(att_v, w_att)

    def mem_send(i):
        q = pl.ds(pl.multiple_of(c * 2 * BLOCK + i * BLOCK, BLOCK), BLOCK)
        return push(memory_v.at[q, :], memory_v.at[q, :], mem_sent.at[i], mem_got.at[i], at.beside)

    def mem_forward(i, core):
        q = pl.ds(pl.multiple_of(core * 2 * BLOCK + i * BLOCK, BLOCK), BLOCK)
        return push(memory_v.at[q, :], memory_v.at[q, :], mf_sent.at[i], mf_got.at[i], at.twin)

    settle("up")
    put(up_v, w_up)

    @pl.when(at.encodes)
    def _():
        def run(i):
            q = strip(i, BLOCK)
            for b in range(2):
                value, grade = gelu_parts(mm(second_v[q, :], up_v[b]))
                act_v[b, q, :] = value.astype(LOW)
                slope_v[b, q, :] = grade.astype(LOW)

        each(tiles, run)

    relay("dn", 2)
    relay("dn", 3)
    settle("dn")
    put(dn_v, w_dn)
    put(act_v, act)
    put(slope_v, slope)

    @pl.when(at.encodes)
    def _():
        def run(i):
            q = strip(i, BLOCK)
            part = mm_nt(act_v[0, q, :], dn_v[0]) + mm_nt(act_v[1, q, :], dn_v[1])
            send_v[1, q, :] = part.astype(LOW)
            exchange(1, i).start()

        each(tiles, run)

        def finish(n):
            i = lax.rem(n + 2 * c, 4)
            q = strip(i, BLOCK)
            value = mid_v[q, :] + joined(1, i)
            late_v[q, :] = value
            memory_v[q, :] = (center(value)[0] * gains[2:3, :]).astype(LOW)

            @pl.when(n < 2)
            def _():
                mem_send(n).start()

        each(tiles, finish)

    p_put.wait()
    o_put.wait()
    lse_put.wait()
    puts[0].wait()
    settle("crs")

    @pl.when(at.decodes)
    def _():
        project(second_v, crs_v, "q")
        for i in range(2):
            mem_send(i).wait_recv()
            mem_forward(i, c).start()
        for i in range(2):
            mem_forward(i, 1 - c).wait_recv()
        project(memory_v, crs_v, "kv")
        o_v[...] = jnp.zeros_like(o_v)
        lse_v[...] = jnp.zeros_like(lse_v)
        attend_half(0, bias_cross, False)
        attend_half(1, bias_cross, False)
        out_project(1, crs_v)

        def finish(i):
            q = strip(i, BLOCK)
            value = mid_v[q, :] + joined(1, i)
            late_v[q, :] = value
            first_v[q, :] = (center(value)[0] * gains[2:3, :]).astype(LOW)

        each(tiles, finish)

    put(crs_v, w_crs)
    put(p_v, p_cross)
    put(o_v, o_cross)
    put(lse_v, lse_cross)
    put(late_v, late)
    put(first_v, third)
    put(memory_v, memory)
    put(gains, gains_out)

    skip = (id(puts[0]), id(p_put), id(o_put), id(lse_put))
    for copy in puts:
        if id(copy) not in skip:
            copy.wait()
    gain_copy.wait_send()
    rows_on.wait_send()

    @pl.when(jnp.logical_not(stays))
    def _():
        for g in ("att", "up", "dn"):
            push(shard[g], vmem[g].at[r, here, :], x_sent.at[GROUPS.index(g)], x_sem.at[0, 0], relay_dev).wait_send()

    @pl.when(jnp.logical_not(crs_stays))
    def _():
        push(crs_in, crs_goal(r, c), x_sent.at[1], c_sem.at[0, 0], crs_dev).wait_send()

    for s in range(2):

        @pl.when(jnp.logical_not(both(both(c == y, r == c), y == s)))
        def _():
            push(x_in.at[s], row_goal, row_sent.at[s], row_got.at[r], at.twin).wait_send()

    @pl.when(jnp.logical_not(cot_stays))
    def _():
        push(cot_in.at[c], cot_goal, row_sent.at[2], cot_got.at[r], at.twin).wait_send()

    for g in GROUPS:

        @pl.when(member(g))
        def _():
            for k in range(1, planes):
                ring(g, k).wait_send()
            for k in range(planes):
                cross_over(g, k).wait_send()

    def drain(i):
        exchange(0, i).wait_send()
        exchange(1, i).wait_send()

    each(tiles, drain)

    @pl.when(at.encodes)
    def _():
        for i in range(2):
            mem_send(i).wait_send()

    @pl.when(at.decodes)
    def _():
        for i in range(2):
            mem_forward(i, c).wait_send()
        cot_on = push(cot.at[half, :], cot.at[half, :], fwd_sem.at[2], fwd_sem.at[3], at.twin)
        cot_on.wait_send()
        push(cot.at[far_half, :], cot.at[far_half, :], fwd_sem.at[2], fwd_sem.at[3], at.twin).wait_recv()


def forward_call(planes, slot, width, hidden, args):
    shape = jax.ShapeDtypeStruct
    weights = [(2, width, width), (2, width, width), (2, width, hidden), (2, width, hidden)]
    packed, outs, square = (2, slot, 640), (2, slot, 256), (slot, width)
    out_shape = (
        [shape(s, LOW) for s in weights]
        + [shape(square, LOW)] * 3
        + [shape(packed, LOW), shape(outs, LOW), shape((8, slot), WIDE)]
        + [shape(square, WIDE), shape(square, LOW), shape((2, slot, hidden), LOW), shape((2, slot, hidden), LOW)]
        + [shape(square, WIDE), shape(square, LOW), shape(square, LOW)]
        + [shape(packed, LOW), shape(outs, LOW), shape((8, slot), WIDE), shape((8, width), WIDE)]
    )
    groups = len(GROUPS)
    dma = pltpu.SemaphoreType.DMA
    scratch = (
        [pltpu.VMEM(square, LOW)]
        + [pltpu.VMEM(s, LOW) for s in weights]
        + [pltpu.VMEM(square, LOW), pltpu.VMEM(packed, LOW), pltpu.VMEM(outs, LOW), pltpu.VMEM((8, slot), WIDE)]
        + [pltpu.VMEM(square, WIDE), pltpu.VMEM(square, LOW)]
        + [pltpu.VMEM((2, slot, hidden), LOW)] * 2
        + [pltpu.VMEM(square, WIDE), pltpu.VMEM(square, LOW)]
        + [pltpu.VMEM((2,) + square, LOW)] * 2
        + [pltpu.VMEM((2, 8, width), WIDE)]
        + [pltpu.VMEM((slot, TILE), LOW)] * 2
        + [pltpu.VMEM((TILE, slot), LOW)]
        + [dma((groups, 2)), dma((groups,)), dma((groups, planes)), dma((groups, planes))]
        + [dma((groups, planes)), dma((groups, planes)), dma((2, 2))]
        + [dma((2,)), dma((3,)), dma((4,)), dma((2,)), dma((2, 4)), dma((2, 4))]
        + [dma((2,)), dma((2,)), dma((2,)), dma((2,)), dma((3,)), dma((24,))]
    )
    any_spec = pl.BlockSpec(memory_space=pl.ANY)
    vmem_spec = pl.BlockSpec(memory_space=pltpu.VMEM)
    return pl.pallas_call(
        functools.partial(forward_kernel, planes),
        out_shape=out_shape,
        in_specs=[any_spec] * 6 + [vmem_spec] * 3,
        out_specs=[any_spec] * len(out_shape),
        scratch_shapes=scratch,
        compiler_params=pltpu.CompilerParams(collective_id=0, has_side_effects=True, vmem_limit_bytes=VMEM_BYTES),
    )(*args)


BUFFER = (0, 1, 0, 1, 0)
SUMS = ("ffn", "crs", "att")


def split_three(value):
    high = value.astype(LOW).astype(WIDE)
    middle = (value - high).astype(LOW).astype(WIDE)
    return high, middle, value - high - middle


def attend_back_block(h, p, o, d_o, d_p, lse, lse_row, bias, kx, qx, vx, gx, kt_v, causal):
    count = p.shape[0]
    qt, kt, vtile, ot, qlo, vlo = head_place(h)
    lane = lanes((count, TILE))
    in_q = both(lane >= qlo, lane < qlo + HEAD)
    in_v = both(lane >= vlo, lane < vlo + HEAD)
    sq, sv = HEAD - qlo, HEAD - vlo
    keys = jnp.where(
        in_q, p[:, strip(kt, TILE)].astype(WIDE), jnp.where(both(lane > sq, lane < sq + 4), 1.0, 0.0)
    )
    keys = jnp.where(lane == sq, bias[...].astype(WIDE), keys)
    kx[...] = keys.astype(LOW)
    kt_v[...] = keys.T.astype(LOW)
    vx[...] = jnp.where(
        in_v, p[:, strip(vtile, TILE)].astype(WIDE), jnp.where(both(lane >= sv, lane < sv + 3), 1.0, 0.0)
    ).astype(LOW)
    own = jnp.sum(jnp.where(subs((8, count)) == lse_row, lse[...], 0.0), axis=0, keepdims=True)
    a, b, c = split_three(-jnp.broadcast_to(own, (TILE, count)).T)
    extra = jnp.where(
        lane == sq,
        1.0,
        jnp.where(lane == sq + 1, a, jnp.where(lane == sq + 2, b, jnp.where(lane == sq + 3, c, 0.0))),
    )
    qx[...] = jnp.where(in_q, p[:, strip(qt, TILE)].astype(WIDE) * SCORE_SCALE, extra).astype(LOW)
    grad = jnp.where(in_v, d_o[:, strip(ot, TILE)].astype(WIDE), 0.0)
    inner = jnp.sum(grad * o[:, strip(ot, TILE)].astype(WIDE), axis=-1, keepdims=True)
    a, b, c = split_three(-inner)
    gx[...] = (
        grad + jnp.where(lane == sv, a, jnp.where(lane == sv + 1, b, jnp.where(lane == sv + 2, c, 0.0)))
    ).astype(LOW)
    scores = mm_nt(kx[...], qx[...])
    if causal:
        scores = jnp.where(subs(scores.shape) <= lanes(scores.shape), scores, NEG_FILL)
    probs = jnp.exp(scores)
    d_scores = (probs * mm_nt(vx[...], gx[...])).astype(LOW)
    d_v = mm(probs.astype(LOW), gx[...])
    d_k = mm(d_scores, qx[...])
    d_q = mm(kt_v[...], d_scores).T * SCORE_SCALE

    def place(tile_index, inside, value):
        cut = strip(tile_index, TILE)
        d_p[:, cut] = jnp.where(inside, value, d_p[:, cut].astype(WIDE)).astype(LOW)

    place(qt, in_q, d_q)
    place(kt, in_q, d_k)
    place(vtile, in_v, d_v)


def backward_kernel(
    planes, w_att, w_crs, w_up, w_dn, x_rows, cot, first, p_self, o_self, lse_self, mid, second, act, slope, late,
    third, memory, p_cross, o_cross, lse_cross, gains, bias_self, bias_cross,
    block_out, grad_out, home_ffn, home_crs, home_att, gain_out, act_keep, y3_keep, grad_keep,
    dw_ffn, dw_crs, dw_att, yb_ffn, yb_crs, yb_att, zb_ffn, zb_crs, zb_att,
    att_v, crs_v, up_v, dn_v, a_v, b_v, o_v, do_v, base_v, dres_v, cot_v, grad_v, stage_v, ta, tb, tc,
    send_v, recv_v, kx, qx, vx, gx, kt_v, lse_v, gain_v, gain_buf, out_st, dw_st, sum_st,
    load_sem, put_sem, ex_got, ex_sent, dm_got, dm_sent, df_got, df_sent, y_got, y_sent, z_got, z_sent,
    home_got, home_sent, blk_got, blk_sent, gr_got, gr_sent, gain_got, gain_sent, sum_sem, dw_sem,
):
    at = Place(planes)
    c, z, t, y, r = at.c, at.z, at.t, at.y, at.r
    slot = cot_v.shape[0]
    rows = slot // 4
    tiles = slot // BLOCK
    depth = home_ffn.shape[0]
    at.meet()
    relay = at.relays
    other = jnp.logical_not(relay)
    dw = {"ffn": dw_ffn, "crs": dw_crs, "att": dw_att}
    yb = {"ffn": yb_ffn, "crs": yb_crs, "att": yb_att}
    zb = {"ffn": zb_ffn, "crs": zb_crs, "att": zb_att}
    home = {"ffn": home_ffn, "crs": home_crs, "att": home_att}
    loads = {}

    def load(name, source, goal):
        index = loads.setdefault(name, len(loads))
        return pltpu.make_async_copy(source, goal, load_sem.at[index])

    def exchange(e, i):
        q = strip(i, BLOCK)
        k = BUFFER[e]
        return push(send_v.at[k, q, :], recv_v.at[k, q, :], ex_sent.at[e, i], ex_got.at[e, i], at.twin)

    def joined(e, i):
        q = strip(i, BLOCK)
        exchange(e, i).wait_recv()
        return send_v[BUFFER[e], q, :].astype(WIDE) + recv_v[BUFFER[e], q, :].astype(WIDE)

    def ours(i):
        return lax.div(i, 2) == c

    def norm_grad(values, gain, grad, gain_row, counted):
        normal, scale = center(values)
        scaled = grad * gain
        one = jnp.mean(scaled, axis=-1, keepdims=True)
        two = jnp.mean(scaled * normal, axis=-1, keepdims=True)
        total = jnp.sum(grad * normal, axis=0, keepdims=True)
        gain_v[gain_row : gain_row + 1, :] += jnp.where(counted, total, 0.0)
        return (scaled - one - normal * two) * scale

    def row_home(k, source, goal, sent, got):
        dev = (r, z, 2 * c + k)
        stays = both(both(c == r, y == c), r == k)
        return stays, source, goal.at[y], sent.at[k], got.at[y], dev

    def go_home(k, source, goal, sent, got):
        stays, source, goal, sent, got, dev = row_home(k, source, goal, sent, got)

        @pl.when(stays)
        def _():
            pltpu.make_async_copy(source, goal, got).start()

        @pl.when(jnp.logical_not(stays))
        def _():
            push(source, goal, sent, got, dev).start()

    def went_home(k, source, goal, sent, got):
        stays, source, goal, sent, got, dev = row_home(k, source, goal, sent, got)

        @pl.when(jnp.logical_not(stays))
        def _():
            push(source, goal, sent, got, dev).wait_send()

    def home_block(k, held):
        return held.at[strip(2 * c + k, rows), :]

    def block_of(k):
        return lax.rem(z - 1 - k + 2 * planes, planes)

    def y_hop(g, k):
        i = SUMS.index(g)
        return push(dw[g].at[k], yb[g].at[k], y_sent.at[i, k], y_got.at[i, k], at.across)

    def z_hop(g, k):
        i = SUMS.index(g)
        return push(dw[g].at[k], zb[g].at[k], z_sent.at[i, k], z_got.at[i, k], at.above)

    def emit(g, compute):
        columns = dw[g].shape[3]

        def put(k, s):
            return pltpu.make_async_copy(dw_st.at[s, :, :, 0:columns], dw[g].at[k], dw_sem.at[s])

        def run(k):
            s = lax.rem(k, 2)
            j = block_of(k)
            compute(s, pl.ds(pl.multiple_of(j * depth, depth), depth))
            put(k, s).start()

            @pl.when(k >= 1)
            def _():
                put(k - 1, 1 - s).wait()
                pl.when(other)(lambda: y_hop(g, k - 1).start())

        each(planes, run)
        put(planes - 1, (planes - 1) % 2).wait()
        pl.when(other)(lambda: y_hop(g, planes - 1).start())

    def homes(g):
        columns = dw[g].shape[3]
        source = dw[g].at[planes - 1]
        result = []
        for b in range(2):
            if g == "crs":
                for section in range(2):
                    cut = pl.ds((1 - section) * (columns // 2), columns // 2)
                    result.append(
                        (both(c == section, r == b), source.at[b, :, cut], (section, z, 2 * y + b), 2 * b + section)
                    )
            else:
                result.append((both(c == r, r == b), source.at[b], (r, z, 2 * y + b), b))
        return result

    def sum_step(g, k):
        i = SUMS.index(g)
        columns = dw[g].shape[3]
        members = both(relay, at.decodes) if g == "crs" else relay

        @pl.when(members)
        def _():
            y_hop(g, k).wait_recv()
            parts = [dw[g].at[k], yb[g].at[k]]
            if k:
                z_hop(g, k - 1).wait_recv()
                parts.append(zb[g].at[k - 1])
            copies = [
                pltpu.make_async_copy(part, sum_st.at[n, :, :, 0:columns], sum_sem.at[n])
                for n, part in enumerate(parts)
            ]
            for copy in copies:
                copy.start()
            for copy in copies:
                copy.wait()
            for b in range(2):
                total = sum_st[0, b, :, 0:columns].astype(WIDE) + sum_st[1, b, :, 0:columns].astype(WIDE)
                if k:
                    total = total + sum_st[2, b, :, 0:columns].astype(WIDE)
                sum_st[0, b, :, 0:columns] = total.astype(LOW)
            back = pltpu.make_async_copy(sum_st.at[0, :, :, 0:columns], dw[g].at[k], sum_sem.at[0])
            back.start()
            back.wait()
            if k + 1 < planes:
                z_hop(g, k).start()
            else:
                for stays, source, dev, n in homes(g):

                    @pl.when(stays)
                    def _():
                        pltpu.make_async_copy(source, home[g], home_got.at[i]).start()

                    @pl.when(jnp.logical_not(stays))
                    def _():
                        push(source, home[g], home_sent.at[i, n], home_got.at[i], dev).start()

    def turn(source, goal):
        def run(i):
            q = strip(i, BLOCK)
            goal[:, q] = source[q, :].astype(WIDE).T.astype(LOW)

        each(tiles, run)

    gain_v[...] = jnp.zeros_like(gain_v)
    g1, g2 = gains[1:2, :], gains[2:3, :]

    early = [
        load("up", w_up, up_v),
        load("dn", w_dn, dn_v),
        load("late", late, base_v),
        load("att", w_att, att_v),
    ]
    for copy in early:
        copy.start()

    @pl.when(at.decodes)
    def _():
        copies = [load("third", third, stage_v), load("cot", cot, cot_v), load("crs", w_crs, crs_v)]
        for copy in copies:
            copy.start()
        for copy in copies[:2]:
            copy.wait()

    @pl.when(at.encodes)
    def _():
        for k in range(2):
            go_home(k, home_block(k, memory), block_out, blk_sent, blk_got)
        copies = [load("second", second, stage_v), load("act", act, a_v), load("slope", slope, b_v)]
        for copy in copies:
            copy.start()
        for copy in copies:
            copy.wait()

    for copy in early[:3]:
        copy.wait()

    @pl.when(at.decodes)
    def _():
        def run(i):
            q = strip(i, BLOCK)
            part = None
            for b in range(2):
                value, grade = gelu_parts(mm(stage_v[q, :], up_v[b]))
                a_v[b, q, :] = value.astype(LOW)
                d_pre = (mm(cot_v[q, :], dn_v[b]) * grade).astype(LOW)
                b_v[b, q, :] = d_pre
                term = mm_nt(d_pre, up_v[b])
                part = term if part is None else part + term
            send_v[0, q, :] = part.astype(LOW)
            exchange(0, i).start()

        each(tiles, run)
        keep = load("keep", a_v, act_keep)
        keep.start()

    def dm_hop(n):
        q = pl.ds(pl.multiple_of((2 * c + n) * BLOCK, BLOCK), BLOCK)
        return push(send_v.at[1, q, :], recv_v.at[1, q, :], dm_sent.at[n], dm_got.at[n], at.beside)

    def df_hop(n, core):
        q = pl.ds(pl.multiple_of((2 * core + n) * BLOCK, BLOCK), BLOCK)
        return push(recv_v.at[1, q, :], recv_v.at[1, q, :], df_sent.at[n], df_got.at[n], at.twin)

    @pl.when(at.encodes)
    def _():
        def run(n):
            i = lax.rem(n + 2 * c, 4)
            q = strip(i, BLOCK)

            @pl.when(n < 2)
            def _():
                dm_hop(n).wait_recv()
                df_hop(n, c).start()

            @pl.when(n >= 2)
            def _():
                df_hop(n - 2, 1 - c).wait_recv()
                df_hop(n - 2, c).wait_send()

            grad = norm_grad(base_v[q, :], g2, recv_v[1, q, :].astype(WIDE), 2, ours(i))
            dres_v[q, :] = grad
            low = grad.astype(LOW)
            cot_v[q, :] = low
            part = None
            for b in range(2):
                d_pre = (mm(low, dn_v[b]) * b_v[b, q, :].astype(WIDE)).astype(LOW)
                b_v[b, q, :] = d_pre
                term = mm_nt(d_pre, up_v[b])
                part = term if part is None else part + term
            send_v[0, q, :] = part.astype(LOW)
            exchange(0, i).start()

        each(tiles, run)

    turn(stage_v, ta)
    turn(cot_v, tb)

    def ffn_block(s, j):
        for b in range(2):
            dw_st[s, b, :, 0:768] = mm(ta[j, :], b_v[b]).astype(LOW)
            dw_st[s, b, :, 768:1536] = mm(tb[j, :], a_v[b]).astype(LOW)

    emit("ffn", ffn_block)

    @pl.when(at.decodes)
    def _():
        load("keep", a_v, act_keep).wait()
        packed = load("p", p_cross, a_v.at[:, :, 0:640])
        small = [load("o", o_cross, o_v), load("lse", lse_cross, lse_v), load("second", second, stage_v)]
        packed.start()
        for copy in small:
            copy.start()

        def run(i):
            q = strip(i, BLOCK)
            grad = cot_v[q, :].astype(WIDE) + norm_grad(base_v[q, :], g2, joined(0, i), 2, ours(i))
            dres_v[q, :] = grad
            grad_v[q, :] = grad.astype(LOW)

        each(tiles, run)
        next_base = load("mid", mid, base_v)
        next_base.start()
        load("crs", w_crs, crs_v).wait()

        def spread_out(i):
            q = strip(i, BLOCK)
            for b in range(2):
                do_v[b, q, :] = mm(grad_v[q, :], crs_v[b, :, 128:384]).astype(LOW)

        each(tiles, spread_out)
        for copy in small:
            copy.wait()
        packed.wait()
        b_v[...] = jnp.zeros_like(b_v)

        def head(n):
            b = lax.div(n, 3)
            attend_back_block(
                lax.rem(n, 3), a_v.at[b], o_v.at[b], do_v.at[b], b_v.at[b], lse_v, n, bias_cross,
                kx, qx, vx, gx, kt_v, False,
            )

        each(6, head)

        def to_memory(q):
            return mm_nt(b_v[0, q, 256:640], crs_v[0, :, 384:768]) + mm_nt(b_v[1, q, 256:640], crs_v[1, :, 384:768])

        def far(n):
            i = 2 * (1 - c) + n
            q = strip(i, BLOCK)
            send_v[1, q, :] = to_memory(q).astype(LOW)
            exchange(1, i).start()

        each(2, far)

        def near(n):
            i = 2 * c + n
            q = strip(i, BLOCK)
            part = to_memory(q)
            exchange(1, i).wait_recv()
            send_v[1, q, :] = (part + recv_v[1, q, :].astype(WIDE)).astype(LOW)
            dm_hop(n).start()

        each(2, near)

        def to_query(i):
            q = strip(i, BLOCK)
            part = mm_nt(b_v[0, q, 0:256], crs_v[0, :, 0:256]) + mm_nt(b_v[1, q, 0:256], crs_v[1, :, 0:256])
            send_v[0, q, :] = part.astype(LOW)
            exchange(2, i).start()

        def drained(i):
            exchange(0, i).wait_send()

        each(tiles, drained)
        each(tiles, to_query)
        turn(stage_v, ta)
        stage_in = load("memory", memory, stage_v)
        stage_in.start()
        turn(grad_v, tc)
        stage_in.wait()
        turn(stage_v, tb)
        load("first", first, stage_v).start()

        def crs_block(s, j):
            for b in range(2):
                left = mm(ta[j, :], b_v[b, :, 0:256])
                out = mm(tc[j, :], o_v[b])
                dw_st[s, b, :, 0:128] = left[:, 0:128].astype(LOW)
                dw_st[s, b, :, 128:256] = (left[:, 128:256] + out[:, 0:128]).astype(LOW)
                dw_st[s, b, :, 256:384] = out[:, 128:256].astype(LOW)
                dw_st[s, b, :, 384:768] = mm(tb[j, :], b_v[b, :, 256:640]).astype(LOW)

        emit("crs", crs_block)
        next_base.wait()

        def below(i):
            q = strip(i, BLOCK)
            grad = dres_v[q, :] + norm_grad(base_v[q, :], g1, joined(2, i), 1, ours(i))
            dres_v[q, :] = grad
            grad_v[q, :] = grad.astype(LOW)

        each(tiles, below)
        load("first", first, stage_v).wait()

    @pl.when(at.encodes)
    def _():
        next_base = load("mid", mid, base_v)
        next_base.start()
        load("first", first, stage_v).start()
        next_base.wait()

        def run(i):
            q = strip(i, BLOCK)
            grad = dres_v[q, :] + norm_grad(base_v[q, :], g1, joined(0, i), 1, ours(i))
            dres_v[q, :] = grad
            grad_v[q, :] = grad.astype(LOW)

        each(tiles, run)
        load("first", first, stage_v).wait()

    packed = load("p", p_self, a_v.at[:, :, 0:640])
    small = [load("o", o_self, o_v), load("lse", lse_self, lse_v)]
    packed.start()
    for copy in small:
        copy.start()
    early[3].wait()

    def spread_self(i):
        q = strip(i, BLOCK)
        for b in range(2):
            do_v[b, q, :] = mm(grad_v[q, :], att_v[b, :, 128:384]).astype(LOW)

    each(tiles, spread_self)
    b_v[...] = jnp.zeros_like(b_v)
    for copy in small:
        copy.wait()
    packed.wait()

    def self_heads(b, causal):
        def run(h):
            attend_back_block(
                h, a_v.at[b], o_v.at[b], do_v.at[b], b_v.at[b], lse_v, 3 * b + h, bias_self,
                kx, qx, vx, gx, kt_v, causal,
            )

        each(3, run)

    for b in range(2):
        pl.when(at.encodes)(functools.partial(self_heads, b, False))
        pl.when(at.decodes)(functools.partial(self_heads, b, True))
        sum_step("ffn", b)

    def to_rows(q):
        part = None
        for b in range(2):
            term = mm_nt(b_v[b, q, 0:256], att_v[b, :, 0:256]) + mm_nt(b_v[b, q, 256:640], att_v[b, :, 384:768])
            part = term if part is None else part + term
        return part

    @pl.when(at.decodes)
    def _():
        def gone(n):
            exchange(1, 2 * (1 - c) + n).wait_send()
            dm_hop(n).wait_send()

        each(2, gone)

    def far_rows(n):
        i = 2 * (1 - c) + n
        q = strip(i, BLOCK)
        send_v[1, q, :] = to_rows(q).astype(LOW)
        exchange(3, i).start()

    each(2, far_rows)
    turn(stage_v, ta)
    x_in = load("x", x_rows, stage_v)
    x_in.start()
    turn(grad_v, tc)

    def att_block(s, j):
        for b in range(2):
            left = mm(ta[j, :], b_v[b, :, 0:256])
            out = mm(tc[j, :], o_v[b])
            dw_st[s, b, :, 0:128] = left[:, 0:128].astype(LOW)
            dw_st[s, b, :, 128:256] = (left[:, 128:256] + out[:, 0:128]).astype(LOW)
            dw_st[s, b, :, 256:384] = out[:, 128:256].astype(LOW)
            dw_st[s, b, :, 384:768] = mm(ta[j, :], b_v[b, :, 256:640]).astype(LOW)

    emit("att", att_block)
    x_in.wait()
    gain0 = gains[0:1, :]

    def near_rows(n):
        i = 2 * c + n
        q = strip(i, BLOCK)
        part = to_rows(q)
        exchange(3, i).wait_recv()
        grad = part + recv_v[1, q, :].astype(WIDE)
        value = dres_v[q, :] + norm_grad(stage_v[q, :].astype(WIDE), gain0, grad, 0, True)
        out_st[strip(n, BLOCK), :] = value.astype(LOW)

    each(2, near_rows)
    out_put = load("out", out_st, grad_keep)
    out_put.start()
    out_put.wait()
    for k in range(2):
        go_home(k, grad_keep.at[strip(k, rows), :], grad_out, gr_sent, gr_got)

    def gain_hop(n, source, device):
        return push(source, gain_buf.at[n], gain_sent.at[n], gain_got.at[n], device)

    gain_buf[0] = gain_v[...]
    hop = gain_hop(1, gain_buf.at[0], at.twin)
    hop.start()
    hop.wait()
    gain_buf[2] = gain_buf[0] + gain_buf[1]
    hop = gain_hop(3, gain_buf.at[2], at.across)
    hop.start()
    hop.wait()
    gain_buf[4] = gain_buf[2] + gain_buf[3]
    source = 4
    for n in range(planes - 1):
        hop = gain_hop(5 + n, gain_buf.at[source], at.above)
        hop.start()
        hop.wait()
        source = 5 + n
    total = None
    for j in range(planes):
        held = gain_buf[jnp.where(z == j, 4, 5 + lax.rem(z - 1 - j + planes, planes))]
        total = held if total is None else total + held
    last = 4 + planes
    gain_buf[last] = total
    hop = gain_hop(last + 1, gain_buf.at[last], at.beside)
    hop.start()
    hop.wait()
    gain_v[...] = jnp.where(r == c, gain_buf[last], gain_buf[last + 1])
    gains_home = load("gains", gain_v, gain_out)
    gains_home.start()

    @pl.when(at.decodes)
    def _():
        copies = [load("act", act_keep, a_v), load("late", late, base_v)]
        for copy in copies:
            copy.start()
        for copy in copies:
            copy.wait()

        def free(i):
            exchange(2, i).wait_send()

        each(tiles, free)

        def to_out(q):
            return mm_nt(a_v[0, q, :], dn_v[0]) + mm_nt(a_v[1, q, :], dn_v[1])

        def far(n):
            i = 2 * (1 - c) + n
            q = strip(i, BLOCK)
            send_v[0, q, :] = to_out(q).astype(LOW)
            exchange(4, i).start()

        each(2, far)

        def near(n):
            i = 2 * c + n
            q = strip(i, BLOCK)
            part = to_out(q)
            exchange(4, i).wait_recv()
            out_st[strip(n, BLOCK), :] = (base_v[q, :] + part + recv_v[0, q, :].astype(WIDE)).astype(LOW)

        each(2, near)
        y3_put = load("out", out_st, y3_keep)
        y3_put.start()
        y3_put.wait()
        for k in range(2):
            go_home(k, y3_keep.at[strip(k, rows), :], block_out, blk_sent, blk_got)

    for k in range(2, planes):
        sum_step("ffn", k)
    for k in range(planes):
        sum_step("crs", k)
    for k in range(planes):
        sum_step("att", k)

    gains_home.wait()
    for s in range(2):
        for goal, got in ((block_out, blk_got), (grad_out, gr_got)):
            push(goal.at[s], goal.at[s], blk_sent.at[0], got.at[s], at.twin).wait_recv()
    for i, g in enumerate(SUMS):
        push(home[g], home[g], home_sent.at[i, 0], home_got.at[i], at.twin).wait_recv()
    for k in range(2):
        went_home(k, grad_keep.at[strip(k, rows), :], grad_out, gr_sent, gr_got)

    @pl.when(at.encodes)
    def _():
        for k in range(2):
            went_home(k, home_block(k, memory), block_out, blk_sent, blk_got)

        def done(i):
            exchange(0, i).wait_send()

        each(tiles, done)

    @pl.when(at.decodes)
    def _():
        for k in range(2):
            went_home(k, y3_keep.at[strip(k, rows), :], block_out, blk_sent, blk_got)

        def done(n):
            exchange(4, 2 * (1 - c) + n).wait_send()

        each(2, done)

    def done_rows(n):
        exchange(3, 2 * (1 - c) + n).wait_send()

    each(2, done_rows)
    for g in SUMS:
        there = at.decodes if g == "crs" else jnp.logical_or(at.decodes, at.encodes)

        @pl.when(both(other, there))
        def _():
            for k in range(planes):
                y_hop(g, k).wait_send()

        @pl.when(both(relay, there))
        def _():
            for k in range(planes - 1):
                z_hop(g, k).wait_send()
            for stays, source, dev, n in homes(g):

                @pl.when(jnp.logical_not(stays))
                def _():
                    i = SUMS.index(g)
                    push(source, home[g], home_sent.at[i, n], home_got.at[i], dev).wait_send()


def backward_call(planes, slot, width, hidden, depth, args):
    shape = jax.ShapeDtypeStruct
    rows = slot // 4
    square = (slot, width)
    wides = {"ffn": 2 * hidden, "crs": width, "att": width}
    out_shape = (
        [shape((2, rows, width), LOW)] * 2
        + [shape((depth, 2 * hidden), LOW), shape((depth, width // 2), LOW), shape((depth, width), LOW)]
        + [shape((8, width), WIDE), shape((2, slot, hidden), LOW)]
        + [shape((2 * rows, width), LOW)] * 2
        + [shape((planes, 2, depth, wides[g]), LOW) for g in SUMS] * 3
    )
    dma = pltpu.SemaphoreType.DMA
    v = pltpu.VMEM
    scratch = (
        [v((2, width, width), LOW)] * 2
        + [v((2, width, hidden), LOW)] * 2
        + [v((2, slot, hidden), LOW)] * 2
        + [v((2, slot, 256), LOW)] * 2
        + [v(square, WIDE)] * 2
        + [v(square, LOW)] * 3
        + [v((width, slot), LOW)] * 3
        + [v((2,) + square, LOW)] * 2
        + [v((slot, TILE), LOW)] * 4
        + [v((TILE, slot), LOW), v((8, slot), WIDE), v((8, width), WIDE), v((planes + 6, 8, width), WIDE)]
        + [v((2 * rows, width), LOW), v((2, 2, depth, 2 * hidden), LOW), v((3, 2, depth, 2 * hidden), LOW)]
        + [dma((24,)), dma((1,)), dma((5, 4)), dma((5, 4))]
        + [dma((2,))] * 4
        + [dma((3, planes))] * 4
        + [dma((3,)), dma((3, 4))]
        + [dma((2,))] * 4
        + [dma((planes + 6,))] * 2
        + [dma((3,)), dma((2,))]
    )
    any_spec = pl.BlockSpec(memory_space=pl.ANY)
    vmem_spec = pl.BlockSpec(memory_space=pltpu.VMEM)
    return pl.pallas_call(
        functools.partial(backward_kernel, planes),
        out_shape=out_shape,
        in_specs=[any_spec] * 20 + [vmem_spec] * 3,
        out_specs=[any_spec] * len(out_shape),
        scratch_shapes=scratch,
        compiler_params=pltpu.CompilerParams(collective_id=1, has_side_effects=True, vmem_limit_bytes=VMEM_BYTES),
    )(*args)


def ring_gather(lay, shard):
    planes = lay.planes
    rows = shard.shape[1]
    if planes > 4:
        piece = lax.all_gather(shard, "dp", axis=1, tiled=True)
        across = lay.route(piece, lambda c, z, t: (c, z, (t + 2) % 4) if c == t // 2 else None)
        return jnp.where(lay.relays, piece, across)
    relay = lambda c, z, t: (c, (z + 1) % planes, t) if c == t // 2 else None
    whole = jnp.zeros((shard.shape[0], planes * rows, shard.shape[2]), shard.dtype)
    piece = shard
    for step in range(planes):
        across = lay.route(piece, lambda c, z, t: (c, z, (t + 2) % 4) if c == t // 2 else None)
        chosen = jnp.where(lay.relays, piece, across)
        whole = lax.dynamic_update_slice(whole, chosen, (0, ((lay.plane - step) % planes) * rows, 0))
        if step + 1 < planes:
            piece = lay.route(piece, relay)
    return whole


def ring_scatter(lay, total, holder):
    planes = lay.planes
    rows = total.shape[1] // planes
    low = total.astype(LOW)
    across = lay.route(
        low, lambda c, z, t: (c, z, (t + 2) % 4) if (c != t // 2 and t % 2 == holder) else None
    )
    summed = low.astype(WIDE) + across.astype(WIDE)
    if planes > 4:
        return lax.psum_scatter(summed.astype(LOW), "dp", scatter_dimension=1, tiled=True)
    relay = lambda c, z, t: (c, (z + 1) % planes, t) if (c == t // 2 and t % 2 == holder) else None
    take = lambda j: lax.dynamic_slice_in_dim(summed, (j % planes) * rows, rows, 1)
    running = take(lay.plane - 1)
    for step in range(1, planes):
        running = lay.route(running.astype(LOW), relay).astype(WIDE) + take(lay.plane - 1 - step)
    return running.astype(LOW)


def hand_back(lay, value, holder, section):
    same = lay.route(
        value[0], lambda c, z, t: (section, z, t) if (c == t // 2 and t % 2 == holder) else None
    )
    beside = lay.route(
        value[1], lambda c, z, t: (section, z, t ^ 1) if (c == t // 2 and t % 2 == holder) else None
    )
    return same.astype(WIDE) + beside.astype(WIDE)


def general_body(block_input, w_self, w_self_out, w_cross, w_up, w_down, norm_gains, lengths, task_mask, out_grad):
    lay = Layout()
    seqs, rows, width = block_input.shape[1:]
    slot = rows * lay.chips
    sec = lay.core
    item = lay.item

    def spread(value, first):
        pick = value[jnp.where(first, lay.chip % 2, 1 - lay.chip % 2)]
        flip = 0 if first else 1
        return lay.route(pick, lambda c, z, t: (t // 2, z, 2 * ((t % 2) ^ flip) + c))

    def merge_rows(mine, theirs):
        low_half = jnp.where(lay.core == 0, mine, theirs)
        high_half = jnp.where(lay.core == 0, theirs, mine)
        return jnp.concatenate([low_half[0], low_half[1], high_half[0], high_half[1]], axis=0)

    first = spread(block_input[0], True)
    second = spread(block_input[0], False)
    mine = jnp.where(item == 0, jnp.stack([first, second]), jnp.stack([second, first]))
    x_rows = merge_rows(mine, lay.other_core(mine)).astype(WIDE)

    picked = out_grad[lay.core]
    even = lay.route(picked, lambda c, z, t: (t // 2, z, 2 * c + 1) if t % 2 == 0 else None)
    odd = lay.route(picked, lambda c, z, t: (t // 2, z, 2 * c + 1) if t % 2 == 1 else None)
    mine = jnp.stack([even, odd])
    cotangent = merge_rows(mine, lay.other_core(mine))

    gains_here = norm_gains[0].astype(WIDE)
    gains = jnp.where(sec == lay.role, gains_here, lay.other_core(norm_gains[0]).astype(WIDE))

    depth = w_self.shape[1]
    wide = w_self.shape[3]
    self_block = pack_heads(
        {"q": w_self[0, :, 0], "k": w_self[0, :, 1], "v": w_self[0, :, 2], "o": w_self_out[0].T}
    )
    feed_block = jnp.concatenate([w_up[0], w_down[0].T], axis=1)
    cross_block = w_cross[0].reshape(depth, 2 * wide)

    def collect(block):
        same = lay.route(block, lambda c, z, t: (t // 2, z, t) if c == t % 2 else None)
        beside = lay.route(block, lambda c, z, t: (t // 2, z, t ^ 1) if c != t % 2 else None)
        return jnp.stack([same, beside])

    def collect_cross(block, section):
        same = lay.route(block, lambda c, z, t: (t // 2, z, t) if (c == section and t % 2 == 1) else None)
        beside = lay.route(block, lambda c, z, t: (t // 2, z, t ^ 1) if (c == section and t % 2 == 0) else None)
        return same, beside

    w_att = ring_gather(lay, collect(self_block))
    w_ffn = ring_gather(lay, collect(feed_block))
    memory_side = collect_cross(cross_block, 0)
    query_side = collect_cross(cross_block, 1)
    w_crs = ring_gather(
        lay,
        jnp.stack(
            [
                pack_heads({"q": q[:, :wide], "k": m[:, :wide], "v": m[:, wide:], "o": q[:, wide:]})
                for m, q in zip(memory_side, query_side)
            ]
        ),
    )
    hidden = w_up.shape[2]
    part = lambda w, name: jnp.concatenate([unpack_heads(w[0], name), unpack_heads(w[1], name)], axis=1)
    att = {n: part(w_att, n) for n in "qkvo"}
    crs = {n: part(w_crs, n) for n in "qkvo"}
    up = jnp.concatenate([w_ffn[0, :, :hidden], w_ffn[1, :, :hidden]], axis=1)
    down_t = jnp.concatenate([w_ffn[0, :, hidden:], w_ffn[1, :, hidden:]], axis=1)

    positions = jnp.arange(slot)
    own_length = jnp.where(lay.is_decoder, lengths[1, item], lengths[0, item])
    self_allowed = (positions[None, :] < own_length) & (
        (positions[None, :] <= positions[:, None]) | jnp.logical_not(lay.is_decoder)
    )
    cross_allowed = jnp.broadcast_to(
        ((positions < lengths[0, item]) & (task_mask[item] == 1))[None], (slot, slot)
    )

    def joined(partial):
        low = partial.astype(LOW)
        return low.astype(WIDE) + lay.other_core(low).astype(WIDE)

    normed0 = layer_norm(x_rows, gains[0]).astype(LOW)
    q, k, v = (mm(normed0, att[n]).astype(LOW) for n in "qkv")
    out_self, lse_self = attend(q, k, v, self_allowed)
    x_mid = x_rows + joined(mm_nt(out_self, att["o"]))
    normed1 = layer_norm(x_mid, gains[1]).astype(LOW)

    pre_enc = mm(normed1, up)
    act_enc, slope_enc = gelu_parts(pre_enc)
    act_enc = act_enc.astype(LOW)
    x_late_enc = x_mid + joined(mm_nt(act_enc, down_t))
    memory_enc = layer_norm(x_late_enc, gains[2]).astype(LOW)
    memory = lay.route(memory_enc, lambda c, z, t: (c, z, t ^ 1) if t % 2 == 0 else None)

    cq = mm(normed1, crs["q"]).astype(LOW)
    ck, cv = (mm(memory, crs[n]).astype(LOW) for n in "kv")
    out_cross, lse_cross = attend(cq, ck, cv, cross_allowed)
    x_late = x_mid + joined(mm_nt(out_cross, crs["o"]))
    normed2 = layer_norm(x_late, gains[2]).astype(LOW)
    pre_dec = mm(normed2, up)
    act_dec, slope_dec = gelu_parts(pre_dec)
    act_dec = act_dec.astype(LOW)
    result_dec = (x_late + joined(mm_nt(act_dec, down_t))).astype(LOW)

    d_out = cotangent.astype(WIDE)
    d_pre = (slope_dec * mm(cotangent, down_t)).astype(LOW)
    d_ffn_dec = jnp.concatenate([mm_tn(normed2, d_pre), mm_tn(cotangent, act_dec)], axis=1)
    d_late_norm, d_gain2_dec = norm_back(x_late, gains[2], joined(mm_nt(d_pre, up)))
    d_late = d_out + d_late_norm
    grad_late = d_late.astype(LOW)
    d_att = mm(grad_late, crs["o"]).astype(LOW)
    d_cq, d_ck, d_cv = attend_back(cq, ck, cv, lse_cross, d_att, cross_allowed)
    d_memory = joined(mm_nt(d_ck, crs["k"]) + mm_nt(d_cv, crs["v"]))
    d_crs = {
        "q": mm_tn(normed1, d_cq),
        "k": mm_tn(memory, d_ck),
        "v": mm_tn(memory, d_cv),
        "o": mm_tn(grad_late, out_cross),
    }
    d_mid_norm, d_gain1_dec = norm_back(x_mid, gains[1], joined(mm_nt(d_cq, crs["q"])))
    d_mid_dec = d_late + d_mid_norm

    d_memory = lay.route(d_memory.astype(LOW), lambda c, z, t: (c, z, t ^ 1) if t % 2 == 1 else None).astype(WIDE)
    d_late_enc, d_gain2_enc = norm_back(x_late_enc, gains[2], d_memory)
    grad_late_enc = d_late_enc.astype(LOW)
    d_pre = (slope_enc * mm(grad_late_enc, down_t)).astype(LOW)
    d_ffn_enc = jnp.concatenate([mm_tn(normed1, d_pre), mm_tn(grad_late_enc, act_enc)], axis=1)
    d_mid_norm, d_gain1_enc = norm_back(x_mid, gains[1], joined(mm_nt(d_pre, up)))
    d_mid_enc = d_late_enc + d_mid_norm

    d_mid = jnp.where(lay.is_decoder, d_mid_dec, d_mid_enc)
    grad_mid = d_mid.astype(LOW)
    d_att = mm(grad_mid, att["o"]).astype(LOW)
    d_q, d_k, d_v = attend_back(q, k, v, lse_self, d_att, self_allowed)
    d_norm = joined(mm_nt(d_q, att["q"]) + mm_nt(d_k, att["k"]) + mm_nt(d_v, att["v"]))
    d_att_w = {
        "q": mm_tn(normed0, d_q),
        "k": mm_tn(normed0, d_k),
        "v": mm_tn(normed0, d_v),
        "o": mm_tn(grad_mid, out_self),
    }
    d_first, d_gain0 = norm_back(x_rows, gains[0], d_norm)
    d_rows = d_mid + d_first

    half = 3 * HEAD

    def blocks(parts):
        return jnp.stack(
            [pack_heads({n: parts[n][:, half * b : half * (b + 1)] for n in parts}) for b in range(2)]
        )

    def feed_blocks(both):
        total = both.shape[1] // 2
        return jnp.stack(
            [
                jnp.concatenate(
                    [both[:, hidden * b : hidden * (b + 1)], both[:, total + hidden * b : total + hidden * (b + 1)]],
                    axis=1,
                )
                for b in range(2)
            ]
        )

    self_total = blocks(d_att_w)
    home_self = hand_back(lay, ring_scatter(lay, self_total, 0), 0, 0) + hand_back(
        lay, ring_scatter(lay, self_total, 1), 1, 1
    )
    home_feed = hand_back(lay, ring_scatter(lay, feed_blocks(d_ffn_enc), 0), 0, 0) + hand_back(
        lay, ring_scatter(lay, feed_blocks(d_ffn_dec), 1), 1, 1
    )
    cross_total = ring_scatter(lay, blocks(d_crs), 1)
    side = lambda names: jnp.stack(
        [jnp.concatenate([unpack_heads(cross_total[b], n) for n in names], axis=1) for b in range(2)]
    )
    home_cross = hand_back(lay, side("kv"), 1, 0) + hand_back(lay, side("qo"), 1, 1)

    g_self = jnp.stack([unpack_heads(home_self, n) for n in "qkv"], axis=1)[None]
    g_self_out = unpack_heads(home_self, "o").T[None]
    g_cross = home_cross.reshape(1, depth, 2, wide)
    g_up = home_feed[:, :hidden][None]
    g_down = home_feed[:, hidden:].T[None]

    gain2 = jnp.where(lay.is_decoder, d_gain2_dec, d_gain2_enc)
    gain1 = jnp.where(lay.is_decoder, d_gain1_dec, d_gain1_enc)
    gain_rows = jnp.stack([d_gain0, gain1, gain2])
    slots = jnp.stack(
        [
            jnp.where((lay.role == r) & (lay.core == 0), gain_rows, 0.0)
            for r in range(2)
        ]
    )
    gain_total = lax.psum(slots, AXES)[sec][None]

    def rows_home(value):
        mine = lax.dynamic_slice_in_dim(value, lay.core * 2 * rows, 2 * rows, 0).reshape(2, rows, width)
        a = lay.route(mine[item], lambda c, z, t: (t % 2, z, 2 * c + t // 2))
        b = lay.route(mine[1 - item], lambda c, z, t: (t % 2, z, 2 * c + 1 - t // 2))
        even = lay.chip % 2 == 0
        return jnp.where(even, jnp.stack([a, b]), jnp.stack([b, a]))[None]

    block_output = rows_home(jnp.where(lay.is_decoder, result_dec, memory_enc))
    input_grad = rows_home(d_rows.astype(LOW)).astype(WIDE)
    return (
        block_output,
        input_grad,
        g_self,
        g_self_out,
        g_cross,
        g_up,
        g_down,
        gain_total[:, :2],
        gain_total[:, 2],
    )


def body(block_input, w_self, w_self_out, w_cross, w_up, w_down, norm_gains, lengths, task_mask, out_grad):
    lay = Layout()
    seqs, rows, width = block_input.shape[1:]
    slot = rows * lay.chips
    sec = lay.core
    item = lay.item

    if lay.planes != 4:
        return general_body(
            block_input, w_self, w_self_out, w_cross, w_up, w_down, norm_gains, lengths, task_mask, out_grad
        )

    depth = w_self.shape[1]
    wide = w_self.shape[3]
    hidden = w_up.shape[2]
    self_block = pack_heads(
        {"q": w_self[0, :, 0], "k": w_self[0, :, 1], "v": w_self[0, :, 2], "o": w_self_out[0].T}
    )
    pair = {"q": w_cross[0, :, 0], "o": w_cross[0, :, 1], "k": w_cross[0, :, 0], "v": w_cross[0, :, 1]}
    pieces = [pair[n][:, HEAD * h : HEAD * (h + 1)] for n, h in ORDER]
    cross_block = jnp.where(
        sec == 1, jnp.concatenate(pieces[:6], axis=1), jnp.concatenate(pieces[6:], axis=1)
    )
    gain_block = jnp.concatenate([norm_gains[0].astype(WIDE), jnp.zeros((5, width), WIDE)], axis=0)

    positions = jnp.arange(slot)
    own_length = jnp.where(lay.is_decoder, lengths[1, item], lengths[0, item])

    def key_bias(allowed):
        return jnp.broadcast_to(jnp.where(allowed, 0.0, NEG_FILL)[:, None], (slot, TILE)).astype(LOW)

    biases = (
        key_bias(positions < own_length),
        key_bias((positions < lengths[0, item]) & (task_mask[item] == 1)),
    )
    kept = forward_call(
        lay.planes,
        slot,
        width,
        hidden,
        (self_block, cross_block, w_up[0], w_down[0].T, block_input[0], out_grad, gain_block) + biases,
    )
    block_output, input_grad, home_feed, home_cross, home_self, gain_total = backward_call(
        lay.planes, slot, width, hidden, depth, tuple(kept) + biases
    )[:6]
    home_self, home_feed, home_cross = (v.astype(WIDE) for v in (home_self, home_feed, home_cross))
    g_self = jnp.stack([unpack_heads(home_self, n) for n in "qkv"], axis=1)[None]
    g_self_out = unpack_heads(home_self, "o").T[None]
    halves = (ORDER[:6], ORDER[6:])
    take = lambda order, name: jnp.concatenate(
        [home_cross[:, HEAD * order.index((name, h)) : HEAD * (order.index((name, h)) + 1)] for h in range(3)], axis=1
    )
    g_cross = jnp.where(
        sec == 1,
        jnp.stack([take(halves[0], "q"), take(halves[0], "o")], axis=1),
        jnp.stack([take(halves[1], "k"), take(halves[1], "v")], axis=1),
    )[None]
    g_up = home_feed[:, :hidden][None]
    g_down = home_feed[:, hidden:].T[None]
    gain_total = gain_total[None]
    return (
        block_output[None],
        input_grad.astype(WIDE)[None],
        g_self,
        g_self_out,
        g_cross,
        g_up,
        g_down,
        gain_total[:, :2],
        gain_total[:, 2],
    )


def solution(mesh):
    placed = (
        P("section", "dp", "tensor", None),
        P("section", "dp", None, "tensor"),
        P("section", "tensor", "dp"),
        P("section", "dp", None, "tensor"),
        P("section", "dp", "tensor"),
        P("section", "tensor", "dp"),
        P("section", None, None),
        P(None, "dp"),
        P("dp", None),
        P("dp", "tensor", None),
    )
    return jax.shard_map(
        body,
        mesh=mesh,
        in_specs=placed,
        out_specs=(
            P("section", "dp", "tensor", None),
            P("section", "dp", "tensor", None),
            P("section", "dp", None, "tensor"),
            P("section", "tensor", "dp"),
            P("section", "dp", None, "tensor"),
            P("section", "dp", "tensor"),
            P("section", "tensor", "dp"),
            P("section", None, None),
            P("section", None),
        ),
        check_vma=False,
    )
```

```python
import functools

import jax
import jax.numpy as jnp
from jax import lax
from jax.experimental import pallas as pl
from jax.experimental.pallas import tpu as pltpu
from jax.sharding import PartitionSpec as P

HEAD = 64
TILE = 128
EPSILON = 1e-05
SCORE_SCALE = 0.125
NEG_FILL = -1000000000.0
AXES = ("section", "dp", "tensor")
LOW = jnp.bfloat16
WIDE = jnp.float32


class Layout:
    def __init__(self):
        self.cores = lax.axis_size("section")
        self.planes = lax.axis_size("dp")
        self.chips = lax.axis_size("tensor")
        self.core = lax.axis_index("section")
        self.plane = lax.axis_index("dp")
        self.chip = lax.axis_index("tensor")
        self.role = self.chip % 2
        self.item = self.chip // 2
        self.is_decoder = self.role == 1
        self.relays = self.core == self.item

    def route(self, value, target):
        pairs = []
        for core in range(self.cores):
            for plane in range(self.planes):
                for chip in range(self.chips):
                    to = target(core, plane, chip)
                    if to is None:
                        continue
                    source = (core * self.planes + plane) * self.chips + chip
                    goal = (to[0] * self.planes + to[1]) * self.chips + to[2]
                    pairs.append((source, goal))
        return lax.ppermute(value, AXES, pairs)

    def other_core(self, value):
        return self.route(value, lambda c, z, t: (1 - c, z, t))


def normalize(values):
    centred = values - jnp.mean(values, axis=-1, keepdims=True)
    spread = jnp.mean(centred * centred, axis=-1, keepdims=True)
    scale = lax.rsqrt(spread + EPSILON)
    return centred * scale, scale


def layer_norm(values, gain):
    return normalize(values)[0] * gain


def norm_back(values, gain, grad):
    normal, scale = normalize(values)
    scaled = grad * gain
    first = jnp.mean(scaled, axis=-1, keepdims=True)
    second = jnp.mean(scaled * normal, axis=-1, keepdims=True)
    return (scaled - first - normal * second) * scale, jnp.sum(grad * normal, axis=0)


ORDER = (("q", 0), ("q", 1), ("q", 2), ("o", 2), ("o", 0), ("o", 1), ("k", 0), ("k", 1), ("v", 0), ("v", 1), ("k", 2), ("v", 2))


def pack_heads(parts):
    return jnp.concatenate([parts[n][:, HEAD * h : HEAD * (h + 1)] for n, h in ORDER], axis=1)


def unpack_heads(block, name):
    where = {(n, h): i for i, (n, h) in enumerate(ORDER)}
    return jnp.concatenate(
        [block[:, HEAD * where[(name, h)] : HEAD * (where[(name, h)] + 1)] for h in range(3)], axis=1
    )


def mm(left, right):
    return jnp.dot(left, right, preferred_element_type=WIDE)


def mm_nt(left, right):
    return lax.dot_general(left, right, (((1,), (1,)), ((), ())), preferred_element_type=WIDE)


def mm_tn(left, right):
    return lax.dot_general(left, right, (((0,), (0,)), ((), ())), preferred_element_type=WIDE)


def split_heads(value):
    return value.reshape(value.shape[0], -1, HEAD)


def attend(q, k, v, allowed):
    scores = jnp.einsum("qhd,khd->hqk", split_heads(q), split_heads(k), preferred_element_type=WIDE) * SCORE_SCALE
    scores = jnp.where(allowed[None], scores, NEG_FILL)
    top = jnp.max(scores, axis=-1, keepdims=True)
    power = jnp.exp(scores - top)
    total = jnp.sum(power, axis=-1, keepdims=True)
    probs = (power / total).astype(LOW)
    out = jnp.einsum("hqk,khd->qhd", probs, split_heads(v), preferred_element_type=WIDE)
    return out.astype(LOW).reshape(q.shape), top + jnp.log(total)


def attend_back(q, k, v, log_sum, d_out, allowed):
    scores = jnp.einsum("qhd,khd->hqk", split_heads(q), split_heads(k), preferred_element_type=WIDE) * SCORE_SCALE
    scores = jnp.where(allowed[None], scores, NEG_FILL)
    probs = jnp.exp(scores - log_sum)
    d_probs = jnp.einsum("qhd,khd->hqk", split_heads(d_out), split_heads(v), preferred_element_type=WIDE)
    inner = jnp.sum(probs * d_probs, axis=-1, keepdims=True)
    d_scores = (probs * (d_probs - inner)).astype(LOW)
    d_v = jnp.einsum("hqk,qhd->khd", probs.astype(LOW), split_heads(d_out), preferred_element_type=WIDE)
    d_q = jnp.einsum("hqk,khd->qhd", d_scores, split_heads(k), preferred_element_type=WIDE) * SCORE_SCALE
    d_k = jnp.einsum("hqk,qhd->khd", d_scores, split_heads(q), preferred_element_type=WIDE) * SCORE_SCALE
    return tuple(g.astype(LOW).reshape(q.shape) for g in (d_q, d_k, d_v))


def gelu_parts(value):
    coef = 0.7978845608028654
    cube = 0.044715
    inner = coef * (value + cube * value * value * value)
    soft = jnp.tanh(inner)
    slope = 0.5 * (1.0 + soft) + 0.5 * value * (1.0 - soft * soft) * coef * (1.0 + 3.0 * cube * value * value)
    return 0.5 * value * (1.0 + soft), slope


MESH = pl.DeviceIdType.MESH
GROUPS = ("att", "crs", "up", "dn")
BLOCK = 256
VMEM_BYTES = 62 * 2**20


def lanes(shape):
    return lax.broadcasted_iota(jnp.int32, shape, len(shape) - 1)


def subs(shape):
    return lax.broadcasted_iota(jnp.int32, shape, 0)


def strip(i, size):
    return pl.ds(pl.multiple_of(i * size, size), size)


def head_place(h):
    two = (h == 2).astype(jnp.int32)
    one = (h >= 1).astype(jnp.int32)
    return two, 2 + 2 * two, 3 + two, 1 - two, HEAD * (one - two), HEAD * one


def each(count, step, name=None):
    def run(i, carry):
        step(i)
        return carry

    with jax.named_scope(name or step.__name__):
        lax.fori_loop(0, count, run, 0)


class Place:
    def __init__(self, planes):
        self.planes = planes
        self.c = lax.axis_index("section")
        self.z = lax.axis_index("dp")
        self.t = lax.axis_index("tensor")
        self.y = lax.div(self.t, 2)
        self.r = lax.rem(self.t, 2)
        self.twin = (1 - self.c, self.z, self.t)
        self.above = (self.c, lax.rem(self.z + 1, planes), self.t)
        self.below = (self.c, lax.rem(self.z + planes - 1, planes), self.t)
        self.across = (self.c, self.z, lax.rem(self.t + 2, 4))
        self.beside = (self.c, self.z, self.t + 1 - 2 * self.r)
        self.relays = self.c == self.y
        self.encodes = self.r == 0
        self.decodes = self.r == 1

    def meet(self):
        barrier = pltpu.get_barrier_semaphore()
        peers = [self.above, self.below]
        for dc in range(2):
            for dt in range(4):
                if dc or dt:
                    peers.append((lax.rem(self.c + dc, 2), self.z, lax.rem(self.t + dt, 4)))
        for peer in peers:
            pl.semaphore_signal(barrier, inc=1, device_id=peer, device_id_type=MESH)
        pl.semaphore_wait(barrier, len(peers))


def push(source, goal, sent, got, device):
    return pltpu.make_async_remote_copy(
        src_ref=source, dst_ref=goal, send_sem=sent, recv_sem=got, device_id=device, device_id_type=MESH
    )


def both(first, second):
    return jnp.logical_and(first, second)


def center(values):
    middle = values - jnp.mean(values, axis=-1, keepdims=True)
    scale = lax.rsqrt(jnp.mean(middle * middle, axis=-1, keepdims=True) + EPSILON)
    return middle * scale, scale


def attend_block(h, p, o, lse, lse_row, bias, kx, qx, vt, causal):
    count = p.shape[0]
    qt, kt, vtile, ot, qlo, vlo = head_place(h)
    lane = lanes((count, TILE))
    in_q = both(lane >= qlo, lane < qlo + HEAD)
    in_v = both(lane >= vlo, lane < vlo + HEAD)
    spare = HEAD - qlo
    kx[...] = jnp.where(lane == spare, bias[...], jnp.where(in_q, p[:, strip(kt, TILE)], jnp.zeros((), LOW)))
    vt[...] = jnp.where(in_v, p[:, strip(vtile, TILE)].astype(WIDE), 1.0).T.astype(LOW)
    qx[...] = jnp.where(
        in_q, p[:, strip(qt, TILE)].astype(WIDE) * SCORE_SCALE, jnp.where(lane == spare, 1.0, 0.0)
    ).astype(LOW)
    scores = mm_nt(kx[...], qx[...])
    if causal:
        scores = jnp.where(subs(scores.shape) <= lanes(scores.shape), scores, NEG_FILL)
    top = jnp.max(scores, axis=0, keepdims=True)
    power = jnp.exp(scores - top).astype(LOW)
    out = mm(vt[...], power)
    total = jnp.where(vlo == 0, out[HEAD : HEAD + 1, :], out[0:1, :])
    result = (out / total).T
    o[:, strip(ot, TILE)] = jnp.where(in_v, result, o[:, strip(ot, TILE)].astype(WIDE)).astype(LOW)
    row = subs((8, count))
    lse[...] = jnp.where(row == lse_row, top + jnp.log(total), lse[...])


SUMS = ("ffn", "crs", "att")
DIRECT = ("att", "up")


def split_three(value):
    high = value.astype(LOW).astype(WIDE)
    middle = (value - high).astype(LOW).astype(WIDE)
    return high, middle, value - high - middle


def attend_back_block(h, p, o, d_o, d_p, lse, lse_row, bias, kx, qx, vx, gx, kt_v, causal):
    count = p.shape[0]
    qt, kt, vtile, ot, qlo, vlo = head_place(h)
    lane = lanes((count, TILE))
    in_q = both(lane >= qlo, lane < qlo + HEAD)
    in_v = both(lane >= vlo, lane < vlo + HEAD)
    sq, sv = HEAD - qlo, HEAD - vlo
    keys = jnp.where(
        in_q, p[:, strip(kt, TILE)].astype(WIDE), jnp.where(both(lane > sq, lane < sq + 4), 1.0, 0.0)
    )
    keys = jnp.where(lane == sq, bias[...].astype(WIDE), keys)
    kx[...] = keys.astype(LOW)
    kt_v[...] = keys.T.astype(LOW)
    vx[...] = jnp.where(
        in_v, p[:, strip(vtile, TILE)].astype(WIDE), jnp.where(both(lane >= sv, lane < sv + 3), 1.0, 0.0)
    ).astype(LOW)
    own = jnp.sum(jnp.where(subs((8, count)) == lse_row, lse[...], 0.0), axis=0, keepdims=True)
    a, b, c = split_three(-jnp.broadcast_to(own, (TILE, count)).T)
    extra = jnp.where(
        lane == sq,
        1.0,
        jnp.where(lane == sq + 1, a, jnp.where(lane == sq + 2, b, jnp.where(lane == sq + 3, c, 0.0))),
    )
    qx[...] = jnp.where(in_q, p[:, strip(qt, TILE)].astype(WIDE) * SCORE_SCALE, extra).astype(LOW)
    grad = jnp.where(in_v, d_o[:, strip(ot, TILE)].astype(WIDE), 0.0)
    inner = jnp.sum(grad * o[:, strip(ot, TILE)].astype(WIDE), axis=-1, keepdims=True)
    a, b, c = split_three(-inner)
    gx[...] = (
        grad + jnp.where(lane == sv, a, jnp.where(lane == sv + 1, b, jnp.where(lane == sv + 2, c, 0.0)))
    ).astype(LOW)
    scores = mm_nt(kx[...], qx[...])
    if causal:
        scores = jnp.where(subs(scores.shape) <= lanes(scores.shape), scores, NEG_FILL)
    probs = jnp.exp(scores)
    d_scores = (probs * mm_nt(vx[...], gx[...])).astype(LOW)
    d_v = mm(probs.astype(LOW), gx[...])
    d_k = mm(d_scores, qx[...])
    d_q = mm(kt_v[...], d_scores).T * SCORE_SCALE

    def place(tile_index, inside, value):
        cut = strip(tile_index, TILE)
        d_p[:, cut] = jnp.where(inside, value, d_p[:, cut].astype(WIDE)).astype(LOW)

    place(qt, in_q, d_q)
    place(kt, in_q, d_k)
    place(vtile, in_v, d_v)


def block_kernel(
    planes, self_in, crs_in, up_in, dn_in, x_in, cot_in, gain_in, bias_self, bias_cross,
    block_out, grad_out, home_ffn, home_crs, home_att, gain_out,
    cot, first_k, x_k, second_k, late_k, memory_k, p_k, o_k, lse_k, pc_k, oc_k, lsec_k, act_k, grad_k, y3_k,
    dw_ffn, dw_crs, dw_att, yb_ffn, yb_crs, yb_att, zb_ffn, zb_crs, zb_att,
    att_v, crs_v, up_v, dn_v, a_v, b_v, o_v, do_v, mid_v, late_v, s_v, g_v, c_v, ta, tb, tc,
    send_v, recv_v, kx, qx, vx, gx, kt_v, lse_v, gain_v, gain_in_v, gain_buf, out_st, dw_st, sum_st,
    x_sem, x_sent, y0_sent, c_sem, zw_got, zw_sent, yw_got, yw_sent,
    row_got, row_sent, fwd_sem, cot_got, gain_sem, copy_sem, ex_got, ex_sent, mem_got, mem_sent, mf_got, mf_sent,
    dm_got, dm_sent, df_got, df_sent, y_got, y_sent, z_got, z_sent, home_got, home_sent,
    blk_got, blk_sent, gr_got, gr_sent, gr_hop_got, gr_hop_sent, sum_sem, dw_sem,
):
    at = Place(planes)
    c, z, t, y, r = at.c, at.z, at.t, at.y, at.r
    rows = x_in.shape[1]
    slot = s_v.shape[0]
    tiles = slot // BLOCK
    depth = up_in.shape[0]
    side = crs_in.shape[1]
    relay = at.relays
    other = jnp.logical_not(relay)
    vmem = {"att": att_v, "crs": crs_v, "up": up_v, "dn": dn_v}
    shard = {"att": self_in, "up": up_in, "dn": dn_in}
    here = pl.ds(pl.multiple_of(z * depth, depth), depth)
    dw = {"ffn": dw_ffn, "crs": dw_crs, "att": dw_att}
    yb = {"ffn": yb_ffn, "crs": yb_crs, "att": yb_att}
    zb = {"ffn": zb_ffn, "crs": zb_crs, "att": zb_att}
    home = {"ffn": home_ffn, "crs": home_crs, "att": home_att}
    names = {}

    def copying(name, source, goal):
        index = names.setdefault(name, len(names))
        return pltpu.make_async_copy(source, goal, copy_sem.at[index])

    def half_of(core):
        return pl.ds(pl.multiple_of(core * 2 * rows, 2 * rows), 2 * rows)

    at.meet()

    relay_dev = (y, z, 2 * y + c)
    over_dev = (y, z, 2 * (1 - y) + c)
    stays = both(c == y, r == c)

    def launch(g):
        i = GROUPS.index(g)
        goal = vmem[g].at[r, here, :]

        @pl.when(stays)
        def _():
            pltpu.make_async_copy(shard[g], goal, x_sem.at[i, r]).start()

        @pl.when(jnp.logical_not(stays))
        def _():
            push(shard[g], goal, x_sent.at[i], x_sem.at[i, r], relay_dev).start()

    def launch_over(g):
        i = GROUPS.index(g)
        return push(shard[g], vmem[g].at[r, here, :], y0_sent.at[i], yw_got.at[i, 0, r], over_dev)

    crs_dev = (y, z, 2 * y + 1)
    crs_stays = both(c == y, r == 1)

    def crs_goal(block, section):
        return crs_v.at[block, here, pl.ds(pl.multiple_of((1 - section) * side, side), side)]

    def launch_crs():
        @pl.when(crs_stays)
        def _():
            pltpu.make_async_copy(crs_in, crs_goal(r, c), c_sem.at[r, c]).start()

        @pl.when(jnp.logical_not(crs_stays))
        def _():
            push(crs_in, crs_goal(r, c), x_sent.at[1], c_sem.at[r, c], crs_dev).start()

    row_goal = s_v.at[strip(t, rows), :]
    cot_goal = cot.at[strip(t, rows), :]

    def row_stays(s):
        return both(both(c == y, r == c), y == s)

    def launch_rows(s):
        dev = (y, z, 2 * s + c)

        @pl.when(row_stays(s))
        def _():
            pltpu.make_async_copy(x_in.at[s], row_goal, row_got.at[r]).start()

        @pl.when(jnp.logical_not(row_stays(s)))
        def _():
            push(x_in.at[s], row_goal, row_sent.at[s], row_got.at[r], dev).start()

    def launch_cot():
        dev = (y, z, 2 * c + 1)

        @pl.when(crs_stays)
        def _():
            pltpu.make_async_copy(cot_in.at[c], cot_goal, cot_got.at[r]).start()

        @pl.when(jnp.logical_not(crs_stays))
        def _():
            push(cot_in.at[c], cot_goal, row_sent.at[2], cot_got.at[r], dev).start()

    gain_copy = push(gain_in, gain_in_v.at[c], gain_sem.at[0], gain_sem.at[1], at.twin)
    gain_copy.start()
    launch("att")
    launch_over("att").start()
    launch_rows(0)
    launch_rows(1)
    launch("up")
    launch_over("up").start()
    launch_crs()
    launch("dn")
    launch_cot()

    def piece(g, k, b):
        j = lax.rem(z - k + planes, planes)
        return vmem[g].at[b, pl.ds(pl.multiple_of(j * depth, depth), depth), :]

    def ring(g, k, b):
        i = GROUPS.index(g)
        return push(
            piece(g, k - 1, b), piece(g, k - 1, b), zw_sent.at[i, k - 1, b], zw_got.at[i, k - 1, b], at.above
        )

    def ring_in(g, k, b):
        i = GROUPS.index(g)
        return push(piece(g, k, b), piece(g, k, b), zw_sent.at[i, k - 1, b], zw_got.at[i, k - 1, b], at.above)

    def cross_over(g, k, b):
        i = GROUPS.index(g)
        return push(piece(g, k, b), piece(g, k, b), yw_sent.at[i, k, b], yw_got.at[i, k, b], at.across)

    def arrive(g, k, b):
        if k:
            ring_in(g, k, b).wait_recv()
        elif g == "crs":
            for section in range(2):
                goal = crs_goal(b, section)
                push(goal, goal, x_sent.at[1], c_sem.at[b, section], at.twin).wait_recv()
        else:
            i = GROUPS.index(g)
            goal = vmem[g].at[b, here, :]
            push(goal, goal, x_sent.at[i], x_sem.at[i, b], at.twin).wait_recv()

    def passing(g, k, up=True, over=True):
        def run():
            for b in range(2):
                if up:
                    arrive(g, k, b)
                    if k + 1 < planes:
                        ring(g, k + 1, b).start()
                if over and not (k == 0 and g in DIRECT):
                    cross_over(g, k, b).start()

        return run

    def schedule(order):
        events = []
        for n, g in enumerate(order):
            for k in range(planes):
                if k == 0 and n == 0:
                    events.append(passing(g, 0))
                elif k:
                    events.append(passing(g, k))
                if n + 1 < len(order):
                    if k == planes - 2:
                        events[-1] = chained(events[-1], passing(order[n + 1], 0, True, False))
                    if k == planes - 1:
                        events[-1] = chained(events[-1], passing(order[n + 1], 0, False, True))
        return events

    def chained(one, two):
        def run():
            one()
            two()

        return run

    enc_events = schedule(("att", "up", "dn"))
    dec_events = schedule(("att", "crs", "up", "dn"))

    def pump_enc(count):
        for _ in range(min(count, len(enc_events))):
            pl.when(both(relay, at.encodes))(enc_events.pop(0))

    def pump_dec(count):
        for _ in range(min(count, len(dec_events))):
            pl.when(both(relay, at.decodes))(dec_events.pop(0))

    def pump(count):
        pump_enc(count)
        pump_dec(count)

    def settle(g):
        listens = both(other, at.decodes) if g == "crs" else other

        @pl.when(listens)
        def _():
            for k in range(planes):
                for b in range(2):
                    cross_over(g, k, b).wait_recv()

    def exchange(e, i):
        q = strip(i, BLOCK)
        k = e % 2
        return push(send_v.at[k, q, :], recv_v.at[k, q, :], ex_sent.at[e, i], ex_got.at[e, i], at.twin)

    def joined(e, i):
        q = strip(i, BLOCK)
        exchange(e, i).wait_recv()
        return send_v[e % 2, q, :].astype(WIDE) + recv_v[e % 2, q, :].astype(WIDE)

    def sent(e):
        each(tiles, lambda i: exchange(e, i).wait_send())

    pump(1)
    for k in range(2):
        goal = s_v.at[strip(2 * c + k, rows), :]
        push(goal, goal, row_sent.at[0], row_got.at[k], at.twin).wait_recv()
    half, far_half = half_of(c), half_of(1 - c)
    rows_on = push(s_v.at[half, :], s_v.at[half, :], fwd_sem.at[0], fwd_sem.at[1], at.twin)
    rows_on.start()
    pump(1)
    push(gain_in, gain_in_v.at[1 - c], gain_sem.at[0], gain_sem.at[1], at.twin).wait_recv()
    gain_here = pltpu.make_async_copy(gain_in, gain_in_v.at[c], gain_sem.at[2])
    gain_here.start()
    gain_here.wait()
    gains = gain_in_v.at[r]
    g0, g1, g2 = gains[0:1, :], gains[1:2, :], gains[2:3, :]
    gain_v[...] = jnp.zeros_like(gain_v)
    push(s_v.at[far_half, :], s_v.at[far_half, :], fwd_sem.at[0], fwd_sem.at[1], at.twin).wait_recv()
    x_put = copying("x", s_v, x_k)
    x_put.start()

    def enter(i):
        q = strip(i, BLOCK)
        c_v[q, :] = (center(s_v[q, :].astype(WIDE))[0] * g0).astype(LOW)

    each(tiles, enter)
    first_put = copying("first", c_v, first_k)
    first_put.start()
    pump(2)
    settle("att")

    def project(source, weights, part):
        def project_rows(i):
            q = strip(i, BLOCK)
            for b in range(2):
                if part != "kv":
                    a_v[b, q, 0:256] = mm(source[q, :], weights[b, :, 0:256]).astype(LOW)
                if part != "q":
                    a_v[b, q, 256:640] = mm(source[q, :], weights[b, :, 384:768]).astype(LOW)

        each(tiles, project_rows)

    packed_v = a_v.at[:, :, 0:640]
    project(c_v, att_v, "all")
    p_put = copying("p", packed_v, p_k)
    p_put.start()
    o_v[...] = jnp.zeros_like(o_v)
    lse_v[...] = jnp.zeros_like(lse_v)
    pump(1)

    def attend_heads(bias, causal, hooks):
        def head_forward(n):
            b = lax.div(n, 3)
            attend_block(lax.rem(n, 3), a_v.at[b], o_v.at[b], lse_v, n, bias, kx, qx, kt_v, causal)
            for when, event in hooks:
                pl.when(both(n == when, relay))(event)

        each(6, head_forward)

    enc_hooks = [(2, enc_events.pop(0)), (5, enc_events.pop(0))]
    dec_hooks = [(2, dec_events.pop(0)), (5, dec_events.pop(0))]
    pl.when(at.encodes)(lambda: attend_heads(bias_self, False, enc_hooks))
    pl.when(at.decodes)(lambda: attend_heads(bias_self, True, dec_hooks))
    o_put, lse_put = copying("o", o_v, o_k), copying("lse", lse_v, lse_k)
    o_put.start()
    lse_put.start()

    def out_project(e, weights):
        def out_rows(i):
            q = strip(i, BLOCK)
            part = mm_nt(o_v[0, q, :], weights[0, :, 128:384]) + mm_nt(o_v[1, q, :], weights[1, :, 128:384])
            send_v[e % 2, q, :] = part.astype(LOW)
            exchange(e, i).start()

        each(tiles, out_rows)

    out_project(0, att_v)
    pump(1)
    x_put.wait()
    rows_on.wait_send()

    def middle(i):
        q = strip(i, BLOCK)
        value = s_v[q, :].astype(WIDE) + joined(0, i)
        mid_v[q, :] = value
        s_v[q, :] = (center(value)[0] * g1).astype(LOW)

    each(tiles, middle)
    first_put.wait()
    p_put.wait()
    o_put.wait()
    lse_put.wait()

    def mem_send(i):
        q = pl.ds(pl.multiple_of((2 * c + i) * BLOCK, BLOCK), BLOCK)
        return push(g_v.at[q, :], g_v.at[q, :], mem_sent.at[i], mem_got.at[i], at.beside)

    def mem_forward(i, core):
        q = pl.ds(pl.multiple_of((2 * core + i) * BLOCK, BLOCK), BLOCK)
        return push(g_v.at[q, :], g_v.at[q, :], mf_sent.at[i], mf_got.at[i], at.twin)

    def row_home(k, source, goal, sent_by, got):
        dev = (r, z, 2 * c + k)
        keeps = both(both(c == r, y == c), r == k)
        return keeps, source, goal.at[y], sent_by.at[k], got.at[y], dev

    def go_home(*spec):
        keeps, source, goal, sent_by, got, dev = row_home(*spec)

        @pl.when(keeps)
        def _():
            pltpu.make_async_copy(source, goal, got).start()

        @pl.when(jnp.logical_not(keeps))
        def _():
            push(source, goal, sent_by, got, dev).start()

    def went_home(*spec):
        keeps, source, goal, sent_by, got, dev = row_home(*spec)

        @pl.when(jnp.logical_not(keeps))
        def _():
            push(source, goal, sent_by, got, dev).wait_send()

    def memory_home(k):
        return k, memory_k.at[strip(2 * c + k, rows), :], block_out, blk_sent, blk_got

    settle_up = lambda: settle("up")
    pl.when(at.encodes)(settle_up)

    @pl.when(at.encodes)
    def _():
        def up_rows(i):
            q = strip(i, BLOCK)
            for b in range(2):
                value, grade = gelu_parts(mm(s_v[q, :], up_v[b]))
                a_v[b, q, :] = value.astype(LOW)
                b_v[b, q, :] = grade.astype(LOW)

        each(tiles, up_rows)

    pump_enc(9)

    @pl.when(at.encodes)
    def _():
        settle("dn")

        def down_rows(i):
            q = strip(i, BLOCK)
            part = mm_nt(a_v[0, q, :], dn_v[0]) + mm_nt(a_v[1, q, :], dn_v[1])
            send_v[1, q, :] = part.astype(LOW)
            exchange(1, i).start()

        each(tiles, down_rows)

        def finish(n):
            i = lax.rem(n + 2 * c, 4)
            q = strip(i, BLOCK)
            value = mid_v[q, :] + joined(1, i)
            late_v[q, :] = value
            g_v[q, :] = (center(value)[0] * g2).astype(LOW)

            @pl.when(n < 2)
            def _():
                mem_send(n).start()

        each(tiles, finish)
        keep = copying("memory", g_v, memory_k)
        keep.start()
        keep.wait()
        for k in range(2):
            go_home(*memory_home(k))
        sent(0)

    def norm_grad(values, gain, grad, gain_row, counted):
        normal, scale = center(values)
        scaled = grad * gain
        one = jnp.mean(scaled, axis=-1, keepdims=True)
        two = jnp.mean(scaled * normal, axis=-1, keepdims=True)
        total = jnp.sum(grad * normal, axis=0, keepdims=True)
        gain_v[gain_row : gain_row + 1, :] += jnp.where(counted, total, 0.0)
        return (scaled - one - normal * two) * scale

    def ours(i):
        return lax.div(i, 2) == c

    @pl.when(at.decodes)
    def _():
        second_put = copying("second", s_v, second_k)
        second_put.start()
        for k in range(2):
            goal = cot.at[strip(2 * c + k, rows), :]
            push(goal, goal, row_sent.at[2], cot_got.at[k], at.twin).wait_recv()
        cot_on = push(cot.at[half, :], cot.at[half, :], fwd_sem.at[2], fwd_sem.at[3], at.twin)
        cot_on.start()
        for _ in range(len(dec_events) - 3):
            pl.when(relay)(dec_events.pop(0))
        settle("crs")
        project(s_v, crs_v, "q")
        for _ in range(len(dec_events)):
            pl.when(relay)(dec_events.pop(0))
        push(cot.at[far_half, :], cot.at[far_half, :], fwd_sem.at[2], fwd_sem.at[3], at.twin).wait_recv()
        cot_in_v = copying("cot", cot, c_v)
        cot_in_v.start()
        o_v[...] = jnp.zeros_like(o_v)
        lse_v[...] = jnp.zeros_like(lse_v)
        for i in range(2):
            mem_send(i).wait_recv()
            mem_forward(i, c).start()
        for i in range(2):
            mem_forward(i, 1 - c).wait_recv()
        project(g_v, crs_v, "kv")
        puts = [copying("pc", packed_v, pc_k), copying("memory", g_v, memory_k)]
        for copy in puts:
            copy.start()
        attend_heads(bias_cross, False, [])
        puts += [copying("oc", o_v, oc_k), copying("lsec", lse_v, lsec_k)]
        for copy in puts[2:]:
            copy.start()
        out_project(1, crs_v)
        second_put.wait()

        def finish(i):
            q = strip(i, BLOCK)
            value = mid_v[q, :] + joined(1, i)
            late_v[q, :] = value
            s_v[q, :] = (center(value)[0] * g2).astype(LOW)

        each(tiles, finish)
        late_put = copying("late", late_v, late_k)
        late_put.start()
        settle("up")
        settle("dn")
        cot_in_v.wait()
        sent(0)
        for copy in puts:
            copy.wait()

        def feed_rows(i):
            q = strip(i, BLOCK)
            part = None
            for b in range(2):
                value, grade = gelu_parts(mm(s_v[q, :], up_v[b]))
                a_v[b, q, :] = value.astype(LOW)
                d_pre = (mm(c_v[q, :], dn_v[b]) * grade).astype(LOW)
                b_v[b, q, :] = d_pre
                term = mm_nt(d_pre, up_v[b])
                part = term if part is None else part + term
            send_v[0, q, :] = part.astype(LOW)
            exchange(2, i).start()

        each(tiles, feed_rows)
        copying("act", a_v, act_k).start()
        late_put.wait()
        cot_on.wait_send()
        each(2, lambda i: mem_forward(i, c).wait_send())

    def block_of(k):
        return lax.rem(z - 1 - k + 2 * planes, planes)

    def y_hop(g, k):
        i = SUMS.index(g)
        return push(dw[g].at[k], yb[g].at[k], y_sent.at[i, k], y_got.at[i, k], at.across)

    def z_hop(g, k):
        i = SUMS.index(g)
        return push(dw[g].at[k], zb[g].at[k], z_sent.at[i, k], z_got.at[i, k], at.above)

    def emit(g, compute):
        columns = dw[g].shape[3]

        def put(k, s):
            return pltpu.make_async_copy(dw_st.at[s, :, :, 0:columns], dw[g].at[k], dw_sem.at[s])

        def run(k):
            s = lax.rem(k, 2)
            j = block_of(k)
            compute(s, pl.ds(pl.multiple_of(j * depth, depth), depth))
            put(k, s).start()

            @pl.when(k >= 1)
            def _():
                put(k - 1, 1 - s).wait()
                pl.when(other)(lambda: y_hop(g, k - 1).start())

        each(planes, run, "emit_" + g)
        put(planes - 1, (planes - 1) % 2).wait()
        pl.when(other)(lambda: y_hop(g, planes - 1).start())

    def homes(g):
        columns = dw[g].shape[3]
        source = dw[g].at[planes - 1]
        result = []
        for b in range(2):
            if g == "crs":
                for section in range(2):
                    cut = pl.ds((1 - section) * (columns // 2), columns // 2)
                    result.append(
                        (both(c == section, r == b), source.at[b, :, cut], (section, z, 2 * y + b), 2 * b + section)
                    )
            else:
                result.append((both(c == r, r == b), source.at[b], (r, z, 2 * y + b), b))
        return result

    def summing(g, k):
        i = SUMS.index(g)
        columns = dw[g].shape[3]

        def run():
            y_hop(g, k).wait_recv()
            parts = [dw[g].at[k], yb[g].at[k]]
            if k:
                z_hop(g, k - 1).wait_recv()
                parts.append(zb[g].at[k - 1])
            copies = [
                pltpu.make_async_copy(part, sum_st.at[n, :, :, 0:columns], sum_sem.at[n])
                for n, part in enumerate(parts)
            ]
            for copy in copies:
                copy.start()
            for copy in copies:
                copy.wait()
            for b in range(2):
                total = sum_st[0, b, :, 0:columns].astype(WIDE) + sum_st[1, b, :, 0:columns].astype(WIDE)
                if k:
                    total = total + sum_st[2, b, :, 0:columns].astype(WIDE)
                sum_st[0, b, :, 0:columns] = total.astype(LOW)
            back = pltpu.make_async_copy(sum_st.at[0, :, :, 0:columns], dw[g].at[k], sum_sem.at[0])
            back.start()
            back.wait()
            if k + 1 < planes:
                z_hop(g, k).start()
            else:
                for keeps, source, dev, n in homes(g):

                    @pl.when(keeps)
                    def _():
                        pltpu.make_async_copy(source, home[g], home_got.at[i]).start()

                    @pl.when(jnp.logical_not(keeps))
                    def _():
                        push(source, home[g], home_sent.at[i, n], home_got.at[i], dev).start()

        return run

    enc_sums = [summing(g, k) for g in ("ffn", "att") for k in range(planes)]
    dec_sums = [summing(g, k) for g in ("ffn", "crs", "att") for k in range(planes)]

    def add_enc(count):
        for _ in range(min(count, len(enc_sums))):
            pl.when(both(relay, at.encodes))(enc_sums.pop(0))

    def add_dec(count):
        for _ in range(min(count, len(dec_sums))):
            pl.when(both(relay, at.decodes))(dec_sums.pop(0))

    def turn(source, goal):
        def run(i):
            q = strip(i, BLOCK)
            goal[:, q] = source[q, :].astype(WIDE).T.astype(LOW)

        each(tiles, run, "turn")

    def dm_hop(n, source):
        q = pl.ds(pl.multiple_of((2 * c + n) * BLOCK, BLOCK), BLOCK)
        return push(source.at[q, :], c_v.at[q, :], dm_sent.at[n], dm_got.at[n], at.beside)

    def df_hop(n, core):
        q = pl.ds(pl.multiple_of((2 * core + n) * BLOCK, BLOCK), BLOCK)
        return push(c_v.at[q, :], c_v.at[q, :], df_sent.at[n], df_got.at[n], at.twin)

    @pl.when(at.encodes)
    def _():
        def back_rows(m):
            n = lax.div(m, 2)
            own = lax.rem(m, 2) == 0
            i = jnp.where(own, 2 * c + n, 2 * (1 - c) + n)
            q = strip(i, BLOCK)

            @pl.when(own)
            def _():
                dm_hop(n, c_v).wait_recv()
                df_hop(n, c).start()

            @pl.when(jnp.logical_not(own))
            def _():
                df_hop(n, 1 - c).wait_recv()

            grad = norm_grad(late_v[q, :], g2, c_v[q, :].astype(WIDE), 2, ours(i))
            late_v[q, :] = grad
            low = grad.astype(LOW)
            part = None
            for b in range(2):
                d_pre = (mm(low, dn_v[b]) * b_v[b, q, :].astype(WIDE)).astype(LOW)
                b_v[b, q, :] = d_pre
                term = mm_nt(d_pre, up_v[b])
                part = term if part is None else part + term
            send_v[0, q, :] = part.astype(LOW)

            @pl.when(own)
            def _():
                df_hop(n, c).wait_send()

            c_v[q, :] = low
            exchange(2, i).start()

        each(tiles, back_rows)

    turn(s_v, ta)
    turn(c_v, tb)

    def ffn_block(s, j):
        for b in range(2):
            dw_st[s, b, :, 0:768] = mm(ta[j, :], b_v[b]).astype(LOW)
            dw_st[s, b, :, 768:1536] = mm(tb[j, :], a_v[b]).astype(LOW)

    emit("ffn", ffn_block)

    @pl.when(at.decodes)
    def _():
        copying("act", a_v, act_k).wait()
        packed = copying("pc", pc_k, packed_v)
        small = [copying("oc", oc_k, o_v), copying("lsec", lsec_k, lse_v), copying("second", second_k, s_v)]
        packed.start()
        for copy in small:
            copy.start()

        def late_rows(i):
            q = strip(i, BLOCK)
            grad = c_v[q, :].astype(WIDE) + norm_grad(late_v[q, :], g2, joined(2, i), 2, ours(i))
            late_v[q, :] = grad
            g_v[q, :] = grad.astype(LOW)

        each(tiles, late_rows)

        def cross_out(i):
            q = strip(i, BLOCK)
            for b in range(2):
                do_v[b, q, :] = mm(g_v[q, :], crs_v[b, :, 128:384]).astype(LOW)

        each(tiles, cross_out)
        for copy in small:
            copy.wait()
        packed.wait()
        b_v[...] = jnp.zeros_like(b_v)

        def cross_head(n):
            b = lax.div(n, 3)
            attend_back_block(
                lax.rem(n, 3), a_v.at[b], o_v.at[b], do_v.at[b], b_v.at[b], lse_v, n, bias_cross,
                kx, qx, vx, gx, kt_v, False,
            )

        each(6, cross_head)
        sent(1)

        def to_memory(q):
            return mm_nt(b_v[0, q, 256:640], crs_v[0, :, 384:768]) + mm_nt(b_v[1, q, 256:640], crs_v[1, :, 384:768])

        def far(n):
            i = 2 * (1 - c) + n
            q = strip(i, BLOCK)
            send_v[1, q, :] = to_memory(q).astype(LOW)
            exchange(3, i).start()

        each(2, far)

        def near(n):
            i = 2 * c + n
            q = strip(i, BLOCK)
            part = to_memory(q)
            exchange(3, i).wait_recv()
            send_v[1, q, :] = (part + recv_v[1, q, :].astype(WIDE)).astype(LOW)
            dm_hop(n, send_v.at[1]).start()

        each(2, near)

        def to_query(i):
            q = strip(i, BLOCK)
            part = mm_nt(b_v[0, q, 0:256], crs_v[0, :, 0:256]) + mm_nt(b_v[1, q, 0:256], crs_v[1, :, 0:256])
            send_v[0, q, :] = part.astype(LOW)
            exchange(4, i).start()

        sent(2)
        each(tiles, to_query)
        add_dec(1)
        turn(s_v, ta)
        stage_in = copying("memory", memory_k, s_v)
        stage_in.start()
        turn(g_v, tc)
        stage_in.wait()
        turn(s_v, tb)
        copying("first", first_k, s_v).start()

        def crs_block(s, j):
            for b in range(2):
                left = mm(ta[j, :], b_v[b, :, 0:256])
                out = mm(tc[j, :], o_v[b])
                dw_st[s, b, :, 0:128] = left[:, 0:128].astype(LOW)
                dw_st[s, b, :, 128:256] = (left[:, 128:256] + out[:, 0:128]).astype(LOW)
                dw_st[s, b, :, 256:384] = out[:, 128:256].astype(LOW)
                dw_st[s, b, :, 384:768] = mm(tb[j, :], b_v[b, :, 256:640]).astype(LOW)

        emit("crs", crs_block)
        add_dec(1)

        def below(i):
            q = strip(i, BLOCK)
            grad = late_v[q, :] + norm_grad(mid_v[q, :], g1, joined(4, i), 1, ours(i))
            late_v[q, :] = grad
            g_v[q, :] = grad.astype(LOW)

        each(tiles, below)
        copying("first", first_k, s_v).wait()

        def gone(n):
            exchange(3, 2 * (1 - c) + n).wait_send()
            dm_hop(n, send_v.at[1]).wait_send()

        each(2, gone)

    @pl.when(at.encodes)
    def _():
        copying("first", first_k, s_v).start()
        each(2, lambda i: mem_send(i).wait_send())

        def below(i):
            q = strip(i, BLOCK)
            grad = late_v[q, :] + norm_grad(mid_v[q, :], g1, joined(2, i), 1, ours(i))
            late_v[q, :] = grad
            g_v[q, :] = grad.astype(LOW)

        each(tiles, below)
        copying("first", first_k, s_v).wait()
        sent(1)

    packed = copying("p", p_k, packed_v)
    small = [copying("o", o_k, o_v), copying("lse", lse_k, lse_v)]
    packed.start()
    for copy in small:
        copy.start()

    def self_out(i):
        q = strip(i, BLOCK)
        for b in range(2):
            do_v[b, q, :] = mm(g_v[q, :], att_v[b, :, 128:384]).astype(LOW)

    each(tiles, self_out)
    b_v[...] = jnp.zeros_like(b_v)
    for copy in small:
        copy.wait()
    packed.wait()

    def self_heads(causal, hooks):
        def self_head(n):
            b = lax.div(n, 3)
            attend_back_block(
                lax.rem(n, 3), a_v.at[b], o_v.at[b], do_v.at[b], b_v.at[b], lse_v, n, bias_self,
                kx, qx, vx, gx, kt_v, causal,
            )
            for when, event in hooks:
                pl.when(both(n == when, relay))(event)

        each(6, self_head)

    enc_back = [(1, enc_sums.pop(0))]
    dec_back = [(2, dec_sums.pop(0)), (5, dec_sums.pop(0))]
    pl.when(at.encodes)(lambda: self_heads(False, enc_back))
    pl.when(at.decodes)(lambda: self_heads(True, dec_back))

    def to_rows(q):
        part = None
        for b in range(2):
            term = mm_nt(b_v[b, q, 0:256], att_v[b, :, 0:256]) + mm_nt(b_v[b, q, 256:640], att_v[b, :, 384:768])
            part = term if part is None else part + term
        return part

    def far_rows(n):
        i = 2 * (1 - c) + n
        q = strip(i, BLOCK)
        send_v[1, q, :] = to_rows(q).astype(LOW)
        exchange(5, i).start()

    each(2, far_rows)
    turn(s_v, ta)
    x_in_v = copying("x", x_k, s_v)
    x_in_v.start()
    turn(g_v, tc)

    def att_block(s, j):
        for b in range(2):
            left = mm(ta[j, :], b_v[b, :, 0:256])
            out = mm(tc[j, :], o_v[b])
            dw_st[s, b, :, 0:128] = left[:, 0:128].astype(LOW)
            dw_st[s, b, :, 128:256] = (left[:, 128:256] + out[:, 0:128]).astype(LOW)
            dw_st[s, b, :, 256:384] = out[:, 128:256].astype(LOW)
            dw_st[s, b, :, 384:768] = mm(ta[j, :], b_v[b, :, 256:640]).astype(LOW)

    emit("att", att_block)
    add_enc(1)
    x_in_v.wait()

    def near_rows(n):
        i = 2 * c + n
        q = strip(i, BLOCK)
        part = to_rows(q)
        exchange(5, i).wait_recv()
        grad = part + recv_v[1, q, :].astype(WIDE)
        value = late_v[q, :] + norm_grad(s_v[q, :].astype(WIDE), g0, grad, 0, True)
        out_st[strip(n, BLOCK), :] = value.astype(LOW)

    each(2, near_rows)
    out_put = copying("out", out_st, grad_k)
    out_put.start()
    out_put.wait()

    def grad_home(k):
        return k, grad_k.at[strip(k, rows), :], grad_out, gr_sent, gr_got

    for k in range(2):
        go_home(*grad_home(k))

    def gain_hop(n, source, device):
        return push(source, gain_buf.at[n], gr_hop_sent.at[n], gr_hop_got.at[n], device)

    gain_buf[0] = gain_v[...]
    twin_hop = gain_hop(1, gain_buf.at[0], at.twin)
    twin_hop.start()
    twin_hop.wait()
    peer_hop = gain_hop(3, gain_buf.at[2], (1 - c, z, lax.rem(t + 2, 4)))
    last = 4 + planes

    @pl.when(relay)
    def _():
        gain_buf[2] = gain_buf[0] + gain_buf[1]
        peer_hop.start()

    def ring_hop(n):
        return gain_hop(5 + n, gain_buf.at[4 + n], at.above)

    def gain_step(n):
        @pl.when(relay)
        def _():
            if n == 0:
                peer_hop.wait()
                gain_buf[4] = gain_buf[2] + gain_buf[3]
            else:
                ring_hop(n - 1).wait()
            if n < planes - 1:
                ring_hop(n).start()
            else:
                total = None
                for j in range(planes):
                    held = gain_buf[jnp.where(z == j, 4, 5 + lax.rem(z - 1 - j + planes, planes))]
                    total = held if total is None else total + held
                gain_buf[last] = total
                for b in range(2):
                    keeps = both(c == r, r == b)

                    @pl.when(keeps)
                    def _():
                        pltpu.make_async_copy(gain_buf.at[last], gain_buf.at[last + 1], gr_hop_got.at[last + 1]).start()

                    @pl.when(jnp.logical_not(keeps))
                    def _():
                        final_hop(b).start()

    def final_hop(b):
        return push(
            gain_buf.at[last], gain_buf.at[last + 1], gr_hop_sent.at[last + b], gr_hop_got.at[last + 1],
            (r, z, 2 * y + b),
        )

    def y3_home(k):
        return k, y3_k.at[strip(k, rows), :], block_out, blk_sent, blk_got

    @pl.when(at.decodes)
    def _():
        copies = [copying("act", act_k, a_v), copying("late", late_k, mid_v)]
        for copy in copies:
            copy.start()
        sent(4)
        for copy in copies:
            copy.wait()

        def to_out(q):
            return mm_nt(a_v[0, q, :], dn_v[0]) + mm_nt(a_v[1, q, :], dn_v[1])

        def far_out(n):
            i = 2 * (1 - c) + n
            q = strip(i, BLOCK)
            send_v[0, q, :] = to_out(q).astype(LOW)
            exchange(6, i).start()

        each(2, far_out)

        def near_out(n):
            i = 2 * c + n
            q = strip(i, BLOCK)
            part = to_out(q)
            exchange(6, i).wait_recv()
            out_st[strip(n, BLOCK), :] = (mid_v[q, :] + part + recv_v[0, q, :].astype(WIDE)).astype(LOW)

        each(2, near_out)
        y3_put = copying("out", out_st, y3_k)
        y3_put.start()
        y3_put.wait()
        for k in range(2):
            go_home(*y3_home(k))

    for n in range(planes):
        add_enc(1)
        add_dec(2)
        gain_step(n)
    add_enc(9)
    add_dec(99)

    for s in range(2):
        for goal, got in ((block_out, blk_got), (grad_out, gr_got)):
            push(goal.at[s], goal.at[s], blk_sent.at[0], got.at[s], at.twin).wait_recv()
    push(gain_buf.at[last], gain_buf.at[last + 1], gr_hop_sent.at[last], gr_hop_got.at[last + 1], at.twin).wait_recv()
    gains_home = copying("gains", gain_buf.at[last + 1], gain_out)
    gains_home.start()
    gains_home.wait()
    for i, g in enumerate(SUMS):
        push(home[g], home[g], home_sent.at[i, 0], home_got.at[i], at.twin).wait_recv()
    for k in range(2):
        went_home(*grad_home(k))

    @pl.when(at.encodes)
    def _():
        for k in range(2):
            went_home(*memory_home(k))
        sent(2)

    @pl.when(at.decodes)
    def _():
        for k in range(2):
            went_home(*y3_home(k))
        each(2, lambda n: exchange(6, 2 * (1 - c) + n).wait_send())

    each(2, lambda n: exchange(5, 2 * (1 - c) + n).wait_send())

    @pl.when(relay)
    def _():
        for b in range(2):
            pl.when(jnp.logical_not(both(c == r, r == b)))(lambda: final_hop(b).wait_send())

    for g in SUMS:
        there = at.decodes if g == "crs" else jnp.logical_or(at.decodes, at.encodes)

        @pl.when(both(other, there))
        def _():
            for k in range(planes):
                y_hop(g, k).wait_send()

        @pl.when(both(relay, there))
        def _():
            for k in range(planes - 1):
                z_hop(g, k).wait_send()
            for keeps, source, dev, n in homes(g):

                @pl.when(jnp.logical_not(keeps))
                def _():
                    i = SUMS.index(g)
                    push(source, home[g], home_sent.at[i, n], home_got.at[i], dev).wait_send()

    gain_copy.wait_send()
    for g in DIRECT:
        launch_over(g).wait_send()

    @pl.when(jnp.logical_not(stays))
    def _():
        for g in ("att", "up", "dn"):
            push(shard[g], vmem[g].at[r, here, :], x_sent.at[GROUPS.index(g)], x_sem.at[0, 0], relay_dev).wait_send()

    @pl.when(jnp.logical_not(crs_stays))
    def _():
        push(crs_in, crs_goal(r, c), x_sent.at[1], c_sem.at[0, 0], crs_dev).wait_send()
        push(cot_in.at[c], cot_goal, row_sent.at[2], cot_got.at[r], at.twin).wait_send()

    for s in range(2):

        @pl.when(jnp.logical_not(row_stays(s)))
        def _():
            push(x_in.at[s], row_goal, row_sent.at[s], row_got.at[r], at.twin).wait_send()

    for g in GROUPS:
        member = both(relay, at.decodes) if g == "crs" else relay

        @pl.when(member)
        def _():
            for k in range(planes):
                for b in range(2):
                    if k:
                        ring(g, k, b).wait_send()
                    if k or g not in DIRECT:
                        cross_over(g, k, b).wait_send()


def block_call(planes, slot, width, hidden, depth, args):
    shape = jax.ShapeDtypeStruct
    rows = slot // 4
    square = (slot, width)
    wides = {"ffn": 2 * hidden, "crs": width, "att": width}
    packed, outs, logs, acts = (2, slot, 640), (2, slot, 256), (8, slot), (2, slot, hidden)
    out_shape = (
        [shape((2, rows, width), LOW)] * 2
        + [shape((depth, 2 * hidden), LOW), shape((depth, width // 2), LOW), shape((depth, width), LOW)]
        + [shape((8, width), WIDE)]
        + [shape(square, LOW)] * 4
        + [shape(square, WIDE), shape(square, LOW)]
        + [shape(packed, LOW), shape(outs, LOW), shape(logs, WIDE)] * 2
        + [shape(acts, LOW)]
        + [shape((2 * rows, width), LOW)] * 2
        + [shape((planes, 2, depth, wides[g]), LOW) for g in SUMS] * 3
    )
    dma = pltpu.SemaphoreType.DMA
    v = pltpu.VMEM
    groups = len(GROUPS)
    scratch = (
        [v((2, width, width), LOW)] * 2
        + [v((2, width, hidden), LOW)] * 2
        + [v(acts, LOW)] * 2
        + [v(outs, LOW)] * 2
        + [v(square, WIDE)] * 2
        + [v(square, LOW)] * 3
        + [v((width, slot), LOW)] * 3
        + [v((2,) + square, LOW)] * 2
        + [v((slot, TILE), LOW)] * 4
        + [v((TILE, slot), LOW), v(logs, WIDE), v((8, width), WIDE), v((2, 8, width), WIDE)]
        + [v((planes + 6, 8, width), WIDE)]
        + [v((2 * rows, width), LOW), v((2, 2, depth, 2 * hidden), LOW), v((3, 2, depth, 2 * hidden), LOW)]
        + [dma((groups, 2)), dma((groups,)), dma((groups,)), dma((2, 2))]
        + [dma((groups, planes, 2))] * 4
        + [dma((2,)), dma((3,)), dma((4,)), dma((2,)), dma((3,)), dma((24,)), dma((7, 4)), dma((7, 4))]
        + [dma((2,))] * 8
        + [dma((3, planes))] * 4
        + [dma((3,)), dma((3, 4))]
        + [dma((2,))] * 4
        + [dma((planes + 6,))] * 2
        + [dma((3,)), dma((2,))]
    )
    any_spec = pl.BlockSpec(memory_space=pl.ANY)
    vmem_spec = pl.BlockSpec(memory_space=pltpu.VMEM)
    return pl.pallas_call(
        functools.partial(block_kernel, planes),
        out_shape=out_shape,
        in_specs=[any_spec] * 6 + [vmem_spec] * 3,
        out_specs=[any_spec] * len(out_shape),
        scratch_shapes=scratch,
        compiler_params=pltpu.CompilerParams(collective_id=0, has_side_effects=True, vmem_limit_bytes=VMEM_BYTES),
    )(*args)


def ring_gather(lay, shard):
    planes = lay.planes
    rows = shard.shape[1]
    if planes > 4:
        piece = lax.all_gather(shard, "dp", axis=1, tiled=True)
        across = lay.route(piece, lambda c, z, t: (c, z, (t + 2) % 4) if c == t // 2 else None)
        return jnp.where(lay.relays, piece, across)
    relay = lambda c, z, t: (c, (z + 1) % planes, t) if c == t // 2 else None
    whole = jnp.zeros((shard.shape[0], planes * rows, shard.shape[2]), shard.dtype)
    piece = shard
    for step in range(planes):
        across = lay.route(piece, lambda c, z, t: (c, z, (t + 2) % 4) if c == t // 2 else None)
        chosen = jnp.where(lay.relays, piece, across)
        whole = lax.dynamic_update_slice(whole, chosen, (0, ((lay.plane - step) % planes) * rows, 0))
        if step + 1 < planes:
            piece = lay.route(piece, relay)
    return whole


def ring_scatter(lay, total, holder):
    planes = lay.planes
    rows = total.shape[1] // planes
    low = total.astype(LOW)
    across = lay.route(
        low, lambda c, z, t: (c, z, (t + 2) % 4) if (c != t // 2 and t % 2 == holder) else None
    )
    summed = low.astype(WIDE) + across.astype(WIDE)
    if planes > 4:
        return lax.psum_scatter(summed.astype(LOW), "dp", scatter_dimension=1, tiled=True)
    relay = lambda c, z, t: (c, (z + 1) % planes, t) if (c == t // 2 and t % 2 == holder) else None
    take = lambda j: lax.dynamic_slice_in_dim(summed, (j % planes) * rows, rows, 1)
    running = take(lay.plane - 1)
    for step in range(1, planes):
        running = lay.route(running.astype(LOW), relay).astype(WIDE) + take(lay.plane - 1 - step)
    return running.astype(LOW)


def hand_back(lay, value, holder, section):
    same = lay.route(
        value[0], lambda c, z, t: (section, z, t) if (c == t // 2 and t % 2 == holder) else None
    )
    beside = lay.route(
        value[1], lambda c, z, t: (section, z, t ^ 1) if (c == t // 2 and t % 2 == holder) else None
    )
    return same.astype(WIDE) + beside.astype(WIDE)


def general_body(block_input, w_self, w_self_out, w_cross, w_up, w_down, norm_gains, lengths, task_mask, out_grad):
    lay = Layout()
    seqs, rows, width = block_input.shape[1:]
    slot = rows * lay.chips
    sec = lay.core
    item = lay.item

    def spread(value, first):
        pick = value[jnp.where(first, lay.chip % 2, 1 - lay.chip % 2)]
        flip = 0 if first else 1
        return lay.route(pick, lambda c, z, t: (t // 2, z, 2 * ((t % 2) ^ flip) + c))

    def merge_rows(mine, theirs):
        low_half = jnp.where(lay.core == 0, mine, theirs)
        high_half = jnp.where(lay.core == 0, theirs, mine)
        return jnp.concatenate([low_half[0], low_half[1], high_half[0], high_half[1]], axis=0)

    first = spread(block_input[0], True)
    second = spread(block_input[0], False)
    mine = jnp.where(item == 0, jnp.stack([first, second]), jnp.stack([second, first]))
    x_rows = merge_rows(mine, lay.other_core(mine)).astype(WIDE)

    picked = out_grad[lay.core]
    even = lay.route(picked, lambda c, z, t: (t // 2, z, 2 * c + 1) if t % 2 == 0 else None)
    odd = lay.route(picked, lambda c, z, t: (t // 2, z, 2 * c + 1) if t % 2 == 1 else None)
    mine = jnp.stack([even, odd])
    cotangent = merge_rows(mine, lay.other_core(mine))

    gains_here = norm_gains[0].astype(WIDE)
    gains = jnp.where(sec == lay.role, gains_here, lay.other_core(norm_gains[0]).astype(WIDE))

    depth = w_self.shape[1]
    wide = w_self.shape[3]
    self_block = pack_heads(
        {"q": w_self[0, :, 0], "k": w_self[0, :, 1], "v": w_self[0, :, 2], "o": w_self_out[0].T}
    )
    feed_block = jnp.concatenate([w_up[0], w_down[0].T], axis=1)
    cross_block = w_cross[0].reshape(depth, 2 * wide)

    def collect(block):
        same = lay.route(block, lambda c, z, t: (t // 2, z, t) if c == t % 2 else None)
        beside = lay.route(block, lambda c, z, t: (t // 2, z, t ^ 1) if c != t % 2 else None)
        return jnp.stack([same, beside])

    def collect_cross(block, section):
        same = lay.route(block, lambda c, z, t: (t // 2, z, t) if (c == section and t % 2 == 1) else None)
        beside = lay.route(block, lambda c, z, t: (t // 2, z, t ^ 1) if (c == section and t % 2 == 0) else None)
        return same, beside

    w_att = ring_gather(lay, collect(self_block))
    w_ffn = ring_gather(lay, collect(feed_block))
    memory_side = collect_cross(cross_block, 0)
    query_side = collect_cross(cross_block, 1)
    w_crs = ring_gather(
        lay,
        jnp.stack(
            [
                pack_heads({"q": q[:, :wide], "k": m[:, :wide], "v": m[:, wide:], "o": q[:, wide:]})
                for m, q in zip(memory_side, query_side)
            ]
        ),
    )
    hidden = w_up.shape[2]
    part = lambda w, name: jnp.concatenate([unpack_heads(w[0], name), unpack_heads(w[1], name)], axis=1)
    att = {n: part(w_att, n) for n in "qkvo"}
    crs = {n: part(w_crs, n) for n in "qkvo"}
    up = jnp.concatenate([w_ffn[0, :, :hidden], w_ffn[1, :, :hidden]], axis=1)
    down_t = jnp.concatenate([w_ffn[0, :, hidden:], w_ffn[1, :, hidden:]], axis=1)

    positions = jnp.arange(slot)
    own_length = jnp.where(lay.is_decoder, lengths[1, item], lengths[0, item])
    self_allowed = (positions[None, :] < own_length) & (
        (positions[None, :] <= positions[:, None]) | jnp.logical_not(lay.is_decoder)
    )
    cross_allowed = jnp.broadcast_to(
        ((positions < lengths[0, item]) & (task_mask[item] == 1))[None], (slot, slot)
    )

    def joined(partial):
        low = partial.astype(LOW)
        return low.astype(WIDE) + lay.other_core(low).astype(WIDE)

    normed0 = layer_norm(x_rows, gains[0]).astype(LOW)
    q, k, v = (mm(normed0, att[n]).astype(LOW) for n in "qkv")
    out_self, lse_self = attend(q, k, v, self_allowed)
    x_mid = x_rows + joined(mm_nt(out_self, att["o"]))
    normed1 = layer_norm(x_mid, gains[1]).astype(LOW)

    pre_enc = mm(normed1, up)
    act_enc, slope_enc = gelu_parts(pre_enc)
    act_enc = act_enc.astype(LOW)
    x_late_enc = x_mid + joined(mm_nt(act_enc, down_t))
    memory_enc = layer_norm(x_late_enc, gains[2]).astype(LOW)
    memory = lay.route(memory_enc, lambda c, z, t: (c, z, t ^ 1) if t % 2 == 0 else None)

    cq = mm(normed1, crs["q"]).astype(LOW)
    ck, cv = (mm(memory, crs[n]).astype(LOW) for n in "kv")
    out_cross, lse_cross = attend(cq, ck, cv, cross_allowed)
    x_late = x_mid + joined(mm_nt(out_cross, crs["o"]))
    normed2 = layer_norm(x_late, gains[2]).astype(LOW)
    pre_dec = mm(normed2, up)
    act_dec, slope_dec = gelu_parts(pre_dec)
    act_dec = act_dec.astype(LOW)
    result_dec = (x_late + joined(mm_nt(act_dec, down_t))).astype(LOW)

    d_out = cotangent.astype(WIDE)
    d_pre = (slope_dec * mm(cotangent, down_t)).astype(LOW)
    d_ffn_dec = jnp.concatenate([mm_tn(normed2, d_pre), mm_tn(cotangent, act_dec)], axis=1)
    d_late_norm, d_gain2_dec = norm_back(x_late, gains[2], joined(mm_nt(d_pre, up)))
    d_late = d_out + d_late_norm
    grad_late = d_late.astype(LOW)
    d_att = mm(grad_late, crs["o"]).astype(LOW)
    d_cq, d_ck, d_cv = attend_back(cq, ck, cv, lse_cross, d_att, cross_allowed)
    d_memory = joined(mm_nt(d_ck, crs["k"]) + mm_nt(d_cv, crs["v"]))
    d_crs = {
        "q": mm_tn(normed1, d_cq),
        "k": mm_tn(memory, d_ck),
        "v": mm_tn(memory, d_cv),
        "o": mm_tn(grad_late, out_cross),
    }
    d_mid_norm, d_gain1_dec = norm_back(x_mid, gains[1], joined(mm_nt(d_cq, crs["q"])))
    d_mid_dec = d_late + d_mid_norm

    d_memory = lay.route(d_memory.astype(LOW), lambda c, z, t: (c, z, t ^ 1) if t % 2 == 1 else None).astype(WIDE)
    d_late_enc, d_gain2_enc = norm_back(x_late_enc, gains[2], d_memory)
    grad_late_enc = d_late_enc.astype(LOW)
    d_pre = (slope_enc * mm(grad_late_enc, down_t)).astype(LOW)
    d_ffn_enc = jnp.concatenate([mm_tn(normed1, d_pre), mm_tn(grad_late_enc, act_enc)], axis=1)
    d_mid_norm, d_gain1_enc = norm_back(x_mid, gains[1], joined(mm_nt(d_pre, up)))
    d_mid_enc = d_late_enc + d_mid_norm

    d_mid = jnp.where(lay.is_decoder, d_mid_dec, d_mid_enc)
    grad_mid = d_mid.astype(LOW)
    d_att = mm(grad_mid, att["o"]).astype(LOW)
    d_q, d_k, d_v = attend_back(q, k, v, lse_self, d_att, self_allowed)
    d_norm = joined(mm_nt(d_q, att["q"]) + mm_nt(d_k, att["k"]) + mm_nt(d_v, att["v"]))
    d_att_w = {
        "q": mm_tn(normed0, d_q),
        "k": mm_tn(normed0, d_k),
        "v": mm_tn(normed0, d_v),
        "o": mm_tn(grad_mid, out_self),
    }
    d_first, d_gain0 = norm_back(x_rows, gains[0], d_norm)
    d_rows = d_mid + d_first

    half = 3 * HEAD

    def blocks(parts):
        return jnp.stack(
            [pack_heads({n: parts[n][:, half * b : half * (b + 1)] for n in parts}) for b in range(2)]
        )

    def feed_blocks(both):
        total = both.shape[1] // 2
        return jnp.stack(
            [
                jnp.concatenate(
                    [both[:, hidden * b : hidden * (b + 1)], both[:, total + hidden * b : total + hidden * (b + 1)]],
                    axis=1,
                )
                for b in range(2)
            ]
        )

    self_total = blocks(d_att_w)
    home_self = hand_back(lay, ring_scatter(lay, self_total, 0), 0, 0) + hand_back(
        lay, ring_scatter(lay, self_total, 1), 1, 1
    )
    home_feed = hand_back(lay, ring_scatter(lay, feed_blocks(d_ffn_enc), 0), 0, 0) + hand_back(
        lay, ring_scatter(lay, feed_blocks(d_ffn_dec), 1), 1, 1
    )
    cross_total = ring_scatter(lay, blocks(d_crs), 1)
    side = lambda names: jnp.stack(
        [jnp.concatenate([unpack_heads(cross_total[b], n) for n in names], axis=1) for b in range(2)]
    )
    home_cross = hand_back(lay, side("kv"), 1, 0) + hand_back(lay, side("qo"), 1, 1)

    g_self = jnp.stack([unpack_heads(home_self, n) for n in "qkv"], axis=1)[None]
    g_self_out = unpack_heads(home_self, "o").T[None]
    g_cross = home_cross.reshape(1, depth, 2, wide)
    g_up = home_feed[:, :hidden][None]
    g_down = home_feed[:, hidden:].T[None]

    gain2 = jnp.where(lay.is_decoder, d_gain2_dec, d_gain2_enc)
    gain1 = jnp.where(lay.is_decoder, d_gain1_dec, d_gain1_enc)
    gain_rows = jnp.stack([d_gain0, gain1, gain2])
    slots = jnp.stack(
        [
            jnp.where((lay.role == r) & (lay.core == 0), gain_rows, 0.0)
            for r in range(2)
        ]
    )
    gain_total = lax.psum(slots, AXES)[sec][None]

    def rows_home(value):
        mine = lax.dynamic_slice_in_dim(value, lay.core * 2 * rows, 2 * rows, 0).reshape(2, rows, width)
        a = lay.route(mine[item], lambda c, z, t: (t % 2, z, 2 * c + t // 2))
        b = lay.route(mine[1 - item], lambda c, z, t: (t % 2, z, 2 * c + 1 - t // 2))
        even = lay.chip % 2 == 0
        return jnp.where(even, jnp.stack([a, b]), jnp.stack([b, a]))[None]

    block_output = rows_home(jnp.where(lay.is_decoder, result_dec, memory_enc))
    input_grad = rows_home(d_rows.astype(LOW)).astype(WIDE)
    return (
        block_output,
        input_grad,
        g_self,
        g_self_out,
        g_cross,
        g_up,
        g_down,
        gain_total[:, :2],
        gain_total[:, 2],
    )


def body(block_input, w_self, w_self_out, w_cross, w_up, w_down, norm_gains, lengths, task_mask, out_grad):
    lay = Layout()
    seqs, rows, width = block_input.shape[1:]
    slot = rows * lay.chips
    sec = lay.core
    item = lay.item

    if lay.planes != 4:
        return general_body(
            block_input, w_self, w_self_out, w_cross, w_up, w_down, norm_gains, lengths, task_mask, out_grad
        )

    depth = w_self.shape[1]
    wide = w_self.shape[3]
    hidden = w_up.shape[2]
    self_block = pack_heads(
        {"q": w_self[0, :, 0], "k": w_self[0, :, 1], "v": w_self[0, :, 2], "o": w_self_out[0].T}
    )
    pair = {"q": w_cross[0, :, 0], "o": w_cross[0, :, 1], "k": w_cross[0, :, 0], "v": w_cross[0, :, 1]}
    pieces = [pair[n][:, HEAD * h : HEAD * (h + 1)] for n, h in ORDER]
    cross_block = jnp.where(
        sec == 1, jnp.concatenate(pieces[:6], axis=1), jnp.concatenate(pieces[6:], axis=1)
    )
    gain_block = jnp.concatenate([norm_gains[0].astype(WIDE), jnp.zeros((5, width), WIDE)], axis=0)

    positions = jnp.arange(slot)
    own_length = jnp.where(lay.is_decoder, lengths[1, item], lengths[0, item])

    def key_bias(allowed):
        return jnp.broadcast_to(jnp.where(allowed, 0.0, NEG_FILL)[:, None], (slot, TILE)).astype(LOW)

    biases = (
        key_bias(positions < own_length),
        key_bias((positions < lengths[0, item]) & (task_mask[item] == 1)),
    )
    block_output, input_grad, home_feed, home_cross, home_self, gain_total = block_call(
        lay.planes,
        slot,
        width,
        hidden,
        depth,
        (self_block, cross_block, w_up[0], w_down[0].T, block_input[0], out_grad, gain_block) + biases,
    )[:6]
    home_self, home_feed, home_cross = (v.astype(WIDE) for v in (home_self, home_feed, home_cross))
    g_self = jnp.stack([unpack_heads(home_self, n) for n in "qkv"], axis=1)[None]
    g_self_out = unpack_heads(home_self, "o").T[None]
    halves = (ORDER[:6], ORDER[6:])
    take = lambda order, name: jnp.concatenate(
        [home_cross[:, HEAD * order.index((name, h)) : HEAD * (order.index((name, h)) + 1)] for h in range(3)], axis=1
    )
    g_cross = jnp.where(
        sec == 1,
        jnp.stack([take(halves[0], "q"), take(halves[0], "o")], axis=1),
        jnp.stack([take(halves[1], "k"), take(halves[1], "v")], axis=1),
    )[None]
    g_up = home_feed[:, :hidden][None]
    g_down = home_feed[:, hidden:].T[None]
    gain_total = gain_total[None]
    return (
        block_output[None],
        input_grad.astype(WIDE)[None],
        g_self,
        g_self_out,
        g_cross,
        g_up,
        g_down,
        gain_total[:, :2],
        gain_total[:, 2],
    )


def solution(mesh):
    placed = (
        P("section", "dp", "tensor", None),
        P("section", "dp", None, "tensor"),
        P("section", "tensor", "dp"),
        P("section", "dp", None, "tensor"),
        P("section", "dp", "tensor"),
        P("section", "tensor", "dp"),
        P("section", None, None),
        P(None, "dp"),
        P("dp", None),
        P("dp", "tensor", None),
    )
    return jax.shard_map(
        body,
        mesh=mesh,
        in_specs=placed,
        out_specs=(
            P("section", "dp", "tensor", None),
            P("section", "dp", "tensor", None),
            P("section", "dp", None, "tensor"),
            P("section", "tensor", "dp"),
            P("section", "dp", None, "tensor"),
            P("section", "dp", "tensor"),
            P("section", "tensor", "dp"),
            P("section", None, None),
            P("section", None),
        ),
        check_vma=False,
    )
```

```python
import functools

import jax
import jax.numpy as jnp
from jax import lax
from jax.experimental import pallas as pl
from jax.experimental.pallas import tpu as pltpu
from jax.sharding import PartitionSpec as P

HEAD = 64
TILE = 128
EPSILON = 1e-05
SCORE_SCALE = 0.125
NEG_FILL = -1000000000.0
AXES = ("section", "dp", "tensor")
LOW = jnp.bfloat16
WIDE = jnp.float32


class Layout:
    def __init__(self):
        self.cores = lax.axis_size("section")
        self.planes = lax.axis_size("dp")
        self.chips = lax.axis_size("tensor")
        self.core = lax.axis_index("section")
        self.plane = lax.axis_index("dp")
        self.chip = lax.axis_index("tensor")
        self.role = self.chip % 2
        self.item = self.chip // 2
        self.is_decoder = self.role == 1
        self.relays = self.core == self.item

    def route(self, value, target):
        pairs = []
        for core in range(self.cores):
            for plane in range(self.planes):
                for chip in range(self.chips):
                    to = target(core, plane, chip)
                    if to is None:
                        continue
                    source = (core * self.planes + plane) * self.chips + chip
                    goal = (to[0] * self.planes + to[1]) * self.chips + to[2]
                    pairs.append((source, goal))
        return lax.ppermute(value, AXES, pairs)

    def other_core(self, value):
        return self.route(value, lambda c, z, t: (1 - c, z, t))


def normalize(values):
    centred = values - jnp.mean(values, axis=-1, keepdims=True)
    spread = jnp.mean(centred * centred, axis=-1, keepdims=True)
    scale = lax.rsqrt(spread + EPSILON)
    return centred * scale, scale


def layer_norm(values, gain):
    return normalize(values)[0] * gain


def norm_back(values, gain, grad):
    normal, scale = normalize(values)
    scaled = grad * gain
    first = jnp.mean(scaled, axis=-1, keepdims=True)
    second = jnp.mean(scaled * normal, axis=-1, keepdims=True)
    return (scaled - first - normal * second) * scale, jnp.sum(grad * normal, axis=0)


ORDER = (("q", 0), ("q", 1), ("q", 2), ("o", 2), ("o", 0), ("o", 1), ("k", 0), ("k", 1), ("v", 0), ("v", 1), ("k", 2), ("v", 2))


def pack_heads(parts):
    return jnp.concatenate([parts[n][:, HEAD * h : HEAD * (h + 1)] for n, h in ORDER], axis=1)


def unpack_heads(block, name):
    where = {(n, h): i for i, (n, h) in enumerate(ORDER)}
    return jnp.concatenate(
        [block[:, HEAD * where[(name, h)] : HEAD * (where[(name, h)] + 1)] for h in range(3)], axis=1
    )


def mm(left, right):
    return jnp.dot(left, right, preferred_element_type=WIDE)


def mm_nt(left, right):
    return lax.dot_general(left, right, (((1,), (1,)), ((), ())), preferred_element_type=WIDE)


def mm_tn(left, right):
    return lax.dot_general(left, right, (((0,), (0,)), ((), ())), preferred_element_type=WIDE)


def split_heads(value):
    return value.reshape(value.shape[0], -1, HEAD)


def attend(q, k, v, allowed):
    scores = jnp.einsum("qhd,khd->hqk", split_heads(q), split_heads(k), preferred_element_type=WIDE) * SCORE_SCALE
    scores = jnp.where(allowed[None], scores, NEG_FILL)
    top = jnp.max(scores, axis=-1, keepdims=True)
    power = jnp.exp(scores - top)
    total = jnp.sum(power, axis=-1, keepdims=True)
    probs = (power / total).astype(LOW)
    out = jnp.einsum("hqk,khd->qhd", probs, split_heads(v), preferred_element_type=WIDE)
    return out.astype(LOW).reshape(q.shape), top + jnp.log(total)


def attend_back(q, k, v, log_sum, d_out, allowed):
    scores = jnp.einsum("qhd,khd->hqk", split_heads(q), split_heads(k), preferred_element_type=WIDE) * SCORE_SCALE
    scores = jnp.where(allowed[None], scores, NEG_FILL)
    probs = jnp.exp(scores - log_sum)
    d_probs = jnp.einsum("qhd,khd->hqk", split_heads(d_out), split_heads(v), preferred_element_type=WIDE)
    inner = jnp.sum(probs * d_probs, axis=-1, keepdims=True)
    d_scores = (probs * (d_probs - inner)).astype(LOW)
    d_v = jnp.einsum("hqk,qhd->khd", probs.astype(LOW), split_heads(d_out), preferred_element_type=WIDE)
    d_q = jnp.einsum("hqk,khd->qhd", d_scores, split_heads(k), preferred_element_type=WIDE) * SCORE_SCALE
    d_k = jnp.einsum("hqk,qhd->khd", d_scores, split_heads(q), preferred_element_type=WIDE) * SCORE_SCALE
    return tuple(g.astype(LOW).reshape(q.shape) for g in (d_q, d_k, d_v))


def gelu_parts(value):
    coef = 0.7978845608028654
    cube = 0.044715
    inner = coef * (value + cube * value * value * value)
    soft = jnp.tanh(inner)
    slope = 0.5 * (1.0 + soft) + 0.5 * value * (1.0 - soft * soft) * coef * (1.0 + 3.0 * cube * value * value)
    return 0.5 * value * (1.0 + soft), slope


MESH = pl.DeviceIdType.MESH
GROUPS = ("att", "crs", "up", "dn")
BLOCK = 256
VMEM_BYTES = 62 * 2**20


def lanes(shape):
    return lax.broadcasted_iota(jnp.int32, shape, len(shape) - 1)


def subs(shape):
    return lax.broadcasted_iota(jnp.int32, shape, 0)


def strip(i, size):
    return pl.ds(pl.multiple_of(i * size, size), size)


def head_place(h):
    two = (h == 2).astype(jnp.int32)
    one = (h >= 1).astype(jnp.int32)
    return two, 2 + 2 * two, 3 + two, 1 - two, HEAD * (one - two), HEAD * one


def each(count, step, name=None):
    def run(i, carry):
        step(i)
        return carry

    with jax.named_scope(name or step.__name__):
        lax.fori_loop(0, count, run, 0)


class Place:
    def __init__(self, planes):
        self.planes = planes
        self.c = lax.axis_index("section")
        self.z = lax.axis_index("dp")
        self.t = lax.axis_index("tensor")
        self.y = lax.div(self.t, 2)
        self.r = lax.rem(self.t, 2)
        self.twin = (1 - self.c, self.z, self.t)
        self.above = (self.c, lax.rem(self.z + 1, planes), self.t)
        self.below = (self.c, lax.rem(self.z + planes - 1, planes), self.t)
        self.across = (self.c, self.z, lax.rem(self.t + 2, 4))
        self.beside = (self.c, self.z, self.t + 1 - 2 * self.r)
        self.relays = self.c == self.y
        self.encodes = self.r == 0
        self.decodes = self.r == 1

    def meet(self):
        barrier = pltpu.get_barrier_semaphore()
        peers = [self.above, self.below]
        for dc in range(2):
            for dt in range(4):
                if dc or dt:
                    peers.append((lax.rem(self.c + dc, 2), self.z, lax.rem(self.t + dt, 4)))
        for peer in peers:
            pl.semaphore_signal(barrier, inc=1, device_id=peer, device_id_type=MESH)
        pl.semaphore_wait(barrier, len(peers))


def push(source, goal, sent, got, device):
    return pltpu.make_async_remote_copy(
        src_ref=source, dst_ref=goal, send_sem=sent, recv_sem=got, device_id=device, device_id_type=MESH
    )


def both(first, second):
    return jnp.logical_and(first, second)


def center(values):
    middle = values - jnp.mean(values, axis=-1, keepdims=True)
    scale = lax.rsqrt(jnp.mean(middle * middle, axis=-1, keepdims=True) + EPSILON)
    return middle * scale, scale


def attend_block(h, p, o, lse, lse_row, bias, kx, qx, vt, causal):
    count = p.shape[0]
    qt, kt, vtile, ot, qlo, vlo = head_place(h)
    lane = lanes((count, TILE))
    in_q = both(lane >= qlo, lane < qlo + HEAD)
    in_v = both(lane >= vlo, lane < vlo + HEAD)
    spare = HEAD - qlo
    kx[...] = jnp.where(lane == spare, bias[...], jnp.where(in_q, p[:, strip(kt, TILE)], jnp.zeros((), LOW)))
    vt[...] = jnp.where(in_v, p[:, strip(vtile, TILE)].astype(WIDE), 1.0).T.astype(LOW)
    qx[...] = jnp.where(
        in_q, p[:, strip(qt, TILE)].astype(WIDE) * SCORE_SCALE, jnp.where(lane == spare, 1.0, 0.0)
    ).astype(LOW)
    scores = mm_nt(kx[...], qx[...])
    if causal:
        scores = jnp.where(subs(scores.shape) <= lanes(scores.shape), scores, NEG_FILL)
    top = jnp.max(scores, axis=0, keepdims=True)
    power = jnp.exp(scores - top).astype(LOW)
    out = mm(vt[...], power)
    total = jnp.where(vlo == 0, out[HEAD : HEAD + 1, :], out[0:1, :])
    result = (out / total).T
    o[:, strip(ot, TILE)] = jnp.where(in_v, result, o[:, strip(ot, TILE)].astype(WIDE)).astype(LOW)
    row = subs((8, count))
    lse[...] = jnp.where(row == lse_row, top + jnp.log(total), lse[...])


SUMS = ("ffn", "crs", "att")
DIRECT = ("att", "up")
ASIDE = (("up", 0), ("dn", 0))


def split_three(value):
    high = value.astype(LOW).astype(WIDE)
    middle = (value - high).astype(LOW).astype(WIDE)
    return high, middle, value - high - middle


def attend_back_block(h, p, o, d_o, d_p, lse, lse_row, bias, kx, qx, vx, gx, kt_v, causal):
    count = p.shape[0]
    qt, kt, vtile, ot, qlo, vlo = head_place(h)
    lane = lanes((count, TILE))
    in_q = both(lane >= qlo, lane < qlo + HEAD)
    in_v = both(lane >= vlo, lane < vlo + HEAD)
    sq, sv = HEAD - qlo, HEAD - vlo
    keys = jnp.where(
        in_q, p[:, strip(kt, TILE)].astype(WIDE), jnp.where(both(lane > sq, lane < sq + 4), 1.0, 0.0)
    )
    keys = jnp.where(lane == sq, bias[...].astype(WIDE), keys)
    kx[...] = keys.astype(LOW)
    kt_v[...] = keys.T.astype(LOW)
    vx[...] = jnp.where(
        in_v, p[:, strip(vtile, TILE)].astype(WIDE), jnp.where(both(lane >= sv, lane < sv + 3), 1.0, 0.0)
    ).astype(LOW)
    own = jnp.sum(jnp.where(subs((8, count)) == lse_row, lse[...], 0.0), axis=0, keepdims=True)
    a, b, c = split_three(-jnp.broadcast_to(own, (TILE, count)).T)
    extra = jnp.where(
        lane == sq,
        1.0,
        jnp.where(lane == sq + 1, a, jnp.where(lane == sq + 2, b, jnp.where(lane == sq + 3, c, 0.0))),
    )
    qx[...] = jnp.where(in_q, p[:, strip(qt, TILE)].astype(WIDE) * SCORE_SCALE, extra).astype(LOW)
    grad = jnp.where(in_v, d_o[:, strip(ot, TILE)].astype(WIDE), 0.0)
    inner = jnp.sum(grad * o[:, strip(ot, TILE)].astype(WIDE), axis=-1, keepdims=True)
    a, b, c = split_three(-inner)
    gx[...] = (
        grad + jnp.where(lane == sv, a, jnp.where(lane == sv + 1, b, jnp.where(lane == sv + 2, c, 0.0)))
    ).astype(LOW)
    scores = mm_nt(kx[...], qx[...])
    if causal:
        scores = jnp.where(subs(scores.shape) <= lanes(scores.shape), scores, NEG_FILL)
    probs = jnp.exp(scores)
    d_scores = (probs * mm_nt(vx[...], gx[...])).astype(LOW)
    d_v = mm(probs.astype(LOW), gx[...])
    d_k = mm(d_scores, qx[...])
    d_q = mm(kt_v[...], d_scores).T * SCORE_SCALE

    def place(tile_index, inside, value):
        cut = strip(tile_index, TILE)
        d_p[:, cut] = jnp.where(inside, value, d_p[:, cut].astype(WIDE)).astype(LOW)

    place(qt, in_q, d_q)
    place(kt, in_q, d_k)
    place(vtile, in_v, d_v)


def block_kernel(
    planes, self_in, crs_in, up_in, dn_in, x_in, cot_in, gain_in, bias_self, bias_cross,
    block_out, grad_out, home_ffn, home_crs, home_att, gain_out,
    cot, first_k, x_k, second_k, late_k, memory_k, p_k, o_k, lse_k, pc_k, oc_k, lsec_k, act_k, grad_k, y3_k,
    dw_ffn, dw_crs, dw_att, yb_ffn, yb_crs, yb_att, zb_ffn, zb_crs, zb_att,
    att_v, crs_v, up_v, dn_v, a_v, b_v, o_v, do_v, mid_v, late_v, s_v, g_v, c_v, ta, tb, tc,
    send_v, recv_v, kx, qx, vx, gx, kt_v, lse_v, gain_v, gain_in_v, gain_buf, out_st, dw_st, sum_st,
    x_sem, x_sent, y0_sent, c_sem, zw_got, zw_sent, yw_got, yw_sent, side_got, side_sent,
    row_got, row_sent, fwd_sem, cot_got, gain_sem, copy_sem, ex_got, ex_sent, mem_got, mem_sent, mf_got, mf_sent,
    dm_got, dm_sent, df_got, df_sent, y_got, y_sent, z_got, z_sent, home_got, home_sent,
    blk_got, blk_sent, gr_got, gr_sent, gr_hop_got, gr_hop_sent, sum_sem, dw_sem,
):
    at = Place(planes)
    c, z, t, y, r = at.c, at.z, at.t, at.y, at.r
    rows = x_in.shape[1]
    slot = s_v.shape[0]
    tiles = slot // BLOCK
    depth = up_in.shape[0]
    side = crs_in.shape[1]
    relay = at.relays
    other = jnp.logical_not(relay)
    vmem = {"att": att_v, "crs": crs_v, "up": up_v, "dn": dn_v}
    shard = {"att": self_in, "up": up_in, "dn": dn_in}
    here = pl.ds(pl.multiple_of(z * depth, depth), depth)
    dw = {"ffn": dw_ffn, "crs": dw_crs, "att": dw_att}
    yb = {"ffn": yb_ffn, "crs": yb_crs, "att": yb_att}
    zb = {"ffn": zb_ffn, "crs": zb_crs, "att": zb_att}
    home = {"ffn": home_ffn, "crs": home_crs, "att": home_att}
    names = {}

    def copying(name, source, goal):
        index = names.setdefault(name, len(names))
        return pltpu.make_async_copy(source, goal, copy_sem.at[index])

    def half_of(core):
        return pl.ds(pl.multiple_of(core * 2 * rows, 2 * rows), 2 * rows)

    at.meet()

    relay_dev = (y, z, 2 * y + c)
    over_dev = (y, z, 2 * (1 - y) + c)
    stays = both(c == y, r == c)

    def launch(g):
        i = GROUPS.index(g)
        goal = vmem[g].at[r, here, :]

        @pl.when(stays)
        def _():
            pltpu.make_async_copy(shard[g], goal, x_sem.at[i, r]).start()

        @pl.when(jnp.logical_not(stays))
        def _():
            push(shard[g], goal, x_sent.at[i], x_sem.at[i, r], relay_dev).start()

    def launch_over(g):
        i = GROUPS.index(g)
        return push(shard[g], vmem[g].at[r, here, :], y0_sent.at[i], yw_got.at[i, 0, r], over_dev)

    crs_dev = (y, z, 2 * y + 1)
    crs_stays = both(c == y, r == 1)

    def crs_goal(block, section):
        return crs_v.at[block, here, pl.ds(pl.multiple_of((1 - section) * side, side), side)]

    def launch_crs():
        @pl.when(crs_stays)
        def _():
            pltpu.make_async_copy(crs_in, crs_goal(r, c), c_sem.at[r, c]).start()

        @pl.when(jnp.logical_not(crs_stays))
        def _():
            push(crs_in, crs_goal(r, c), x_sent.at[1], c_sem.at[r, c], crs_dev).start()

    row_goal = s_v.at[strip(t, rows), :]
    cot_goal = cot.at[strip(t, rows), :]

    def row_stays(s):
        return both(both(c == y, r == c), y == s)

    def launch_rows(s):
        dev = (y, z, 2 * s + c)

        @pl.when(row_stays(s))
        def _():
            pltpu.make_async_copy(x_in.at[s], row_goal, row_got.at[r]).start()

        @pl.when(jnp.logical_not(row_stays(s)))
        def _():
            push(x_in.at[s], row_goal, row_sent.at[s], row_got.at[r], dev).start()

    def launch_cot():
        dev = (y, z, 2 * c + 1)

        @pl.when(crs_stays)
        def _():
            pltpu.make_async_copy(cot_in.at[c], cot_goal, cot_got.at[r]).start()

        @pl.when(jnp.logical_not(crs_stays))
        def _():
            push(cot_in.at[c], cot_goal, row_sent.at[2], cot_got.at[r], dev).start()

    gain_copy = push(gain_in, gain_in_v.at[c], gain_sem.at[0], gain_sem.at[1], at.twin)
    gain_copy.start()
    launch("att")
    launch_over("att").start()
    launch_rows(0)
    launch_rows(1)
    launch("up")
    launch_over("up").start()
    launch_crs()
    launch("dn")
    launch_cot()

    def piece(g, k, b):
        j = lax.rem(z - k + planes, planes)
        return vmem[g].at[b, pl.ds(pl.multiple_of(j * depth, depth), depth), :]

    def ring(g, k, b):
        i = GROUPS.index(g)
        return push(
            piece(g, k - 1, b), piece(g, k - 1, b), zw_sent.at[i, k - 1, b], zw_got.at[i, k - 1, b], at.above
        )

    def ring_in(g, k, b):
        i = GROUPS.index(g)
        return push(piece(g, k, b), piece(g, k, b), zw_sent.at[i, k - 1, b], zw_got.at[i, k - 1, b], at.above)

    def cross_over(g, k, b):
        i = GROUPS.index(g)
        return push(piece(g, k, b), piece(g, k, b), yw_sent.at[i, k, b], yw_got.at[i, k, b], at.across)

    def arrive(g, k, b):
        if k:
            ring_in(g, k, b).wait_recv()
        elif g == "crs":
            for section in range(2):
                goal = crs_goal(b, section)
                push(goal, goal, x_sent.at[1], c_sem.at[b, section], at.twin).wait_recv()
        else:
            i = GROUPS.index(g)
            goal = vmem[g].at[b, here, :]
            push(goal, goal, x_sent.at[i], x_sem.at[i, b], at.twin).wait_recv()

    def passing(g, k, up=True, over=True):
        def run():
            for b in range(2):
                if up:
                    with jax.named_scope("await_" + g + str(k)):
                        arrive(g, k, b)
                    if k + 1 < planes:
                        ring(g, k + 1, b).start()
                if over and not (k == 0 and g in DIRECT) and not (k == 1 and (g, b) in ASIDE):
                    cross_over(g, k, b).start()

        return run

    def schedule(order):
        events = []
        for n, g in enumerate(order):
            for k in range(planes):
                if k == 0 and n == 0:
                    events.append(passing(g, 0))
                elif k:
                    events.append(passing(g, k))
                if n + 1 < len(order):
                    if k == planes - 2:
                        events[-1] = chained(events[-1], passing(order[n + 1], 0, True, False))
                    if k == planes - 1:
                        events[-1] = chained(events[-1], passing(order[n + 1], 0, False, True))
        return events

    def chained(one, two):
        def run():
            one()
            two()

        return run

    enc_events = schedule(("att", "up", "dn"))
    dec_events = schedule(("att", "crs", "up", "dn"))

    def pump_enc(count):
        for _ in range(min(count, len(enc_events))):
            pl.when(both(relay, at.encodes))(enc_events.pop(0))

    def pump_dec(count):
        for _ in range(min(count, len(dec_events))):
            pl.when(both(relay, at.decodes))(dec_events.pop(0))

    def pump(count):
        pump_enc(count)
        pump_dec(count)

    def side_hop(g, b):
        i = GROUPS.index(g)
        return push(piece(g, 0, b), piece(g, 0, b), side_sent.at[i, b], side_got.at[i, b], at.above)

    def side_in(g, b):
        i = GROUPS.index(g)
        return push(piece(g, 1, b), piece(g, 1, b), side_sent.at[i, b], side_got.at[i, b], at.above)

    def pass_aside(g):
        @pl.when(other)
        def _():
            for b in range(2):
                cross_over(g, 0, b).wait_recv()
                if (g, b) in ASIDE:
                    side_hop(g, b).start()

    def settle(g):
        listens = both(other, at.decodes) if g == "crs" else other

        @pl.when(listens)
        def _():
            for k in range(planes):
                for b in range(2):
                    if k == 1 and (g, b) in ASIDE:
                        side_in(g, b).wait_recv()
                    elif k or g in ("att", "crs"):
                        cross_over(g, k, b).wait_recv()

    def exchange(e, i):
        q = strip(i, BLOCK)
        k = e % 2
        return push(send_v.at[k, q, :], recv_v.at[k, q, :], ex_sent.at[e, i], ex_got.at[e, i], at.twin)

    def joined(e, i):
        q = strip(i, BLOCK)
        exchange(e, i).wait_recv()
        return send_v[e % 2, q, :].astype(WIDE) + recv_v[e % 2, q, :].astype(WIDE)

    def sent(e):
        each(tiles, lambda i: exchange(e, i).wait_send())

    pump(3)
    for k in range(2):
        goal = s_v.at[strip(2 * c + k, rows), :]
        push(goal, goal, row_sent.at[0], row_got.at[k], at.twin).wait_recv()
    half, far_half = half_of(c), half_of(1 - c)
    rows_on = push(s_v.at[half, :], s_v.at[half, :], fwd_sem.at[0], fwd_sem.at[1], at.twin)
    rows_on.start()
    push(gain_in, gain_in_v.at[1 - c], gain_sem.at[0], gain_sem.at[1], at.twin).wait_recv()
    gain_here = pltpu.make_async_copy(gain_in, gain_in_v.at[c], gain_sem.at[2])
    gain_here.start()
    gain_here.wait()
    gains = gain_in_v.at[r]
    g0, g1, g2 = gains[0:1, :], gains[1:2, :], gains[2:3, :]
    gain_v[...] = jnp.zeros_like(gain_v)
    push(s_v.at[far_half, :], s_v.at[far_half, :], fwd_sem.at[0], fwd_sem.at[1], at.twin).wait_recv()
    x_put = copying("x", s_v, x_k)
    x_put.start()

    def enter(i):
        q = strip(i, BLOCK)
        c_v[q, :] = (center(s_v[q, :].astype(WIDE))[0] * g0).astype(LOW)

    each(tiles, enter)
    first_put = copying("first", c_v, first_k)
    first_put.start()
    pump(1)
    settle("att")

    def project(source, weights, part):
        def project_rows(i):
            q = strip(i, BLOCK)
            for b in range(2):
                if part != "kv":
                    a_v[b, q, 0:256] = mm(source[q, :], weights[b, :, 0:256]).astype(LOW)
                if part != "q":
                    a_v[b, q, 256:640] = mm(source[q, :], weights[b, :, 384:768]).astype(LOW)

        each(tiles, project_rows)

    packed_v = a_v.at[:, :, 0:640]
    project(c_v, att_v, "all")
    pass_aside("up")
    p_put = copying("p", packed_v, p_k)
    p_put.start()
    o_v[...] = jnp.zeros_like(o_v)
    lse_v[...] = jnp.zeros_like(lse_v)
    pump(1)

    def attend_heads(bias, causal, hooks):
        def head_forward(n):
            b = lax.div(n, 3)
            attend_block(lax.rem(n, 3), a_v.at[b], o_v.at[b], lse_v, n, bias, kx, qx, kt_v, causal)
            for when, event in hooks:
                pl.when(both(n == when, relay))(event)

        each(6, head_forward)

    enc_hooks = [(2, enc_events.pop(0)), (5, enc_events.pop(0))]
    dec_hooks = [(2, dec_events.pop(0)), (5, dec_events.pop(0))]
    pl.when(at.encodes)(lambda: attend_heads(bias_self, False, enc_hooks))
    pl.when(at.decodes)(lambda: attend_heads(bias_self, True, dec_hooks))
    o_put, lse_put = copying("o", o_v, o_k), copying("lse", lse_v, lse_k)
    o_put.start()
    lse_put.start()

    def out_project(e, weights):
        def out_rows(i):
            q = strip(i, BLOCK)
            part = mm_nt(o_v[0, q, :], weights[0, :, 128:384]) + mm_nt(o_v[1, q, :], weights[1, :, 128:384])
            send_v[e % 2, q, :] = part.astype(LOW)
            exchange(e, i).start()

        each(tiles, out_rows)

    out_project(0, att_v)
    pump(1)
    x_put.wait()
    pass_aside("dn")
    rows_on.wait_send()

    def middle(i):
        q = strip(i, BLOCK)
        value = s_v[q, :].astype(WIDE) + joined(0, i)
        mid_v[q, :] = value
        s_v[q, :] = (center(value)[0] * g1).astype(LOW)

    each(tiles, middle)
    first_put.wait()
    p_put.wait()
    o_put.wait()
    lse_put.wait()

    def mem_send(i):
        q = pl.ds(pl.multiple_of((2 * c + i) * BLOCK, BLOCK), BLOCK)
        return push(g_v.at[q, :], g_v.at[q, :], mem_sent.at[i], mem_got.at[i], at.beside)

    def mem_forward(i, core):
        q = pl.ds(pl.multiple_of((2 * core + i) * BLOCK, BLOCK), BLOCK)
        return push(g_v.at[q, :], g_v.at[q, :], mf_sent.at[i], mf_got.at[i], at.twin)

    def row_home(k, source, goal, sent_by, got):
        dev = (r, z, 2 * c + k)
        keeps = both(both(c == r, y == c), r == k)
        return keeps, source, goal.at[y], sent_by.at[k], got.at[y], dev

    def go_home(*spec):
        keeps, source, goal, sent_by, got, dev = row_home(*spec)

        @pl.when(keeps)
        def _():
            pltpu.make_async_copy(source, goal, got).start()

        @pl.when(jnp.logical_not(keeps))
        def _():
            push(source, goal, sent_by, got, dev).start()

    def went_home(*spec):
        keeps, source, goal, sent_by, got, dev = row_home(*spec)

        @pl.when(jnp.logical_not(keeps))
        def _():
            push(source, goal, sent_by, got, dev).wait_send()

    def memory_home(k):
        return k, memory_k.at[strip(2 * c + k, rows), :], block_out, blk_sent, blk_got

    settle_up = lambda: settle("up")
    pl.when(at.encodes)(settle_up)

    @pl.when(at.encodes)
    def _():
        def up_rows(i):
            q = strip(i, BLOCK)
            for b in range(2):
                value, grade = gelu_parts(mm(s_v[q, :], up_v[b]))
                a_v[b, q, :] = value.astype(LOW)
                b_v[b, q, :] = grade.astype(LOW)

        each(tiles, up_rows)

    pump_enc(9)

    @pl.when(at.encodes)
    def _():
        settle("dn")

        def down_rows(i):
            q = strip(i, BLOCK)
            part = mm_nt(a_v[0, q, :], dn_v[0]) + mm_nt(a_v[1, q, :], dn_v[1])
            send_v[1, q, :] = part.astype(LOW)
            exchange(1, i).start()

        each(tiles, down_rows)

        def finish(n):
            i = lax.rem(n + 2 * c, 4)
            q = strip(i, BLOCK)
            value = mid_v[q, :] + joined(1, i)
            late_v[q, :] = value
            g_v[q, :] = (center(value)[0] * g2).astype(LOW)

            @pl.when(n < 2)
            def _():
                mem_send(n).start()

        each(tiles, finish)
        keep = copying("memory", g_v, memory_k)
        keep.start()
        keep.wait()
        for k in range(2):
            go_home(*memory_home(k))
        sent(0)

    def norm_grad(values, gain, grad, gain_row, counted):
        normal, scale = center(values)
        scaled = grad * gain
        one = jnp.mean(scaled, axis=-1, keepdims=True)
        two = jnp.mean(scaled * normal, axis=-1, keepdims=True)
        total = jnp.sum(grad * normal, axis=0, keepdims=True)
        gain_v[gain_row : gain_row + 1, :] += jnp.where(counted, total, 0.0)
        return (scaled - one - normal * two) * scale

    def ours(i):
        return lax.div(i, 2) == c

    @pl.when(at.decodes)
    def _():
        second_put = copying("second", s_v, second_k)
        second_put.start()
        for k in range(2):
            goal = cot.at[strip(2 * c + k, rows), :]
            push(goal, goal, row_sent.at[2], cot_got.at[k], at.twin).wait_recv()
        cot_on = push(cot.at[half, :], cot.at[half, :], fwd_sem.at[2], fwd_sem.at[3], at.twin)
        cot_on.start()
        for _ in range(len(dec_events) - 3):
            pl.when(relay)(dec_events.pop(0))
        settle("crs")
        project(s_v, crs_v, "q")
        for _ in range(len(dec_events)):
            pl.when(relay)(dec_events.pop(0))
        push(cot.at[far_half, :], cot.at[far_half, :], fwd_sem.at[2], fwd_sem.at[3], at.twin).wait_recv()
        cot_in_v = copying("cot", cot, c_v)
        cot_in_v.start()
        o_v[...] = jnp.zeros_like(o_v)
        lse_v[...] = jnp.zeros_like(lse_v)
        for i in range(2):
            mem_send(i).wait_recv()
            mem_forward(i, c).start()
        for i in range(2):
            mem_forward(i, 1 - c).wait_recv()
        project(g_v, crs_v, "kv")
        puts = [copying("pc", packed_v, pc_k), copying("memory", g_v, memory_k)]
        for copy in puts:
            copy.start()
        attend_heads(bias_cross, False, [])
        puts += [copying("oc", o_v, oc_k), copying("lsec", lse_v, lsec_k)]
        for copy in puts[2:]:
            copy.start()
        out_project(1, crs_v)
        second_put.wait()

        def finish(i):
            q = strip(i, BLOCK)
            value = mid_v[q, :] + joined(1, i)
            late_v[q, :] = value
            s_v[q, :] = (center(value)[0] * g2).astype(LOW)

        each(tiles, finish)
        late_put = copying("late", late_v, late_k)
        late_put.start()
        settle("up")
        settle("dn")
        cot_in_v.wait()
        sent(0)
        for copy in puts:
            copy.wait()

        def feed_rows(i):
            q = strip(i, BLOCK)
            part = None
            for b in range(2):
                value, grade = gelu_parts(mm(s_v[q, :], up_v[b]))
                a_v[b, q, :] = value.astype(LOW)
                d_pre = (mm(c_v[q, :], dn_v[b]) * grade).astype(LOW)
                b_v[b, q, :] = d_pre
                term = mm_nt(d_pre, up_v[b])
                part = term if part is None else part + term
            send_v[0, q, :] = part.astype(LOW)
            exchange(2, i).start()

        each(tiles, feed_rows)
        copying("act", a_v, act_k).start()
        late_put.wait()
        cot_on.wait_send()
        each(2, lambda i: mem_forward(i, c).wait_send())

    def block_of(k):
        return lax.rem(z - 1 - k + 2 * planes, planes)

    def y_hop(g, k, b):
        i = SUMS.index(g)
        return push(dw[g].at[k, b], yb[g].at[k, b], y_sent.at[i, k, b], y_got.at[i, k, b], at.across)

    def z_hop(g, k, b):
        i = SUMS.index(g)
        return push(dw[g].at[k, b], zb[g].at[k, b], z_sent.at[i, k, b], z_got.at[i, k, b], at.above)

    def leave(g, k):
        @pl.when(other)
        def _():
            for b in range(2):
                y_hop(g, k, b).start()

    def emit(g, compute):
        columns = dw[g].shape[3]

        def put(k, s):
            return pltpu.make_async_copy(dw_st.at[s, :, :, 0:columns], dw[g].at[k], dw_sem.at[s])

        def run(k):
            s = lax.rem(k, 2)
            j = block_of(k)
            compute(s, pl.ds(pl.multiple_of(j * depth, depth), depth))
            put(k, s).start()

            @pl.when(k >= 1)
            def _():
                put(k - 1, 1 - s).wait()
                leave(g, k - 1)

        each(planes, run, "emit_" + g)
        put(planes - 1, (planes - 1) % 2).wait()
        leave(g, planes - 1)

    def homes(g, b):
        columns = dw[g].shape[3]
        source = dw[g].at[planes - 1, b]
        if g == "crs":
            return [
                (
                    both(c == section, r == b),
                    source.at[:, pl.ds((1 - section) * (columns // 2), columns // 2)],
                    (section, z, 2 * y + b),
                    2 * b + section,
                )
                for section in range(2)
            ]
        return [(both(c == r, r == b), source, (r, z, 2 * y + b), b)]

    def summing(g, k, b):
        i = SUMS.index(g)
        columns = dw[g].shape[3]

        def fetch(n, source):
            copy = pltpu.make_async_copy(source, sum_st.at[n, :, 0:columns], sum_sem.at[n])
            copy.start()
            return copy

        def run():
            with jax.named_scope("await_y_" + g + str(k)):
                y_hop(g, k, b).wait_recv()
            copies = [fetch(0, dw[g].at[k, b]), fetch(1, yb[g].at[k, b])]
            if k:
                with jax.named_scope("await_z_" + g + str(k)):
                    z_hop(g, k - 1, b).wait_recv()
                copies.append(fetch(2, zb[g].at[k - 1, b]))
            for copy in copies:
                copy.wait()
            total = sum_st[0, :, 0:columns].astype(WIDE) + sum_st[1, :, 0:columns].astype(WIDE)
            if k:
                total = total + sum_st[2, :, 0:columns].astype(WIDE)
            sum_st[0, :, 0:columns] = total.astype(LOW)
            back = pltpu.make_async_copy(sum_st.at[0, :, 0:columns], dw[g].at[k, b], sum_sem.at[0])
            back.start()
            back.wait()
            if k + 1 < planes:
                z_hop(g, k, b).start()
            else:
                for keeps, source, dev, n in homes(g, b):

                    @pl.when(keeps)
                    def _():
                        pltpu.make_async_copy(source, home[g], home_got.at[i]).start()

                    @pl.when(jnp.logical_not(keeps))
                    def _():
                        push(source, home[g], home_sent.at[i, n], home_got.at[i], dev).start()

        return run

    enc_sums = [summing(g, k, b) for g in ("ffn", "att") for k in range(planes) for b in range(2)]
    dec_sums = [summing(g, k, b) for g in ("ffn", "crs", "att") for k in range(planes) for b in range(2)]

    def add_enc(count):
        for _ in range(min(count, len(enc_sums))):
            pl.when(both(relay, at.encodes))(enc_sums.pop(0))

    def add_dec(count):
        for _ in range(min(count, len(dec_sums))):
            pl.when(both(relay, at.decodes))(dec_sums.pop(0))

    def turn(source, goal):
        def run(i):
            q = strip(i, BLOCK)
            goal[:, q] = source[q, :].astype(WIDE).T.astype(LOW)

        each(tiles, run, "turn")

    def dm_hop(n, source):
        q = pl.ds(pl.multiple_of((2 * c + n) * BLOCK, BLOCK), BLOCK)
        return push(source.at[q, :], c_v.at[q, :], dm_sent.at[n], dm_got.at[n], at.beside)

    def df_hop(n, core):
        q = pl.ds(pl.multiple_of((2 * core + n) * BLOCK, BLOCK), BLOCK)
        return push(c_v.at[q, :], c_v.at[q, :], df_sent.at[n], df_got.at[n], at.twin)

    @pl.when(at.encodes)
    def _():
        def back_rows(m):
            n = lax.div(m, 2)
            own = lax.rem(m, 2) == 0
            i = jnp.where(own, 2 * c + n, 2 * (1 - c) + n)
            q = strip(i, BLOCK)

            @pl.when(own)
            def _():
                dm_hop(n, c_v).wait_recv()
                df_hop(n, c).start()

            @pl.when(jnp.logical_not(own))
            def _():
                df_hop(n, 1 - c).wait_recv()

            grad = norm_grad(late_v[q, :], g2, c_v[q, :].astype(WIDE), 2, ours(i))
            late_v[q, :] = grad
            low = grad.astype(LOW)
            part = None
            for b in range(2):
                d_pre = (mm(low, dn_v[b]) * b_v[b, q, :].astype(WIDE)).astype(LOW)
                b_v[b, q, :] = d_pre
                term = mm_nt(d_pre, up_v[b])
                part = term if part is None else part + term
            send_v[0, q, :] = part.astype(LOW)

            @pl.when(own)
            def _():
                df_hop(n, c).wait_send()

            c_v[q, :] = low
            exchange(2, i).start()

        each(tiles, back_rows)

    turn(s_v, ta)
    turn(c_v, tb)

    def ffn_block(s, j):
        for b in range(2):
            dw_st[s, b, :, 0:768] = mm(ta[j, :], b_v[b]).astype(LOW)
            dw_st[s, b, :, 768:1536] = mm(tb[j, :], a_v[b]).astype(LOW)

    emit("ffn", ffn_block)

    @pl.when(at.decodes)
    def _():
        copying("act", a_v, act_k).wait()
        packed = copying("pc", pc_k, packed_v)
        small = [copying("oc", oc_k, o_v), copying("lsec", lsec_k, lse_v), copying("second", second_k, s_v)]
        packed.start()
        for copy in small:
            copy.start()

        def late_rows(i):
            q = strip(i, BLOCK)
            grad = c_v[q, :].astype(WIDE) + norm_grad(late_v[q, :], g2, joined(2, i), 2, ours(i))
            late_v[q, :] = grad
            g_v[q, :] = grad.astype(LOW)

        each(tiles, late_rows)

        def cross_out(i):
            q = strip(i, BLOCK)
            for b in range(2):
                do_v[b, q, :] = mm(g_v[q, :], crs_v[b, :, 128:384]).astype(LOW)

        each(tiles, cross_out)
        for copy in small:
            copy.wait()
        packed.wait()
        b_v[...] = jnp.zeros_like(b_v)

        def cross_head(n):
            b = lax.div(n, 3)
            attend_back_block(
                lax.rem(n, 3), a_v.at[b], o_v.at[b], do_v.at[b], b_v.at[b], lse_v, n, bias_cross,
                kx, qx, vx, gx, kt_v, False,
            )

        each(6, cross_head)
        sent(1)

        def to_memory(q):
            return mm_nt(b_v[0, q, 256:640], crs_v[0, :, 384:768]) + mm_nt(b_v[1, q, 256:640], crs_v[1, :, 384:768])

        def far(n):
            i = 2 * (1 - c) + n
            q = strip(i, BLOCK)
            send_v[1, q, :] = to_memory(q).astype(LOW)
            exchange(3, i).start()

        each(2, far)

        def near(n):
            i = 2 * c + n
            q = strip(i, BLOCK)
            part = to_memory(q)
            exchange(3, i).wait_recv()
            send_v[1, q, :] = (part + recv_v[1, q, :].astype(WIDE)).astype(LOW)
            dm_hop(n, send_v.at[1]).start()

        each(2, near)

        def to_query(i):
            q = strip(i, BLOCK)
            part = mm_nt(b_v[0, q, 0:256], crs_v[0, :, 0:256]) + mm_nt(b_v[1, q, 0:256], crs_v[1, :, 0:256])
            send_v[0, q, :] = part.astype(LOW)
            exchange(4, i).start()

        sent(2)
        each(tiles, to_query)
        add_dec(2)
        turn(s_v, ta)
        stage_in = copying("memory", memory_k, s_v)
        stage_in.start()
        turn(g_v, tc)
        stage_in.wait()
        turn(s_v, tb)
        copying("first", first_k, s_v).start()

        def crs_block(s, j):
            for b in range(2):
                left = mm(ta[j, :], b_v[b, :, 0:256])
                out = mm(tc[j, :], o_v[b])
                dw_st[s, b, :, 0:128] = left[:, 0:128].astype(LOW)
                dw_st[s, b, :, 128:256] = (left[:, 128:256] + out[:, 0:128]).astype(LOW)
                dw_st[s, b, :, 256:384] = out[:, 128:256].astype(LOW)
                dw_st[s, b, :, 384:768] = mm(tb[j, :], b_v[b, :, 256:640]).astype(LOW)

        emit("crs", crs_block)
        add_dec(2)

        def below(i):
            q = strip(i, BLOCK)
            grad = late_v[q, :] + norm_grad(mid_v[q, :], g1, joined(4, i), 1, ours(i))
            late_v[q, :] = grad
            g_v[q, :] = grad.astype(LOW)

        each(tiles, below)
        copying("first", first_k, s_v).wait()

        def gone(n):
            exchange(3, 2 * (1 - c) + n).wait_send()
            dm_hop(n, send_v.at[1]).wait_send()

        each(2, gone)

    @pl.when(at.encodes)
    def _():
        copying("first", first_k, s_v).start()
        each(2, lambda i: mem_send(i).wait_send())

        def below(i):
            q = strip(i, BLOCK)
            grad = late_v[q, :] + norm_grad(mid_v[q, :], g1, joined(2, i), 1, ours(i))
            late_v[q, :] = grad
            g_v[q, :] = grad.astype(LOW)

        each(tiles, below)
        copying("first", first_k, s_v).wait()
        sent(1)

    packed = copying("p", p_k, packed_v)
    small = [copying("o", o_k, o_v), copying("lse", lse_k, lse_v)]
    packed.start()
    for copy in small:
        copy.start()

    def self_out(i):
        q = strip(i, BLOCK)
        for b in range(2):
            do_v[b, q, :] = mm(g_v[q, :], att_v[b, :, 128:384]).astype(LOW)

    each(tiles, self_out)
    b_v[...] = jnp.zeros_like(b_v)
    for copy in small:
        copy.wait()
    packed.wait()

    def self_heads(causal, hooks):
        def self_head(n):
            b = lax.div(n, 3)
            attend_back_block(
                lax.rem(n, 3), a_v.at[b], o_v.at[b], do_v.at[b], b_v.at[b], lse_v, n, bias_self,
                kx, qx, vx, gx, kt_v, causal,
            )
            for when, event in hooks:
                pl.when(both(n == when, relay))(event)

        each(6, self_head)

    enc_back = [(n, enc_sums.pop(0)) for n in (1, 2, 4, 5)]
    dec_back = [(n, dec_sums.pop(0)) for n in (0, 1, 2, 3, 4, 5)]
    pl.when(at.encodes)(lambda: self_heads(False, enc_back))
    pl.when(at.decodes)(lambda: self_heads(True, dec_back))

    def to_rows(q):
        part = None
        for b in range(2):
            term = mm_nt(b_v[b, q, 0:256], att_v[b, :, 0:256]) + mm_nt(b_v[b, q, 256:640], att_v[b, :, 384:768])
            part = term if part is None else part + term
        return part

    def far_rows(n):
        i = 2 * (1 - c) + n
        q = strip(i, BLOCK)
        send_v[1, q, :] = to_rows(q).astype(LOW)
        exchange(5, i).start()

    each(2, far_rows)
    add_enc(1)
    add_dec(2)
    turn(s_v, ta)
    x_in_v = copying("x", x_k, s_v)
    x_in_v.start()
    turn(g_v, tc)

    def att_block(s, j):
        for b in range(2):
            left = mm(ta[j, :], b_v[b, :, 0:256])
            out = mm(tc[j, :], o_v[b])
            dw_st[s, b, :, 0:128] = left[:, 0:128].astype(LOW)
            dw_st[s, b, :, 128:256] = (left[:, 128:256] + out[:, 0:128]).astype(LOW)
            dw_st[s, b, :, 256:384] = out[:, 128:256].astype(LOW)
            dw_st[s, b, :, 384:768] = mm(ta[j, :], b_v[b, :, 256:640]).astype(LOW)

    emit("att", att_block)
    add_enc(1)
    add_dec(2)
    x_in_v.wait()

    def near_rows(n):
        i = 2 * c + n
        q = strip(i, BLOCK)
        part = to_rows(q)
        exchange(5, i).wait_recv()
        grad = part + recv_v[1, q, :].astype(WIDE)
        value = late_v[q, :] + norm_grad(s_v[q, :].astype(WIDE), g0, grad, 0, True)
        out_st[strip(n, BLOCK), :] = value.astype(LOW)

    each(2, near_rows)
    out_put = copying("out", out_st, grad_k)
    out_put.start()
    out_put.wait()

    def grad_home(k):
        return k, grad_k.at[strip(k, rows), :], grad_out, gr_sent, gr_got

    for k in range(2):
        go_home(*grad_home(k))

    def gain_hop(n, source, device):
        return push(source, gain_buf.at[n], gr_hop_sent.at[n], gr_hop_got.at[n], device)

    gain_buf[0] = gain_v[...]
    twin_hop = gain_hop(1, gain_buf.at[0], at.twin)
    twin_hop.start()
    twin_hop.wait()
    peer_hop = gain_hop(3, gain_buf.at[2], (1 - c, z, lax.rem(t + 2, 4)))
    last = 4 + planes

    @pl.when(relay)
    def _():
        gain_buf[2] = gain_buf[0] + gain_buf[1]
        peer_hop.start()

    def ring_hop(n):
        return gain_hop(5 + n, gain_buf.at[4 + n], at.above)

    def gain_step(n):
        @pl.when(relay)
        @jax.named_scope("gains")
        def _():
            if n == 0:
                peer_hop.wait()
                gain_buf[4] = gain_buf[2] + gain_buf[3]
            else:
                ring_hop(n - 1).wait()
            if n < planes - 1:
                ring_hop(n).start()
            else:
                total = None
                for j in range(planes):
                    held = gain_buf[jnp.where(z == j, 4, 5 + lax.rem(z - 1 - j + planes, planes))]
                    total = held if total is None else total + held
                gain_buf[last] = total
                for b in range(2):
                    keeps = both(c == r, r == b)

                    @pl.when(keeps)
                    def _():
                        pltpu.make_async_copy(gain_buf.at[last], gain_buf.at[last + 1], gr_hop_got.at[last + 1]).start()

                    @pl.when(jnp.logical_not(keeps))
                    def _():
                        final_hop(b).start()

    def final_hop(b):
        return push(
            gain_buf.at[last], gain_buf.at[last + 1], gr_hop_sent.at[last + b], gr_hop_got.at[last + 1],
            (r, z, 2 * y + b),
        )

    def y3_home(k):
        return k, y3_k.at[strip(k, rows), :], block_out, blk_sent, blk_got

    @pl.when(at.decodes)
    def _():
        copies = [copying("act", act_k, a_v), copying("late", late_k, mid_v)]
        for copy in copies:
            copy.start()
        sent(4)
        for copy in copies:
            copy.wait()

        def to_out(q):
            return mm_nt(a_v[0, q, :], dn_v[0]) + mm_nt(a_v[1, q, :], dn_v[1])

        def far_out(n):
            i = 2 * (1 - c) + n
            q = strip(i, BLOCK)
            send_v[0, q, :] = to_out(q).astype(LOW)
            exchange(6, i).start()

        each(2, far_out)

        def near_out(n):
            i = 2 * c + n
            q = strip(i, BLOCK)
            part = to_out(q)
            exchange(6, i).wait_recv()
            out_st[strip(n, BLOCK), :] = (mid_v[q, :] + part + recv_v[0, q, :].astype(WIDE)).astype(LOW)

        each(2, near_out)
        y3_put = copying("out", out_st, y3_k)
        y3_put.start()
        y3_put.wait()
        for k in range(2):
            go_home(*y3_home(k))

    for n in range(planes):
        add_enc(2)
        add_dec(3)
        gain_step(n)
    add_enc(99)
    add_dec(99)

    with jax.named_scope("await_rows"):
        for s in range(2):
            for goal, got in ((block_out, blk_got), (grad_out, gr_got)):
                push(goal.at[s], goal.at[s], blk_sent.at[0], got.at[s], at.twin).wait_recv()
    push(gain_buf.at[last], gain_buf.at[last + 1], gr_hop_sent.at[last], gr_hop_got.at[last + 1], at.twin).wait_recv()
    gains_home = copying("gains", gain_buf.at[last + 1], gain_out)
    gains_home.start()
    gains_home.wait()
    for i, g in enumerate(SUMS):
        with jax.named_scope("await_home_" + g):
            push(home[g], home[g], home_sent.at[i, 0], home_got.at[i], at.twin).wait_recv()
    for k in range(2):
        went_home(*grad_home(k))

    @pl.when(at.encodes)
    def _():
        for k in range(2):
            went_home(*memory_home(k))
        sent(2)

    @pl.when(at.decodes)
    def _():
        for k in range(2):
            went_home(*y3_home(k))
        each(2, lambda n: exchange(6, 2 * (1 - c) + n).wait_send())

    each(2, lambda n: exchange(5, 2 * (1 - c) + n).wait_send())

    @pl.when(relay)
    def _():
        for b in range(2):
            pl.when(jnp.logical_not(both(c == r, r == b)))(lambda: final_hop(b).wait_send())

    for g in SUMS:
        there = at.decodes if g == "crs" else jnp.logical_or(at.decodes, at.encodes)

        @pl.when(both(other, there))
        def _():
            for k in range(planes):
                for b in range(2):
                    y_hop(g, k, b).wait_send()

        @pl.when(both(relay, there))
        def _():
            for b in range(2):
                for k in range(planes - 1):
                    z_hop(g, k, b).wait_send()
                for keeps, source, dev, n in homes(g, b):

                    @pl.when(jnp.logical_not(keeps))
                    def _():
                        i = SUMS.index(g)
                        push(source, home[g], home_sent.at[i, n], home_got.at[i], dev).wait_send()

    gain_copy.wait_send()
    for g in DIRECT:
        launch_over(g).wait_send()

    @pl.when(jnp.logical_not(stays))
    def _():
        for g in ("att", "up", "dn"):
            push(shard[g], vmem[g].at[r, here, :], x_sent.at[GROUPS.index(g)], x_sem.at[0, 0], relay_dev).wait_send()

    @pl.when(jnp.logical_not(crs_stays))
    def _():
        push(crs_in, crs_goal(r, c), x_sent.at[1], c_sem.at[0, 0], crs_dev).wait_send()
        push(cot_in.at[c], cot_goal, row_sent.at[2], cot_got.at[r], at.twin).wait_send()

    for s in range(2):

        @pl.when(jnp.logical_not(row_stays(s)))
        def _():
            push(x_in.at[s], row_goal, row_sent.at[s], row_got.at[r], at.twin).wait_send()

    for g in GROUPS:
        member = both(relay, at.decodes) if g == "crs" else relay

        @pl.when(member)
        def _():
            for k in range(planes):
                for b in range(2):
                    if k:
                        ring(g, k, b).wait_send()
                    if (k or g not in DIRECT) and (k != 1 or (g, b) not in ASIDE):
                        cross_over(g, k, b).wait_send()

    @pl.when(other)
    def _():
        for g, b in ASIDE:
            side_hop(g, b).wait_send()


def block_call(planes, slot, width, hidden, depth, args):
    shape = jax.ShapeDtypeStruct
    rows = slot // 4
    square = (slot, width)
    wides = {"ffn": 2 * hidden, "crs": width, "att": width}
    packed, outs, logs, acts = (2, slot, 640), (2, slot, 256), (8, slot), (2, slot, hidden)
    out_shape = (
        [shape((2, rows, width), LOW)] * 2
        + [shape((depth, 2 * hidden), LOW), shape((depth, width // 2), LOW), shape((depth, width), LOW)]
        + [shape((8, width), WIDE)]
        + [shape(square, LOW)] * 4
        + [shape(square, WIDE), shape(square, LOW)]
        + [shape(packed, LOW), shape(outs, LOW), shape(logs, WIDE)] * 2
        + [shape(acts, LOW)]
        + [shape((2 * rows, width), LOW)] * 2
        + [shape((planes, 2, depth, wides[g]), LOW) for g in SUMS] * 3
    )
    dma = pltpu.SemaphoreType.DMA
    v = pltpu.VMEM
    groups = len(GROUPS)
    scratch = (
        [v((2, width, width), LOW)] * 2
        + [v((2, width, hidden), LOW)] * 2
        + [v(acts, LOW)] * 2
        + [v(outs, LOW)] * 2
        + [v(square, WIDE)] * 2
        + [v(square, LOW)] * 3
        + [v((width, slot), LOW)] * 3
        + [v((2,) + square, LOW)] * 2
        + [v((slot, TILE), LOW)] * 4
        + [v((TILE, slot), LOW), v(logs, WIDE), v((8, width), WIDE), v((2, 8, width), WIDE)]
        + [v((planes + 6, 8, width), WIDE)]
        + [v((2 * rows, width), LOW), v((2, 2, depth, 2 * hidden), LOW), v((3, depth, 2 * hidden), LOW)]
        + [dma((groups, 2)), dma((groups,)), dma((groups,)), dma((2, 2))]
        + [dma((groups, planes, 2))] * 4
        + [dma((groups, 2))] * 2
        + [dma((2,)), dma((3,)), dma((4,)), dma((2,)), dma((3,)), dma((24,)), dma((7, 4)), dma((7, 4))]
        + [dma((2,))] * 8
        + [dma((3, planes, 2))] * 4
        + [dma((3,)), dma((3, 4))]
        + [dma((2,))] * 4
        + [dma((planes + 6,))] * 2
        + [dma((3,)), dma((2,))]
    )
    any_spec = pl.BlockSpec(memory_space=pl.ANY)
    vmem_spec = pl.BlockSpec(memory_space=pltpu.VMEM)
    return pl.pallas_call(
        functools.partial(block_kernel, planes),
        out_shape=out_shape,
        in_specs=[any_spec] * 6 + [vmem_spec] * 3,
        out_specs=[any_spec] * len(out_shape),
        scratch_shapes=scratch,
        compiler_params=pltpu.CompilerParams(collective_id=0, has_side_effects=True, vmem_limit_bytes=VMEM_BYTES),
    )(*args)


def ring_gather(lay, shard):
    planes = lay.planes
    rows = shard.shape[1]
    if planes > 4:
        piece = lax.all_gather(shard, "dp", axis=1, tiled=True)
        across = lay.route(piece, lambda c, z, t: (c, z, (t + 2) % 4) if c == t // 2 else None)
        return jnp.where(lay.relays, piece, across)
    relay = lambda c, z, t: (c, (z + 1) % planes, t) if c == t // 2 else None
    whole = jnp.zeros((shard.shape[0], planes * rows, shard.shape[2]), shard.dtype)
    piece = shard
    for step in range(planes):
        across = lay.route(piece, lambda c, z, t: (c, z, (t + 2) % 4) if c == t // 2 else None)
        chosen = jnp.where(lay.relays, piece, across)
        whole = lax.dynamic_update_slice(whole, chosen, (0, ((lay.plane - step) % planes) * rows, 0))
        if step + 1 < planes:
            piece = lay.route(piece, relay)
    return whole


def ring_scatter(lay, total, holder):
    planes = lay.planes
    rows = total.shape[1] // planes
    low = total.astype(LOW)
    across = lay.route(
        low, lambda c, z, t: (c, z, (t + 2) % 4) if (c != t // 2 and t % 2 == holder) else None
    )
    summed = low.astype(WIDE) + across.astype(WIDE)
    if planes > 4:
        return lax.psum_scatter(summed.astype(LOW), "dp", scatter_dimension=1, tiled=True)
    relay = lambda c, z, t: (c, (z + 1) % planes, t) if (c == t // 2 and t % 2 == holder) else None
    take = lambda j: lax.dynamic_slice_in_dim(summed, (j % planes) * rows, rows, 1)
    running = take(lay.plane - 1)
    for step in range(1, planes):
        running = lay.route(running.astype(LOW), relay).astype(WIDE) + take(lay.plane - 1 - step)
    return running.astype(LOW)


def hand_back(lay, value, holder, section):
    same = lay.route(
        value[0], lambda c, z, t: (section, z, t) if (c == t // 2 and t % 2 == holder) else None
    )
    beside = lay.route(
        value[1], lambda c, z, t: (section, z, t ^ 1) if (c == t // 2 and t % 2 == holder) else None
    )
    return same.astype(WIDE) + beside.astype(WIDE)


def general_body(block_input, w_self, w_self_out, w_cross, w_up, w_down, norm_gains, lengths, task_mask, out_grad):
    lay = Layout()
    seqs, rows, width = block_input.shape[1:]
    slot = rows * lay.chips
    sec = lay.core
    item = lay.item

    def spread(value, first):
        pick = value[jnp.where(first, lay.chip % 2, 1 - lay.chip % 2)]
        flip = 0 if first else 1
        return lay.route(pick, lambda c, z, t: (t // 2, z, 2 * ((t % 2) ^ flip) + c))

    def merge_rows(mine, theirs):
        low_half = jnp.where(lay.core == 0, mine, theirs)
        high_half = jnp.where(lay.core == 0, theirs, mine)
        return jnp.concatenate([low_half[0], low_half[1], high_half[0], high_half[1]], axis=0)

    first = spread(block_input[0], True)
    second = spread(block_input[0], False)
    mine = jnp.where(item == 0, jnp.stack([first, second]), jnp.stack([second, first]))
    x_rows = merge_rows(mine, lay.other_core(mine)).astype(WIDE)

    picked = out_grad[lay.core]
    even = lay.route(picked, lambda c, z, t: (t // 2, z, 2 * c + 1) if t % 2 == 0 else None)
    odd = lay.route(picked, lambda c, z, t: (t // 2, z, 2 * c + 1) if t % 2 == 1 else None)
    mine = jnp.stack([even, odd])
    cotangent = merge_rows(mine, lay.other_core(mine))

    gains_here = norm_gains[0].astype(WIDE)
    gains = jnp.where(sec == lay.role, gains_here, lay.other_core(norm_gains[0]).astype(WIDE))

    depth = w_self.shape[1]
    wide = w_self.shape[3]
    self_block = pack_heads(
        {"q": w_self[0, :, 0], "k": w_self[0, :, 1], "v": w_self[0, :, 2], "o": w_self_out[0].T}
    )
    feed_block = jnp.concatenate([w_up[0], w_down[0].T], axis=1)
    cross_block = w_cross[0].reshape(depth, 2 * wide)

    def collect(block):
        same = lay.route(block, lambda c, z, t: (t // 2, z, t) if c == t % 2 else None)
        beside = lay.route(block, lambda c, z, t: (t // 2, z, t ^ 1) if c != t % 2 else None)
        return jnp.stack([same, beside])

    def collect_cross(block, section):
        same = lay.route(block, lambda c, z, t: (t // 2, z, t) if (c == section and t % 2 == 1) else None)
        beside = lay.route(block, lambda c, z, t: (t // 2, z, t ^ 1) if (c == section and t % 2 == 0) else None)
        return same, beside

    w_att = ring_gather(lay, collect(self_block))
    w_ffn = ring_gather(lay, collect(feed_block))
    memory_side = collect_cross(cross_block, 0)
    query_side = collect_cross(cross_block, 1)
    w_crs = ring_gather(
        lay,
        jnp.stack(
            [
                pack_heads({"q": q[:, :wide], "k": m[:, :wide], "v": m[:, wide:], "o": q[:, wide:]})
                for m, q in zip(memory_side, query_side)
            ]
        ),
    )
    hidden = w_up.shape[2]
    part = lambda w, name: jnp.concatenate([unpack_heads(w[0], name), unpack_heads(w[1], name)], axis=1)
    att = {n: part(w_att, n) for n in "qkvo"}
    crs = {n: part(w_crs, n) for n in "qkvo"}
    up = jnp.concatenate([w_ffn[0, :, :hidden], w_ffn[1, :, :hidden]], axis=1)
    down_t = jnp.concatenate([w_ffn[0, :, hidden:], w_ffn[1, :, hidden:]], axis=1)

    positions = jnp.arange(slot)
    own_length = jnp.where(lay.is_decoder, lengths[1, item], lengths[0, item])
    self_allowed = (positions[None, :] < own_length) & (
        (positions[None, :] <= positions[:, None]) | jnp.logical_not(lay.is_decoder)
    )
    cross_allowed = jnp.broadcast_to(
        ((positions < lengths[0, item]) & (task_mask[item] == 1))[None], (slot, slot)
    )

    def joined(partial):
        low = partial.astype(LOW)
        return low.astype(WIDE) + lay.other_core(low).astype(WIDE)

    normed0 = layer_norm(x_rows, gains[0]).astype(LOW)
    q, k, v = (mm(normed0, att[n]).astype(LOW) for n in "qkv")
    out_self, lse_self = attend(q, k, v, self_allowed)
    x_mid = x_rows + joined(mm_nt(out_self, att["o"]))
    normed1 = layer_norm(x_mid, gains[1]).astype(LOW)

    pre_enc = mm(normed1, up)
    act_enc, slope_enc = gelu_parts(pre_enc)
    act_enc = act_enc.astype(LOW)
    x_late_enc = x_mid + joined(mm_nt(act_enc, down_t))
    memory_enc = layer_norm(x_late_enc, gains[2]).astype(LOW)
    memory = lay.route(memory_enc, lambda c, z, t: (c, z, t ^ 1) if t % 2 == 0 else None)

    cq = mm(normed1, crs["q"]).astype(LOW)
    ck, cv = (mm(memory, crs[n]).astype(LOW) for n in "kv")
    out_cross, lse_cross = attend(cq, ck, cv, cross_allowed)
    x_late = x_mid + joined(mm_nt(out_cross, crs["o"]))
    normed2 = layer_norm(x_late, gains[2]).astype(LOW)
    pre_dec = mm(normed2, up)
    act_dec, slope_dec = gelu_parts(pre_dec)
    act_dec = act_dec.astype(LOW)
    result_dec = (x_late + joined(mm_nt(act_dec, down_t))).astype(LOW)

    d_out = cotangent.astype(WIDE)
    d_pre = (slope_dec * mm(cotangent, down_t)).astype(LOW)
    d_ffn_dec = jnp.concatenate([mm_tn(normed2, d_pre), mm_tn(cotangent, act_dec)], axis=1)
    d_late_norm, d_gain2_dec = norm_back(x_late, gains[2], joined(mm_nt(d_pre, up)))
    d_late = d_out + d_late_norm
    grad_late = d_late.astype(LOW)
    d_att = mm(grad_late, crs["o"]).astype(LOW)
    d_cq, d_ck, d_cv = attend_back(cq, ck, cv, lse_cross, d_att, cross_allowed)
    d_memory = joined(mm_nt(d_ck, crs["k"]) + mm_nt(d_cv, crs["v"]))
    d_crs = {
        "q": mm_tn(normed1, d_cq),
        "k": mm_tn(memory, d_ck),
        "v": mm_tn(memory, d_cv),
        "o": mm_tn(grad_late, out_cross),
    }
    d_mid_norm, d_gain1_dec = norm_back(x_mid, gains[1], joined(mm_nt(d_cq, crs["q"])))
    d_mid_dec = d_late + d_mid_norm

    d_memory = lay.route(d_memory.astype(LOW), lambda c, z, t: (c, z, t ^ 1) if t % 2 == 1 else None).astype(WIDE)
    d_late_enc, d_gain2_enc = norm_back(x_late_enc, gains[2], d_memory)
    grad_late_enc = d_late_enc.astype(LOW)
    d_pre = (slope_enc * mm(grad_late_enc, down_t)).astype(LOW)
    d_ffn_enc = jnp.concatenate([mm_tn(normed1, d_pre), mm_tn(grad_late_enc, act_enc)], axis=1)
    d_mid_norm, d_gain1_enc = norm_back(x_mid, gains[1], joined(mm_nt(d_pre, up)))
    d_mid_enc = d_late_enc + d_mid_norm

    d_mid = jnp.where(lay.is_decoder, d_mid_dec, d_mid_enc)
    grad_mid = d_mid.astype(LOW)
    d_att = mm(grad_mid, att["o"]).astype(LOW)
    d_q, d_k, d_v = attend_back(q, k, v, lse_self, d_att, self_allowed)
    d_norm = joined(mm_nt(d_q, att["q"]) + mm_nt(d_k, att["k"]) + mm_nt(d_v, att["v"]))
    d_att_w = {
        "q": mm_tn(normed0, d_q),
        "k": mm_tn(normed0, d_k),
        "v": mm_tn(normed0, d_v),
        "o": mm_tn(grad_mid, out_self),
    }
    d_first, d_gain0 = norm_back(x_rows, gains[0], d_norm)
    d_rows = d_mid + d_first

    half = 3 * HEAD

    def blocks(parts):
        return jnp.stack(
            [pack_heads({n: parts[n][:, half * b : half * (b + 1)] for n in parts}) for b in range(2)]
        )

    def feed_blocks(both):
        total = both.shape[1] // 2
        return jnp.stack(
            [
                jnp.concatenate(
                    [both[:, hidden * b : hidden * (b + 1)], both[:, total + hidden * b : total + hidden * (b + 1)]],
                    axis=1,
                )
                for b in range(2)
            ]
        )

    self_total = blocks(d_att_w)
    home_self = hand_back(lay, ring_scatter(lay, self_total, 0), 0, 0) + hand_back(
        lay, ring_scatter(lay, self_total, 1), 1, 1
    )
    home_feed = hand_back(lay, ring_scatter(lay, feed_blocks(d_ffn_enc), 0), 0, 0) + hand_back(
        lay, ring_scatter(lay, feed_blocks(d_ffn_dec), 1), 1, 1
    )
    cross_total = ring_scatter(lay, blocks(d_crs), 1)
    side = lambda names: jnp.stack(
        [jnp.concatenate([unpack_heads(cross_total[b], n) for n in names], axis=1) for b in range(2)]
    )
    home_cross = hand_back(lay, side("kv"), 1, 0) + hand_back(lay, side("qo"), 1, 1)

    g_self = jnp.stack([unpack_heads(home_self, n) for n in "qkv"], axis=1)[None]
    g_self_out = unpack_heads(home_self, "o").T[None]
    g_cross = home_cross.reshape(1, depth, 2, wide)
    g_up = home_feed[:, :hidden][None]
    g_down = home_feed[:, hidden:].T[None]

    gain2 = jnp.where(lay.is_decoder, d_gain2_dec, d_gain2_enc)
    gain1 = jnp.where(lay.is_decoder, d_gain1_dec, d_gain1_enc)
    gain_rows = jnp.stack([d_gain0, gain1, gain2])
    slots = jnp.stack(
        [
            jnp.where((lay.role == r) & (lay.core == 0), gain_rows, 0.0)
            for r in range(2)
        ]
    )
    gain_total = lax.psum(slots, AXES)[sec][None]

    def rows_home(value):
        mine = lax.dynamic_slice_in_dim(value, lay.core * 2 * rows, 2 * rows, 0).reshape(2, rows, width)
        a = lay.route(mine[item], lambda c, z, t: (t % 2, z, 2 * c + t // 2))
        b = lay.route(mine[1 - item], lambda c, z, t: (t % 2, z, 2 * c + 1 - t // 2))
        even = lay.chip % 2 == 0
        return jnp.where(even, jnp.stack([a, b]), jnp.stack([b, a]))[None]

    block_output = rows_home(jnp.where(lay.is_decoder, result_dec, memory_enc))
    input_grad = rows_home(d_rows.astype(LOW)).astype(WIDE)
    return (
        block_output,
        input_grad,
        g_self,
        g_self_out,
        g_cross,
        g_up,
        g_down,
        gain_total[:, :2],
        gain_total[:, 2],
    )


def body(block_input, w_self, w_self_out, w_cross, w_up, w_down, norm_gains, lengths, task_mask, out_grad):
    lay = Layout()
    seqs, rows, width = block_input.shape[1:]
    slot = rows * lay.chips
    sec = lay.core
    item = lay.item

    if lay.planes != 4:
        return general_body(
            block_input, w_self, w_self_out, w_cross, w_up, w_down, norm_gains, lengths, task_mask, out_grad
        )

    depth = w_self.shape[1]
    wide = w_self.shape[3]
    hidden = w_up.shape[2]
    self_block = pack_heads(
        {"q": w_self[0, :, 0], "k": w_self[0, :, 1], "v": w_self[0, :, 2], "o": w_self_out[0].T}
    )
    pair = {"q": w_cross[0, :, 0], "o": w_cross[0, :, 1], "k": w_cross[0, :, 0], "v": w_cross[0, :, 1]}
    pieces = [pair[n][:, HEAD * h : HEAD * (h + 1)] for n, h in ORDER]
    cross_block = jnp.where(
        sec == 1, jnp.concatenate(pieces[:6], axis=1), jnp.concatenate(pieces[6:], axis=1)
    )
    gain_block = jnp.concatenate([norm_gains[0].astype(WIDE), jnp.zeros((5, width), WIDE)], axis=0)

    positions = jnp.arange(slot)
    own_length = jnp.where(lay.is_decoder, lengths[1, item], lengths[0, item])

    def key_bias(allowed):
        return jnp.broadcast_to(jnp.where(allowed, 0.0, NEG_FILL)[:, None], (slot, TILE)).astype(LOW)

    biases = (
        key_bias(positions < own_length),
        key_bias((positions < lengths[0, item]) & (task_mask[item] == 1)),
    )
    block_output, input_grad, home_feed, home_cross, home_self, gain_total = block_call(
        lay.planes,
        slot,
        width,
        hidden,
        depth,
        (self_block, cross_block, w_up[0], w_down[0].T, block_input[0], out_grad, gain_block) + biases,
    )[:6]
    home_self, home_feed, home_cross = (v.astype(WIDE) for v in (home_self, home_feed, home_cross))
    g_self = jnp.stack([unpack_heads(home_self, n) for n in "qkv"], axis=1)[None]
    g_self_out = unpack_heads(home_self, "o").T[None]
    halves = (ORDER[:6], ORDER[6:])
    take = lambda order, name: jnp.concatenate(
        [home_cross[:, HEAD * order.index((name, h)) : HEAD * (order.index((name, h)) + 1)] for h in range(3)], axis=1
    )
    g_cross = jnp.where(
        sec == 1,
        jnp.stack([take(halves[0], "q"), take(halves[0], "o")], axis=1),
        jnp.stack([take(halves[1], "k"), take(halves[1], "v")], axis=1),
    )[None]
    g_up = home_feed[:, :hidden][None]
    g_down = home_feed[:, hidden:].T[None]
    gain_total = gain_total[None]
    return (
        block_output[None],
        input_grad.astype(WIDE)[None],
        g_self,
        g_self_out,
        g_cross,
        g_up,
        g_down,
        gain_total[:, :2],
        gain_total[:, 2],
    )


def solution(mesh):
    placed = (
        P("section", "dp", "tensor", None),
        P("section", "dp", None, "tensor"),
        P("section", "tensor", "dp"),
        P("section", "dp", None, "tensor"),
        P("section", "dp", "tensor"),
        P("section", "tensor", "dp"),
        P("section", None, None),
        P(None, "dp"),
        P("dp", None),
        P("dp", "tensor", None),
    )
    return jax.shard_map(
        body,
        mesh=mesh,
        in_specs=placed,
        out_specs=(
            P("section", "dp", "tensor", None),
            P("section", "dp", "tensor", None),
            P("section", "dp", None, "tensor"),
            P("section", "tensor", "dp"),
            P("section", "dp", None, "tensor"),
            P("section", "dp", "tensor"),
            P("section", "tensor", "dp"),
            P("section", None, None),
            P("section", None),
        ),
        check_vma=False,
    )
```

```python
import functools

import jax
import jax.numpy as jnp
from jax import lax
from jax.experimental import pallas as pl
from jax.experimental.pallas import tpu as pltpu
from jax.sharding import PartitionSpec as P

HEAD = 64
TILE = 128
EPSILON = 1e-05
SCORE_SCALE = 0.125
NEG_FILL = -1000000000.0
AXES = ("section", "dp", "tensor")
LOW = jnp.bfloat16
WIDE = jnp.float32


class Layout:
    def __init__(self):
        self.cores = lax.axis_size("section")
        self.planes = lax.axis_size("dp")
        self.chips = lax.axis_size("tensor")
        self.core = lax.axis_index("section")
        self.plane = lax.axis_index("dp")
        self.chip = lax.axis_index("tensor")
        self.role = self.chip % 2
        self.item = self.chip // 2
        self.is_decoder = self.role == 1
        self.relays = self.core == self.item

    def route(self, value, target):
        pairs = []
        for core in range(self.cores):
            for plane in range(self.planes):
                for chip in range(self.chips):
                    to = target(core, plane, chip)
                    if to is None:
                        continue
                    source = (core * self.planes + plane) * self.chips + chip
                    goal = (to[0] * self.planes + to[1]) * self.chips + to[2]
                    pairs.append((source, goal))
        return lax.ppermute(value, AXES, pairs)

    def other_core(self, value):
        return self.route(value, lambda c, z, t: (1 - c, z, t))


def normalize(values):
    centred = values - jnp.mean(values, axis=-1, keepdims=True)
    spread = jnp.mean(centred * centred, axis=-1, keepdims=True)
    scale = lax.rsqrt(spread + EPSILON)
    return centred * scale, scale


def layer_norm(values, gain):
    return normalize(values)[0] * gain


def norm_back(values, gain, grad):
    normal, scale = normalize(values)
    scaled = grad * gain
    first = jnp.mean(scaled, axis=-1, keepdims=True)
    second = jnp.mean(scaled * normal, axis=-1, keepdims=True)
    return (scaled - first - normal * second) * scale, jnp.sum(grad * normal, axis=0)


ORDER = (("q", 0), ("q", 1), ("q", 2), ("o", 2), ("o", 0), ("o", 1), ("k", 0), ("k", 1), ("v", 0), ("v", 1), ("k", 2), ("v", 2))


def pack_heads(parts):
    return jnp.concatenate([parts[n][:, HEAD * h : HEAD * (h + 1)] for n, h in ORDER], axis=1)


def unpack_heads(block, name):
    where = {(n, h): i for i, (n, h) in enumerate(ORDER)}
    return jnp.concatenate(
        [block[:, HEAD * where[(name, h)] : HEAD * (where[(name, h)] + 1)] for h in range(3)], axis=1
    )


def mm(left, right):
    return jnp.dot(left, right, preferred_element_type=WIDE)


def mm_nt(left, right):
    return lax.dot_general(left, right, (((1,), (1,)), ((), ())), preferred_element_type=WIDE)


def mm_tn(left, right):
    return lax.dot_general(left, right, (((0,), (0,)), ((), ())), preferred_element_type=WIDE)


def split_heads(value):
    return value.reshape(value.shape[0], -1, HEAD)


def attend(q, k, v, allowed):
    scores = jnp.einsum("qhd,khd->hqk", split_heads(q), split_heads(k), preferred_element_type=WIDE) * SCORE_SCALE
    scores = jnp.where(allowed[None], scores, NEG_FILL)
    top = jnp.max(scores, axis=-1, keepdims=True)
    power = jnp.exp(scores - top)
    total = jnp.sum(power, axis=-1, keepdims=True)
    probs = (power / total).astype(LOW)
    out = jnp.einsum("hqk,khd->qhd", probs, split_heads(v), preferred_element_type=WIDE)
    return out.astype(LOW).reshape(q.shape), top + jnp.log(total)


def attend_back(q, k, v, log_sum, d_out, allowed):
    scores = jnp.einsum("qhd,khd->hqk", split_heads(q), split_heads(k), preferred_element_type=WIDE) * SCORE_SCALE
    scores = jnp.where(allowed[None], scores, NEG_FILL)
    probs = jnp.exp(scores - log_sum)
    d_probs = jnp.einsum("qhd,khd->hqk", split_heads(d_out), split_heads(v), preferred_element_type=WIDE)
    inner = jnp.sum(probs * d_probs, axis=-1, keepdims=True)
    d_scores = (probs * (d_probs - inner)).astype(LOW)
    d_v = jnp.einsum("hqk,qhd->khd", probs.astype(LOW), split_heads(d_out), preferred_element_type=WIDE)
    d_q = jnp.einsum("hqk,khd->qhd", d_scores, split_heads(k), preferred_element_type=WIDE) * SCORE_SCALE
    d_k = jnp.einsum("hqk,qhd->khd", d_scores, split_heads(q), preferred_element_type=WIDE) * SCORE_SCALE
    return tuple(g.astype(LOW).reshape(q.shape) for g in (d_q, d_k, d_v))


def gelu_parts(value):
    coef = 0.7978845608028654
    cube = 0.044715
    inner = coef * (value + cube * value * value * value)
    soft = jnp.tanh(inner)
    slope = 0.5 * (1.0 + soft) + 0.5 * value * (1.0 - soft * soft) * coef * (1.0 + 3.0 * cube * value * value)
    return 0.5 * value * (1.0 + soft), slope


MESH = pl.DeviceIdType.MESH
GROUPS = ("att", "crs", "up", "dn")
BLOCK = 256
VMEM_BYTES = 62 * 2**20


def lanes(shape):
    return lax.broadcasted_iota(jnp.int32, shape, len(shape) - 1)


def subs(shape):
    return lax.broadcasted_iota(jnp.int32, shape, 0)


def strip(i, size):
    return pl.ds(pl.multiple_of(i * size, size), size)


def head_place(h):
    two = (h == 2).astype(jnp.int32)
    one = (h >= 1).astype(jnp.int32)
    return two, 2 + 2 * two, 3 + two, 1 - two, HEAD * (one - two), HEAD * one


def each(count, step, name=None):
    def run(i, carry):
        step(i)
        return carry

    with jax.named_scope(name or step.__name__):
        lax.fori_loop(0, count, run, 0)


class Place:
    def __init__(self, planes):
        self.planes = planes
        self.c = lax.axis_index("section")
        self.z = lax.axis_index("dp")
        self.t = lax.axis_index("tensor")
        self.y = lax.div(self.t, 2)
        self.r = lax.rem(self.t, 2)
        self.twin = (1 - self.c, self.z, self.t)
        self.above = (self.c, lax.rem(self.z + 1, planes), self.t)
        self.below = (self.c, lax.rem(self.z + planes - 1, planes), self.t)
        self.across = (self.c, self.z, lax.rem(self.t + 2, 4))
        self.beside = (self.c, self.z, self.t + 1 - 2 * self.r)
        self.relays = self.c == self.y
        self.encodes = self.r == 0
        self.decodes = self.r == 1

    def meet(self):
        barrier = pltpu.get_barrier_semaphore()
        peers = [self.above, self.below]
        for dc in range(2):
            for dt in range(4):
                if dc or dt:
                    peers.append((lax.rem(self.c + dc, 2), self.z, lax.rem(self.t + dt, 4)))
        for peer in peers:
            pl.semaphore_signal(barrier, inc=1, device_id=peer, device_id_type=MESH)
        pl.semaphore_wait(barrier, len(peers))


def push(source, goal, sent, got, device):
    return pltpu.make_async_remote_copy(
        src_ref=source, dst_ref=goal, send_sem=sent, recv_sem=got, device_id=device, device_id_type=MESH
    )


def both(first, second):
    return jnp.logical_and(first, second)


def center(values):
    middle = values - jnp.mean(values, axis=-1, keepdims=True)
    scale = lax.rsqrt(jnp.mean(middle * middle, axis=-1, keepdims=True) + EPSILON)
    return middle * scale, scale


def attend_block(h, p, o, lse, lse_row, bias, kx, qx, vt, causal):
    count = p.shape[0]
    qt, kt, vtile, ot, qlo, vlo = head_place(h)
    lane = lanes((count, TILE))
    in_q = both(lane >= qlo, lane < qlo + HEAD)
    in_v = both(lane >= vlo, lane < vlo + HEAD)
    spare = HEAD - qlo
    kx[...] = jnp.where(lane == spare, bias[...], jnp.where(in_q, p[:, strip(kt, TILE)], jnp.zeros((), LOW)))
    vt[...] = jnp.where(in_v, p[:, strip(vtile, TILE)].astype(WIDE), 1.0).T.astype(LOW)
    qx[...] = jnp.where(
        in_q, p[:, strip(qt, TILE)].astype(WIDE) * SCORE_SCALE, jnp.where(lane == spare, 1.0, 0.0)
    ).astype(LOW)
    size = count // 2 if causal else count

    def queries(i):
        q = strip(i, size) if causal else pl.ds(0, count)
        scores = mm_nt(kx[...], qx[q, :])
        if causal:
            scores = jnp.where(subs(scores.shape) <= lanes(scores.shape) + i * size, scores, NEG_FILL)
        top = jnp.max(scores, axis=0, keepdims=True)
        power = jnp.exp(scores - top).astype(LOW)
        out = mm(vt[...], power)
        total = jnp.where(vlo == 0, out[HEAD : HEAD + 1, :], out[0:1, :])
        result = (out / total).T
        lane = lanes((size, TILE))
        in_v = both(lane >= vlo, lane < vlo + HEAD)
        o[q, strip(ot, TILE)] = jnp.where(in_v, result, o[q, strip(ot, TILE)].astype(WIDE)).astype(LOW)
        row = subs((8, size))
        lse[:, q] = jnp.where(row == lse_row, top + jnp.log(total), lse[:, q])

    if causal:
        each(count // size, queries)
    else:
        queries(0)


SUMS = ("ffn", "crs", "att")
DIRECT = ("att", "up")
ASIDE = (("up", 0), ("dn", 0))


def split_three(value):
    high = value.astype(LOW).astype(WIDE)
    middle = (value - high).astype(LOW).astype(WIDE)
    return high, middle, value - high - middle


def attend_back_block(h, p, o, d_o, d_p, lse, lse_row, bias, kx, qx, vx, gx, kt_v, dk_v, dv_v, causal):
    count = p.shape[0]
    qt, kt, vtile, ot, qlo, vlo = head_place(h)
    lane = lanes((count, TILE))
    in_q = both(lane >= qlo, lane < qlo + HEAD)
    in_v = both(lane >= vlo, lane < vlo + HEAD)
    sq, sv = HEAD - qlo, HEAD - vlo
    keys = jnp.where(
        in_q, p[:, strip(kt, TILE)].astype(WIDE), jnp.where(both(lane > sq, lane < sq + 4), 1.0, 0.0)
    )
    keys = jnp.where(lane == sq, bias[...].astype(WIDE), keys)
    kx[...] = keys.astype(LOW)
    kt_v[...] = keys.T.astype(LOW)
    vx[...] = jnp.where(
        in_v, p[:, strip(vtile, TILE)].astype(WIDE), jnp.where(both(lane >= sv, lane < sv + 3), 1.0, 0.0)
    ).astype(LOW)
    own = jnp.sum(jnp.where(subs((8, count)) == lse_row, lse[...], 0.0), axis=0, keepdims=True)
    a, b, c = split_three(-jnp.broadcast_to(own, (TILE, count)).T)
    extra = jnp.where(
        lane == sq,
        1.0,
        jnp.where(lane == sq + 1, a, jnp.where(lane == sq + 2, b, jnp.where(lane == sq + 3, c, 0.0))),
    )
    qx[...] = jnp.where(in_q, p[:, strip(qt, TILE)].astype(WIDE) * SCORE_SCALE, extra).astype(LOW)
    grad = jnp.where(in_v, d_o[:, strip(ot, TILE)].astype(WIDE), 0.0)
    inner = jnp.sum(grad * o[:, strip(ot, TILE)].astype(WIDE), axis=-1, keepdims=True)
    a, b, c = split_three(-inner)
    gx[...] = (
        grad + jnp.where(lane == sv, a, jnp.where(lane == sv + 1, b, jnp.where(lane == sv + 2, c, 0.0)))
    ).astype(LOW)
    size = count // 2 if causal else count

    def place(q, tile_index, low, value):
        cut = strip(tile_index, TILE)
        lane = lanes(value.shape)
        inside = both(lane >= low, lane < low + HEAD)
        d_p[q, cut] = jnp.where(inside, value, d_p[q, cut].astype(WIDE)).astype(LOW)

    whole = pl.ds(0, count)
    if causal:
        dk_v[...] = jnp.zeros_like(dk_v)
        dv_v[...] = jnp.zeros_like(dv_v)

    def queries(i):
        q = strip(i, size) if causal else pl.ds(0, count)
        scores = mm_nt(kx[...], qx[q, :])
        if causal:
            scores = jnp.where(subs(scores.shape) <= lanes(scores.shape) + i * size, scores, NEG_FILL)
        probs = jnp.exp(scores)
        d_scores = (probs * mm_nt(vx[...], gx[q, :])).astype(LOW)
        d_v = mm(probs.astype(LOW), gx[q, :])
        d_k = mm(d_scores, qx[q, :])
        place(q, qt, qlo, mm(kt_v[...], d_scores).T * SCORE_SCALE)
        if causal:
            dk_v[...] += d_k
            dv_v[...] += d_v
        else:
            place(whole, kt, qlo, d_k)
            place(whole, vtile, vlo, d_v)

    if not causal:
        queries(0)
    else:
        each(count // size, queries)
        place(whole, kt, qlo, dk_v[...])
        place(whole, vtile, vlo, dv_v[...])


def block_kernel(
    planes, self_in, crs_in, up_in, dn_in, x_in, cot_in, gain_in, lengths, task_mask,
    block_out, grad_low, home_ffn, home_crs, home_att, gain_out,
    cot, first_k, x_k, second_k, late_k, memory_k, p_k, o_k, lse_k, pc_k, oc_k, lsec_k, act_k, grad_k, y3_k,
    dw_ffn, dw_crs, dw_att, yb_ffn, yb_crs, yb_att, zb_ffn, zb_crs, zb_att,
    att_v, crs_v, up_v, dn_v, a_v, b_v, o_v, do_v, mid_v, late_v, s_v, g_v, c_v, ta, tb, tc,
    send_v, recv_v, kx, qx, vx, gx, dk_v, dv_v, kt_v, lse_v, gain_v, gain_in_v, gain_buf, out_st, dw_st, sum_st,
    bias_self, bias_cross,
    x_sem, x_sent, y0_sent, c_sem, zw_got, zw_sent, yw_got, yw_sent, side_got, side_sent,
    row_got, row_sent, fwd_sem, cot_got, gain_sem, copy_sem, ex_got, ex_sent, mem_got, mem_sent, mf_got, mf_sent,
    dm_got, dm_sent, df_got, df_sent, y_got, y_sent, z_got, z_sent, home_got, home_sent,
    blk_got, blk_sent, gr_got, gr_sent, gr_hop_got, gr_hop_sent, sum_sem, dw_sem,
):
    at = Place(planes)
    c, z, t, y, r = at.c, at.z, at.t, at.y, at.r
    rows = x_in.shape[1]
    slot = s_v.shape[0]
    tiles = slot // BLOCK
    depth = up_in.shape[0]
    side = crs_in.shape[1]
    relay = at.relays
    other = jnp.logical_not(relay)
    vmem = {"att": att_v, "crs": crs_v, "up": up_v, "dn": dn_v}
    shard = {"att": self_in, "up": up_in, "dn": dn_in}
    here = pl.ds(pl.multiple_of(z * depth, depth), depth)
    dw = {"ffn": dw_ffn, "crs": dw_crs, "att": dw_att}
    yb = {"ffn": yb_ffn, "crs": yb_crs, "att": yb_att}
    zb = {"ffn": zb_ffn, "crs": zb_crs, "att": zb_att}
    home = {"ffn": home_ffn, "crs": home_crs, "att": home_att}
    names = {}

    def copying(name, source, goal):
        index = names.setdefault(name, len(names))
        return pltpu.make_async_copy(source, goal, copy_sem.at[index])

    def half_of(core):
        return pl.ds(pl.multiple_of(core * 2 * rows, 2 * rows), 2 * rows)

    at.meet()

    relay_dev = (y, z, 2 * y + c)
    over_dev = (y, z, 2 * (1 - y) + c)
    stays = both(c == y, r == c)

    def launch(g):
        i = GROUPS.index(g)
        goal = vmem[g].at[r, here, :]

        @pl.when(stays)
        def _():
            pltpu.make_async_copy(shard[g], goal, x_sem.at[i, r]).start()

        @pl.when(jnp.logical_not(stays))
        def _():
            push(shard[g], goal, x_sent.at[i], x_sem.at[i, r], relay_dev).start()

    def launch_over(g):
        i = GROUPS.index(g)
        return push(shard[g], vmem[g].at[r, here, :], y0_sent.at[i], yw_got.at[i, 0, r], over_dev)

    crs_dev = (y, z, 2 * y + 1)
    crs_stays = both(c == y, r == 1)

    def crs_goal(block, section):
        return crs_v.at[block, here, pl.ds(pl.multiple_of((1 - section) * side, side), side)]

    def launch_crs():
        @pl.when(crs_stays)
        def _():
            pltpu.make_async_copy(crs_in, crs_goal(r, c), c_sem.at[r, c]).start()

        @pl.when(jnp.logical_not(crs_stays))
        def _():
            push(crs_in, crs_goal(r, c), x_sent.at[1], c_sem.at[r, c], crs_dev).start()

    row_goal = s_v.at[strip(t, rows), :]
    cot_goal = cot.at[strip(t, rows), :]

    def row_stays(s):
        return both(both(c == y, r == c), y == s)

    def launch_rows(s):
        dev = (y, z, 2 * s + c)

        @pl.when(row_stays(s))
        def _():
            pltpu.make_async_copy(x_in.at[s], row_goal, row_got.at[r]).start()

        @pl.when(jnp.logical_not(row_stays(s)))
        def _():
            push(x_in.at[s], row_goal, row_sent.at[s], row_got.at[r], dev).start()

    def launch_cot():
        dev = (y, z, 2 * c + 1)

        @pl.when(crs_stays)
        def _():
            pltpu.make_async_copy(cot_in.at[c], cot_goal, cot_got.at[r]).start()

        @pl.when(jnp.logical_not(crs_stays))
        def _():
            push(cot_in.at[c], cot_goal, row_sent.at[2], cot_got.at[r], dev).start()

    gain_copy = push(gain_in, gain_in_v.at[c], gain_sem.at[0], gain_sem.at[1], at.twin)
    gain_copy.start()
    launch("att")
    launch_over("att").start()
    launch_rows(0)
    launch_rows(1)
    launch("up")
    launch_over("up").start()
    launch_crs()
    launch("dn")
    launch_cot()

    place = subs((slot, TILE))
    seen = jnp.where(y == 0, task_mask[0:1, :], task_mask[1:2, :]) == 1
    seen = jnp.broadcast_to(jnp.where(seen, 1.0, 0.0), (TILE, slot)).T > 0.5
    bias_self[...] = jnp.where(place < lengths[r, y], 0.0, NEG_FILL).astype(LOW)
    bias_cross[...] = jnp.where(both(place < lengths[0, y], seen), 0.0, NEG_FILL).astype(LOW)

    def piece(g, k, b):
        j = lax.rem(z - k + planes, planes)
        return vmem[g].at[b, pl.ds(pl.multiple_of(j * depth, depth), depth), :]

    def ring(g, k, b):
        i = GROUPS.index(g)
        return push(
            piece(g, k - 1, b), piece(g, k - 1, b), zw_sent.at[i, k - 1, b], zw_got.at[i, k - 1, b], at.above
        )

    def ring_in(g, k, b):
        i = GROUPS.index(g)
        return push(piece(g, k, b), piece(g, k, b), zw_sent.at[i, k - 1, b], zw_got.at[i, k - 1, b], at.above)

    def cross_over(g, k, b):
        i = GROUPS.index(g)
        return push(piece(g, k, b), piece(g, k, b), yw_sent.at[i, k, b], yw_got.at[i, k, b], at.across)

    def arrive(g, k, b):
        if k:
            ring_in(g, k, b).wait_recv()
        elif g == "crs":
            for section in range(2):
                goal = crs_goal(b, section)
                push(goal, goal, x_sent.at[1], c_sem.at[b, section], at.twin).wait_recv()
        else:
            i = GROUPS.index(g)
            goal = vmem[g].at[b, here, :]
            push(goal, goal, x_sent.at[i], x_sem.at[i, b], at.twin).wait_recv()

    def passing(g, k, up=True, over=True):
        skips = [b for b in range(2) if k == 1 and (g, b) in ASIDE]

        def half(b):
            if up:
                with jax.named_scope("await_" + g + str(k)):
                    arrive(g, k, b)
                if k + 1 < planes:
                    ring(g, k + 1, b).start()
            if over and not (k == 0 and g in DIRECT):
                if skips:
                    pl.when(b != skips[0])(lambda: cross_over(g, k, b).start())
                else:
                    cross_over(g, k, b).start()

        def run():
            each(2, half, "pass_" + g)

        return run

    def schedule(order):
        events = []
        for n, g in enumerate(order):
            for k in range(planes):
                if k == 0 and n == 0:
                    events.append(passing(g, 0))
                elif k:
                    events.append(passing(g, k))
                if n + 1 < len(order):
                    if k == planes - 2:
                        events[-1] = chained(events[-1], passing(order[n + 1], 0, True, False))
                    if k == planes - 1:
                        events[-1] = chained(events[-1], passing(order[n + 1], 0, False, True))
        return events

    def chained(one, two):
        def run():
            one()
            two()

        return run

    enc_events = schedule(("att", "up", "dn"))
    dec_events = schedule(("att", "crs", "up", "dn"))

    def pump_enc(count):
        for _ in range(min(count, len(enc_events))):
            pl.when(both(relay, at.encodes))(enc_events.pop(0))

    def pump_dec(count):
        for _ in range(min(count, len(dec_events))):
            pl.when(both(relay, at.decodes))(dec_events.pop(0))

    def pump(count):
        pump_enc(count)
        pump_dec(count)

    def side_hop(g, b):
        i = GROUPS.index(g)
        return push(piece(g, 0, b), piece(g, 0, b), side_sent.at[i, b], side_got.at[i, b], at.above)

    def side_in(g, b):
        i = GROUPS.index(g)
        return push(piece(g, 1, b), piece(g, 1, b), side_sent.at[i, b], side_got.at[i, b], at.above)

    def pass_aside(g):
        @pl.when(other)
        def _():
            for b in range(2):
                cross_over(g, 0, b).wait_recv()
                if (g, b) in ASIDE:
                    side_hop(g, b).start()

    def settle(g):
        listens = both(other, at.decodes) if g == "crs" else other

        @pl.when(listens)
        @jax.named_scope("settle_" + g)
        def _():
            for k in range(planes):
                for b in range(2):
                    if k == 1 and (g, b) in ASIDE:
                        side_in(g, b).wait_recv()
                    elif k or g in ("att", "crs"):
                        cross_over(g, k, b).wait_recv()

    def exchange(e, i):
        q = strip(i, BLOCK)
        k = e % 2
        return push(send_v.at[k, q, :], recv_v.at[k, q, :], ex_sent.at[e, i], ex_got.at[e, i], at.twin)

    def joined(e, i):
        q = strip(i, BLOCK)
        exchange(e, i).wait_recv()
        return send_v[e % 2, q, :].astype(WIDE) + recv_v[e % 2, q, :].astype(WIDE)

    def sent(e):
        each(tiles, lambda i: exchange(e, i).wait_send())

    pump(3)
    for k in range(2):
        goal = s_v.at[strip(2 * c + k, rows), :]
        push(goal, goal, row_sent.at[0], row_got.at[k], at.twin).wait_recv()
    half, far_half = half_of(c), half_of(1 - c)
    rows_on = push(s_v.at[half, :], s_v.at[half, :], fwd_sem.at[0], fwd_sem.at[1], at.twin)
    rows_on.start()
    push(gain_in, gain_in_v.at[1 - c], gain_sem.at[0], gain_sem.at[1], at.twin).wait_recv()
    gain_here = pltpu.make_async_copy(gain_in, gain_in_v.at[c], gain_sem.at[2])
    gain_here.start()
    gain_here.wait()
    gains = gain_in_v[r].astype(WIDE)
    g0, g1, g2 = gains[0:1, :], gains[1:2, :], gains[2:3, :]
    gain_v[...] = jnp.zeros_like(gain_v)
    push(s_v.at[far_half, :], s_v.at[far_half, :], fwd_sem.at[0], fwd_sem.at[1], at.twin).wait_recv()
    x_put = copying("x", s_v, x_k)
    x_put.start()

    def enter(i):
        q = strip(i, BLOCK)
        c_v[q, :] = (center(s_v[q, :].astype(WIDE))[0] * g0).astype(LOW)

    each(tiles, enter)
    first_put = copying("first", c_v, first_k)
    first_put.start()
    pump(1)
    settle("att")

    def project(source, weights, part):
        def project_rows(n):
            b, q = lax.rem(n, 2), strip(lax.div(n, 2), BLOCK)
            if part != "kv":
                a_v[b, q, 0:256] = mm(source[q, :], weights[b, :, 0:256]).astype(LOW)
            if part != "q":
                a_v[b, q, 256:640] = mm(source[q, :], weights[b, :, 384:768]).astype(LOW)

        each(2 * tiles, project_rows)

    packed_v = a_v.at[:, :, 0:640]
    project(c_v, att_v, "all")
    pass_aside("up")
    p_put = copying("p", packed_v, p_k)
    p_put.start()
    o_v[...] = jnp.zeros_like(o_v)
    lse_v[...] = jnp.zeros_like(lse_v)
    pump(1)

    def attend_heads(bias, causal, hooks):
        def head_forward(n):
            b = lax.div(n, 3)
            attend_block(lax.rem(n, 3), a_v.at[b], o_v.at[b], lse_v, n, bias, kx, qx, kt_v, causal)
            for when, event in hooks:
                pl.when(both(n == when, relay))(event)

        each(6, head_forward)

    enc_hooks = [(2, enc_events.pop(0)), (5, enc_events.pop(0))]
    dec_hooks = [(2, dec_events.pop(0)), (4, dec_events.pop(0))]
    pl.when(at.encodes)(lambda: attend_heads(bias_self, False, enc_hooks))
    pl.when(at.decodes)(lambda: attend_heads(bias_self, True, dec_hooks))
    o_put, lse_put = copying("o", o_v, o_k), copying("lse", lse_v, lse_k)
    o_put.start()
    lse_put.start()

    def out_project(e, weights):
        def out_rows(i):
            q = strip(i, BLOCK)
            part = mm_nt(o_v[0, q, :], weights[0, :, 128:384]) + mm_nt(o_v[1, q, :], weights[1, :, 128:384])
            send_v[e % 2, q, :] = part.astype(LOW)
            exchange(e, i).start()

        each(tiles, out_rows)

    out_project(0, att_v)
    pump(1)
    x_put.wait()
    pass_aside("dn")
    rows_on.wait_send()

    def middle(i):
        q = strip(i, BLOCK)
        value = s_v[q, :].astype(WIDE) + joined(0, i)
        mid_v[q, :] = value
        s_v[q, :] = (center(value)[0] * g1).astype(LOW)

    each(tiles, middle)
    first_put.wait()
    p_put.wait()
    o_put.wait()
    lse_put.wait()

    def mem_send(i):
        q = pl.ds(pl.multiple_of((2 * c + i) * BLOCK, BLOCK), BLOCK)
        return push(g_v.at[q, :], g_v.at[q, :], mem_sent.at[i], mem_got.at[i], at.beside)

    def mem_forward(i, core):
        q = pl.ds(pl.multiple_of((2 * core + i) * BLOCK, BLOCK), BLOCK)
        return push(g_v.at[q, :], g_v.at[q, :], mf_sent.at[i], mf_got.at[i], at.twin)

    def row_home(k, source, goal, sent_by, got):
        dev = (r, z, 2 * c + k)
        keeps = both(both(c == r, y == c), r == k)
        return keeps, source, goal.at[y], sent_by.at[k], got.at[y], dev

    def go_home(*spec):
        keeps, source, goal, sent_by, got, dev = row_home(*spec)

        @pl.when(keeps)
        def _():
            pltpu.make_async_copy(source, goal, got).start()

        @pl.when(jnp.logical_not(keeps))
        def _():
            push(source, goal, sent_by, got, dev).start()

    def went_home(*spec):
        keeps, source, goal, sent_by, got, dev = row_home(*spec)

        @pl.when(jnp.logical_not(keeps))
        def _():
            push(source, goal, sent_by, got, dev).wait_send()

    def memory_home(k):
        return k, memory_k.at[strip(2 * c + k, rows), :], block_out, blk_sent, blk_got

    settle_up = lambda: settle("up")
    pl.when(at.encodes)(settle_up)

    @pl.when(at.encodes)
    def _():
        def up_rows(n):
            b, q = lax.rem(n, 2), strip(lax.div(n, 2), BLOCK)
            value, grade = gelu_parts(mm(s_v[q, :], up_v[b]))
            a_v[b, q, :] = value.astype(LOW)
            b_v[b, q, :] = grade.astype(LOW)

        each(2 * tiles, up_rows)

    pump_enc(9)

    @pl.when(at.encodes)
    def _():
        settle("dn")

        def down_rows(i):
            q = strip(i, BLOCK)
            part = mm_nt(a_v[0, q, :], dn_v[0]) + mm_nt(a_v[1, q, :], dn_v[1])
            send_v[1, q, :] = part.astype(LOW)
            exchange(1, i).start()

        each(tiles, down_rows)

        def finish(n):
            i = lax.rem(n + 2 * c, 4)
            q = strip(i, BLOCK)
            value = mid_v[q, :] + joined(1, i)
            late_v[q, :] = value
            g_v[q, :] = (center(value)[0] * g2).astype(LOW)

            @pl.when(n < 2)
            def _():
                mem_send(n).start()

        each(tiles, finish)
        keep = copying("memory", g_v, memory_k)
        keep.start()
        keep.wait()
        for k in range(2):
            go_home(*memory_home(k))
        sent(0)

    def norm_grad(values, gain, grad, gain_row, counted):
        normal, scale = center(values)
        scaled = grad * gain
        one = jnp.mean(scaled, axis=-1, keepdims=True)
        two = jnp.mean(scaled * normal, axis=-1, keepdims=True)
        total = jnp.sum(grad * normal, axis=0, keepdims=True)
        gain_v[gain_row : gain_row + 1, :] += jnp.where(counted, total, 0.0)
        return (scaled - one - normal * two) * scale

    def ours(i):
        return lax.div(i, 2) == c

    @pl.when(at.decodes)
    def _():
        second_put = copying("second", s_v, second_k)
        second_put.start()
        for k in range(2):
            goal = cot.at[strip(2 * c + k, rows), :]
            push(goal, goal, row_sent.at[2], cot_got.at[k], at.twin).wait_recv()
        cot_on = push(cot.at[half, :], cot.at[half, :], fwd_sem.at[2], fwd_sem.at[3], at.twin)
        cot_on.start()
        for _ in range(len(dec_events) - 3):
            pl.when(relay)(dec_events.pop(0))
        settle("crs")
        project(s_v, crs_v, "q")
        pl.when(relay)(dec_events.pop(0))
        pl.when(relay)(dec_events.pop(0))
        push(cot.at[far_half, :], cot.at[far_half, :], fwd_sem.at[2], fwd_sem.at[3], at.twin).wait_recv()
        cot_in_v = copying("cot", cot, c_v)
        cot_in_v.start()
        o_v[...] = jnp.zeros_like(o_v)
        lse_v[...] = jnp.zeros_like(lse_v)
        for i in range(2):
            mem_send(i).wait_recv()
            mem_forward(i, c).start()
        for i in range(2):
            mem_forward(i, 1 - c).wait_recv()
        project(g_v, crs_v, "kv")
        puts = [copying("pc", packed_v, pc_k), copying("memory", g_v, memory_k)]
        for copy in puts:
            copy.start()
        attend_heads(bias_cross, False, [(0, dec_events.pop(0))])
        puts += [copying("oc", o_v, oc_k), copying("lsec", lse_v, lsec_k)]
        for copy in puts[2:]:
            copy.start()
        out_project(1, crs_v)
        second_put.wait()

        def finish(i):
            q = strip(i, BLOCK)
            value = mid_v[q, :] + joined(1, i)
            late_v[q, :] = value
            s_v[q, :] = (center(value)[0] * g2).astype(LOW)

        each(tiles, finish)
        late_put = copying("late", late_v, late_k)
        late_put.start()
        settle("up")
        settle("dn")
        cot_in_v.wait()
        sent(0)
        for copy in puts:
            copy.wait()

        def feed_rows(i):
            q = strip(i, BLOCK)

            def feed_half(b):
                value, grade = gelu_parts(mm(s_v[q, :], up_v[b]))
                a_v[b, q, :] = value.astype(LOW)
                b_v[b, q, :] = (mm(c_v[q, :], dn_v[b]) * grade).astype(LOW)

            each(2, feed_half)
            part = mm_nt(b_v[0, q, :], up_v[0]) + mm_nt(b_v[1, q, :], up_v[1])
            send_v[0, q, :] = part.astype(LOW)
            exchange(2, i).start()

        each(tiles, feed_rows)
        copying("act", a_v, act_k).start()
        late_put.wait()
        cot_on.wait_send()
        each(2, lambda i: mem_forward(i, c).wait_send())

    def block_of(k):
        return lax.rem(z - 1 - k + 2 * planes, planes)

    def y_hop(g, k, b):
        i = SUMS.index(g)
        return push(dw[g].at[k, b], yb[g].at[k, b], y_sent.at[i, k, b], y_got.at[i, k, b], at.across)

    def z_hop(g, k, b):
        i = SUMS.index(g)
        return push(dw[g].at[k, b], zb[g].at[k, b], z_sent.at[i, k, b], z_got.at[i, k, b], at.above)

    def leave(g, k):
        @pl.when(other)
        def _():
            for b in range(2):
                y_hop(g, k, b).start()

    def emit(g, compute):
        columns = dw[g].shape[3]

        def put(k, s):
            return pltpu.make_async_copy(dw_st.at[s, :, :, 0:columns], dw[g].at[k], dw_sem.at[s])

        def run(k):
            s = lax.rem(k, 2)
            j = block_of(k)
            compute(s, pl.ds(pl.multiple_of(j * depth, depth), depth))
            put(k, s).start()

            @pl.when(k >= 1)
            def _():
                put(k - 1, 1 - s).wait()
                leave(g, k - 1)

        each(planes, run, "emit_" + g)
        put(planes - 1, (planes - 1) % 2).wait()
        leave(g, planes - 1)

    def home_copy(g, b, section):
        i = SUMS.index(g)
        columns = dw[g].shape[3]
        source = dw[g].at[planes - 1, b]
        if g == "crs":
            source = source.at[:, pl.ds((1 - section) * (columns // 2), columns // 2)]
        device = (section, z, 2 * y + b)
        keeps = both(c == section, r == b)
        return keeps, source, push(source, home[g], home_sent.at[i, b, section if g == "crs" else 0], home_got.at[i], device)

    def sections(g):
        return (0, 1) if g == "crs" else (r,)

    def sum_at(g, n):
        i = SUMS.index(g)
        columns = dw[g].shape[3]
        k, b = lax.div(n, 2), lax.rem(n, 2)

        def fetch(m, source):
            return pltpu.make_async_copy(source, sum_st.at[m, :, 0:columns], sum_sem.at[m])

        @pl.when(relay)
        @jax.named_scope("sum_" + g)
        def _():
            before = lax.max(k - 1, 0)
            y_hop(g, k, b).wait_recv()
            fetch(0, dw[g].at[k, b]).start()
            fetch(1, yb[g].at[k, b]).start()

            @pl.when(k > 0)
            def _():
                z_hop(g, before, b).wait_recv()
                fetch(2, zb[g].at[before, b]).start()
                fetch(2, zb[g].at[before, b]).wait()

            fetch(0, dw[g].at[k, b]).wait()
            fetch(1, yb[g].at[k, b]).wait()
            share = depth // 4

            def add_rows(m):
                q = strip(m, share)
                total = sum_st[0, q, 0:columns].astype(WIDE) + sum_st[1, q, 0:columns].astype(WIDE)
                total = total + jnp.where(k > 0, sum_st[2, q, 0:columns].astype(WIDE), 0.0)
                sum_st[0, q, 0:columns] = total.astype(LOW)

            each(4, add_rows)
            back = pltpu.make_async_copy(sum_st.at[0, :, 0:columns], dw[g].at[k, b], sum_sem.at[0])
            back.start()
            back.wait()

            @pl.when(k + 1 < planes)
            def _():
                z_hop(g, k, b).start()

            @pl.when(k + 1 == planes)
            def _():
                for section in sections(g):
                    keeps, source, copy = home_copy(g, b, section)

                    @pl.when(keeps)
                    def _():
                        pltpu.make_async_copy(source, home[g], home_got.at[i]).start()

                    @pl.when(jnp.logical_not(keeps))
                    def _():
                        copy.start()

    def sums(g, first_step, count):
        each(count, lambda n: sum_at(g, first_step + n), "sums_" + g)

    def turn(source, goal):
        def run(i):
            q = strip(i, BLOCK)
            goal[:, q] = source[q, :].astype(WIDE).T.astype(LOW)

        each(tiles, run, "turn")

    def dm_hop(n, source):
        q = pl.ds(pl.multiple_of((2 * c + n) * BLOCK, BLOCK), BLOCK)
        return push(source.at[q, :], c_v.at[q, :], dm_sent.at[n], dm_got.at[n], at.beside)

    def df_hop(n, core):
        q = pl.ds(pl.multiple_of((2 * core + n) * BLOCK, BLOCK), BLOCK)
        return push(c_v.at[q, :], c_v.at[q, :], df_sent.at[n], df_got.at[n], at.twin)

    @pl.when(at.encodes)
    def _():
        def back_rows(m):
            n = lax.div(m, 2)
            own = lax.rem(m, 2) == 0
            i = jnp.where(own, 2 * c + n, 2 * (1 - c) + n)
            q = strip(i, BLOCK)

            @pl.when(own)
            def _():
                dm_hop(n, c_v).wait_recv()
                df_hop(n, c).start()

            @pl.when(jnp.logical_not(own))
            def _():
                df_hop(n, 1 - c).wait_recv()

            grad = norm_grad(late_v[q, :], g2, c_v[q, :].astype(WIDE), 2, ours(i))
            late_v[q, :] = grad
            low = grad.astype(LOW)
            part = None
            for b in range(2):
                d_pre = (mm(low, dn_v[b]) * b_v[b, q, :].astype(WIDE)).astype(LOW)
                b_v[b, q, :] = d_pre
                term = mm_nt(d_pre, up_v[b])
                part = term if part is None else part + term
            send_v[0, q, :] = part.astype(LOW)

            @pl.when(own)
            def _():
                df_hop(n, c).wait_send()

            c_v[q, :] = low
            exchange(2, i).start()

        each(tiles, back_rows)

    turn(s_v, ta)
    turn(c_v, tb)

    def ffn_block(s, j):
        def ffn_half(b):
            dw_st[s, b, :, 0:768] = mm(ta[j, :], b_v[b]).astype(LOW)
            dw_st[s, b, :, 768:1536] = mm(tb[j, :], a_v[b]).astype(LOW)

        each(2, ffn_half)

    emit("ffn", ffn_block)

    @pl.when(at.decodes)
    def _():
        copying("act", a_v, act_k).wait()
        packed = copying("pc", pc_k, packed_v)
        small = [copying("oc", oc_k, o_v), copying("lsec", lsec_k, lse_v), copying("second", second_k, s_v)]
        packed.start()
        for copy in small:
            copy.start()

        def late_rows(i):
            q = strip(i, BLOCK)
            grad = c_v[q, :].astype(WIDE) + norm_grad(late_v[q, :], g2, joined(2, i), 2, ours(i))
            late_v[q, :] = grad
            g_v[q, :] = grad.astype(LOW)

        each(tiles, late_rows)

        def cross_out(i):
            q = strip(i, BLOCK)
            for b in range(2):
                do_v[b, q, :] = mm(g_v[q, :], crs_v[b, :, 128:384]).astype(LOW)

        each(tiles, cross_out)
        for copy in small:
            copy.wait()
        packed.wait()
        b_v[...] = jnp.zeros_like(b_v)

        def cross_head(n):
            b = lax.div(n, 3)
            attend_back_block(
                lax.rem(n, 3), a_v.at[b], o_v.at[b], do_v.at[b], b_v.at[b], lse_v, n, bias_cross,
                kx, qx, vx, gx, kt_v, dk_v, dv_v, False,
            )

        each(6, cross_head)
        sent(1)

        def to_memory(q):
            return mm_nt(b_v[0, q, 256:640], crs_v[0, :, 384:768]) + mm_nt(b_v[1, q, 256:640], crs_v[1, :, 384:768])

        def far(n):
            i = 2 * (1 - c) + n
            q = strip(i, BLOCK)
            send_v[1, q, :] = to_memory(q).astype(LOW)
            exchange(3, i).start()

        each(2, far)

        def near(n):
            i = 2 * c + n
            q = strip(i, BLOCK)
            part = to_memory(q)
            exchange(3, i).wait_recv()
            send_v[1, q, :] = (part + recv_v[1, q, :].astype(WIDE)).astype(LOW)
            dm_hop(n, send_v.at[1]).start()

        each(2, near)

        def to_query(i):
            q = strip(i, BLOCK)
            part = mm_nt(b_v[0, q, 0:256], crs_v[0, :, 0:256]) + mm_nt(b_v[1, q, 0:256], crs_v[1, :, 0:256])
            send_v[0, q, :] = part.astype(LOW)
            exchange(4, i).start()

        sent(2)
        each(tiles, to_query)
        sums("ffn", 0, 2)
        turn(s_v, ta)
        stage_in = copying("memory", memory_k, s_v)
        stage_in.start()
        turn(g_v, tc)
        stage_in.wait()
        turn(s_v, tb)
        copying("first", first_k, s_v).start()

        def crs_block(s, j):
            def att_half(b):
                left = mm(ta[j, :], b_v[b, :, 0:256])
                out = mm(tc[j, :], o_v[b])
                dw_st[s, b, :, 0:128] = left[:, 0:128].astype(LOW)
                dw_st[s, b, :, 128:256] = (left[:, 128:256] + out[:, 0:128]).astype(LOW)
                dw_st[s, b, :, 256:384] = out[:, 128:256].astype(LOW)
                dw_st[s, b, :, 384:768] = mm(tb[j, :], b_v[b, :, 256:640]).astype(LOW)

            each(2, att_half)

        emit("crs", crs_block)
        sums("ffn", 2, 2)

        def below(i):
            q = strip(i, BLOCK)
            grad = late_v[q, :] + norm_grad(mid_v[q, :], g1, joined(4, i), 1, ours(i))
            late_v[q, :] = grad
            g_v[q, :] = grad.astype(LOW)

        each(tiles, below)
        copying("first", first_k, s_v).wait()

        def gone(n):
            exchange(3, 2 * (1 - c) + n).wait_send()
            dm_hop(n, send_v.at[1]).wait_send()

        each(2, gone)

    @pl.when(at.encodes)
    def _():
        copying("first", first_k, s_v).start()
        each(2, lambda i: mem_send(i).wait_send())

        def below(i):
            q = strip(i, BLOCK)
            grad = late_v[q, :] + norm_grad(mid_v[q, :], g1, joined(2, i), 1, ours(i))
            late_v[q, :] = grad
            g_v[q, :] = grad.astype(LOW)

        each(tiles, below)
        copying("first", first_k, s_v).wait()
        sent(1)

    packed = copying("p", p_k, packed_v)
    small = [copying("o", o_k, o_v), copying("lse", lse_k, lse_v)]
    packed.start()
    for copy in small:
        copy.start()

    def self_out(i):
        q = strip(i, BLOCK)
        for b in range(2):
            do_v[b, q, :] = mm(g_v[q, :], att_v[b, :, 128:384]).astype(LOW)

    each(tiles, self_out)
    b_v[...] = jnp.zeros_like(b_v)
    for copy in small:
        copy.wait()
    packed.wait()

    def self_heads(causal, hook):
        def self_head(n):
            b = lax.div(n, 3)
            attend_back_block(
                lax.rem(n, 3), a_v.at[b], o_v.at[b], do_v.at[b], b_v.at[b], lse_v, n, bias_self,
                kx, qx, vx, gx, kt_v, dk_v, dv_v, causal,
            )
            hook(n)

        each(6, self_head)

    def enc_hook(n):
        @pl.when(jnp.logical_and(n != 0, n != 3))
        def _():
            sum_at("ffn", n - 1 - lax.div(n, 4))

    def dec_hook(n):
        @pl.when(n < 4)
        def _():
            sum_at("ffn", 4 + n)

        @pl.when(n >= 4)
        def _():
            sum_at("crs", n - 4)

    pl.when(at.encodes)(lambda: self_heads(False, enc_hook))
    pl.when(at.decodes)(lambda: self_heads(True, dec_hook))

    def to_rows(q):
        part = None
        for b in range(2):
            term = mm_nt(b_v[b, q, 0:256], att_v[b, :, 0:256]) + mm_nt(b_v[b, q, 256:640], att_v[b, :, 384:768])
            part = term if part is None else part + term
        return part

    def far_rows(n):
        i = 2 * (1 - c) + n
        q = strip(i, BLOCK)
        send_v[1, q, :] = to_rows(q).astype(LOW)
        exchange(5, i).start()

    each(2, far_rows)
    turn(s_v, ta)
    x_in_v = copying("x", x_k, s_v)
    x_in_v.start()
    turn(g_v, tc)

    def att_block(s, j):
        def att_half(b):
            left = mm(ta[j, :], b_v[b, :, 0:256])
            out = mm(tc[j, :], o_v[b])
            dw_st[s, b, :, 0:128] = left[:, 0:128].astype(LOW)
            dw_st[s, b, :, 128:256] = (left[:, 128:256] + out[:, 0:128]).astype(LOW)
            dw_st[s, b, :, 256:384] = out[:, 128:256].astype(LOW)
            dw_st[s, b, :, 384:768] = mm(ta[j, :], b_v[b, :, 256:640]).astype(LOW)

        each(2, att_half)

    emit("att", att_block)
    pl.when(at.encodes)(lambda: sums("ffn", 4, 2))
    pl.when(at.decodes)(lambda: sums("crs", 2, 2))
    x_in_v.wait()

    def near_rows(n):
        i = 2 * c + n
        q = strip(i, BLOCK)
        part = to_rows(q)
        exchange(5, i).wait_recv()
        grad = part + recv_v[1, q, :].astype(WIDE)
        value = late_v[q, :] + norm_grad(s_v[q, :].astype(WIDE), g0, grad, 0, True)
        out_st[strip(n, BLOCK), :] = value.astype(LOW)

    each(2, near_rows)
    out_put = copying("out", out_st, grad_k)
    out_put.start()
    out_put.wait()

    def grad_home(k):
        return k, grad_k.at[strip(k, rows), :], grad_low, gr_sent, gr_got

    for k in range(2):
        go_home(*grad_home(k))

    def gain_hop(n, source, device):
        return push(source, gain_buf.at[n], gr_hop_sent.at[n], gr_hop_got.at[n], device)

    gain_buf[0] = gain_v[...]
    twin_hop = gain_hop(1, gain_buf.at[0], at.twin)
    twin_hop.start()
    twin_hop.wait()
    peer_hop = gain_hop(3, gain_buf.at[2], (1 - c, z, lax.rem(t + 2, 4)))
    last = 4 + planes

    @pl.when(relay)
    def _():
        gain_buf[2] = gain_buf[0] + gain_buf[1]
        peer_hop.start()

    def ring_hop(n):
        return gain_hop(5 + n, gain_buf.at[4 + n], at.above)

    def gain_step(n):
        @pl.when(relay)
        @jax.named_scope("gains")
        def _():
            if n == 0:
                peer_hop.wait()
                gain_buf[4] = gain_buf[2] + gain_buf[3]
            else:
                ring_hop(n - 1).wait()
            if n < planes - 1:
                ring_hop(n).start()
            else:
                total = None
                for j in range(planes):
                    held = gain_buf[jnp.where(z == j, 4, 5 + lax.rem(z - 1 - j + planes, planes))]
                    total = held if total is None else total + held
                gain_buf[last] = total
                for b in range(2):
                    keeps = both(c == r, r == b)

                    @pl.when(keeps)
                    def _():
                        pltpu.make_async_copy(gain_buf.at[last], gain_buf.at[last + 1], gr_hop_got.at[last + 1]).start()

                    @pl.when(jnp.logical_not(keeps))
                    def _():
                        final_hop(b).start()

    def final_hop(b):
        return push(
            gain_buf.at[last], gain_buf.at[last + 1], gr_hop_sent.at[last + b], gr_hop_got.at[last + 1],
            (r, z, 2 * y + b),
        )

    def y3_home(k):
        return k, y3_k.at[strip(k, rows), :], block_out, blk_sent, blk_got

    @pl.when(at.decodes)
    def _():
        copies = [copying("act", act_k, a_v), copying("late", late_k, mid_v)]
        for copy in copies:
            copy.start()
        sent(4)
        for copy in copies:
            copy.wait()

        def to_out(q):
            return mm_nt(a_v[0, q, :], dn_v[0]) + mm_nt(a_v[1, q, :], dn_v[1])

        def far_out(n):
            i = 2 * (1 - c) + n
            q = strip(i, BLOCK)
            send_v[0, q, :] = to_out(q).astype(LOW)
            exchange(6, i).start()

        each(2, far_out)

        def near_out(n):
            i = 2 * c + n
            q = strip(i, BLOCK)
            part = to_out(q)
            exchange(6, i).wait_recv()
            out_st[strip(n, BLOCK), :] = (mid_v[q, :] + part + recv_v[0, q, :].astype(WIDE)).astype(LOW)

        each(2, near_out)
        y3_put = copying("out", out_st, y3_k)
        y3_put.start()
        y3_put.wait()
        for k in range(2):
            go_home(*y3_home(k))

    pl.when(at.encodes)(lambda: sums("ffn", 6, 2))
    pl.when(at.decodes)(lambda: sums("crs", 4, 4))

    def last_sums(n):
        sum_at("att", n)
        for m in range(planes):
            pl.when(n == m)(functools.partial(gain_step, m))

    each(2 * planes, last_sums)

    with jax.named_scope("await_gains"):
        final = gain_buf.at[last + 1]
        push(gain_buf.at[last], final, gr_hop_sent.at[last], gr_hop_got.at[last + 1], at.twin).wait_recv()
    gains_home = copying("gains", final, gain_out)
    gains_home.start()
    with jax.named_scope("await_rows"):
        for n in range(2):
            for goal, got in ((block_out, blk_got), (grad_low, gr_got)):
                push(goal.at[n], goal.at[n], blk_sent.at[0], got.at[n], at.twin).wait_recv()
    for i, g in enumerate(SUMS):
        with jax.named_scope("await_home_" + g):
            push(home[g], home[g], home_sent.at[i, 0, 0], home_got.at[i], at.twin).wait_recv()
    gains_home.wait()
    for k in range(2):
        went_home(*grad_home(k))

    @pl.when(at.encodes)
    def _():
        for k in range(2):
            went_home(*memory_home(k))
        sent(2)

    @pl.when(at.decodes)
    def _():
        for k in range(2):
            went_home(*y3_home(k))
        each(2, lambda n: exchange(6, 2 * (1 - c) + n).wait_send())

    each(2, lambda n: exchange(5, 2 * (1 - c) + n).wait_send())

    @pl.when(relay)
    def _():
        for b in range(2):
            pl.when(jnp.logical_not(both(c == r, r == b)))(lambda: final_hop(b).wait_send())

    for g in SUMS:
        there = at.decodes if g == "crs" else jnp.logical_or(at.decodes, at.encodes)

        @pl.when(both(other, there))
        def _():
            for k in range(planes):
                for b in range(2):
                    y_hop(g, k, b).wait_send()

        @pl.when(both(relay, there))
        def _():
            for b in range(2):
                for k in range(planes - 1):
                    z_hop(g, k, b).wait_send()
                for section in sections(g):
                    keeps, source, copy = home_copy(g, b, section)

                    @pl.when(jnp.logical_not(keeps))
                    def _():
                        copy.wait_send()

    gain_copy.wait_send()
    for g in DIRECT:
        launch_over(g).wait_send()

    @pl.when(jnp.logical_not(stays))
    def _():
        for g in ("att", "up", "dn"):
            push(shard[g], vmem[g].at[r, here, :], x_sent.at[GROUPS.index(g)], x_sem.at[0, 0], relay_dev).wait_send()

    @pl.when(jnp.logical_not(crs_stays))
    def _():
        push(crs_in, crs_goal(r, c), x_sent.at[1], c_sem.at[0, 0], crs_dev).wait_send()
        push(cot_in.at[c], cot_goal, row_sent.at[2], cot_got.at[r], at.twin).wait_send()

    for s in range(2):

        @pl.when(jnp.logical_not(row_stays(s)))
        def _():
            push(x_in.at[s], row_goal, row_sent.at[s], row_got.at[r], at.twin).wait_send()

    for g in GROUPS:
        member = both(relay, at.decodes) if g == "crs" else relay

        @pl.when(member)
        def _():
            for k in range(planes):
                for b in range(2):
                    if k:
                        ring(g, k, b).wait_send()
                    if (k or g not in DIRECT) and (k != 1 or (g, b) not in ASIDE):
                        cross_over(g, k, b).wait_send()

    @pl.when(other)
    def _():
        for g, b in ASIDE:
            side_hop(g, b).wait_send()


def block_call(planes, slot, width, hidden, depth, args):
    shape = jax.ShapeDtypeStruct
    rows = slot // 4
    square = (slot, width)
    wides = {"ffn": 2 * hidden, "crs": width, "att": width}
    packed, outs, logs, acts = (2, slot, 640), (2, slot, 256), (8, slot), (2, slot, hidden)
    out_shape = (
        [shape((2, rows, width), LOW)] * 2
        + [shape((depth, 2 * hidden), LOW), shape((depth, width // 2), LOW), shape((depth, width), LOW)]
        + [shape((8, width), WIDE)]
        + [shape(square, LOW)] * 4
        + [shape(square, WIDE), shape(square, LOW)]
        + [shape(packed, LOW), shape(outs, LOW), shape(logs, WIDE)] * 2
        + [shape(acts, LOW)]
        + [shape((2 * rows, width), LOW)] * 2
        + [shape((planes, 2, depth, wides[g]), LOW) for g in SUMS] * 3
    )
    dma = pltpu.SemaphoreType.DMA
    v = pltpu.VMEM
    groups = len(GROUPS)
    scratch = (
        [v((2, width, width), LOW)] * 2
        + [v((2, width, hidden), LOW)] * 2
        + [v(acts, LOW)] * 2
        + [v(outs, LOW)] * 2
        + [v(square, WIDE)] * 2
        + [v(square, LOW)] * 3
        + [v((width, slot), LOW)] * 3
        + [v((2,) + square, LOW)] * 2
        + [v((slot, TILE), LOW)] * 4
        + [v((slot, TILE), WIDE)] * 2
        + [v((TILE, slot), LOW), v(logs, WIDE), v((8, width), WIDE), v((2, 3, width), LOW)]
        + [v((planes + 6, 8, width), WIDE)]
        + [v((2 * rows, width), LOW), v((2, 2, depth, 2 * hidden), LOW), v((3, depth, 2 * hidden), LOW)]
        + [v((slot, TILE), LOW)] * 2
        + [dma((groups, 2)), dma((groups,)), dma((groups,)), dma((2, 2))]
        + [dma((groups, planes, 2))] * 4
        + [dma((groups, 2))] * 2
        + [dma((2,)), dma((3,)), dma((4,)), dma((2,)), dma((3,)), dma((40,)), dma((7, 4)), dma((7, 4))]
        + [dma((2,))] * 8
        + [dma((3, planes, 2))] * 4
        + [dma((3,)), dma((3, 2, 2))]
        + [dma((2,))] * 4
        + [dma((planes + 6,))] * 2
        + [dma((3,)), dma((2,))]
    )
    any_spec = pl.BlockSpec(memory_space=pl.ANY)
    vmem_spec = pl.BlockSpec(memory_space=pltpu.VMEM)
    return pl.pallas_call(
        functools.partial(block_kernel, planes),
        out_shape=out_shape,
        in_specs=[any_spec] * 6 + [vmem_spec, pl.BlockSpec(memory_space=pltpu.SMEM), vmem_spec],
        out_specs=[any_spec] * len(out_shape),
        scratch_shapes=scratch,
        compiler_params=pltpu.CompilerParams(collective_id=0, has_side_effects=True, vmem_limit_bytes=VMEM_BYTES),
    )(*args)


def widen_kernel(
    block_in, grad_in, ffn_in, crs_in, att_in, gain_in,
    block_out, grad_out, up_out, dn_out, qkv_out, out_out, crs_out, gain_out, last_out,
):
    c = lax.axis_index("section")
    hidden = up_out.shape[1]
    share, part = block_in.shape[1] // 4, ffn_in.shape[0] // 4

    def strips(i):
        q = strip(i, share)
        for n in range(2):
            block_out[n, q, :] = block_in[n, q, :]
            grad_out[n, q, :] = grad_in[n, q, :].astype(WIDE)
        q = strip(i, part)
        up_out[q, :] = ffn_in[q, 0:hidden].astype(WIDE)
        dn_out[q, :] = ffn_in[q, hidden : 2 * hidden].astype(WIDE)

    each(4, strips)
    tiles = [crs_in[:, TILE * n : TILE * (n + 1)].astype(WIDE) for n in range(3)]
    mixed = jnp.where(c == 1, tiles[1], tiles[2])
    crs_out[0, :, 0:TILE] = tiles[0]
    crs_out[0, :, TILE : TILE + HEAD] = mixed[:, 0:HEAD]
    crs_out[1, :, 0:TILE] = jnp.where(c == 1, tiles[2], tiles[1])
    crs_out[1, :, TILE : TILE + HEAD] = pltpu.roll(mixed, HEAD, 1)[:, 0:HEAD]
    q_tile, q_o, o_tile, k_tile, v_tile, k_v = (att_in[:, TILE * n : TILE * (n + 1)].astype(WIDE) for n in range(6))
    for n, (whole, rest) in enumerate(((q_tile, q_o), (k_tile, k_v), (v_tile, pltpu.roll(k_v, HEAD, 1)))):
        qkv_out[n, :, 0:TILE] = whole
        qkv_out[n, :, TILE : TILE + HEAD] = rest[:, 0:HEAD]
    out_out[0:TILE, :] = o_tile.T
    out_out[TILE : TILE + HEAD, :] = pltpu.roll(q_o, HEAD, 1).T[0:HEAD, :]
    gain_out[...] = gain_in[0:2, :]
    last_out[...] = gain_in[2:3, :]


def widen_call(kept):
    shape = jax.ShapeDtypeStruct
    rows, width = kept[0].shape[1:]
    depth, hidden = kept[2].shape[0], kept[2].shape[1] // 2
    wide = width // 4
    return pl.pallas_call(
        widen_kernel,
        out_shape=[
            shape((2, rows, width), LOW), shape((2, rows, width), WIDE), shape((depth, hidden), WIDE),
            shape((depth, hidden), WIDE), shape((3, depth, wide), WIDE), shape((wide, depth), WIDE),
            shape((2, depth, wide), WIDE), shape((2, width), WIDE), shape((1, width), WIDE),
        ],
    )(*kept)


def ring_gather(lay, shard):
    planes = lay.planes
    rows = shard.shape[1]
    if planes > 4:
        piece = lax.all_gather(shard, "dp", axis=1, tiled=True)
        across = lay.route(piece, lambda c, z, t: (c, z, (t + 2) % 4) if c == t // 2 else None)
        return jnp.where(lay.relays, piece, across)
    relay = lambda c, z, t: (c, (z + 1) % planes, t) if c == t // 2 else None
    whole = jnp.zeros((shard.shape[0], planes * rows, shard.shape[2]), shard.dtype)
    piece = shard
    for step in range(planes):
        across = lay.route(piece, lambda c, z, t: (c, z, (t + 2) % 4) if c == t // 2 else None)
        chosen = jnp.where(lay.relays, piece, across)
        whole = lax.dynamic_update_slice(whole, chosen, (0, ((lay.plane - step) % planes) * rows, 0))
        if step + 1 < planes:
            piece = lay.route(piece, relay)
    return whole


def ring_scatter(lay, total, holder):
    planes = lay.planes
    rows = total.shape[1] // planes
    low = total.astype(LOW)
    across = lay.route(
        low, lambda c, z, t: (c, z, (t + 2) % 4) if (c != t // 2 and t % 2 == holder) else None
    )
    summed = low.astype(WIDE) + across.astype(WIDE)
    if planes > 4:
        return lax.psum_scatter(summed.astype(LOW), "dp", scatter_dimension=1, tiled=True)
    relay = lambda c, z, t: (c, (z + 1) % planes, t) if (c == t // 2 and t % 2 == holder) else None
    take = lambda j: lax.dynamic_slice_in_dim(summed, (j % planes) * rows, rows, 1)
    running = take(lay.plane - 1)
    for step in range(1, planes):
        running = lay.route(running.astype(LOW), relay).astype(WIDE) + take(lay.plane - 1 - step)
    return running.astype(LOW)


def hand_back(lay, value, holder, section):
    same = lay.route(
        value[0], lambda c, z, t: (section, z, t) if (c == t // 2 and t % 2 == holder) else None
    )
    beside = lay.route(
        value[1], lambda c, z, t: (section, z, t ^ 1) if (c == t // 2 and t % 2 == holder) else None
    )
    return same.astype(WIDE) + beside.astype(WIDE)


def general_body(block_input, w_self, w_self_out, w_cross, w_up, w_down, norm_gains, lengths, task_mask, out_grad):
    lay = Layout()
    seqs, rows, width = block_input.shape[1:]
    slot = rows * lay.chips
    sec = lay.core
    item = lay.item

    def spread(value, first):
        pick = value[jnp.where(first, lay.chip % 2, 1 - lay.chip % 2)]
        flip = 0 if first else 1
        return lay.route(pick, lambda c, z, t: (t // 2, z, 2 * ((t % 2) ^ flip) + c))

    def merge_rows(mine, theirs):
        low_half = jnp.where(lay.core == 0, mine, theirs)
        high_half = jnp.where(lay.core == 0, theirs, mine)
        return jnp.concatenate([low_half[0], low_half[1], high_half[0], high_half[1]], axis=0)

    first = spread(block_input[0], True)
    second = spread(block_input[0], False)
    mine = jnp.where(item == 0, jnp.stack([first, second]), jnp.stack([second, first]))
    x_rows = merge_rows(mine, lay.other_core(mine)).astype(WIDE)

    picked = out_grad[lay.core]
    even = lay.route(picked, lambda c, z, t: (t // 2, z, 2 * c + 1) if t % 2 == 0 else None)
    odd = lay.route(picked, lambda c, z, t: (t // 2, z, 2 * c + 1) if t % 2 == 1 else None)
    mine = jnp.stack([even, odd])
    cotangent = merge_rows(mine, lay.other_core(mine))

    gains_here = norm_gains[0].astype(WIDE)
    gains = jnp.where(sec == lay.role, gains_here, lay.other_core(norm_gains[0]).astype(WIDE))

    depth = w_self.shape[1]
    wide = w_self.shape[3]
    self_block = pack_heads(
        {"q": w_self[0, :, 0], "k": w_self[0, :, 1], "v": w_self[0, :, 2], "o": w_self_out[0].T}
    )
    feed_block = jnp.concatenate([w_up[0], w_down[0].T], axis=1)
    cross_block = w_cross[0].reshape(depth, 2 * wide)

    def collect(block):
        same = lay.route(block, lambda c, z, t: (t // 2, z, t) if c == t % 2 else None)
        beside = lay.route(block, lambda c, z, t: (t // 2, z, t ^ 1) if c != t % 2 else None)
        return jnp.stack([same, beside])

    def collect_cross(block, section):
        same = lay.route(block, lambda c, z, t: (t // 2, z, t) if (c == section and t % 2 == 1) else None)
        beside = lay.route(block, lambda c, z, t: (t // 2, z, t ^ 1) if (c == section and t % 2 == 0) else None)
        return same, beside

    w_att = ring_gather(lay, collect(self_block))
    w_ffn = ring_gather(lay, collect(feed_block))
    memory_side = collect_cross(cross_block, 0)
    query_side = collect_cross(cross_block, 1)
    w_crs = ring_gather(
        lay,
        jnp.stack(
            [
                pack_heads({"q": q[:, :wide], "k": m[:, :wide], "v": m[:, wide:], "o": q[:, wide:]})
                for m, q in zip(memory_side, query_side)
            ]
        ),
    )
    hidden = w_up.shape[2]
    part = lambda w, name: jnp.concatenate([unpack_heads(w[0], name), unpack_heads(w[1], name)], axis=1)
    att = {n: part(w_att, n) for n in "qkvo"}
    crs = {n: part(w_crs, n) for n in "qkvo"}
    up = jnp.concatenate([w_ffn[0, :, :hidden], w_ffn[1, :, :hidden]], axis=1)
    down_t = jnp.concatenate([w_ffn[0, :, hidden:], w_ffn[1, :, hidden:]], axis=1)

    positions = jnp.arange(slot)
    own_length = jnp.where(lay.is_decoder, lengths[1, item], lengths[0, item])
    self_allowed = (positions[None, :] < own_length) & (
        (positions[None, :] <= positions[:, None]) | jnp.logical_not(lay.is_decoder)
    )
    cross_allowed = jnp.broadcast_to(
        ((positions < lengths[0, item]) & (task_mask[item] == 1))[None], (slot, slot)
    )

    def joined(partial):
        low = partial.astype(LOW)
        return low.astype(WIDE) + lay.other_core(low).astype(WIDE)

    normed0 = layer_norm(x_rows, gains[0]).astype(LOW)
    q, k, v = (mm(normed0, att[n]).astype(LOW) for n in "qkv")
    out_self, lse_self = attend(q, k, v, self_allowed)
    x_mid = x_rows + joined(mm_nt(out_self, att["o"]))
    normed1 = layer_norm(x_mid, gains[1]).astype(LOW)

    pre_enc = mm(normed1, up)
    act_enc, slope_enc = gelu_parts(pre_enc)
    act_enc = act_enc.astype(LOW)
    x_late_enc = x_mid + joined(mm_nt(act_enc, down_t))
    memory_enc = layer_norm(x_late_enc, gains[2]).astype(LOW)
    memory = lay.route(memory_enc, lambda c, z, t: (c, z, t ^ 1) if t % 2 == 0 else None)

    cq = mm(normed1, crs["q"]).astype(LOW)
    ck, cv = (mm(memory, crs[n]).astype(LOW) for n in "kv")
    out_cross, lse_cross = attend(cq, ck, cv, cross_allowed)
    x_late = x_mid + joined(mm_nt(out_cross, crs["o"]))
    normed2 = layer_norm(x_late, gains[2]).astype(LOW)
    pre_dec = mm(normed2, up)
    act_dec, slope_dec = gelu_parts(pre_dec)
    act_dec = act_dec.astype(LOW)
    result_dec = (x_late + joined(mm_nt(act_dec, down_t))).astype(LOW)

    d_out = cotangent.astype(WIDE)
    d_pre = (slope_dec * mm(cotangent, down_t)).astype(LOW)
    d_ffn_dec = jnp.concatenate([mm_tn(normed2, d_pre), mm_tn(cotangent, act_dec)], axis=1)
    d_late_norm, d_gain2_dec = norm_back(x_late, gains[2], joined(mm_nt(d_pre, up)))
    d_late = d_out + d_late_norm
    grad_late = d_late.astype(LOW)
    d_att = mm(grad_late, crs["o"]).astype(LOW)
    d_cq, d_ck, d_cv = attend_back(cq, ck, cv, lse_cross, d_att, cross_allowed)
    d_memory = joined(mm_nt(d_ck, crs["k"]) + mm_nt(d_cv, crs["v"]))
    d_crs = {
        "q": mm_tn(normed1, d_cq),
        "k": mm_tn(memory, d_ck),
        "v": mm_tn(memory, d_cv),
        "o": mm_tn(grad_late, out_cross),
    }
    d_mid_norm, d_gain1_dec = norm_back(x_mid, gains[1], joined(mm_nt(d_cq, crs["q"])))
    d_mid_dec = d_late + d_mid_norm

    d_memory = lay.route(d_memory.astype(LOW), lambda c, z, t: (c, z, t ^ 1) if t % 2 == 1 else None).astype(WIDE)
    d_late_enc, d_gain2_enc = norm_back(x_late_enc, gains[2], d_memory)
    grad_late_enc = d_late_enc.astype(LOW)
    d_pre = (slope_enc * mm(grad_late_enc, down_t)).astype(LOW)
    d_ffn_enc = jnp.concatenate([mm_tn(normed1, d_pre), mm_tn(grad_late_enc, act_enc)], axis=1)
    d_mid_norm, d_gain1_enc = norm_back(x_mid, gains[1], joined(mm_nt(d_pre, up)))
    d_mid_enc = d_late_enc + d_mid_norm

    d_mid = jnp.where(lay.is_decoder, d_mid_dec, d_mid_enc)
    grad_mid = d_mid.astype(LOW)
    d_att = mm(grad_mid, att["o"]).astype(LOW)
    d_q, d_k, d_v = attend_back(q, k, v, lse_self, d_att, self_allowed)
    d_norm = joined(mm_nt(d_q, att["q"]) + mm_nt(d_k, att["k"]) + mm_nt(d_v, att["v"]))
    d_att_w = {
        "q": mm_tn(normed0, d_q),
        "k": mm_tn(normed0, d_k),
        "v": mm_tn(normed0, d_v),
        "o": mm_tn(grad_mid, out_self),
    }
    d_first, d_gain0 = norm_back(x_rows, gains[0], d_norm)
    d_rows = d_mid + d_first

    half = 3 * HEAD

    def blocks(parts):
        return jnp.stack(
            [pack_heads({n: parts[n][:, half * b : half * (b + 1)] for n in parts}) for b in range(2)]
        )

    def feed_blocks(both):
        total = both.shape[1] // 2
        return jnp.stack(
            [
                jnp.concatenate(
                    [both[:, hidden * b : hidden * (b + 1)], both[:, total + hidden * b : total + hidden * (b + 1)]],
                    axis=1,
                )
                for b in range(2)
            ]
        )

    self_total = blocks(d_att_w)
    home_self = hand_back(lay, ring_scatter(lay, self_total, 0), 0, 0) + hand_back(
        lay, ring_scatter(lay, self_total, 1), 1, 1
    )
    home_feed = hand_back(lay, ring_scatter(lay, feed_blocks(d_ffn_enc), 0), 0, 0) + hand_back(
        lay, ring_scatter(lay, feed_blocks(d_ffn_dec), 1), 1, 1
    )
    cross_total = ring_scatter(lay, blocks(d_crs), 1)
    side = lambda names: jnp.stack(
        [jnp.concatenate([unpack_heads(cross_total[b], n) for n in names], axis=1) for b in range(2)]
    )
    home_cross = hand_back(lay, side("kv"), 1, 0) + hand_back(lay, side("qo"), 1, 1)

    g_self = jnp.stack([unpack_heads(home_self, n) for n in "qkv"], axis=1)[None]
    g_self_out = unpack_heads(home_self, "o").T[None]
    g_cross = home_cross.reshape(1, depth, 2, wide)
    g_up = home_feed[:, :hidden][None]
    g_down = home_feed[:, hidden:].T[None]

    gain2 = jnp.where(lay.is_decoder, d_gain2_dec, d_gain2_enc)
    gain1 = jnp.where(lay.is_decoder, d_gain1_dec, d_gain1_enc)
    gain_rows = jnp.stack([d_gain0, gain1, gain2])
    slots = jnp.stack(
        [
            jnp.where((lay.role == r) & (lay.core == 0), gain_rows, 0.0)
            for r in range(2)
        ]
    )
    gain_total = lax.psum(slots, AXES)[sec][None]

    def rows_home(value):
        mine = lax.dynamic_slice_in_dim(value, lay.core * 2 * rows, 2 * rows, 0).reshape(2, rows, width)
        a = lay.route(mine[item], lambda c, z, t: (t % 2, z, 2 * c + t // 2))
        b = lay.route(mine[1 - item], lambda c, z, t: (t % 2, z, 2 * c + 1 - t // 2))
        even = lay.chip % 2 == 0
        return jnp.where(even, jnp.stack([a, b]), jnp.stack([b, a]))[None]

    block_output = rows_home(jnp.where(lay.is_decoder, result_dec, memory_enc))
    input_grad = rows_home(d_rows.astype(LOW)).astype(WIDE)
    return (
        block_output,
        input_grad,
        g_self,
        g_self_out,
        g_cross,
        g_up,
        g_down,
        gain_total[:, :2],
        gain_total[:, 2],
    )


def body(block_input, w_self, w_self_out, w_cross, w_up, w_down, norm_gains, lengths, task_mask, out_grad):
    lay = Layout()
    seqs, rows, width = block_input.shape[1:]
    slot = rows * lay.chips
    sec = lay.core
    item = lay.item

    if lay.planes != 4:
        return general_body(
            block_input, w_self, w_self_out, w_cross, w_up, w_down, norm_gains, lengths, task_mask, out_grad
        )

    depth = w_self.shape[1]
    wide = w_self.shape[3]
    hidden = w_up.shape[2]
    self_block = pack_heads(
        {"q": w_self[0, :, 0], "k": w_self[0, :, 1], "v": w_self[0, :, 2], "o": w_self_out[0].T}
    )
    pair = {"q": w_cross[0, :, 0], "o": w_cross[0, :, 1], "k": w_cross[0, :, 0], "v": w_cross[0, :, 1]}
    pieces = [pair[n][:, HEAD * h : HEAD * (h + 1)] for n, h in ORDER]
    cross_block = jnp.where(
        sec == 1, jnp.concatenate(pieces[:6], axis=1), jnp.concatenate(pieces[6:], axis=1)
    )
    kept = block_call(
        lay.planes,
        slot,
        width,
        hidden,
        depth,
        (self_block, cross_block, w_up[0], w_down[0].T, block_input[0], out_grad, norm_gains[0], lengths, task_mask),
    )[:6]
    block_output, input_grad, g_up, g_down, g_qkv, g_out, g_cross, g_gain, g_last = widen_call(kept)
    return (
        block_output[None],
        input_grad[None],
        jnp.swapaxes(g_qkv, 0, 1)[None],
        g_out[None],
        jnp.swapaxes(g_cross, 0, 1)[None],
        g_up[None],
        g_down.T[None],
        g_gain[None],
        g_last,
    )


def solution(mesh):
    placed = (
        P("section", "dp", "tensor", None),
        P("section", "dp", None, "tensor"),
        P("section", "tensor", "dp"),
        P("section", "dp", None, "tensor"),
        P("section", "dp", "tensor"),
        P("section", "tensor", "dp"),
        P("section", None, None),
        P(None, "dp"),
        P("dp", None),
        P("dp", "tensor", None),
    )
    return jax.shard_map(
        body,
        mesh=mesh,
        in_specs=placed,
        out_specs=(
            P("section", "dp", "tensor", None),
            P("section", "dp", "tensor", None),
            P("section", "dp", None, "tensor"),
            P("section", "tensor", "dp"),
            P("section", "dp", None, "tensor"),
            P("section", "dp", "tensor"),
            P("section", "tensor", "dp"),
            P("section", None, None),
            P("section", None),
        ),
        check_vma=False,
    )
```

```python
import functools

import jax
import jax.numpy as jnp
from jax import lax
from jax.experimental import pallas as pl
from jax.experimental.pallas import tpu as pltpu
from jax.sharding import PartitionSpec as P

HEAD = 64
TILE = 128
EPSILON = 1e-05
SCORE_SCALE = 0.125
NEG_FILL = -1000000000.0
AXES = ("section", "dp", "tensor")
LOW = jnp.bfloat16
WIDE = jnp.float32


class Layout:
    def __init__(self):
        self.cores = lax.axis_size("section")
        self.planes = lax.axis_size("dp")
        self.chips = lax.axis_size("tensor")
        self.core = lax.axis_index("section")
        self.plane = lax.axis_index("dp")
        self.chip = lax.axis_index("tensor")
        self.role = self.chip % 2
        self.item = self.chip // 2
        self.is_decoder = self.role == 1
        self.relays = self.core == self.item

    def route(self, value, target):
        pairs = []
        for core in range(self.cores):
            for plane in range(self.planes):
                for chip in range(self.chips):
                    to = target(core, plane, chip)
                    if to is None:
                        continue
                    source = (core * self.planes + plane) * self.chips + chip
                    goal = (to[0] * self.planes + to[1]) * self.chips + to[2]
                    pairs.append((source, goal))
        return lax.ppermute(value, AXES, pairs)

    def other_core(self, value):
        return self.route(value, lambda c, z, t: (1 - c, z, t))


def normalize(values):
    centred = values - jnp.mean(values, axis=-1, keepdims=True)
    spread = jnp.mean(centred * centred, axis=-1, keepdims=True)
    scale = lax.rsqrt(spread + EPSILON)
    return centred * scale, scale


def layer_norm(values, gain):
    return normalize(values)[0] * gain


def norm_back(values, gain, grad):
    normal, scale = normalize(values)
    scaled = grad * gain
    first = jnp.mean(scaled, axis=-1, keepdims=True)
    second = jnp.mean(scaled * normal, axis=-1, keepdims=True)
    return (scaled - first - normal * second) * scale, jnp.sum(grad * normal, axis=0)


ORDER = (("q", 0), ("q", 1), ("q", 2), ("o", 2), ("o", 0), ("o", 1), ("k", 0), ("k", 1), ("v", 0), ("v", 1), ("k", 2), ("v", 2))


def pack_heads(parts):
    return jnp.concatenate([parts[n][:, HEAD * h : HEAD * (h + 1)] for n, h in ORDER], axis=1)


def unpack_heads(block, name):
    where = {(n, h): i for i, (n, h) in enumerate(ORDER)}
    return jnp.concatenate(
        [block[:, HEAD * where[(name, h)] : HEAD * (where[(name, h)] + 1)] for h in range(3)], axis=1
    )


def mm(left, right):
    return jnp.dot(left, right, preferred_element_type=WIDE)


def mm_nt(left, right):
    return lax.dot_general(left, right, (((1,), (1,)), ((), ())), preferred_element_type=WIDE)


def mm_tn(left, right):
    return lax.dot_general(left, right, (((0,), (0,)), ((), ())), preferred_element_type=WIDE)


def split_heads(value):
    return value.reshape(value.shape[0], -1, HEAD)


def attend(q, k, v, allowed):
    scores = jnp.einsum("qhd,khd->hqk", split_heads(q), split_heads(k), preferred_element_type=WIDE) * SCORE_SCALE
    scores = jnp.where(allowed[None], scores, NEG_FILL)
    top = jnp.max(scores, axis=-1, keepdims=True)
    power = jnp.exp(scores - top)
    total = jnp.sum(power, axis=-1, keepdims=True)
    probs = (power / total).astype(LOW)
    out = jnp.einsum("hqk,khd->qhd", probs, split_heads(v), preferred_element_type=WIDE)
    return out.astype(LOW).reshape(q.shape), top + jnp.log(total)


def attend_back(q, k, v, log_sum, d_out, allowed):
    scores = jnp.einsum("qhd,khd->hqk", split_heads(q), split_heads(k), preferred_element_type=WIDE) * SCORE_SCALE
    scores = jnp.where(allowed[None], scores, NEG_FILL)
    probs = jnp.exp(scores - log_sum)
    d_probs = jnp.einsum("qhd,khd->hqk", split_heads(d_out), split_heads(v), preferred_element_type=WIDE)
    inner = jnp.sum(probs * d_probs, axis=-1, keepdims=True)
    d_scores = (probs * (d_probs - inner)).astype(LOW)
    d_v = jnp.einsum("hqk,qhd->khd", probs.astype(LOW), split_heads(d_out), preferred_element_type=WIDE)
    d_q = jnp.einsum("hqk,khd->qhd", d_scores, split_heads(k), preferred_element_type=WIDE) * SCORE_SCALE
    d_k = jnp.einsum("hqk,qhd->khd", d_scores, split_heads(q), preferred_element_type=WIDE) * SCORE_SCALE
    return tuple(g.astype(LOW).reshape(q.shape) for g in (d_q, d_k, d_v))


def gelu_parts(value):
    coef = 0.7978845608028654
    cube = 0.044715
    inner = coef * (value + cube * value * value * value)
    soft = jnp.tanh(inner)
    slope = 0.5 * (1.0 + soft) + 0.5 * value * (1.0 - soft * soft) * coef * (1.0 + 3.0 * cube * value * value)
    return 0.5 * value * (1.0 + soft), slope


MESH = pl.DeviceIdType.MESH
GROUPS = ("att", "crs", "up", "dn")
BLOCK = 256
VMEM_BYTES = 62 * 2**20


def lanes(shape):
    return lax.broadcasted_iota(jnp.int32, shape, len(shape) - 1)


def subs(shape):
    return lax.broadcasted_iota(jnp.int32, shape, 0)


def strip(i, size):
    return pl.ds(pl.multiple_of(i * size, size), size)


def head_place(h):
    two = (h == 2).astype(jnp.int32)
    one = (h >= 1).astype(jnp.int32)
    return two, 2 + 2 * two, 3 + two, 1 - two, HEAD * (one - two), HEAD * one


def each(count, step, name=None):
    def run(i, carry):
        step(i)
        return carry

    with jax.named_scope(name or step.__name__):
        lax.fori_loop(0, count, run, 0)


class Place:
    def __init__(self, planes):
        self.planes = planes
        self.c = lax.axis_index("section")
        self.z = lax.axis_index("dp")
        self.t = lax.axis_index("tensor")
        self.y = lax.div(self.t, 2)
        self.r = lax.rem(self.t, 2)
        self.twin = (1 - self.c, self.z, self.t)
        self.above = (self.c, lax.rem(self.z + 1, planes), self.t)
        self.below = (self.c, lax.rem(self.z + planes - 1, planes), self.t)
        self.across = (self.c, self.z, lax.rem(self.t + 2, 4))
        self.beside = (self.c, self.z, self.t + 1 - 2 * self.r)
        self.relays = self.c == self.y
        self.encodes = self.r == 0
        self.decodes = self.r == 1

    def meet(self):
        barrier = pltpu.get_barrier_semaphore()
        peers = [self.above, self.below]
        for dc in range(2):
            for dt in range(4):
                if dc or dt:
                    peers.append((lax.rem(self.c + dc, 2), self.z, lax.rem(self.t + dt, 4)))
        for peer in peers:
            pl.semaphore_signal(barrier, inc=1, device_id=peer, device_id_type=MESH)
        pl.semaphore_wait(barrier, len(peers))


def push(source, goal, sent, got, device):
    return pltpu.make_async_remote_copy(
        src_ref=source, dst_ref=goal, send_sem=sent, recv_sem=got, device_id=device, device_id_type=MESH
    )


def both(first, second):
    return jnp.logical_and(first, second)


def center(values):
    middle = values - jnp.mean(values, axis=-1, keepdims=True)
    scale = lax.rsqrt(jnp.mean(middle * middle, axis=-1, keepdims=True) + EPSILON)
    return middle * scale, scale


def attend_block(h, p, o, lse, lse_row, bias, kx, qx, vt, causal):
    count = p.shape[0]
    qt, kt, vtile, ot, qlo, vlo = head_place(h)
    lane = lanes((count, TILE))
    in_q = both(lane >= qlo, lane < qlo + HEAD)
    in_v = both(lane >= vlo, lane < vlo + HEAD)
    spare = HEAD - qlo
    kx[...] = jnp.where(lane == spare, bias[...], jnp.where(in_q, p[:, strip(kt, TILE)], jnp.zeros((), LOW)))
    vt[...] = jnp.where(in_v, p[:, strip(vtile, TILE)].astype(WIDE), 1.0).T.astype(LOW)
    qx[...] = jnp.where(
        in_q, p[:, strip(qt, TILE)].astype(WIDE) * SCORE_SCALE, jnp.where(lane == spare, 1.0, 0.0)
    ).astype(LOW)
    size = count // 2 if causal else count

    def queries(i):
        q = strip(i, size) if causal else pl.ds(0, count)
        scores = mm_nt(kx[...], qx[q, :])
        if causal:
            scores = jnp.where(subs(scores.shape) <= lanes(scores.shape) + i * size, scores, NEG_FILL)
        top = jnp.max(scores, axis=0, keepdims=True)
        power = jnp.exp(scores - top).astype(LOW)
        out = mm(vt[...], power)
        total = jnp.where(vlo == 0, out[HEAD : HEAD + 1, :], out[0:1, :])
        result = (out / total).T
        lane = lanes((size, TILE))
        in_v = both(lane >= vlo, lane < vlo + HEAD)
        o[q, strip(ot, TILE)] = jnp.where(in_v, result, o[q, strip(ot, TILE)].astype(WIDE)).astype(LOW)
        row = subs((8, size))
        lse[:, q] = jnp.where(row == lse_row, top + jnp.log(total), lse[:, q])

    if causal:
        each(count // size, queries)
    else:
        queries(0)


SUMS = ("ffn", "crs", "att")
DIRECT = ("att", "up")
ASIDE = (("up", 0), ("up", 1), ("dn", 0))


def split_three(value):
    high = value.astype(LOW).astype(WIDE)
    middle = (value - high).astype(LOW).astype(WIDE)
    return high, middle, value - high - middle


def attend_back_block(h, p, o, d_o, d_p, lse, lse_row, bias, kx, qx, vx, gx, kt_v, dk_v, dv_v, causal):
    count = p.shape[0]
    qt, kt, vtile, ot, qlo, vlo = head_place(h)
    lane = lanes((count, TILE))
    in_q = both(lane >= qlo, lane < qlo + HEAD)
    in_v = both(lane >= vlo, lane < vlo + HEAD)
    sq, sv = HEAD - qlo, HEAD - vlo
    keys = jnp.where(
        in_q, p[:, strip(kt, TILE)].astype(WIDE), jnp.where(both(lane > sq, lane < sq + 4), 1.0, 0.0)
    )
    keys = jnp.where(lane == sq, bias[...].astype(WIDE), keys)
    kx[...] = keys.astype(LOW)
    kt_v[...] = keys.T.astype(LOW)
    vx[...] = jnp.where(
        in_v, p[:, strip(vtile, TILE)].astype(WIDE), jnp.where(both(lane >= sv, lane < sv + 3), 1.0, 0.0)
    ).astype(LOW)
    own = jnp.sum(jnp.where(subs((8, count)) == lse_row, lse[...], 0.0), axis=0, keepdims=True)
    a, b, c = split_three(-jnp.broadcast_to(own, (TILE, count)).T)
    extra = jnp.where(
        lane == sq,
        1.0,
        jnp.where(lane == sq + 1, a, jnp.where(lane == sq + 2, b, jnp.where(lane == sq + 3, c, 0.0))),
    )
    qx[...] = jnp.where(in_q, p[:, strip(qt, TILE)].astype(WIDE) * SCORE_SCALE, extra).astype(LOW)
    grad = jnp.where(in_v, d_o[:, strip(ot, TILE)].astype(WIDE), 0.0)
    inner = jnp.sum(grad * o[:, strip(ot, TILE)].astype(WIDE), axis=-1, keepdims=True)
    a, b, c = split_three(-inner)
    gx[...] = (
        grad + jnp.where(lane == sv, a, jnp.where(lane == sv + 1, b, jnp.where(lane == sv + 2, c, 0.0)))
    ).astype(LOW)
    size = count // 2 if causal else count

    def place(q, tile_index, low, value):
        cut = strip(tile_index, TILE)
        lane = lanes(value.shape)
        inside = both(lane >= low, lane < low + HEAD)
        d_p[q, cut] = jnp.where(inside, value, d_p[q, cut].astype(WIDE)).astype(LOW)

    whole = pl.ds(0, count)
    if causal:
        dk_v[...] = jnp.zeros_like(dk_v)
        dv_v[...] = jnp.zeros_like(dv_v)

    def queries(i):
        q = strip(i, size) if causal else pl.ds(0, count)
        scores = mm_nt(kx[...], qx[q, :])
        if causal:
            scores = jnp.where(subs(scores.shape) <= lanes(scores.shape) + i * size, scores, NEG_FILL)
        probs = jnp.exp(scores)
        d_scores = (probs * mm_nt(vx[...], gx[q, :])).astype(LOW)
        d_v = mm(probs.astype(LOW), gx[q, :])
        d_k = mm(d_scores, qx[q, :])
        place(q, qt, qlo, mm(kt_v[...], d_scores).T * SCORE_SCALE)
        if causal:
            dk_v[...] += d_k
            dv_v[...] += d_v
        else:
            place(whole, kt, qlo, d_k)
            place(whole, vtile, vlo, d_v)

    if not causal:
        queries(0)
    else:
        each(count // size, queries)
        place(whole, kt, qlo, dk_v[...])
        place(whole, vtile, vlo, dv_v[...])


def block_kernel(
    planes, self_in, crs_in, up_in, dn_in, x_in, cot_in, gain_in, lengths, task_mask,
    block_out, grad_low, home_ffn, home_crs, home_att, gain_out,
    cot, first_k, x_k, second_k, late_k, memory_k, p_k, o_k, lse_k, pc_k, oc_k, lsec_k, act_k, grad_k, y3_k,
    dw_ffn, dw_crs, dw_att, yb_ffn, yb_crs, yb_att, zb_ffn, zb_crs, zb_att,
    att_v, crs_v, up_v, dn_v, a_v, b_v, o_v, do_v, mid_v, late_v, s_v, g_v, c_v, ta, tb, tc,
    send_v, recv_v, kx, qx, vx, gx, dk_v, dv_v, kt_v, lse_v, gain_v, gain_in_v, gain_buf, out_st, dw_st, sum_st,
    bias_self, bias_cross, res_ffn, res_crs, res_att,
    x_sem, x_sent, y0_sent, c_sem, zw_got, zw_sent, yw_got, yw_sent, side_got, side_sent,
    row_got, row_sent, fwd_sem, cot_got, gain_sem, copy_sem, ex_got, ex_sent, mem_got, mem_sent, mf_got, mf_sent,
    dm_got, dm_sent, df_got, df_sent, y_got, y_sent, z_got, z_sent, home_got, home_sent,
    blk_got, blk_sent, gr_got, gr_sent, gr_hop_got, gr_hop_sent, sum_sem, dw_sem,
):
    at = Place(planes)
    c, z, t, y, r = at.c, at.z, at.t, at.y, at.r
    rows = x_in.shape[1]
    slot = s_v.shape[0]
    tiles = slot // BLOCK
    depth = up_in.shape[0]
    side = crs_in.shape[1]
    relay = at.relays
    other = jnp.logical_not(relay)
    vmem = {"att": att_v, "crs": crs_v, "up": up_v, "dn": dn_v}
    shard = {"att": self_in, "up": up_in, "dn": dn_in}
    here = pl.ds(pl.multiple_of(z * depth, depth), depth)
    dw = {"ffn": dw_ffn, "crs": dw_crs, "att": dw_att}
    yb = {"ffn": yb_ffn, "crs": yb_crs, "att": yb_att}
    zb = {"ffn": zb_ffn, "crs": zb_crs, "att": zb_att}
    home = {"ffn": home_ffn, "crs": home_crs, "att": home_att}
    res = {"ffn": res_ffn, "crs": res_crs, "att": res_att}
    names = {}

    def copying(name, source, goal):
        index = names.setdefault(name, len(names))
        return pltpu.make_async_copy(source, goal, copy_sem.at[index])

    def half_of(core):
        return pl.ds(pl.multiple_of(core * 2 * rows, 2 * rows), 2 * rows)

    at.meet()

    relay_dev = (y, z, 2 * y + c)
    over_dev = (y, z, 2 * (1 - y) + c)
    stays = both(c == y, r == c)

    def launch(g):
        i = GROUPS.index(g)
        goal = vmem[g].at[r, here, :]

        @pl.when(stays)
        def _():
            pltpu.make_async_copy(shard[g], goal, x_sem.at[i, r]).start()

        @pl.when(jnp.logical_not(stays))
        def _():
            push(shard[g], goal, x_sent.at[i], x_sem.at[i, r], relay_dev).start()

    def launch_over(g):
        i = GROUPS.index(g)
        return push(shard[g], vmem[g].at[r, here, :], y0_sent.at[i], yw_got.at[i, 0, r], over_dev)

    crs_dev = (y, z, 2 * y + 1)
    crs_stays = both(c == y, r == 1)

    def crs_goal(block, section):
        return crs_v.at[block, here, pl.ds(pl.multiple_of((1 - section) * side, side), side)]

    def launch_crs():
        @pl.when(crs_stays)
        def _():
            pltpu.make_async_copy(crs_in, crs_goal(r, c), c_sem.at[r, c]).start()

        @pl.when(jnp.logical_not(crs_stays))
        def _():
            push(crs_in, crs_goal(r, c), x_sent.at[1], c_sem.at[r, c], crs_dev).start()

    row_goal = s_v.at[strip(t, rows), :]
    cot_goal = cot.at[strip(t, rows), :]

    def row_stays(s):
        return both(both(c == y, r == c), y == s)

    def launch_rows(s):
        dev = (y, z, 2 * s + c)

        @pl.when(row_stays(s))
        def _():
            pltpu.make_async_copy(x_in.at[s], row_goal, row_got.at[r]).start()

        @pl.when(jnp.logical_not(row_stays(s)))
        def _():
            push(x_in.at[s], row_goal, row_sent.at[s], row_got.at[r], dev).start()

    def launch_cot():
        dev = (y, z, 2 * c + 1)

        @pl.when(crs_stays)
        def _():
            pltpu.make_async_copy(cot_in.at[c], cot_goal, cot_got.at[r]).start()

        @pl.when(jnp.logical_not(crs_stays))
        def _():
            push(cot_in.at[c], cot_goal, row_sent.at[2], cot_got.at[r], dev).start()

    gain_copy = push(gain_in, gain_in_v.at[c], gain_sem.at[0], gain_sem.at[1], at.twin)
    gain_copy.start()
    launch("att")
    launch_over("att").start()
    launch_rows(0)
    launch_rows(1)
    launch("up")
    launch_over("up").start()
    launch_crs()
    launch("dn")
    launch_cot()

    place = subs((slot, TILE))
    seen = jnp.where(y == 0, task_mask[0:1, :], task_mask[1:2, :]) == 1
    seen = jnp.broadcast_to(jnp.where(seen, 1.0, 0.0), (TILE, slot)).T > 0.5
    bias_self[...] = jnp.where(place < lengths[r, y], 0.0, NEG_FILL).astype(LOW)
    bias_cross[...] = jnp.where(both(place < lengths[0, y], seen), 0.0, NEG_FILL).astype(LOW)

    def piece(g, k, b):
        j = lax.rem(z - k + planes, planes)
        return vmem[g].at[b, pl.ds(pl.multiple_of(j * depth, depth), depth), :]

    def ring(g, k, b):
        i = GROUPS.index(g)
        return push(
            piece(g, k - 1, b), piece(g, k - 1, b), zw_sent.at[i, k - 1, b], zw_got.at[i, k - 1, b], at.above
        )

    def ring_in(g, k, b):
        i = GROUPS.index(g)
        return push(piece(g, k, b), piece(g, k, b), zw_sent.at[i, k - 1, b], zw_got.at[i, k - 1, b], at.above)

    def cross_over(g, k, b):
        i = GROUPS.index(g)
        return push(piece(g, k, b), piece(g, k, b), yw_sent.at[i, k, b], yw_got.at[i, k, b], at.across)

    def arrive(g, k, b):
        if k:
            ring_in(g, k, b).wait_recv()
        elif g == "crs":
            for section in range(2):
                goal = crs_goal(b, section)
                push(goal, goal, x_sent.at[1], c_sem.at[b, section], at.twin).wait_recv()
        else:
            i = GROUPS.index(g)
            goal = vmem[g].at[b, here, :]
            push(goal, goal, x_sent.at[i], x_sem.at[i, b], at.twin).wait_recv()

    def passing(g, k, up=True, over=True):
        skips = [b for b in range(2) if k == 1 and (g, b) in ASIDE]

        def half(b):
            if up:
                with jax.named_scope("await_" + g + str(k)):
                    arrive(g, k, b)
                if k + 1 < planes:
                    ring(g, k + 1, b).start()
            if over and not (k == 0 and g in DIRECT) and len(skips) < 2:
                if skips:
                    pl.when(b != skips[0])(lambda: cross_over(g, k, b).start())
                else:
                    cross_over(g, k, b).start()

        def run():
            each(2, half, "pass_" + g)

        return run

    def schedule(order):
        events = []
        for n, g in enumerate(order):
            for k in range(planes):
                if k == 0 and n == 0:
                    events.append(passing(g, 0))
                elif k:
                    events.append(passing(g, k))
                if n + 1 < len(order):
                    if k == planes - 2:
                        events[-1] = chained(events[-1], passing(order[n + 1], 0, True, False))
                    if k == planes - 1:
                        events[-1] = chained(events[-1], passing(order[n + 1], 0, False, True))
        return events

    def chained(one, two):
        def run():
            one()
            two()

        return run

    enc_events = schedule(("att", "up", "dn"))
    dec_events = schedule(("att", "crs", "up", "dn"))

    def pump_enc(count):
        for _ in range(min(count, len(enc_events))):
            pl.when(both(relay, at.encodes))(enc_events.pop(0))

    def pump_dec(count):
        for _ in range(min(count, len(dec_events))):
            pl.when(both(relay, at.decodes))(dec_events.pop(0))

    def pump(count):
        pump_enc(count)
        pump_dec(count)

    def side_hop(g, b):
        i = GROUPS.index(g)
        return push(piece(g, 0, b), piece(g, 0, b), side_sent.at[i, b], side_got.at[i, b], at.above)

    def side_in(g, b):
        i = GROUPS.index(g)
        return push(piece(g, 1, b), piece(g, 1, b), side_sent.at[i, b], side_got.at[i, b], at.above)

    def pass_aside(g):
        @pl.when(other)
        def _():
            for b in range(2):
                cross_over(g, 0, b).wait_recv()
                if (g, b) in ASIDE:
                    side_hop(g, b).start()

    def settle(g):
        listens = both(other, at.decodes) if g == "crs" else other

        @pl.when(listens)
        @jax.named_scope("settle_" + g)
        def _():
            for k in range(planes):
                for b in range(2):
                    if k == 1 and (g, b) in ASIDE:
                        side_in(g, b).wait_recv()
                    elif k or g in ("att", "crs"):
                        cross_over(g, k, b).wait_recv()

    def exchange(e, i):
        q = strip(i, BLOCK)
        k = e % 2
        return push(send_v.at[k, q, :], recv_v.at[k, q, :], ex_sent.at[e, i], ex_got.at[e, i], at.twin)

    def joined(e, i):
        q = strip(i, BLOCK)
        exchange(e, i).wait_recv()
        return send_v[e % 2, q, :].astype(WIDE) + recv_v[e % 2, q, :].astype(WIDE)

    def sent(e):
        each(tiles, lambda i: exchange(e, i).wait_send())

    pump(3)
    for k in range(2):
        goal = s_v.at[strip(2 * c + k, rows), :]
        push(goal, goal, row_sent.at[0], row_got.at[k], at.twin).wait_recv()
    half, far_half = half_of(c), half_of(1 - c)
    rows_on = push(s_v.at[half, :], s_v.at[half, :], fwd_sem.at[0], fwd_sem.at[1], at.twin)
    rows_on.start()
    push(gain_in, gain_in_v.at[1 - c], gain_sem.at[0], gain_sem.at[1], at.twin).wait_recv()
    gain_here = pltpu.make_async_copy(gain_in, gain_in_v.at[c], gain_sem.at[2])
    gain_here.start()
    gain_here.wait()
    gains = gain_in_v[r].astype(WIDE)
    g0, g1, g2 = gains[0:1, :], gains[1:2, :], gains[2:3, :]
    gain_v[...] = jnp.zeros_like(gain_v)
    push(s_v.at[far_half, :], s_v.at[far_half, :], fwd_sem.at[0], fwd_sem.at[1], at.twin).wait_recv()
    x_put = copying("x", s_v, x_k)
    x_put.start()

    def enter(i):
        q = strip(i, BLOCK)
        c_v[q, :] = (center(s_v[q, :].astype(WIDE))[0] * g0).astype(LOW)

    each(tiles, enter)
    first_put = copying("first", c_v, first_k)
    first_put.start()
    pump(1)
    settle("att")

    def project(source, weights, part):
        def project_rows(n):
            b, q = lax.rem(n, 2), strip(lax.div(n, 2), BLOCK)
            if part != "kv":
                a_v[b, q, 0:256] = mm(source[q, :], weights[b, :, 0:256]).astype(LOW)
            if part != "q":
                a_v[b, q, 256:640] = mm(source[q, :], weights[b, :, 384:768]).astype(LOW)

        each(2 * tiles, project_rows)

    packed_v = a_v.at[:, :, 0:640]
    project(c_v, att_v, "all")
    pass_aside("up")
    p_put = copying("p", packed_v, p_k)
    p_put.start()
    o_v[...] = jnp.zeros_like(o_v)
    lse_v[...] = jnp.zeros_like(lse_v)
    pump(1)

    def attend_heads(bias, causal, hooks):
        def head_forward(n):
            b = lax.div(n, 3)
            attend_block(lax.rem(n, 3), a_v.at[b], o_v.at[b], lse_v, n, bias, kx, qx, kt_v, causal)
            for when, event in hooks:
                pl.when(both(n == when, relay))(event)

        each(6, head_forward)

    enc_hooks = [(2, enc_events.pop(0)), (5, enc_events.pop(0))]
    dec_hooks = [(2, dec_events.pop(0)), (4, dec_events.pop(0))]
    pl.when(at.encodes)(lambda: attend_heads(bias_self, False, enc_hooks))
    pl.when(at.decodes)(lambda: attend_heads(bias_self, True, dec_hooks))
    o_put, lse_put = copying("o", o_v, o_k), copying("lse", lse_v, lse_k)
    o_put.start()
    lse_put.start()

    def out_project(e, weights):
        def out_rows(i):
            q = strip(i, BLOCK)
            part = mm_nt(o_v[0, q, :], weights[0, :, 128:384]) + mm_nt(o_v[1, q, :], weights[1, :, 128:384])
            send_v[e % 2, q, :] = part.astype(LOW)
            exchange(e, i).start()

        each(tiles, out_rows)

    out_project(0, att_v)
    pump(1)
    x_put.wait()
    pass_aside("dn")
    rows_on.wait_send()

    def middle(i):
        q = strip(i, BLOCK)
        value = s_v[q, :].astype(WIDE) + joined(0, i)
        mid_v[q, :] = value
        s_v[q, :] = (center(value)[0] * g1).astype(LOW)

    each(tiles, middle)
    first_put.wait()
    p_put.wait()
    o_put.wait()
    lse_put.wait()

    def mem_send(i):
        q = pl.ds(pl.multiple_of((2 * c + i) * BLOCK, BLOCK), BLOCK)
        return push(g_v.at[q, :], g_v.at[q, :], mem_sent.at[i], mem_got.at[i], at.beside)

    def mem_forward(i, core):
        q = pl.ds(pl.multiple_of((2 * core + i) * BLOCK, BLOCK), BLOCK)
        return push(g_v.at[q, :], g_v.at[q, :], mf_sent.at[i], mf_got.at[i], at.twin)

    def row_home(k, source, goal, sent_by, got):
        dev = (r, z, 2 * c + k)
        keeps = both(both(c == r, y == c), r == k)
        return keeps, source, goal.at[y], sent_by.at[k], got.at[y], dev

    def go_home(*spec):
        keeps, source, goal, sent_by, got, dev = row_home(*spec)

        @pl.when(keeps)
        def _():
            pltpu.make_async_copy(source, goal, got).start()

        @pl.when(jnp.logical_not(keeps))
        def _():
            push(source, goal, sent_by, got, dev).start()

    def went_home(*spec):
        keeps, source, goal, sent_by, got, dev = row_home(*spec)

        @pl.when(jnp.logical_not(keeps))
        def _():
            push(source, goal, sent_by, got, dev).wait_send()

    def memory_home(k):
        return k, memory_k.at[strip(2 * c + k, rows), :], block_out, blk_sent, blk_got

    settle_up = lambda: settle("up")
    pl.when(at.encodes)(settle_up)

    @pl.when(at.encodes)
    def _():
        def up_rows(n):
            b, q = lax.rem(n, 2), strip(lax.div(n, 2), BLOCK)
            value, grade = gelu_parts(mm(s_v[q, :], up_v[b]))
            a_v[b, q, :] = value.astype(LOW)
            b_v[b, q, :] = grade.astype(LOW)

        each(2 * tiles, up_rows)

    pump_enc(9)

    @pl.when(at.encodes)
    def _():
        settle("dn")

        def down_rows(i):
            q = strip(i, BLOCK)
            part = mm_nt(a_v[0, q, :], dn_v[0]) + mm_nt(a_v[1, q, :], dn_v[1])
            send_v[1, q, :] = part.astype(LOW)
            exchange(1, i).start()

        each(tiles, down_rows)

        def finish(n):
            i = lax.rem(n + 2 * c, 4)
            q = strip(i, BLOCK)
            value = mid_v[q, :] + joined(1, i)
            late_v[q, :] = value
            g_v[q, :] = (center(value)[0] * g2).astype(LOW)

            @pl.when(n < 2)
            def _():
                mem_send(n).start()

        each(tiles, finish)
        keep = copying("memory", g_v, memory_k)
        keep.start()
        keep.wait()
        for k in range(2):
            go_home(*memory_home(k))
        sent(0)

    def norm_grad(values, gain, grad, gain_row, counted):
        normal, scale = center(values)
        scaled = grad * gain
        one = jnp.mean(scaled, axis=-1, keepdims=True)
        two = jnp.mean(scaled * normal, axis=-1, keepdims=True)
        total = jnp.sum(grad * normal, axis=0, keepdims=True)
        gain_v[gain_row : gain_row + 1, :] += jnp.where(counted, total, 0.0)
        return (scaled - one - normal * two) * scale

    def ours(i):
        return lax.div(i, 2) == c

    @pl.when(at.decodes)
    def _():
        second_put = copying("second", s_v, second_k)
        second_put.start()
        for k in range(2):
            goal = cot.at[strip(2 * c + k, rows), :]
            push(goal, goal, row_sent.at[2], cot_got.at[k], at.twin).wait_recv()
        cot_on = push(cot.at[half, :], cot.at[half, :], fwd_sem.at[2], fwd_sem.at[3], at.twin)
        cot_on.start()
        for _ in range(len(dec_events) - 3):
            pl.when(relay)(dec_events.pop(0))
        settle("crs")
        project(s_v, crs_v, "q")
        pl.when(relay)(dec_events.pop(0))
        pl.when(relay)(dec_events.pop(0))
        push(cot.at[far_half, :], cot.at[far_half, :], fwd_sem.at[2], fwd_sem.at[3], at.twin).wait_recv()
        cot_in_v = copying("cot", cot, c_v)
        cot_in_v.start()
        o_v[...] = jnp.zeros_like(o_v)
        lse_v[...] = jnp.zeros_like(lse_v)
        for i in range(2):
            mem_send(i).wait_recv()
            mem_forward(i, c).start()
        for i in range(2):
            mem_forward(i, 1 - c).wait_recv()
        project(g_v, crs_v, "kv")
        puts = [copying("pc", packed_v, pc_k), copying("memory", g_v, memory_k)]
        for copy in puts:
            copy.start()
        attend_heads(bias_cross, False, [(0, dec_events.pop(0))])
        puts += [copying("oc", o_v, oc_k), copying("lsec", lse_v, lsec_k)]
        for copy in puts[2:]:
            copy.start()
        out_project(1, crs_v)
        second_put.wait()

        def finish(i):
            q = strip(i, BLOCK)
            value = mid_v[q, :] + joined(1, i)
            late_v[q, :] = value
            s_v[q, :] = (center(value)[0] * g2).astype(LOW)

        each(tiles, finish)
        late_put = copying("late", late_v, late_k)
        late_put.start()
        settle("up")
        settle("dn")
        cot_in_v.wait()
        sent(0)
        for copy in puts:
            copy.wait()

        def feed_rows(i):
            q = strip(i, BLOCK)

            def feed_half(b):
                value, grade = gelu_parts(mm(s_v[q, :], up_v[b]))
                a_v[b, q, :] = value.astype(LOW)
                b_v[b, q, :] = (mm(c_v[q, :], dn_v[b]) * grade).astype(LOW)

            each(2, feed_half)
            part = mm_nt(b_v[0, q, :], up_v[0]) + mm_nt(b_v[1, q, :], up_v[1])
            send_v[0, q, :] = part.astype(LOW)
            exchange(2, i).start()

        each(tiles, feed_rows)
        copying("act", a_v, act_k).start()
        late_put.wait()
        cot_on.wait_send()
        each(2, lambda i: mem_forward(i, c).wait_send())

    def block_of(k):
        return lax.rem(z - 1 - k + 2 * planes, planes)

    def y_hop(g, k, b):
        i = SUMS.index(g)
        return push(dw[g].at[k, b], yb[g].at[k, b], y_sent.at[i, k, b], y_got.at[i, k, b], at.across)

    def z_hop(g, k, b):
        i = SUMS.index(g)
        return push(res[g].at[b], zb[g].at[k, b], z_sent.at[i, k, b], z_got.at[i, k, b], at.above)

    def leave(g, k):
        @pl.when(other)
        def _():
            for b in range(2):
                y_hop(g, k, b).start()

    def emit(g, compute):
        columns = dw[g].shape[3]

        def put(k, s):
            return pltpu.make_async_copy(dw_st.at[s, :, :, 0:columns], dw[g].at[k], dw_sem.at[s])

        def run(k):
            s = lax.rem(k, 2)
            j = block_of(k)
            compute(s, pl.ds(pl.multiple_of(j * depth, depth), depth))
            put(k, s).start()

            @pl.when(k >= 1)
            def _():
                put(k - 1, 1 - s).wait()
                leave(g, k - 1)

        each(planes, run, "emit_" + g)
        put(planes - 1, (planes - 1) % 2).wait()
        leave(g, planes - 1)

    def home_copy(g, b, section):
        i = SUMS.index(g)
        columns = dw[g].shape[3]
        source = res[g].at[b]
        if g == "crs":
            source = source.at[:, pl.ds((1 - section) * (columns // 2), columns // 2)]
        device = (section, z, 2 * y + b)
        keeps = both(c == section, r == b)
        return keeps, source, push(source, home[g], home_sent.at[i, b, section if g == "crs" else 0], home_got.at[i], device)

    def sections(g):
        return (0, 1) if g == "crs" else (r,)

    def sum_at(g, n):
        i = SUMS.index(g)
        columns = dw[g].shape[3]
        k, b = lax.div(n, 2), lax.rem(n, 2)

        def fetch(m, source):
            return pltpu.make_async_copy(source, sum_st.at[m, :, 0:columns], sum_sem.at[m])

        @pl.when(relay)
        @jax.named_scope("sum_" + g)
        def _():
            before = lax.max(k - 1, 0)
            y_hop(g, k, b).wait_recv()
            fetch(0, dw[g].at[k, b]).start()
            fetch(1, yb[g].at[k, b]).start()

            @pl.when(k > 0)
            def _():
                z_hop(g, before, b).wait_recv()
                fetch(2, zb[g].at[before, b]).start()
                z_hop(g, before, b).wait_send()
                fetch(2, zb[g].at[before, b]).wait()

            fetch(0, dw[g].at[k, b]).wait()
            fetch(1, yb[g].at[k, b]).wait()
            share = depth // 4

            def add_rows(m):
                q = strip(m, share)
                total = sum_st[0, q, 0:columns].astype(WIDE) + sum_st[1, q, 0:columns].astype(WIDE)
                total = total + jnp.where(k > 0, sum_st[2, q, 0:columns].astype(WIDE), 0.0)
                res[g][b, q, :] = total.astype(LOW)

            each(4, add_rows)

            @pl.when(k + 1 < planes)
            def _():
                z_hop(g, k, b).start()

            @pl.when(k + 1 == planes)
            def _():
                for section in sections(g):
                    keeps, source, copy = home_copy(g, b, section)

                    @pl.when(keeps)
                    def _():
                        pltpu.make_async_copy(source, home[g], home_got.at[i]).start()

                    @pl.when(jnp.logical_not(keeps))
                    def _():
                        copy.start()

    def sums(g, first_step, count):
        each(count, lambda n: sum_at(g, first_step + n), "sums_" + g)

    def turn(source, goal):
        def run(i):
            q = strip(i, BLOCK)
            goal[:, q] = source[q, :].astype(WIDE).T.astype(LOW)

        each(tiles, run, "turn")

    def dm_hop(n, source):
        q = pl.ds(pl.multiple_of((2 * c + n) * BLOCK, BLOCK), BLOCK)
        return push(source.at[q, :], c_v.at[q, :], dm_sent.at[n], dm_got.at[n], at.beside)

    def df_hop(n, core):
        q = pl.ds(pl.multiple_of((2 * core + n) * BLOCK, BLOCK), BLOCK)
        return push(c_v.at[q, :], c_v.at[q, :], df_sent.at[n], df_got.at[n], at.twin)

    @pl.when(at.encodes)
    def _():
        def back_rows(m):
            n = lax.div(m, 2)
            own = lax.rem(m, 2) == 0
            i = jnp.where(own, 2 * c + n, 2 * (1 - c) + n)
            q = strip(i, BLOCK)

            @pl.when(own)
            def _():
                dm_hop(n, c_v).wait_recv()
                df_hop(n, c).start()

            @pl.when(jnp.logical_not(own))
            def _():
                df_hop(n, 1 - c).wait_recv()

            grad = norm_grad(late_v[q, :], g2, c_v[q, :].astype(WIDE), 2, ours(i))
            late_v[q, :] = grad
            low = grad.astype(LOW)
            part = None
            for b in range(2):
                d_pre = (mm(low, dn_v[b]) * b_v[b, q, :].astype(WIDE)).astype(LOW)
                b_v[b, q, :] = d_pre
                term = mm_nt(d_pre, up_v[b])
                part = term if part is None else part + term
            send_v[0, q, :] = part.astype(LOW)

            @pl.when(own)
            def _():
                df_hop(n, c).wait_send()

            c_v[q, :] = low
            exchange(2, i).start()

        each(tiles, back_rows)

    turn(s_v, ta)
    turn(c_v, tb)

    def ffn_block(s, j):
        def ffn_half(b):
            dw_st[s, b, :, 0:768] = mm(ta[j, :], b_v[b]).astype(LOW)
            dw_st[s, b, :, 768:1536] = mm(tb[j, :], a_v[b]).astype(LOW)

        each(2, ffn_half)

    emit("ffn", ffn_block)

    @pl.when(at.decodes)
    def _():
        copying("act", a_v, act_k).wait()
        packed = copying("pc", pc_k, packed_v)
        small = [copying("oc", oc_k, o_v), copying("lsec", lsec_k, lse_v), copying("second", second_k, s_v)]
        packed.start()
        for copy in small:
            copy.start()

        def late_rows(i):
            q = strip(i, BLOCK)
            grad = c_v[q, :].astype(WIDE) + norm_grad(late_v[q, :], g2, joined(2, i), 2, ours(i))
            late_v[q, :] = grad
            g_v[q, :] = grad.astype(LOW)

        each(tiles, late_rows)

        def cross_out(i):
            q = strip(i, BLOCK)
            for b in range(2):
                do_v[b, q, :] = mm(g_v[q, :], crs_v[b, :, 128:384]).astype(LOW)

        each(tiles, cross_out)
        for copy in small:
            copy.wait()
        packed.wait()
        b_v[...] = jnp.zeros_like(b_v)

        def cross_head(n):
            b = lax.div(n, 3)
            attend_back_block(
                lax.rem(n, 3), a_v.at[b], o_v.at[b], do_v.at[b], b_v.at[b], lse_v, n, bias_cross,
                kx, qx, vx, gx, kt_v, dk_v, dv_v, False,
            )

        each(6, cross_head)
        sent(1)

        def to_memory(q):
            return mm_nt(b_v[0, q, 256:640], crs_v[0, :, 384:768]) + mm_nt(b_v[1, q, 256:640], crs_v[1, :, 384:768])

        def far(n):
            i = 2 * (1 - c) + n
            q = strip(i, BLOCK)
            send_v[1, q, :] = to_memory(q).astype(LOW)
            exchange(3, i).start()

        each(2, far)

        def near(n):
            i = 2 * c + n
            q = strip(i, BLOCK)
            part = to_memory(q)
            exchange(3, i).wait_recv()
            send_v[1, q, :] = (part + recv_v[1, q, :].astype(WIDE)).astype(LOW)
            dm_hop(n, send_v.at[1]).start()

        each(2, near)

        def to_query(i):
            q = strip(i, BLOCK)
            part = mm_nt(b_v[0, q, 0:256], crs_v[0, :, 0:256]) + mm_nt(b_v[1, q, 0:256], crs_v[1, :, 0:256])
            send_v[0, q, :] = part.astype(LOW)
            exchange(4, i).start()

        sent(2)
        each(tiles, to_query)
        sums("ffn", 0, 2)
        turn(s_v, ta)
        stage_in = copying("memory", memory_k, s_v)
        stage_in.start()
        turn(g_v, tc)
        stage_in.wait()
        turn(s_v, tb)
        copying("first", first_k, s_v).start()

        def crs_block(s, j):
            def att_half(b):
                left = mm(ta[j, :], b_v[b, :, 0:256])
                out = mm(tc[j, :], o_v[b])
                dw_st[s, b, :, 0:128] = left[:, 0:128].astype(LOW)
                dw_st[s, b, :, 128:256] = (left[:, 128:256] + out[:, 0:128]).astype(LOW)
                dw_st[s, b, :, 256:384] = out[:, 128:256].astype(LOW)
                dw_st[s, b, :, 384:768] = mm(tb[j, :], b_v[b, :, 256:640]).astype(LOW)

            each(2, att_half)

        emit("crs", crs_block)
        sums("ffn", 2, 2)

        def below(i):
            q = strip(i, BLOCK)
            grad = late_v[q, :] + norm_grad(mid_v[q, :], g1, joined(4, i), 1, ours(i))
            late_v[q, :] = grad
            g_v[q, :] = grad.astype(LOW)

        each(tiles, below)
        copying("first", first_k, s_v).wait()

        def gone(n):
            exchange(3, 2 * (1 - c) + n).wait_send()
            dm_hop(n, send_v.at[1]).wait_send()

        each(2, gone)

    @pl.when(at.encodes)
    def _():
        copying("first", first_k, s_v).start()
        each(2, lambda i: mem_send(i).wait_send())

        def below(i):
            q = strip(i, BLOCK)
            grad = late_v[q, :] + norm_grad(mid_v[q, :], g1, joined(2, i), 1, ours(i))
            late_v[q, :] = grad
            g_v[q, :] = grad.astype(LOW)

        each(tiles, below)
        copying("first", first_k, s_v).wait()
        sent(1)

    packed = copying("p", p_k, packed_v)
    small = [copying("o", o_k, o_v), copying("lse", lse_k, lse_v)]
    packed.start()
    for copy in small:
        copy.start()

    def self_out(i):
        q = strip(i, BLOCK)
        for b in range(2):
            do_v[b, q, :] = mm(g_v[q, :], att_v[b, :, 128:384]).astype(LOW)

    each(tiles, self_out)
    b_v[...] = jnp.zeros_like(b_v)
    for copy in small:
        copy.wait()
    packed.wait()

    def self_heads(causal, hook):
        def self_head(n):
            b = lax.div(n, 3)
            attend_back_block(
                lax.rem(n, 3), a_v.at[b], o_v.at[b], do_v.at[b], b_v.at[b], lse_v, n, bias_self,
                kx, qx, vx, gx, kt_v, dk_v, dv_v, causal,
            )
            hook(n)

        each(6, self_head)

    def enc_hook(n):
        @pl.when(jnp.logical_and(n != 0, n != 3))
        def _():
            sum_at("ffn", n - 1 - lax.div(n, 4))

    def dec_hook(n):
        @pl.when(n < 4)
        def _():
            sum_at("ffn", 4 + n)

        @pl.when(n >= 4)
        def _():
            sum_at("crs", n - 4)

    pl.when(at.encodes)(lambda: self_heads(False, enc_hook))
    pl.when(at.decodes)(lambda: self_heads(True, dec_hook))

    def to_rows(q):
        part = None
        for b in range(2):
            term = mm_nt(b_v[b, q, 0:256], att_v[b, :, 0:256]) + mm_nt(b_v[b, q, 256:640], att_v[b, :, 384:768])
            part = term if part is None else part + term
        return part

    def far_rows(n):
        i = 2 * (1 - c) + n
        q = strip(i, BLOCK)
        send_v[1, q, :] = to_rows(q).astype(LOW)
        exchange(5, i).start()

    each(2, far_rows)
    pl.when(at.encodes)(lambda: sums("ffn", 4, 2))
    pl.when(at.decodes)(lambda: sums("crs", 2, 2))
    turn(s_v, ta)
    x_in_v = copying("x", x_k, s_v)
    x_in_v.start()
    turn(g_v, tc)

    def att_block(s, j):
        def att_half(b):
            left = mm(ta[j, :], b_v[b, :, 0:256])
            out = mm(tc[j, :], o_v[b])
            dw_st[s, b, :, 0:128] = left[:, 0:128].astype(LOW)
            dw_st[s, b, :, 128:256] = (left[:, 128:256] + out[:, 0:128]).astype(LOW)
            dw_st[s, b, :, 256:384] = out[:, 128:256].astype(LOW)
            dw_st[s, b, :, 384:768] = mm(ta[j, :], b_v[b, :, 256:640]).astype(LOW)

        each(2, att_half)

    emit("att", att_block)
    pl.when(at.decodes)(lambda: sums("crs", 4, 2))
    x_in_v.wait()

    def near_rows(n):
        i = 2 * c + n
        q = strip(i, BLOCK)
        part = to_rows(q)
        exchange(5, i).wait_recv()
        grad = part + recv_v[1, q, :].astype(WIDE)
        value = late_v[q, :] + norm_grad(s_v[q, :].astype(WIDE), g0, grad, 0, True)
        out_st[strip(n, BLOCK), :] = value.astype(LOW)

    each(2, near_rows)
    out_put = copying("out", out_st, grad_k)
    out_put.start()
    out_put.wait()

    def grad_home(k):
        return k, grad_k.at[strip(k, rows), :], grad_low, gr_sent, gr_got

    def rows_leave():
        for k in range(2):
            go_home(*grad_home(k))

    pl.when(relay)(rows_leave)

    def gain_hop(n, source, device):
        return push(source, gain_buf.at[n], gr_hop_sent.at[n], gr_hop_got.at[n], device)

    gain_buf[0] = gain_v[...]
    twin_hop = gain_hop(1, gain_buf.at[0], at.twin)
    twin_hop.start()
    twin_hop.wait()
    peer_hop = gain_hop(3, gain_buf.at[2], (1 - c, z, lax.rem(t + 2, 4)))
    last = 4 + planes

    @pl.when(relay)
    def _():
        gain_buf[2] = gain_buf[0] + gain_buf[1]
        peer_hop.start()

    def ring_hop(n):
        return gain_hop(5 + n, gain_buf.at[4 + n], at.above)

    def gain_step(n):
        @pl.when(relay)
        @jax.named_scope("gains")
        def _():
            if n == 0:
                peer_hop.wait()
                gain_buf[4] = gain_buf[2] + gain_buf[3]
            else:
                ring_hop(n - 1).wait()
            if n < planes - 1:
                ring_hop(n).start()
            else:
                total = None
                for j in range(planes):
                    held = gain_buf[jnp.where(z == j, 4, 5 + lax.rem(z - 1 - j + planes, planes))]
                    total = held if total is None else total + held
                gain_buf[last] = total
                for b in range(2):
                    keeps = both(c == r, r == b)

                    @pl.when(keeps)
                    def _():
                        pltpu.make_async_copy(gain_buf.at[last], gain_buf.at[last + 1], gr_hop_got.at[last + 1]).start()

                    @pl.when(jnp.logical_not(keeps))
                    def _():
                        final_hop(b).start()

    def final_hop(b):
        return push(
            gain_buf.at[last], gain_buf.at[last + 1], gr_hop_sent.at[last + b], gr_hop_got.at[last + 1],
            (r, z, 2 * y + b),
        )

    def y3_home(k):
        return k, y3_k.at[strip(k, rows), :], block_out, blk_sent, blk_got

    def out_leaves():
        for k in range(2):
            go_home(*y3_home(k))

    @pl.when(at.decodes)
    def _():
        sums("att", 0, 2)
        copies = [copying("act", act_k, a_v), copying("late", late_k, mid_v)]
        for copy in copies:
            copy.start()
        sent(4)
        for copy in copies:
            copy.wait()

        def to_out(q):
            return mm_nt(a_v[0, q, :], dn_v[0]) + mm_nt(a_v[1, q, :], dn_v[1])

        def far_out(n):
            i = 2 * (1 - c) + n
            q = strip(i, BLOCK)
            send_v[0, q, :] = to_out(q).astype(LOW)
            exchange(6, i).start()

        each(2, far_out)

        def near_out(n):
            i = 2 * c + n
            q = strip(i, BLOCK)
            part = to_out(q)
            exchange(6, i).wait_recv()
            out_st[strip(n, BLOCK), :] = (mid_v[q, :] + part + recv_v[0, q, :].astype(WIDE)).astype(LOW)

        each(2, near_out)
        y3_put = copying("out", out_st, y3_k)
        y3_put.start()
        y3_put.wait()
        pl.when(relay)(out_leaves)

    @pl.when(other)
    def _():
        for k in range(planes):
            for b in range(2):
                y_hop("att", k, b).wait_send()
        rows_leave()
        pl.when(at.decodes)(out_leaves)

    pl.when(at.encodes)(lambda: sums("ffn", 6, 2))
    pl.when(at.decodes)(lambda: sums("crs", 6, 2))

    def last_sums(n):
        @pl.when(jnp.logical_or(at.encodes, n >= 2))
        def _():
            sum_at("att", n)

        for m in range(planes):
            pl.when(n == 2 * m + 1)(functools.partial(gain_step, m))

    each(2 * planes, last_sums)

    with jax.named_scope("await_gains"):
        final = gain_buf.at[last + 1]
        push(gain_buf.at[last], final, gr_hop_sent.at[last], gr_hop_got.at[last + 1], at.twin).wait_recv()
    gains_home = copying("gains", final, gain_out)
    gains_home.start()
    with jax.named_scope("await_rows"):
        for n in range(2):
            for goal, got in ((block_out, blk_got), (grad_low, gr_got)):
                push(goal.at[n], goal.at[n], blk_sent.at[0], got.at[n], at.twin).wait_recv()
    for i, g in enumerate(SUMS):
        with jax.named_scope("await_home_" + g):
            push(home[g], home[g], home_sent.at[i, 0, 0], home_got.at[i], at.twin).wait_recv()
    gains_home.wait()
    for k in range(2):
        went_home(*grad_home(k))

    @pl.when(at.encodes)
    def _():
        for k in range(2):
            went_home(*memory_home(k))
        sent(2)

    @pl.when(at.decodes)
    def _():
        for k in range(2):
            went_home(*y3_home(k))
        each(2, lambda n: exchange(6, 2 * (1 - c) + n).wait_send())

    each(2, lambda n: exchange(5, 2 * (1 - c) + n).wait_send())

    @pl.when(relay)
    def _():
        for b in range(2):
            pl.when(jnp.logical_not(both(c == r, r == b)))(lambda: final_hop(b).wait_send())

    for g in SUMS:
        there = at.decodes if g == "crs" else jnp.logical_or(at.decodes, at.encodes)

        if g != "att":

            @pl.when(both(other, there))
            def _():
                for k in range(planes):
                    for b in range(2):
                        y_hop(g, k, b).wait_send()

        @pl.when(both(relay, there))
        def _():
            for b in range(2):
                for section in sections(g):
                    keeps, source, copy = home_copy(g, b, section)

                    @pl.when(jnp.logical_not(keeps))
                    def _():
                        copy.wait_send()

    gain_copy.wait_send()
    for g in DIRECT:
        launch_over(g).wait_send()

    @pl.when(jnp.logical_not(stays))
    def _():
        for g in ("att", "up", "dn"):
            push(shard[g], vmem[g].at[r, here, :], x_sent.at[GROUPS.index(g)], x_sem.at[0, 0], relay_dev).wait_send()

    @pl.when(jnp.logical_not(crs_stays))
    def _():
        push(crs_in, crs_goal(r, c), x_sent.at[1], c_sem.at[0, 0], crs_dev).wait_send()
        push(cot_in.at[c], cot_goal, row_sent.at[2], cot_got.at[r], at.twin).wait_send()

    for s in range(2):

        @pl.when(jnp.logical_not(row_stays(s)))
        def _():
            push(x_in.at[s], row_goal, row_sent.at[s], row_got.at[r], at.twin).wait_send()

    for g in GROUPS:
        member = both(relay, at.decodes) if g == "crs" else relay

        @pl.when(member)
        def _():
            for k in range(planes):
                for b in range(2):
                    if k:
                        ring(g, k, b).wait_send()
                    if (k or g not in DIRECT) and (k != 1 or (g, b) not in ASIDE):
                        cross_over(g, k, b).wait_send()

    @pl.when(other)
    def _():
        for g, b in ASIDE:
            side_hop(g, b).wait_send()


def block_call(planes, slot, width, hidden, depth, args):
    shape = jax.ShapeDtypeStruct
    rows = slot // 4
    square = (slot, width)
    wides = {"ffn": 2 * hidden, "crs": width, "att": width}
    packed, outs, logs, acts = (2, slot, 640), (2, slot, 256), (8, slot), (2, slot, hidden)
    out_shape = (
        [shape((2, rows, width), LOW)] * 2
        + [shape((depth, 2 * hidden), LOW), shape((depth, width // 2), LOW), shape((depth, width), LOW)]
        + [shape((8, width), WIDE)]
        + [shape(square, LOW)] * 4
        + [shape(square, WIDE), shape(square, LOW)]
        + [shape(packed, LOW), shape(outs, LOW), shape(logs, WIDE)] * 2
        + [shape(acts, LOW)]
        + [shape((2 * rows, width), LOW)] * 2
        + [shape((planes, 2, depth, wides[g]), LOW) for g in SUMS] * 3
    )
    dma = pltpu.SemaphoreType.DMA
    v = pltpu.VMEM
    groups = len(GROUPS)
    scratch = (
        [v((2, width, width), LOW)] * 2
        + [v((2, width, hidden), LOW)] * 2
        + [v(acts, LOW)] * 2
        + [v(outs, LOW)] * 2
        + [v(square, WIDE)] * 2
        + [v(square, LOW)] * 3
        + [v((width, slot), LOW)] * 3
        + [v((2,) + square, LOW)] * 2
        + [v((slot, TILE), LOW)] * 4
        + [v((slot, TILE), WIDE)] * 2
        + [v((TILE, slot), LOW), v(logs, WIDE), v((8, width), WIDE), v((2, 3, width), LOW)]
        + [v((planes + 6, 8, width), WIDE)]
        + [v((2 * rows, width), LOW), v((2, 2, depth, 2 * hidden), LOW), v((3, depth, 2 * hidden), LOW)]
        + [v((slot, TILE), LOW)] * 2
        + [v((2, depth, wides[g]), LOW) for g in SUMS]
        + [dma((groups, 2)), dma((groups,)), dma((groups,)), dma((2, 2))]
        + [dma((groups, planes, 2))] * 4
        + [dma((groups, 2))] * 2
        + [dma((2,)), dma((3,)), dma((4,)), dma((2,)), dma((3,)), dma((40,)), dma((7, 4)), dma((7, 4))]
        + [dma((2,))] * 8
        + [dma((3, planes, 2))] * 4
        + [dma((3,)), dma((3, 2, 2))]
        + [dma((2,))] * 4
        + [dma((planes + 6,))] * 2
        + [dma((3,)), dma((2,))]
    )
    any_spec = pl.BlockSpec(memory_space=pl.ANY)
    vmem_spec = pl.BlockSpec(memory_space=pltpu.VMEM)
    return pl.pallas_call(
        functools.partial(block_kernel, planes),
        out_shape=out_shape,
        in_specs=[any_spec] * 6 + [vmem_spec, pl.BlockSpec(memory_space=pltpu.SMEM), vmem_spec],
        out_specs=[any_spec] * len(out_shape),
        scratch_shapes=scratch,
        compiler_params=pltpu.CompilerParams(collective_id=0, has_side_effects=True, vmem_limit_bytes=VMEM_BYTES),
    )(*args)


def widen_kernel(
    block_in, grad_in, ffn_in, crs_in, att_in, gain_in,
    block_out, grad_out, up_out, dn_out, qkv_out, out_out, crs_out, gain_out, last_out,
):
    c = lax.axis_index("section")
    hidden = up_out.shape[1]
    share, part = block_in.shape[1] // 4, ffn_in.shape[0] // 4

    def strips(i):
        q = strip(i, share)
        for n in range(2):
            block_out[n, q, :] = block_in[n, q, :]
            grad_out[n, q, :] = grad_in[n, q, :].astype(WIDE)
        q = strip(i, part)
        up_out[q, :] = ffn_in[q, 0:hidden].astype(WIDE)
        dn_out[q, :] = ffn_in[q, hidden : 2 * hidden].astype(WIDE)

    each(4, strips)
    tiles = [crs_in[:, TILE * n : TILE * (n + 1)].astype(WIDE) for n in range(3)]
    mixed = jnp.where(c == 1, tiles[1], tiles[2])
    crs_out[:, 0, 0:TILE] = tiles[0]
    crs_out[:, 0, TILE : TILE + HEAD] = mixed[:, 0:HEAD]
    crs_out[:, 1, 0:TILE] = jnp.where(c == 1, tiles[2], tiles[1])
    crs_out[:, 1, TILE : TILE + HEAD] = pltpu.roll(mixed, HEAD, 1)[:, 0:HEAD]
    q_tile, q_o, o_tile, k_tile, v_tile, k_v = (att_in[:, TILE * n : TILE * (n + 1)].astype(WIDE) for n in range(6))
    for n, (whole, rest) in enumerate(((q_tile, q_o), (k_tile, k_v), (v_tile, pltpu.roll(k_v, HEAD, 1)))):
        qkv_out[n, :, 0:TILE] = whole
        qkv_out[n, :, TILE : TILE + HEAD] = rest[:, 0:HEAD]
    out_out[0:TILE, :] = o_tile.T
    out_out[TILE : TILE + HEAD, :] = pltpu.roll(q_o, HEAD, 1).T[0:HEAD, :]
    gain_out[...] = gain_in[0:2, :]
    last_out[...] = gain_in[2:3, :]


def widen_call(kept):
    shape = jax.ShapeDtypeStruct
    rows, width = kept[0].shape[1:]
    depth, hidden = kept[2].shape[0], kept[2].shape[1] // 2
    wide = width // 4
    return pl.pallas_call(
        widen_kernel,
        out_shape=[
            shape((2, rows, width), LOW), shape((2, rows, width), WIDE), shape((depth, hidden), WIDE),
            shape((depth, hidden), WIDE), shape((3, depth, wide), WIDE), shape((wide, depth), WIDE),
            shape((depth, 2, wide), WIDE), shape((2, width), WIDE), shape((1, width), WIDE),
        ],
    )(*kept)


def ring_gather(lay, shard):
    planes = lay.planes
    rows = shard.shape[1]
    if planes > 4:
        piece = lax.all_gather(shard, "dp", axis=1, tiled=True)
        across = lay.route(piece, lambda c, z, t: (c, z, (t + 2) % 4) if c == t // 2 else None)
        return jnp.where(lay.relays, piece, across)
    relay = lambda c, z, t: (c, (z + 1) % planes, t) if c == t // 2 else None
    whole = jnp.zeros((shard.shape[0], planes * rows, shard.shape[2]), shard.dtype)
    piece = shard
    for step in range(planes):
        across = lay.route(piece, lambda c, z, t: (c, z, (t + 2) % 4) if c == t // 2 else None)
        chosen = jnp.where(lay.relays, piece, across)
        whole = lax.dynamic_update_slice(whole, chosen, (0, ((lay.plane - step) % planes) * rows, 0))
        if step + 1 < planes:
            piece = lay.route(piece, relay)
    return whole


def ring_scatter(lay, total, holder):
    planes = lay.planes
    rows = total.shape[1] // planes
    low = total.astype(LOW)
    across = lay.route(
        low, lambda c, z, t: (c, z, (t + 2) % 4) if (c != t // 2 and t % 2 == holder) else None
    )
    summed = low.astype(WIDE) + across.astype(WIDE)
    if planes > 4:
        return lax.psum_scatter(summed.astype(LOW), "dp", scatter_dimension=1, tiled=True)
    relay = lambda c, z, t: (c, (z + 1) % planes, t) if (c == t // 2 and t % 2 == holder) else None
    take = lambda j: lax.dynamic_slice_in_dim(summed, (j % planes) * rows, rows, 1)
    running = take(lay.plane - 1)
    for step in range(1, planes):
        running = lay.route(running.astype(LOW), relay).astype(WIDE) + take(lay.plane - 1 - step)
    return running.astype(LOW)


def hand_back(lay, value, holder, section):
    same = lay.route(
        value[0], lambda c, z, t: (section, z, t) if (c == t // 2 and t % 2 == holder) else None
    )
    beside = lay.route(
        value[1], lambda c, z, t: (section, z, t ^ 1) if (c == t // 2 and t % 2 == holder) else None
    )
    return same.astype(WIDE) + beside.astype(WIDE)


def general_body(block_input, w_self, w_self_out, w_cross, w_up, w_down, norm_gains, lengths, task_mask, out_grad):
    lay = Layout()
    seqs, rows, width = block_input.shape[1:]
    slot = rows * lay.chips
    sec = lay.core
    item = lay.item

    def spread(value, first):
        pick = value[jnp.where(first, lay.chip % 2, 1 - lay.chip % 2)]
        flip = 0 if first else 1
        return lay.route(pick, lambda c, z, t: (t // 2, z, 2 * ((t % 2) ^ flip) + c))

    def merge_rows(mine, theirs):
        low_half = jnp.where(lay.core == 0, mine, theirs)
        high_half = jnp.where(lay.core == 0, theirs, mine)
        return jnp.concatenate([low_half[0], low_half[1], high_half[0], high_half[1]], axis=0)

    first = spread(block_input[0], True)
    second = spread(block_input[0], False)
    mine = jnp.where(item == 0, jnp.stack([first, second]), jnp.stack([second, first]))
    x_rows = merge_rows(mine, lay.other_core(mine)).astype(WIDE)

    picked = out_grad[lay.core]
    even = lay.route(picked, lambda c, z, t: (t // 2, z, 2 * c + 1) if t % 2 == 0 else None)
    odd = lay.route(picked, lambda c, z, t: (t // 2, z, 2 * c + 1) if t % 2 == 1 else None)
    mine = jnp.stack([even, odd])
    cotangent = merge_rows(mine, lay.other_core(mine))

    gains_here = norm_gains[0].astype(WIDE)
    gains = jnp.where(sec == lay.role, gains_here, lay.other_core(norm_gains[0]).astype(WIDE))

    depth = w_self.shape[1]
    wide = w_self.shape[3]
    self_block = pack_heads(
        {"q": w_self[0, :, 0], "k": w_self[0, :, 1], "v": w_self[0, :, 2], "o": w_self_out[0].T}
    )
    feed_block = jnp.concatenate([w_up[0], w_down[0].T], axis=1)
    cross_block = w_cross[0].reshape(depth, 2 * wide)

    def collect(block):
        same = lay.route(block, lambda c, z, t: (t // 2, z, t) if c == t % 2 else None)
        beside = lay.route(block, lambda c, z, t: (t // 2, z, t ^ 1) if c != t % 2 else None)
        return jnp.stack([same, beside])

    def collect_cross(block, section):
        same = lay.route(block, lambda c, z, t: (t // 2, z, t) if (c == section and t % 2 == 1) else None)
        beside = lay.route(block, lambda c, z, t: (t // 2, z, t ^ 1) if (c == section and t % 2 == 0) else None)
        return same, beside

    w_att = ring_gather(lay, collect(self_block))
    w_ffn = ring_gather(lay, collect(feed_block))
    memory_side = collect_cross(cross_block, 0)
    query_side = collect_cross(cross_block, 1)
    w_crs = ring_gather(
        lay,
        jnp.stack(
            [
                pack_heads({"q": q[:, :wide], "k": m[:, :wide], "v": m[:, wide:], "o": q[:, wide:]})
                for m, q in zip(memory_side, query_side)
            ]
        ),
    )
    hidden = w_up.shape[2]
    part = lambda w, name: jnp.concatenate([unpack_heads(w[0], name), unpack_heads(w[1], name)], axis=1)
    att = {n: part(w_att, n) for n in "qkvo"}
    crs = {n: part(w_crs, n) for n in "qkvo"}
    up = jnp.concatenate([w_ffn[0, :, :hidden], w_ffn[1, :, :hidden]], axis=1)
    down_t = jnp.concatenate([w_ffn[0, :, hidden:], w_ffn[1, :, hidden:]], axis=1)

    positions = jnp.arange(slot)
    own_length = jnp.where(lay.is_decoder, lengths[1, item], lengths[0, item])
    self_allowed = (positions[None, :] < own_length) & (
        (positions[None, :] <= positions[:, None]) | jnp.logical_not(lay.is_decoder)
    )
    cross_allowed = jnp.broadcast_to(
        ((positions < lengths[0, item]) & (task_mask[item] == 1))[None], (slot, slot)
    )

    def joined(partial):
        low = partial.astype(LOW)
        return low.astype(WIDE) + lay.other_core(low).astype(WIDE)

    normed0 = layer_norm(x_rows, gains[0]).astype(LOW)
    q, k, v = (mm(normed0, att[n]).astype(LOW) for n in "qkv")
    out_self, lse_self = attend(q, k, v, self_allowed)
    x_mid = x_rows + joined(mm_nt(out_self, att["o"]))
    normed1 = layer_norm(x_mid, gains[1]).astype(LOW)

    pre_enc = mm(normed1, up)
    act_enc, slope_enc = gelu_parts(pre_enc)
    act_enc = act_enc.astype(LOW)
    x_late_enc = x_mid + joined(mm_nt(act_enc, down_t))
    memory_enc = layer_norm(x_late_enc, gains[2]).astype(LOW)
    memory = lay.route(memory_enc, lambda c, z, t: (c, z, t ^ 1) if t % 2 == 0 else None)

    cq = mm(normed1, crs["q"]).astype(LOW)
    ck, cv = (mm(memory, crs[n]).astype(LOW) for n in "kv")
    out_cross, lse_cross = attend(cq, ck, cv, cross_allowed)
    x_late = x_mid + joined(mm_nt(out_cross, crs["o"]))
    normed2 = layer_norm(x_late, gains[2]).astype(LOW)
    pre_dec = mm(normed2, up)
    act_dec, slope_dec = gelu_parts(pre_dec)
    act_dec = act_dec.astype(LOW)
    result_dec = (x_late + joined(mm_nt(act_dec, down_t))).astype(LOW)

    d_out = cotangent.astype(WIDE)
    d_pre = (slope_dec * mm(cotangent, down_t)).astype(LOW)
    d_ffn_dec = jnp.concatenate([mm_tn(normed2, d_pre), mm_tn(cotangent, act_dec)], axis=1)
    d_late_norm, d_gain2_dec = norm_back(x_late, gains[2], joined(mm_nt(d_pre, up)))
    d_late = d_out + d_late_norm
    grad_late = d_late.astype(LOW)
    d_att = mm(grad_late, crs["o"]).astype(LOW)
    d_cq, d_ck, d_cv = attend_back(cq, ck, cv, lse_cross, d_att, cross_allowed)
    d_memory = joined(mm_nt(d_ck, crs["k"]) + mm_nt(d_cv, crs["v"]))
    d_crs = {
        "q": mm_tn(normed1, d_cq),
        "k": mm_tn(memory, d_ck),
        "v": mm_tn(memory, d_cv),
        "o": mm_tn(grad_late, out_cross),
    }
    d_mid_norm, d_gain1_dec = norm_back(x_mid, gains[1], joined(mm_nt(d_cq, crs["q"])))
    d_mid_dec = d_late + d_mid_norm

    d_memory = lay.route(d_memory.astype(LOW), lambda c, z, t: (c, z, t ^ 1) if t % 2 == 1 else None).astype(WIDE)
    d_late_enc, d_gain2_enc = norm_back(x_late_enc, gains[2], d_memory)
    grad_late_enc = d_late_enc.astype(LOW)
    d_pre = (slope_enc * mm(grad_late_enc, down_t)).astype(LOW)
    d_ffn_enc = jnp.concatenate([mm_tn(normed1, d_pre), mm_tn(grad_late_enc, act_enc)], axis=1)
    d_mid_norm, d_gain1_enc = norm_back(x_mid, gains[1], joined(mm_nt(d_pre, up)))
    d_mid_enc = d_late_enc + d_mid_norm

    d_mid = jnp.where(lay.is_decoder, d_mid_dec, d_mid_enc)
    grad_mid = d_mid.astype(LOW)
    d_att = mm(grad_mid, att["o"]).astype(LOW)
    d_q, d_k, d_v = attend_back(q, k, v, lse_self, d_att, self_allowed)
    d_norm = joined(mm_nt(d_q, att["q"]) + mm_nt(d_k, att["k"]) + mm_nt(d_v, att["v"]))
    d_att_w = {
        "q": mm_tn(normed0, d_q),
        "k": mm_tn(normed0, d_k),
        "v": mm_tn(normed0, d_v),
        "o": mm_tn(grad_mid, out_self),
    }
    d_first, d_gain0 = norm_back(x_rows, gains[0], d_norm)
    d_rows = d_mid + d_first

    half = 3 * HEAD

    def blocks(parts):
        return jnp.stack(
            [pack_heads({n: parts[n][:, half * b : half * (b + 1)] for n in parts}) for b in range(2)]
        )

    def feed_blocks(both):
        total = both.shape[1] // 2
        return jnp.stack(
            [
                jnp.concatenate(
                    [both[:, hidden * b : hidden * (b + 1)], both[:, total + hidden * b : total + hidden * (b + 1)]],
                    axis=1,
                )
                for b in range(2)
            ]
        )

    self_total = blocks(d_att_w)
    home_self = hand_back(lay, ring_scatter(lay, self_total, 0), 0, 0) + hand_back(
        lay, ring_scatter(lay, self_total, 1), 1, 1
    )
    home_feed = hand_back(lay, ring_scatter(lay, feed_blocks(d_ffn_enc), 0), 0, 0) + hand_back(
        lay, ring_scatter(lay, feed_blocks(d_ffn_dec), 1), 1, 1
    )
    cross_total = ring_scatter(lay, blocks(d_crs), 1)
    side = lambda names: jnp.stack(
        [jnp.concatenate([unpack_heads(cross_total[b], n) for n in names], axis=1) for b in range(2)]
    )
    home_cross = hand_back(lay, side("kv"), 1, 0) + hand_back(lay, side("qo"), 1, 1)

    g_self = jnp.stack([unpack_heads(home_self, n) for n in "qkv"], axis=1)[None]
    g_self_out = unpack_heads(home_self, "o").T[None]
    g_cross = home_cross.reshape(1, depth, 2, wide)
    g_up = home_feed[:, :hidden][None]
    g_down = home_feed[:, hidden:].T[None]

    gain2 = jnp.where(lay.is_decoder, d_gain2_dec, d_gain2_enc)
    gain1 = jnp.where(lay.is_decoder, d_gain1_dec, d_gain1_enc)
    gain_rows = jnp.stack([d_gain0, gain1, gain2])
    slots = jnp.stack(
        [
            jnp.where((lay.role == r) & (lay.core == 0), gain_rows, 0.0)
            for r in range(2)
        ]
    )
    gain_total = lax.psum(slots, AXES)[sec][None]

    def rows_home(value):
        mine = lax.dynamic_slice_in_dim(value, lay.core * 2 * rows, 2 * rows, 0).reshape(2, rows, width)
        a = lay.route(mine[item], lambda c, z, t: (t % 2, z, 2 * c + t // 2))
        b = lay.route(mine[1 - item], lambda c, z, t: (t % 2, z, 2 * c + 1 - t // 2))
        even = lay.chip % 2 == 0
        return jnp.where(even, jnp.stack([a, b]), jnp.stack([b, a]))[None]

    block_output = rows_home(jnp.where(lay.is_decoder, result_dec, memory_enc))
    input_grad = rows_home(d_rows.astype(LOW)).astype(WIDE)
    return (
        block_output,
        input_grad,
        g_self,
        g_self_out,
        g_cross,
        g_up,
        g_down,
        gain_total[:, :2],
        gain_total[:, 2],
    )


def body(block_input, w_self, w_self_out, w_cross, w_up, w_down, norm_gains, lengths, task_mask, out_grad):
    lay = Layout()
    seqs, rows, width = block_input.shape[1:]
    slot = rows * lay.chips
    sec = lay.core
    item = lay.item

    if lay.planes != 4:
        return general_body(
            block_input, w_self, w_self_out, w_cross, w_up, w_down, norm_gains, lengths, task_mask, out_grad
        )

    depth = w_self.shape[1]
    wide = w_self.shape[3]
    hidden = w_up.shape[2]
    self_block = pack_heads(
        {"q": w_self[0, :, 0], "k": w_self[0, :, 1], "v": w_self[0, :, 2], "o": w_self_out[0].T}
    )
    pair = {"q": w_cross[0, :, 0], "o": w_cross[0, :, 1], "k": w_cross[0, :, 0], "v": w_cross[0, :, 1]}
    pieces = [pair[n][:, HEAD * h : HEAD * (h + 1)] for n, h in ORDER]
    cross_block = jnp.where(
        sec == 1, jnp.concatenate(pieces[:6], axis=1), jnp.concatenate(pieces[6:], axis=1)
    )
    kept = block_call(
        lay.planes,
        slot,
        width,
        hidden,
        depth,
        (self_block, cross_block, w_up[0], w_down[0].T, block_input[0], out_grad, norm_gains[0], lengths, task_mask),
    )[:6]
    block_output, input_grad, g_up, g_down, g_qkv, g_out, g_cross, g_gain, g_last = widen_call(kept)
    return (
        block_output[None],
        input_grad[None],
        jnp.swapaxes(g_qkv, 0, 1)[None],
        g_out[None],
        g_cross[None],
        g_up[None],
        g_down.T[None],
        g_gain[None],
        g_last,
    )


def solution(mesh):
    placed = (
        P("section", "dp", "tensor", None),
        P("section", "dp", None, "tensor"),
        P("section", "tensor", "dp"),
        P("section", "dp", None, "tensor"),
        P("section", "dp", "tensor"),
        P("section", "tensor", "dp"),
        P("section", None, None),
        P(None, "dp"),
        P("dp", None),
        P("dp", "tensor", None),
    )
    return jax.shard_map(
        body,
        mesh=mesh,
        in_specs=placed,
        out_specs=(
            P("section", "dp", "tensor", None),
            P("section", "dp", "tensor", None),
            P("section", "dp", None, "tensor"),
            P("section", "tensor", "dp"),
            P("section", "dp", None, "tensor"),
            P("section", "dp", "tensor"),
            P("section", "tensor", "dp"),
            P("section", None, None),
            P("section", None),
        ),
        check_vma=False,
    )
```

```python
import functools

import jax
import jax.numpy as jnp
from jax import lax
from jax.experimental import pallas as pl
from jax.experimental.pallas import tpu as pltpu
from jax.sharding import PartitionSpec as P

HEAD = 64
TILE = 128
EPSILON = 1e-05
SCORE_SCALE = 0.125
NEG_FILL = -1000000000.0
AXES = ("section", "dp", "tensor")
LOW = jnp.bfloat16
WIDE = jnp.float32


class Layout:
    def __init__(self):
        self.cores = lax.axis_size("section")
        self.planes = lax.axis_size("dp")
        self.chips = lax.axis_size("tensor")
        self.core = lax.axis_index("section")
        self.plane = lax.axis_index("dp")
        self.chip = lax.axis_index("tensor")
        self.role = self.chip % 2
        self.item = self.chip // 2
        self.is_decoder = self.role == 1
        self.relays = self.core == self.item

    def route(self, value, target):
        pairs = []
        for core in range(self.cores):
            for plane in range(self.planes):
                for chip in range(self.chips):
                    to = target(core, plane, chip)
                    if to is None:
                        continue
                    source = (core * self.planes + plane) * self.chips + chip
                    goal = (to[0] * self.planes + to[1]) * self.chips + to[2]
                    pairs.append((source, goal))
        return lax.ppermute(value, AXES, pairs)

    def other_core(self, value):
        return self.route(value, lambda c, z, t: (1 - c, z, t))


def normalize(values):
    centred = values - jnp.mean(values, axis=-1, keepdims=True)
    spread = jnp.mean(centred * centred, axis=-1, keepdims=True)
    scale = lax.rsqrt(spread + EPSILON)
    return centred * scale, scale


def layer_norm(values, gain):
    return normalize(values)[0] * gain


def norm_back(values, gain, grad):
    normal, scale = normalize(values)
    scaled = grad * gain
    first = jnp.mean(scaled, axis=-1, keepdims=True)
    second = jnp.mean(scaled * normal, axis=-1, keepdims=True)
    return (scaled - first - normal * second) * scale, jnp.sum(grad * normal, axis=0)


ORDER = (("q", 0), ("q", 1), ("q", 2), ("o", 2), ("o", 0), ("o", 1), ("k", 0), ("k", 1), ("v", 0), ("v", 1), ("k", 2), ("v", 2))


def pack_heads(parts):
    return jnp.concatenate([parts[n][:, HEAD * h : HEAD * (h + 1)] for n, h in ORDER], axis=1)


def unpack_heads(block, name):
    where = {(n, h): i for i, (n, h) in enumerate(ORDER)}
    return jnp.concatenate(
        [block[:, HEAD * where[(name, h)] : HEAD * (where[(name, h)] + 1)] for h in range(3)], axis=1
    )


def mm(left, right):
    return jnp.dot(left, right, preferred_element_type=WIDE)


def mm_nt(left, right):
    return lax.dot_general(left, right, (((1,), (1,)), ((), ())), preferred_element_type=WIDE)


def mm_tn(left, right):
    return lax.dot_general(left, right, (((0,), (0,)), ((), ())), preferred_element_type=WIDE)


def split_heads(value):
    return value.reshape(value.shape[0], -1, HEAD)


def attend(q, k, v, allowed):
    scores = jnp.einsum("qhd,khd->hqk", split_heads(q), split_heads(k), preferred_element_type=WIDE) * SCORE_SCALE
    scores = jnp.where(allowed[None], scores, NEG_FILL)
    top = jnp.max(scores, axis=-1, keepdims=True)
    power = jnp.exp(scores - top)
    total = jnp.sum(power, axis=-1, keepdims=True)
    probs = (power / total).astype(LOW)
    out = jnp.einsum("hqk,khd->qhd", probs, split_heads(v), preferred_element_type=WIDE)
    return out.astype(LOW).reshape(q.shape), top + jnp.log(total)


def attend_back(q, k, v, log_sum, d_out, allowed):
    scores = jnp.einsum("qhd,khd->hqk", split_heads(q), split_heads(k), preferred_element_type=WIDE) * SCORE_SCALE
    scores = jnp.where(allowed[None], scores, NEG_FILL)
    probs = jnp.exp(scores - log_sum)
    d_probs = jnp.einsum("qhd,khd->hqk", split_heads(d_out), split_heads(v), preferred_element_type=WIDE)
    inner = jnp.sum(probs * d_probs, axis=-1, keepdims=True)
    d_scores = (probs * (d_probs - inner)).astype(LOW)
    d_v = jnp.einsum("hqk,qhd->khd", probs.astype(LOW), split_heads(d_out), preferred_element_type=WIDE)
    d_q = jnp.einsum("hqk,khd->qhd", d_scores, split_heads(k), preferred_element_type=WIDE) * SCORE_SCALE
    d_k = jnp.einsum("hqk,qhd->khd", d_scores, split_heads(q), preferred_element_type=WIDE) * SCORE_SCALE
    return tuple(g.astype(LOW).reshape(q.shape) for g in (d_q, d_k, d_v))


def gelu_parts(value):
    coef = 0.7978845608028654
    cube = 0.044715
    inner = coef * (value + cube * value * value * value)
    soft = jnp.tanh(inner)
    slope = 0.5 * (1.0 + soft) + 0.5 * value * (1.0 - soft * soft) * coef * (1.0 + 3.0 * cube * value * value)
    return 0.5 * value * (1.0 + soft), slope


MESH = pl.DeviceIdType.MESH
GROUPS = ("att", "crs", "up", "dn")
BLOCK = 256
VMEM_BYTES = 62 * 2**20


def lanes(shape):
    return lax.broadcasted_iota(jnp.int32, shape, len(shape) - 1)


def subs(shape):
    return lax.broadcasted_iota(jnp.int32, shape, 0)


def strip(i, size):
    return pl.ds(pl.multiple_of(i * size, size), size)


def head_place(h):
    two = (h == 2).astype(jnp.int32)
    one = (h >= 1).astype(jnp.int32)
    return two, 2 + 2 * two, 3 + two, 1 - two, HEAD * (one - two), HEAD * one


def each(count, step, name=None):
    def run(i, carry):
        step(i)
        return carry

    with jax.named_scope(name or step.__name__):
        lax.fori_loop(0, count, run, 0)


class Place:
    def __init__(self, planes):
        self.planes = planes
        self.c = lax.axis_index("section")
        self.z = lax.axis_index("dp")
        self.t = lax.axis_index("tensor")
        self.y = lax.div(self.t, 2)
        self.r = lax.rem(self.t, 2)
        self.twin = (1 - self.c, self.z, self.t)
        self.above = (self.c, lax.rem(self.z + 1, planes), self.t)
        self.below = (self.c, lax.rem(self.z + planes - 1, planes), self.t)
        self.across = (self.c, self.z, lax.rem(self.t + 2, 4))
        self.beside = (self.c, self.z, self.t + 1 - 2 * self.r)
        self.relays = self.c == self.y
        self.encodes = self.r == 0
        self.decodes = self.r == 1

    def meet(self):
        barrier = pltpu.get_barrier_semaphore()
        peers = [self.above, self.below]
        for dc in range(2):
            for dt in range(4):
                if dc or dt:
                    peers.append((lax.rem(self.c + dc, 2), self.z, lax.rem(self.t + dt, 4)))
        for peer in peers:
            pl.semaphore_signal(barrier, inc=1, device_id=peer, device_id_type=MESH)
        pl.semaphore_wait(barrier, len(peers))


def push(source, goal, sent, got, device):
    return pltpu.make_async_remote_copy(
        src_ref=source, dst_ref=goal, send_sem=sent, recv_sem=got, device_id=device, device_id_type=MESH
    )


def both(first, second):
    return jnp.logical_and(first, second)


def center(values):
    middle = values - jnp.mean(values, axis=-1, keepdims=True)
    scale = lax.rsqrt(jnp.mean(middle * middle, axis=-1, keepdims=True) + EPSILON)
    return middle * scale, scale


def attend_block(h, p, o, lse, lse_row, bias, kx, qx, vt, causal):
    count = p.shape[0]
    qt, kt, vtile, ot, qlo, vlo = head_place(h)
    lane = lanes((count, TILE))
    in_q = both(lane >= qlo, lane < qlo + HEAD)
    in_v = both(lane >= vlo, lane < vlo + HEAD)
    spare = HEAD - qlo
    kx[...] = jnp.where(lane == spare, bias[...], jnp.where(in_q, p[:, strip(kt, TILE)], jnp.zeros((), LOW)))
    vt[...] = jnp.where(in_v, p[:, strip(vtile, TILE)].astype(WIDE), 1.0).T.astype(LOW)
    qx[...] = jnp.where(
        in_q, p[:, strip(qt, TILE)].astype(WIDE) * SCORE_SCALE, jnp.where(lane == spare, 1.0, 0.0)
    ).astype(LOW)
    size = count // 2 if causal else count

    def queries(i):
        q = strip(i, size) if causal else pl.ds(0, count)
        scores = mm_nt(kx[...], qx[q, :])
        if causal:
            scores = jnp.where(subs(scores.shape) <= lanes(scores.shape) + i * size, scores, NEG_FILL)
        top = jnp.max(scores, axis=0, keepdims=True)
        power = jnp.exp(scores - top).astype(LOW)
        out = mm(vt[...], power)
        total = jnp.where(vlo == 0, out[HEAD : HEAD + 1, :], out[0:1, :])
        result = (out / total).T
        lane = lanes((size, TILE))
        in_v = both(lane >= vlo, lane < vlo + HEAD)
        o[q, strip(ot, TILE)] = jnp.where(in_v, result, o[q, strip(ot, TILE)].astype(WIDE)).astype(LOW)
        row = subs((8, size))
        lse[:, q] = jnp.where(row == lse_row, top + jnp.log(total), lse[:, q])

    if causal:
        each(count // size, queries)
    else:
        queries(0)


SUMS = ("ffn", "crs", "att")
DIRECT = ("att", "up")
ASIDE = (("up", 0), ("up", 1), ("dn", 0))


def split_three(value):
    high = value.astype(LOW).astype(WIDE)
    middle = (value - high).astype(LOW).astype(WIDE)
    return high, middle, value - high - middle


def attend_back_block(h, p, o, d_o, d_p, lse, lse_row, bias, kx, qx, vx, gx, kt_v, dk_v, dv_v, causal):
    count = p.shape[0]
    qt, kt, vtile, ot, qlo, vlo = head_place(h)
    lane = lanes((count, TILE))
    in_q = both(lane >= qlo, lane < qlo + HEAD)
    in_v = both(lane >= vlo, lane < vlo + HEAD)
    sq, sv = HEAD - qlo, HEAD - vlo
    keys = jnp.where(
        in_q, p[:, strip(kt, TILE)].astype(WIDE), jnp.where(both(lane > sq, lane < sq + 4), 1.0, 0.0)
    )
    keys = jnp.where(lane == sq, bias[...].astype(WIDE), keys)
    kx[...] = keys.astype(LOW)
    kt_v[...] = keys.T.astype(LOW)
    vx[...] = jnp.where(
        in_v, p[:, strip(vtile, TILE)].astype(WIDE), jnp.where(both(lane >= sv, lane < sv + 3), 1.0, 0.0)
    ).astype(LOW)
    own = jnp.sum(jnp.where(subs((8, count)) == lse_row, lse[...], 0.0), axis=0, keepdims=True)
    a, b, c = split_three(-jnp.broadcast_to(own, (TILE, count)).T)
    extra = jnp.where(
        lane == sq,
        1.0,
        jnp.where(lane == sq + 1, a, jnp.where(lane == sq + 2, b, jnp.where(lane == sq + 3, c, 0.0))),
    )
    qx[...] = jnp.where(in_q, p[:, strip(qt, TILE)].astype(WIDE) * SCORE_SCALE, extra).astype(LOW)
    grad = jnp.where(in_v, d_o[:, strip(ot, TILE)].astype(WIDE), 0.0)
    inner = jnp.sum(grad * o[:, strip(ot, TILE)].astype(WIDE), axis=-1, keepdims=True)
    a, b, c = split_three(-inner)
    gx[...] = (
        grad + jnp.where(lane == sv, a, jnp.where(lane == sv + 1, b, jnp.where(lane == sv + 2, c, 0.0)))
    ).astype(LOW)
    size = count // 2 if causal else count

    def place(q, tile_index, low, value):
        cut = strip(tile_index, TILE)
        lane = lanes(value.shape)
        inside = both(lane >= low, lane < low + HEAD)
        d_p[q, cut] = jnp.where(inside, value, d_p[q, cut].astype(WIDE)).astype(LOW)

    whole = pl.ds(0, count)
    if causal:
        dk_v[...] = jnp.zeros_like(dk_v)
        dv_v[...] = jnp.zeros_like(dv_v)

    def queries(i):
        q = strip(i, size) if causal else pl.ds(0, count)
        scores = mm_nt(kx[...], qx[q, :])
        if causal:
            scores = jnp.where(subs(scores.shape) <= lanes(scores.shape) + i * size, scores, NEG_FILL)
        probs = jnp.exp(scores)
        d_scores = (probs * mm_nt(vx[...], gx[q, :])).astype(LOW)
        d_v = mm(probs.astype(LOW), gx[q, :])
        d_k = mm(d_scores, qx[q, :])
        place(q, qt, qlo, mm(kt_v[...], d_scores).T * SCORE_SCALE)
        if causal:
            dk_v[...] += d_k
            dv_v[...] += d_v
        else:
            place(whole, kt, qlo, d_k)
            place(whole, vtile, vlo, d_v)

    if not causal:
        queries(0)
    else:
        each(count // size, queries)
        place(whole, kt, qlo, dk_v[...])
        place(whole, vtile, vlo, dv_v[...])


def block_kernel(
    planes, self_in, crs_in, up_in, dn_in, x_in, cot_in, gain_in, lengths, task_mask,
    block_out, grad_low, home_ffn, home_crs, home_att, gain_out,
    cot, first_k, x_k, second_k, late_k, memory_k, p_k, o_k, lse_k, pc_k, oc_k, lsec_k, act_k, grad_k, y3_k,
    dw_ffn, dw_crs, dw_att, yb_ffn, yb_crs, yb_att, zb_ffn, zb_crs, zb_att, via_att,
    att_v, crs_v, up_v, dn_v, a_v, b_v, o_v, do_v, mid_v, late_v, s_v, g_v, c_v, ta, tb, tc,
    send_v, recv_v, kx, qx, vx, gx, dk_v, dv_v, kt_v, lse_v, gain_v, gain_in_v, gain_buf, out_st, dw_st, sum_st,
    bias_self, bias_cross, res_ffn, res_crs, res_att,
    x_sem, x_sent, y0_sent, c_sem, zw_got, zw_sent, yw_got, yw_sent, side_got, side_sent,
    row_got, row_sent, fwd_sem, cot_got, gain_sem, copy_sem, ex_got, ex_sent, mem_got, mem_sent, mf_got, mf_sent,
    dm_got, dm_sent, df_got, df_sent, y_got, y_sent, z_got, z_sent, home_got, home_sent,
    blk_got, blk_sent, gr_got, gr_sent, gr_hop_got, gr_hop_sent, sum_sem, dw_sem, via_got, via_sent, hand_got, hand_sent,
):
    at = Place(planes)
    c, z, t, y, r = at.c, at.z, at.t, at.y, at.r
    rows = x_in.shape[1]
    slot = s_v.shape[0]
    tiles = slot // BLOCK
    depth = up_in.shape[0]
    side = crs_in.shape[1]
    relay = at.relays
    other = jnp.logical_not(relay)
    vmem = {"att": att_v, "crs": crs_v, "up": up_v, "dn": dn_v}
    shard = {"att": self_in, "up": up_in, "dn": dn_in}
    here = pl.ds(pl.multiple_of(z * depth, depth), depth)
    dw = {"ffn": dw_ffn, "crs": dw_crs, "att": dw_att}
    yb = {"ffn": yb_ffn, "crs": yb_crs, "att": yb_att}
    zb = {"ffn": zb_ffn, "crs": zb_crs, "att": zb_att}
    home = {"ffn": home_ffn, "crs": home_crs, "att": home_att}
    res = {"ffn": res_ffn, "crs": res_crs, "att": res_att}
    names = {}

    def copying(name, source, goal):
        index = names.setdefault(name, len(names))
        return pltpu.make_async_copy(source, goal, copy_sem.at[index])

    def half_of(core):
        return pl.ds(pl.multiple_of(core * 2 * rows, 2 * rows), 2 * rows)

    at.meet()

    relay_dev = (y, z, 2 * y + c)
    over_dev = (y, z, 2 * (1 - y) + c)
    stays = both(c == y, r == c)

    def launch(g):
        i = GROUPS.index(g)
        goal = vmem[g].at[r, here, :]

        @pl.when(stays)
        def _():
            pltpu.make_async_copy(shard[g], goal, x_sem.at[i, r]).start()

        @pl.when(jnp.logical_not(stays))
        def _():
            push(shard[g], goal, x_sent.at[i], x_sem.at[i, r], relay_dev).start()

    def launch_over(g):
        i = GROUPS.index(g)
        return push(shard[g], vmem[g].at[r, here, :], y0_sent.at[i], yw_got.at[i, 0, r], over_dev)

    crs_dev = (y, z, 2 * y + 1)
    crs_stays = both(c == y, r == 1)

    def crs_goal(block, section):
        return crs_v.at[block, here, pl.ds(pl.multiple_of((1 - section) * side, side), side)]

    def launch_crs():
        @pl.when(crs_stays)
        def _():
            pltpu.make_async_copy(crs_in, crs_goal(r, c), c_sem.at[r, c]).start()

        @pl.when(jnp.logical_not(crs_stays))
        def _():
            push(crs_in, crs_goal(r, c), x_sent.at[1], c_sem.at[r, c], crs_dev).start()

    row_goal = s_v.at[strip(t, rows), :]
    cot_goal = cot.at[strip(t, rows), :]

    def row_stays(s):
        return both(both(c == y, r == c), y == s)

    def launch_rows(s):
        dev = (y, z, 2 * s + c)

        @pl.when(row_stays(s))
        def _():
            pltpu.make_async_copy(x_in.at[s], row_goal, row_got.at[r]).start()

        @pl.when(jnp.logical_not(row_stays(s)))
        def _():
            push(x_in.at[s], row_goal, row_sent.at[s], row_got.at[r], dev).start()

    def launch_cot():
        dev = (y, z, 2 * c + 1)

        @pl.when(crs_stays)
        def _():
            pltpu.make_async_copy(cot_in.at[c], cot_goal, cot_got.at[r]).start()

        @pl.when(jnp.logical_not(crs_stays))
        def _():
            push(cot_in.at[c], cot_goal, row_sent.at[2], cot_got.at[r], dev).start()

    gain_copy = push(gain_in, gain_in_v.at[c], gain_sem.at[0], gain_sem.at[1], at.twin)
    gain_copy.start()
    launch("att")
    launch_over("att").start()
    launch_rows(0)
    launch_rows(1)
    launch("up")
    launch_over("up").start()
    launch_crs()
    launch("dn")
    launch_cot()

    place = subs((slot, TILE))
    seen = jnp.where(y == 0, task_mask[0:1, :], task_mask[1:2, :]) == 1
    seen = jnp.broadcast_to(jnp.where(seen, 1.0, 0.0), (TILE, slot)).T > 0.5
    bias_self[...] = jnp.where(place < lengths[r, y], 0.0, NEG_FILL).astype(LOW)
    bias_cross[...] = jnp.where(both(place < lengths[0, y], seen), 0.0, NEG_FILL).astype(LOW)

    def piece(g, k, b):
        j = lax.rem(z - k + planes, planes)
        return vmem[g].at[b, pl.ds(pl.multiple_of(j * depth, depth), depth), :]

    def ring(g, k, b):
        i = GROUPS.index(g)
        return push(
            piece(g, k - 1, b), piece(g, k - 1, b), zw_sent.at[i, k - 1, b], zw_got.at[i, k - 1, b], at.above
        )

    def ring_in(g, k, b):
        i = GROUPS.index(g)
        return push(piece(g, k, b), piece(g, k, b), zw_sent.at[i, k - 1, b], zw_got.at[i, k - 1, b], at.above)

    def cross_over(g, k, b):
        i = GROUPS.index(g)
        return push(piece(g, k, b), piece(g, k, b), yw_sent.at[i, k, b], yw_got.at[i, k, b], at.across)

    def arrive(g, k, b):
        if k:
            ring_in(g, k, b).wait_recv()
        elif g == "crs":
            for section in range(2):
                goal = crs_goal(b, section)
                push(goal, goal, x_sent.at[1], c_sem.at[b, section], at.twin).wait_recv()
        else:
            i = GROUPS.index(g)
            goal = vmem[g].at[b, here, :]
            push(goal, goal, x_sent.at[i], x_sem.at[i, b], at.twin).wait_recv()

    def passing(g, k, up=True, over=True):
        skips = [b for b in range(2) if k == 1 and (g, b) in ASIDE]

        def half(b):
            if up:
                with jax.named_scope("await_" + g + str(k)):
                    arrive(g, k, b)
                if k + 1 < planes:
                    ring(g, k + 1, b).start()
            if over and not (k == 0 and g in DIRECT) and len(skips) < 2:
                if skips:
                    pl.when(b != skips[0])(lambda: cross_over(g, k, b).start())
                else:
                    cross_over(g, k, b).start()

        def run():
            each(2, half, "pass_" + g)

        return run

    def schedule(order):
        events = []
        for n, g in enumerate(order):
            for k in range(planes):
                if k == 0 and n == 0:
                    events.append(passing(g, 0))
                elif k:
                    events.append(passing(g, k))
                if n + 1 < len(order):
                    if k == planes - 2:
                        events[-1] = chained(events[-1], passing(order[n + 1], 0, True, False))
                    if k == planes - 1:
                        events[-1] = chained(events[-1], passing(order[n + 1], 0, False, True))
        return events

    def chained(one, two):
        def run():
            one()
            two()

        return run

    enc_events = schedule(("att", "up", "dn"))
    dec_events = schedule(("att", "crs", "up", "dn"))

    def pump_enc(count):
        for _ in range(min(count, len(enc_events))):
            pl.when(both(relay, at.encodes))(enc_events.pop(0))

    def pump_dec(count):
        for _ in range(min(count, len(dec_events))):
            pl.when(both(relay, at.decodes))(dec_events.pop(0))

    def pump(count):
        pump_enc(count)
        pump_dec(count)

    def side_hop(g, b):
        i = GROUPS.index(g)
        return push(piece(g, 0, b), piece(g, 0, b), side_sent.at[i, b], side_got.at[i, b], at.above)

    def side_in(g, b):
        i = GROUPS.index(g)
        return push(piece(g, 1, b), piece(g, 1, b), side_sent.at[i, b], side_got.at[i, b], at.above)

    def pass_aside(g):
        @pl.when(other)
        def _():
            for b in range(2):
                cross_over(g, 0, b).wait_recv()
                if (g, b) in ASIDE:
                    side_hop(g, b).start()

    def settle(g):
        listens = both(other, at.decodes) if g == "crs" else other

        @pl.when(listens)
        @jax.named_scope("settle_" + g)
        def _():
            for k in range(planes):
                for b in range(2):
                    if k == 1 and (g, b) in ASIDE:
                        side_in(g, b).wait_recv()
                    elif k or g in ("att", "crs"):
                        cross_over(g, k, b).wait_recv()

    def exchange(e, i):
        q = strip(i, BLOCK)
        k = e % 2
        return push(send_v.at[k, q, :], recv_v.at[k, q, :], ex_sent.at[e, i], ex_got.at[e, i], at.twin)

    def joined(e, i):
        q = strip(i, BLOCK)
        exchange(e, i).wait_recv()
        return send_v[e % 2, q, :].astype(WIDE) + recv_v[e % 2, q, :].astype(WIDE)

    def sent(e):
        each(tiles, lambda i: exchange(e, i).wait_send())

    pump(3)
    for k in range(2):
        goal = s_v.at[strip(2 * c + k, rows), :]
        push(goal, goal, row_sent.at[0], row_got.at[k], at.twin).wait_recv()
    half, far_half = half_of(c), half_of(1 - c)
    rows_on = push(s_v.at[half, :], s_v.at[half, :], fwd_sem.at[0], fwd_sem.at[1], at.twin)
    rows_on.start()
    push(gain_in, gain_in_v.at[1 - c], gain_sem.at[0], gain_sem.at[1], at.twin).wait_recv()
    gain_here = pltpu.make_async_copy(gain_in, gain_in_v.at[c], gain_sem.at[2])
    gain_here.start()
    gain_here.wait()
    gains = gain_in_v[r].astype(WIDE)
    g0, g1, g2 = gains[0:1, :], gains[1:2, :], gains[2:3, :]
    gain_v[...] = jnp.zeros_like(gain_v)
    push(s_v.at[far_half, :], s_v.at[far_half, :], fwd_sem.at[0], fwd_sem.at[1], at.twin).wait_recv()
    x_put = copying("x", s_v, x_k)
    x_put.start()

    def enter(i):
        q = strip(i, BLOCK)
        c_v[q, :] = (center(s_v[q, :].astype(WIDE))[0] * g0).astype(LOW)

    each(tiles, enter)
    first_put = copying("first", c_v, first_k)
    first_put.start()
    pump(1)
    settle("att")

    def project(source, weights, part):
        def project_rows(n):
            b, q = lax.rem(n, 2), strip(lax.div(n, 2), BLOCK)
            if part != "kv":
                a_v[b, q, 0:256] = mm(source[q, :], weights[b, :, 0:256]).astype(LOW)
            if part != "q":
                a_v[b, q, 256:640] = mm(source[q, :], weights[b, :, 384:768]).astype(LOW)

        each(2 * tiles, project_rows)

    packed_v = a_v.at[:, :, 0:640]
    project(c_v, att_v, "all")
    pass_aside("up")
    p_put = copying("p", packed_v, p_k)
    p_put.start()
    o_v[...] = jnp.zeros_like(o_v)
    lse_v[...] = jnp.zeros_like(lse_v)
    pump(1)

    def attend_heads(bias, causal, hooks):
        def head_forward(n):
            b = lax.div(n, 3)
            attend_block(lax.rem(n, 3), a_v.at[b], o_v.at[b], lse_v, n, bias, kx, qx, kt_v, causal)
            for when, event in hooks:
                pl.when(both(n == when, relay))(event)

        each(6, head_forward)

    enc_hooks = [(2, enc_events.pop(0)), (5, enc_events.pop(0))]
    dec_hooks = [(2, dec_events.pop(0)), (4, dec_events.pop(0))]
    pl.when(at.encodes)(lambda: attend_heads(bias_self, False, enc_hooks))
    pl.when(at.decodes)(lambda: attend_heads(bias_self, True, dec_hooks))
    o_put, lse_put = copying("o", o_v, o_k), copying("lse", lse_v, lse_k)
    o_put.start()
    lse_put.start()

    def out_project(e, weights):
        def out_rows(i):
            q = strip(i, BLOCK)
            part = mm_nt(o_v[0, q, :], weights[0, :, 128:384]) + mm_nt(o_v[1, q, :], weights[1, :, 128:384])
            send_v[e % 2, q, :] = part.astype(LOW)
            exchange(e, i).start()

        each(tiles, out_rows)

    out_project(0, att_v)
    pump(1)
    x_put.wait()
    pass_aside("dn")
    rows_on.wait_send()

    def middle(i):
        q = strip(i, BLOCK)
        value = s_v[q, :].astype(WIDE) + joined(0, i)
        mid_v[q, :] = value
        s_v[q, :] = (center(value)[0] * g1).astype(LOW)

    each(tiles, middle)
    first_put.wait()
    p_put.wait()
    o_put.wait()
    lse_put.wait()

    def mem_send(i):
        q = pl.ds(pl.multiple_of((2 * c + i) * BLOCK, BLOCK), BLOCK)
        return push(g_v.at[q, :], g_v.at[q, :], mem_sent.at[i], mem_got.at[i], at.beside)

    def mem_forward(i, core):
        q = pl.ds(pl.multiple_of((2 * core + i) * BLOCK, BLOCK), BLOCK)
        return push(g_v.at[q, :], g_v.at[q, :], mf_sent.at[i], mf_got.at[i], at.twin)

    def row_home(k, source, goal, sent_by, got):
        dev = (r, z, 2 * c + k)
        keeps = both(both(c == r, y == c), r == k)
        return keeps, source, goal.at[y], sent_by.at[k], got.at[y], dev

    def go_home(*spec):
        keeps, source, goal, sent_by, got, dev = row_home(*spec)

        @pl.when(keeps)
        def _():
            pltpu.make_async_copy(source, goal, got).start()

        @pl.when(jnp.logical_not(keeps))
        def _():
            push(source, goal, sent_by, got, dev).start()

    def went_home(*spec):
        keeps, source, goal, sent_by, got, dev = row_home(*spec)

        @pl.when(jnp.logical_not(keeps))
        def _():
            push(source, goal, sent_by, got, dev).wait_send()

    def memory_home(k):
        return k, memory_k.at[strip(2 * c + k, rows), :], block_out, blk_sent, blk_got

    settle_up = lambda: settle("up")
    pl.when(at.encodes)(settle_up)

    @pl.when(at.encodes)
    def _():
        def up_rows(n):
            b, q = lax.rem(n, 2), strip(lax.div(n, 2), BLOCK)
            value, grade = gelu_parts(mm(s_v[q, :], up_v[b]))
            a_v[b, q, :] = value.astype(LOW)
            b_v[b, q, :] = grade.astype(LOW)

        each(2 * tiles, up_rows)

    pump_enc(9)

    @pl.when(at.encodes)
    def _():
        settle("dn")

        def down_rows(i):
            q = strip(i, BLOCK)
            part = mm_nt(a_v[0, q, :], dn_v[0]) + mm_nt(a_v[1, q, :], dn_v[1])
            send_v[1, q, :] = part.astype(LOW)
            exchange(1, i).start()

        each(tiles, down_rows)

        def finish(n):
            i = lax.rem(n + 2 * c, 4)
            q = strip(i, BLOCK)
            value = mid_v[q, :] + joined(1, i)
            late_v[q, :] = value
            g_v[q, :] = (center(value)[0] * g2).astype(LOW)

            @pl.when(n < 2)
            def _():
                mem_send(n).start()

        each(tiles, finish)
        keep = copying("memory", g_v, memory_k)
        keep.start()
        keep.wait()
        for k in range(2):
            go_home(*memory_home(k))
        sent(0)

    def norm_grad(values, gain, grad, gain_row, counted):
        normal, scale = center(values)
        scaled = grad * gain
        one = jnp.mean(scaled, axis=-1, keepdims=True)
        two = jnp.mean(scaled * normal, axis=-1, keepdims=True)
        total = jnp.sum(grad * normal, axis=0, keepdims=True)
        gain_v[gain_row : gain_row + 1, :] += jnp.where(counted, total, 0.0)
        return (scaled - one - normal * two) * scale

    def ours(i):
        return lax.div(i, 2) == c

    @pl.when(at.decodes)
    def _():
        second_put = copying("second", s_v, second_k)
        second_put.start()
        for k in range(2):
            goal = cot.at[strip(2 * c + k, rows), :]
            push(goal, goal, row_sent.at[2], cot_got.at[k], at.twin).wait_recv()
        cot_on = push(cot.at[half, :], cot.at[half, :], fwd_sem.at[2], fwd_sem.at[3], at.twin)
        cot_on.start()
        for _ in range(len(dec_events) - 3):
            pl.when(relay)(dec_events.pop(0))
        settle("crs")
        project(s_v, crs_v, "q")
        pl.when(relay)(dec_events.pop(0))
        pl.when(relay)(dec_events.pop(0))
        push(cot.at[far_half, :], cot.at[far_half, :], fwd_sem.at[2], fwd_sem.at[3], at.twin).wait_recv()
        cot_in_v = copying("cot", cot, c_v)
        cot_in_v.start()
        o_v[...] = jnp.zeros_like(o_v)
        lse_v[...] = jnp.zeros_like(lse_v)
        for i in range(2):
            mem_send(i).wait_recv()
            mem_forward(i, c).start()
        for i in range(2):
            mem_forward(i, 1 - c).wait_recv()
        project(g_v, crs_v, "kv")
        puts = [copying("pc", packed_v, pc_k), copying("memory", g_v, memory_k)]
        for copy in puts:
            copy.start()
        attend_heads(bias_cross, False, [(0, dec_events.pop(0))])
        puts += [copying("oc", o_v, oc_k), copying("lsec", lse_v, lsec_k)]
        for copy in puts[2:]:
            copy.start()
        out_project(1, crs_v)
        second_put.wait()

        def finish(i):
            q = strip(i, BLOCK)
            value = mid_v[q, :] + joined(1, i)
            late_v[q, :] = value
            s_v[q, :] = (center(value)[0] * g2).astype(LOW)

        each(tiles, finish)
        late_put = copying("late", late_v, late_k)
        late_put.start()
        settle("up")
        settle("dn")
        cot_in_v.wait()
        sent(0)
        for copy in puts:
            copy.wait()

        def feed_rows(i):
            q = strip(i, BLOCK)

            def feed_half(b):
                value, grade = gelu_parts(mm(s_v[q, :], up_v[b]))
                a_v[b, q, :] = value.astype(LOW)
                b_v[b, q, :] = (mm(c_v[q, :], dn_v[b]) * grade).astype(LOW)

            each(2, feed_half)
            part = mm_nt(b_v[0, q, :], up_v[0]) + mm_nt(b_v[1, q, :], up_v[1])
            send_v[0, q, :] = part.astype(LOW)
            exchange(2, i).start()

        each(tiles, feed_rows)
        copying("act", a_v, act_k).start()
        late_put.wait()
        cot_on.wait_send()
        each(2, lambda i: mem_forward(i, c).wait_send())

    def block_of(k):
        return lax.rem(z - 1 - k + 2 * planes, planes)

    def y_hop(g, k, b):
        i = SUMS.index(g)
        return push(dw[g].at[k, b], yb[g].at[k, b], y_sent.at[i, k, b], y_got.at[i, k, b], at.across)

    def z_hop(g, k, b):
        i = SUMS.index(g)
        return push(res[g].at[b], zb[g].at[k, b], z_sent.at[i, k, b], z_got.at[i, k, b], at.above)

    def via_hop(k):
        diagonal = (c, z, lax.rem(t + 2, 4) + 1 - 2 * r)
        return push(dw_att.at[k, 1], via_att.at[k], via_sent.at[k], via_got.at[k], diagonal)

    def hand_on(k):
        return push(via_att.at[k], yb_att.at[k, 1], hand_sent.at[k], hand_got.at[k], at.beside)

    def leave(g, k):
        @pl.when(other)
        def _():
            y_hop(g, k, 0).start()
            if g == "att":
                pl.when(at.decodes)(lambda: y_hop(g, k, 1).start())
                pl.when(at.encodes)(lambda: via_hop(k).start())
            else:
                y_hop(g, k, 1).start()

    def emit(g, compute):
        columns = dw[g].shape[3]

        def put(k, s):
            return pltpu.make_async_copy(dw_st.at[s, :, :, 0:columns], dw[g].at[k], dw_sem.at[s])

        def run(k):
            s = lax.rem(k, 2)
            j = block_of(k)
            compute(s, pl.ds(pl.multiple_of(j * depth, depth), depth))
            put(k, s).start()

            @pl.when(k >= 1)
            def _():
                put(k - 1, 1 - s).wait()
                leave(g, k - 1)

        each(planes, run, "emit_" + g)
        put(planes - 1, (planes - 1) % 2).wait()
        leave(g, planes - 1)

    def home_copy(g, b, section):
        i = SUMS.index(g)
        columns = dw[g].shape[3]
        source = res[g].at[b]
        if g == "crs":
            source = source.at[:, pl.ds((1 - section) * (columns // 2), columns // 2)]
        device = (section, z, 2 * y + b)
        keeps = both(c == section, r == b)
        return keeps, source, push(source, home[g], home_sent.at[i, b, section if g == "crs" else 0], home_got.at[i], device)

    def sections(g):
        return (0, 1) if g == "crs" else (r,)

    def sum_at(g, n):
        i = SUMS.index(g)
        columns = dw[g].shape[3]
        k, b = lax.div(n, 2), lax.rem(n, 2)

        def fetch(m, source):
            return pltpu.make_async_copy(source, sum_st.at[m, :, 0:columns], sum_sem.at[m])

        @pl.when(relay)
        @jax.named_scope("sum_" + g)
        def _():
            before = lax.max(k - 1, 0)
            if g == "att":
                detour = both(at.encodes, b == 1)
                pl.when(detour)(lambda: hand_on(k).wait_recv())
                pl.when(jnp.logical_not(detour))(lambda: y_hop(g, k, b).wait_recv())
            else:
                y_hop(g, k, b).wait_recv()
            fetch(0, dw[g].at[k, b]).start()
            fetch(1, yb[g].at[k, b]).start()

            @pl.when(k > 0)
            def _():
                z_hop(g, before, b).wait_recv()
                fetch(2, zb[g].at[before, b]).start()
                z_hop(g, before, b).wait_send()
                fetch(2, zb[g].at[before, b]).wait()

            fetch(0, dw[g].at[k, b]).wait()
            fetch(1, yb[g].at[k, b]).wait()
            share = depth // 4

            def add_rows(m):
                q = strip(m, share)
                total = sum_st[0, q, 0:columns].astype(WIDE) + sum_st[1, q, 0:columns].astype(WIDE)
                total = total + jnp.where(k > 0, sum_st[2, q, 0:columns].astype(WIDE), 0.0)
                res[g][b, q, :] = total.astype(LOW)

            each(4, add_rows)

            @pl.when(k + 1 < planes)
            def _():
                z_hop(g, k, b).start()

            @pl.when(k + 1 == planes)
            def _():
                for section in sections(g):
                    keeps, source, copy = home_copy(g, b, section)

                    @pl.when(keeps)
                    def _():
                        pltpu.make_async_copy(source, home[g], home_got.at[i]).start()

                    @pl.when(jnp.logical_not(keeps))
                    def _():
                        copy.start()

    def sums(g, first_step, count):
        each(count, lambda n: sum_at(g, first_step + n), "sums_" + g)

    def turn(source, goal):
        def run(i):
            q = strip(i, BLOCK)
            goal[:, q] = source[q, :].astype(WIDE).T.astype(LOW)

        each(tiles, run, "turn")

    def dm_hop(n, source):
        q = pl.ds(pl.multiple_of((2 * c + n) * BLOCK, BLOCK), BLOCK)
        return push(source.at[q, :], c_v.at[q, :], dm_sent.at[n], dm_got.at[n], at.beside)

    def df_hop(n, core):
        q = pl.ds(pl.multiple_of((2 * core + n) * BLOCK, BLOCK), BLOCK)
        return push(c_v.at[q, :], c_v.at[q, :], df_sent.at[n], df_got.at[n], at.twin)

    @pl.when(at.encodes)
    def _():
        turn(s_v, ta)

        def back_rows(m):
            n = lax.div(m, 2)
            own = lax.rem(m, 2) == 0
            i = jnp.where(own, 2 * c + n, 2 * (1 - c) + n)
            q = strip(i, BLOCK)

            @pl.when(own)
            def _():
                dm_hop(n, c_v).wait_recv()
                df_hop(n, c).start()

            @pl.when(jnp.logical_not(own))
            def _():
                df_hop(n, 1 - c).wait_recv()

            grad = norm_grad(late_v[q, :], g2, c_v[q, :].astype(WIDE), 2, ours(i))
            late_v[q, :] = grad
            low = grad.astype(LOW)
            part = None
            for b in range(2):
                d_pre = (mm(low, dn_v[b]) * b_v[b, q, :].astype(WIDE)).astype(LOW)
                b_v[b, q, :] = d_pre
                term = mm_nt(d_pre, up_v[b])
                part = term if part is None else part + term
            send_v[0, q, :] = part.astype(LOW)

            @pl.when(own)
            def _():
                df_hop(n, c).wait_send()

            c_v[q, :] = low
            exchange(2, i).start()

        each(tiles, back_rows)

    pl.when(at.decodes)(lambda: turn(s_v, ta))
    turn(c_v, tb)

    def ffn_block(s, j):
        def ffn_half(b):
            dw_st[s, b, :, 0:768] = mm(ta[j, :], b_v[b]).astype(LOW)
            dw_st[s, b, :, 768:1536] = mm(tb[j, :], a_v[b]).astype(LOW)

        each(2, ffn_half)

    emit("ffn", ffn_block)

    @pl.when(at.decodes)
    def _():
        copying("act", a_v, act_k).wait()
        packed = copying("pc", pc_k, packed_v)
        small = [copying("oc", oc_k, o_v), copying("lsec", lsec_k, lse_v), copying("second", second_k, s_v)]
        packed.start()
        for copy in small:
            copy.start()

        def late_rows(i):
            q = strip(i, BLOCK)
            grad = c_v[q, :].astype(WIDE) + norm_grad(late_v[q, :], g2, joined(2, i), 2, ours(i))
            late_v[q, :] = grad
            g_v[q, :] = grad.astype(LOW)

        each(tiles, late_rows)

        def cross_out(i):
            q = strip(i, BLOCK)
            for b in range(2):
                do_v[b, q, :] = mm(g_v[q, :], crs_v[b, :, 128:384]).astype(LOW)

        each(tiles, cross_out)
        for copy in small:
            copy.wait()
        packed.wait()
        b_v[...] = jnp.zeros_like(b_v)

        def cross_head(n):
            b = lax.div(n, 3)
            attend_back_block(
                lax.rem(n, 3), a_v.at[b], o_v.at[b], do_v.at[b], b_v.at[b], lse_v, n, bias_cross,
                kx, qx, vx, gx, kt_v, dk_v, dv_v, False,
            )

        each(6, cross_head)
        sent(1)

        def to_memory(q):
            return mm_nt(b_v[0, q, 256:640], crs_v[0, :, 384:768]) + mm_nt(b_v[1, q, 256:640], crs_v[1, :, 384:768])

        def far(n):
            i = 2 * (1 - c) + n
            q = strip(i, BLOCK)
            send_v[1, q, :] = to_memory(q).astype(LOW)
            exchange(3, i).start()

        each(2, far)

        def near(n):
            i = 2 * c + n
            q = strip(i, BLOCK)
            part = to_memory(q)
            exchange(3, i).wait_recv()
            send_v[1, q, :] = (part + recv_v[1, q, :].astype(WIDE)).astype(LOW)
            dm_hop(n, send_v.at[1]).start()

        each(2, near)

        def to_query(i):
            q = strip(i, BLOCK)
            part = mm_nt(b_v[0, q, 0:256], crs_v[0, :, 0:256]) + mm_nt(b_v[1, q, 0:256], crs_v[1, :, 0:256])
            send_v[0, q, :] = part.astype(LOW)
            exchange(4, i).start()

        sent(2)
        each(tiles, to_query)
        sums("ffn", 0, 2)
        turn(s_v, ta)
        stage_in = copying("memory", memory_k, s_v)
        stage_in.start()
        turn(g_v, tc)
        stage_in.wait()
        turn(s_v, tb)
        copying("first", first_k, s_v).start()

        def crs_block(s, j):
            def att_half(b):
                left = mm(ta[j, :], b_v[b, :, 0:256])
                out = mm(tc[j, :], o_v[b])
                dw_st[s, b, :, 0:128] = left[:, 0:128].astype(LOW)
                dw_st[s, b, :, 128:256] = (left[:, 128:256] + out[:, 0:128]).astype(LOW)
                dw_st[s, b, :, 256:384] = out[:, 128:256].astype(LOW)
                dw_st[s, b, :, 384:768] = mm(tb[j, :], b_v[b, :, 256:640]).astype(LOW)

            each(2, att_half)

        emit("crs", crs_block)
        sums("ffn", 2, 2)

        def below(i):
            q = strip(i, BLOCK)
            grad = late_v[q, :] + norm_grad(mid_v[q, :], g1, joined(4, i), 1, ours(i))
            late_v[q, :] = grad
            g_v[q, :] = grad.astype(LOW)

        each(tiles, below)
        copying("first", first_k, s_v).wait()

        def gone(n):
            exchange(3, 2 * (1 - c) + n).wait_send()
            dm_hop(n, send_v.at[1]).wait_send()

        each(2, gone)

    @pl.when(at.encodes)
    def _():
        copying("first", first_k, s_v).start()
        each(2, lambda i: mem_send(i).wait_send())

        def below(i):
            q = strip(i, BLOCK)
            grad = late_v[q, :] + norm_grad(mid_v[q, :], g1, joined(2, i), 1, ours(i))
            late_v[q, :] = grad
            g_v[q, :] = grad.astype(LOW)

        each(tiles, below)
        copying("first", first_k, s_v).wait()
        sent(1)

    packed = copying("p", p_k, packed_v)
    small = [copying("o", o_k, o_v), copying("lse", lse_k, lse_v)]
    packed.start()
    for copy in small:
        copy.start()

    def self_out(i):
        q = strip(i, BLOCK)
        for b in range(2):
            do_v[b, q, :] = mm(g_v[q, :], att_v[b, :, 128:384]).astype(LOW)

    each(tiles, self_out)
    b_v[...] = jnp.zeros_like(b_v)
    for copy in small:
        copy.wait()
    packed.wait()

    def self_heads(causal, hook):
        def self_head(n):
            b = lax.div(n, 3)
            attend_back_block(
                lax.rem(n, 3), a_v.at[b], o_v.at[b], do_v.at[b], b_v.at[b], lse_v, n, bias_self,
                kx, qx, vx, gx, kt_v, dk_v, dv_v, causal,
            )
            hook(n)

        each(6, self_head)

    def enc_hook(n):
        @pl.when(jnp.logical_and(n != 2, n != 5))
        def _():
            sum_at("ffn", n - lax.div(n, 3))

    def dec_hook(n):
        @pl.when(n < 4)
        def _():
            sum_at("ffn", 4 + n)

        @pl.when(n >= 4)
        def _():
            sum_at("crs", n - 4)

    pl.when(at.encodes)(lambda: self_heads(False, enc_hook))
    pl.when(at.decodes)(lambda: self_heads(True, dec_hook))

    def to_rows(q):
        part = None
        for b in range(2):
            term = mm_nt(b_v[b, q, 0:256], att_v[b, :, 0:256]) + mm_nt(b_v[b, q, 256:640], att_v[b, :, 384:768])
            part = term if part is None else part + term
        return part

    def far_rows(n):
        i = 2 * (1 - c) + n
        q = strip(i, BLOCK)
        send_v[1, q, :] = to_rows(q).astype(LOW)
        exchange(5, i).start()

    each(2, far_rows)
    pl.when(at.encodes)(lambda: sums("ffn", 4, 2))
    pl.when(at.decodes)(lambda: sums("crs", 2, 2))
    turn(s_v, ta)
    x_in_v = copying("x", x_k, s_v)
    x_in_v.start()
    turn(g_v, tc)

    def att_block(s, j):
        def att_half(b):
            left = mm(ta[j, :], b_v[b, :, 0:256])
            out = mm(tc[j, :], o_v[b])
            dw_st[s, b, :, 0:128] = left[:, 0:128].astype(LOW)
            dw_st[s, b, :, 128:256] = (left[:, 128:256] + out[:, 0:128]).astype(LOW)
            dw_st[s, b, :, 256:384] = out[:, 128:256].astype(LOW)
            dw_st[s, b, :, 384:768] = mm(ta[j, :], b_v[b, :, 256:640]).astype(LOW)

        each(2, att_half)

    emit("att", att_block)
    pl.when(at.decodes)(lambda: sums("crs", 4, 2))
    x_in_v.wait()

    def near_rows(n):
        i = 2 * c + n
        q = strip(i, BLOCK)
        part = to_rows(q)
        exchange(5, i).wait_recv()
        grad = part + recv_v[1, q, :].astype(WIDE)
        value = late_v[q, :] + norm_grad(s_v[q, :].astype(WIDE), g0, grad, 0, True)
        out_st[strip(n, BLOCK), :] = value.astype(LOW)

    each(2, near_rows)
    out_put = copying("out", out_st, grad_k)
    out_put.start()
    out_put.wait()

    def grad_home(k):
        return k, grad_k.at[strip(k, rows), :], grad_low, gr_sent, gr_got

    def rows_leave():
        for k in range(2):
            go_home(*grad_home(k))

    pl.when(relay)(rows_leave)

    def gain_hop(n, source, device):
        return push(source, gain_buf.at[n], gr_hop_sent.at[n], gr_hop_got.at[n], device)

    gain_buf[0] = gain_v[...]
    twin_hop = gain_hop(1, gain_buf.at[0], at.twin)
    twin_hop.start()
    twin_hop.wait()
    peer_hop = gain_hop(3, gain_buf.at[2], (1 - c, z, lax.rem(t + 2, 4)))
    last = 4 + planes

    @pl.when(relay)
    def _():
        gain_buf[2] = gain_buf[0] + gain_buf[1]
        peer_hop.start()

    def ring_hop(n):
        return gain_hop(5 + n, gain_buf.at[4 + n], at.above)

    def gain_step(n):
        @pl.when(relay)
        @jax.named_scope("gains")
        def _():
            if n == 0:
                peer_hop.wait()
                gain_buf[4] = gain_buf[2] + gain_buf[3]
            else:
                ring_hop(n - 1).wait()
            if n < planes - 1:
                ring_hop(n).start()
            else:
                total = None
                for j in range(planes):
                    held = gain_buf[jnp.where(z == j, 4, 5 + lax.rem(z - 1 - j + planes, planes))]
                    total = held if total is None else total + held
                gain_buf[last] = total
                for b in range(2):
                    keeps = both(c == r, r == b)

                    @pl.when(keeps)
                    def _():
                        pltpu.make_async_copy(gain_buf.at[last], gain_buf.at[last + 1], gr_hop_got.at[last + 1]).start()

                    @pl.when(jnp.logical_not(keeps))
                    def _():
                        final_hop(b).start()

    def final_hop(b):
        return push(
            gain_buf.at[last], gain_buf.at[last + 1], gr_hop_sent.at[last + b], gr_hop_got.at[last + 1],
            (r, z, 2 * y + b),
        )

    def y3_home(k):
        return k, y3_k.at[strip(k, rows), :], block_out, blk_sent, blk_got

    def out_leaves():
        for k in range(2):
            go_home(*y3_home(k))

    @pl.when(at.decodes)
    def _():
        @pl.when(relay)
        @jax.named_scope("hand_on")
        def _():
            for k in range(planes):
                via_hop(k).wait_recv()
                hand_on(k).start()

        sums("att", 0, 2)
        copies = [copying("act", act_k, a_v), copying("late", late_k, mid_v)]
        for copy in copies:
            copy.start()
        sent(4)
        for copy in copies:
            copy.wait()

        def to_out(q):
            return mm_nt(a_v[0, q, :], dn_v[0]) + mm_nt(a_v[1, q, :], dn_v[1])

        def far_out(n):
            i = 2 * (1 - c) + n
            q = strip(i, BLOCK)
            send_v[0, q, :] = to_out(q).astype(LOW)
            exchange(6, i).start()

        each(2, far_out)

        def near_out(n):
            i = 2 * c + n
            q = strip(i, BLOCK)
            part = to_out(q)
            exchange(6, i).wait_recv()
            out_st[strip(n, BLOCK), :] = (mid_v[q, :] + part + recv_v[0, q, :].astype(WIDE)).astype(LOW)

        each(2, near_out)
        y3_put = copying("out", out_st, y3_k)
        y3_put.start()
        y3_put.wait()
        pl.when(relay)(out_leaves)

    @pl.when(other)
    def _():
        for k in range(planes):
            y_hop("att", k, 0).wait_send()
            pl.when(at.decodes)(lambda: y_hop("att", k, 1).wait_send())
            pl.when(at.encodes)(lambda: via_hop(k).wait_send())
        rows_leave()
        pl.when(at.decodes)(out_leaves)

    pl.when(at.encodes)(lambda: sums("ffn", 6, 2))
    pl.when(at.decodes)(lambda: sums("crs", 6, 2))

    def last_sums(n):
        @pl.when(jnp.logical_or(at.encodes, n >= 2))
        def _():
            sum_at("att", n)

        for m in range(planes):
            pl.when(n == 2 * m)(functools.partial(gain_step, m))

    each(2 * planes, last_sums)

    with jax.named_scope("await_gains"):
        final = gain_buf.at[last + 1]
        push(gain_buf.at[last], final, gr_hop_sent.at[last], gr_hop_got.at[last + 1], at.twin).wait_recv()
    gains_home = copying("gains", final, gain_out)
    gains_home.start()
    with jax.named_scope("await_rows"):
        for n in range(2):
            for goal, got in ((block_out, blk_got), (grad_low, gr_got)):
                push(goal.at[n], goal.at[n], blk_sent.at[0], got.at[n], at.twin).wait_recv()
    for i, g in enumerate(SUMS):
        with jax.named_scope("await_home_" + g):
            push(home[g], home[g], home_sent.at[i, 0, 0], home_got.at[i], at.twin).wait_recv()
    gains_home.wait()
    for k in range(2):
        went_home(*grad_home(k))

    @pl.when(at.encodes)
    def _():
        for k in range(2):
            went_home(*memory_home(k))
        sent(2)

    @pl.when(at.decodes)
    def _():
        for k in range(2):
            went_home(*y3_home(k))
        each(2, lambda n: exchange(6, 2 * (1 - c) + n).wait_send())

    each(2, lambda n: exchange(5, 2 * (1 - c) + n).wait_send())

    @pl.when(relay)
    def _():
        for b in range(2):
            pl.when(jnp.logical_not(both(c == r, r == b)))(lambda: final_hop(b).wait_send())

    for g in SUMS:
        there = at.decodes if g == "crs" else jnp.logical_or(at.decodes, at.encodes)

        if g != "att":

            @pl.when(both(other, there))
            def _():
                for k in range(planes):
                    for b in range(2):
                        y_hop(g, k, b).wait_send()

        @pl.when(both(relay, there))
        def _():
            for b in range(2):
                for section in sections(g):
                    keeps, source, copy = home_copy(g, b, section)

                    @pl.when(jnp.logical_not(keeps))
                    def _():
                        copy.wait_send()

    @pl.when(both(relay, at.decodes))
    def _():
        for k in range(planes):
            hand_on(k).wait_send()

    gain_copy.wait_send()
    for g in DIRECT:
        launch_over(g).wait_send()

    @pl.when(jnp.logical_not(stays))
    def _():
        for g in ("att", "up", "dn"):
            push(shard[g], vmem[g].at[r, here, :], x_sent.at[GROUPS.index(g)], x_sem.at[0, 0], relay_dev).wait_send()

    @pl.when(jnp.logical_not(crs_stays))
    def _():
        push(crs_in, crs_goal(r, c), x_sent.at[1], c_sem.at[0, 0], crs_dev).wait_send()
        push(cot_in.at[c], cot_goal, row_sent.at[2], cot_got.at[r], at.twin).wait_send()

    for s in range(2):

        @pl.when(jnp.logical_not(row_stays(s)))
        def _():
            push(x_in.at[s], row_goal, row_sent.at[s], row_got.at[r], at.twin).wait_send()

    for g in GROUPS:
        member = both(relay, at.decodes) if g == "crs" else relay

        @pl.when(member)
        def _():
            for k in range(planes):
                for b in range(2):
                    if k:
                        ring(g, k, b).wait_send()
                    if (k or g not in DIRECT) and (k != 1 or (g, b) not in ASIDE):
                        cross_over(g, k, b).wait_send()

    @pl.when(other)
    def _():
        for g, b in ASIDE:
            side_hop(g, b).wait_send()


def block_call(planes, slot, width, hidden, depth, args):
    shape = jax.ShapeDtypeStruct
    rows = slot // 4
    square = (slot, width)
    wides = {"ffn": 2 * hidden, "crs": width, "att": width}
    packed, outs, logs, acts = (2, slot, 640), (2, slot, 256), (8, slot), (2, slot, hidden)
    out_shape = (
        [shape((2, rows, width), LOW)] * 2
        + [shape((depth, 2 * hidden), LOW), shape((depth, width // 2), LOW), shape((depth, width), LOW)]
        + [shape((8, width), WIDE)]
        + [shape(square, LOW)] * 4
        + [shape(square, WIDE), shape(square, LOW)]
        + [shape(packed, LOW), shape(outs, LOW), shape(logs, WIDE)] * 2
        + [shape(acts, LOW)]
        + [shape((2 * rows, width), LOW)] * 2
        + [shape((planes, 2, depth, wides[g]), LOW) for g in SUMS] * 3
        + [shape((planes, depth, width), LOW)]
    )
    dma = pltpu.SemaphoreType.DMA
    v = pltpu.VMEM
    groups = len(GROUPS)
    scratch = (
        [v((2, width, width), LOW)] * 2
        + [v((2, width, hidden), LOW)] * 2
        + [v(acts, LOW)] * 2
        + [v(outs, LOW)] * 2
        + [v(square, WIDE)] * 2
        + [v(square, LOW)] * 3
        + [v((width, slot), LOW)] * 3
        + [v((2,) + square, LOW)] * 2
        + [v((slot, TILE), LOW)] * 4
        + [v((slot, TILE), WIDE)] * 2
        + [v((TILE, slot), LOW), v(logs, WIDE), v((8, width), WIDE), v((2, 3, width), LOW)]
        + [v((planes + 6, 8, width), WIDE)]
        + [v((2 * rows, width), LOW), v((2, 2, depth, 2 * hidden), LOW), v((3, depth, 2 * hidden), LOW)]
        + [v((slot, TILE), LOW)] * 2
        + [v((2, depth, wides[g]), LOW) for g in SUMS]
        + [dma((groups, 2)), dma((groups,)), dma((groups,)), dma((2, 2))]
        + [dma((groups, planes, 2))] * 4
        + [dma((groups, 2))] * 2
        + [dma((2,)), dma((3,)), dma((4,)), dma((2,)), dma((3,)), dma((40,)), dma((7, 4)), dma((7, 4))]
        + [dma((2,))] * 8
        + [dma((3, planes, 2))] * 4
        + [dma((3,)), dma((3, 2, 2))]
        + [dma((2,))] * 4
        + [dma((planes + 6,))] * 2
        + [dma((3,)), dma((2,))]
        + [dma((planes,))] * 4
    )
    any_spec = pl.BlockSpec(memory_space=pl.ANY)
    vmem_spec = pl.BlockSpec(memory_space=pltpu.VMEM)
    return pl.pallas_call(
        functools.partial(block_kernel, planes),
        out_shape=out_shape,
        in_specs=[any_spec] * 6 + [vmem_spec, pl.BlockSpec(memory_space=pltpu.SMEM), vmem_spec],
        out_specs=[any_spec] * len(out_shape),
        scratch_shapes=scratch,
        compiler_params=pltpu.CompilerParams(collective_id=0, has_side_effects=True, vmem_limit_bytes=VMEM_BYTES),
    )(*args)


def widen_kernel(
    block_in, grad_in, ffn_in, crs_in, att_in, gain_in,
    block_out, grad_out, up_out, dn_out, qkv_out, out_out, crs_out, gain_out, last_out,
):
    c = lax.axis_index("section")
    hidden = up_out.shape[1]
    share, part = block_in.shape[1] // 4, ffn_in.shape[0] // 4

    def strips(i):
        q = strip(i, share)
        for n in range(2):
            block_out[n, q, :] = block_in[n, q, :]
            grad_out[n, q, :] = grad_in[n, q, :].astype(WIDE)
        q = strip(i, part)
        up_out[q, :] = ffn_in[q, 0:hidden].astype(WIDE)
        dn_out[q, :] = ffn_in[q, hidden : 2 * hidden].astype(WIDE)

    each(4, strips)
    tiles = [crs_in[:, TILE * n : TILE * (n + 1)].astype(WIDE) for n in range(3)]
    mixed = jnp.where(c == 1, tiles[1], tiles[2])
    crs_out[:, 0, 0:TILE] = tiles[0]
    crs_out[:, 0, TILE : TILE + HEAD] = mixed[:, 0:HEAD]
    crs_out[:, 1, 0:TILE] = jnp.where(c == 1, tiles[2], tiles[1])
    crs_out[:, 1, TILE : TILE + HEAD] = pltpu.roll(mixed, HEAD, 1)[:, 0:HEAD]
    q_tile, q_o, o_tile, k_tile, v_tile, k_v = (att_in[:, TILE * n : TILE * (n + 1)].astype(WIDE) for n in range(6))
    for n, (whole, rest) in enumerate(((q_tile, q_o), (k_tile, k_v), (v_tile, pltpu.roll(k_v, HEAD, 1)))):
        qkv_out[n, :, 0:TILE] = whole
        qkv_out[n, :, TILE : TILE + HEAD] = rest[:, 0:HEAD]
    out_out[0:TILE, :] = o_tile.T
    out_out[TILE : TILE + HEAD, :] = pltpu.roll(q_o, HEAD, 1).T[0:HEAD, :]
    gain_out[...] = gain_in[0:2, :]
    last_out[...] = gain_in[2:3, :]


def widen_call(kept):
    shape = jax.ShapeDtypeStruct
    rows, width = kept[0].shape[1:]
    depth, hidden = kept[2].shape[0], kept[2].shape[1] // 2
    wide = width // 4
    return pl.pallas_call(
        widen_kernel,
        out_shape=[
            shape((2, rows, width), LOW), shape((2, rows, width), WIDE), shape((depth, hidden), WIDE),
            shape((depth, hidden), WIDE), shape((3, depth, wide), WIDE), shape((wide, depth), WIDE),
            shape((depth, 2, wide), WIDE), shape((2, width), WIDE), shape((1, width), WIDE),
        ],
    )(*kept)


def ring_gather(lay, shard):
    planes = lay.planes
    rows = shard.shape[1]
    if planes > 4:
        piece = lax.all_gather(shard, "dp", axis=1, tiled=True)
        across = lay.route(piece, lambda c, z, t: (c, z, (t + 2) % 4) if c == t // 2 else None)
        return jnp.where(lay.relays, piece, across)
    relay = lambda c, z, t: (c, (z + 1) % planes, t) if c == t // 2 else None
    whole = jnp.zeros((shard.shape[0], planes * rows, shard.shape[2]), shard.dtype)
    piece = shard
    for step in range(planes):
        across = lay.route(piece, lambda c, z, t: (c, z, (t + 2) % 4) if c == t // 2 else None)
        chosen = jnp.where(lay.relays, piece, across)
        whole = lax.dynamic_update_slice(whole, chosen, (0, ((lay.plane - step) % planes) * rows, 0))
        if step + 1 < planes:
            piece = lay.route(piece, relay)
    return whole


def ring_scatter(lay, total, holder):
    planes = lay.planes
    rows = total.shape[1] // planes
    low = total.astype(LOW)
    across = lay.route(
        low, lambda c, z, t: (c, z, (t + 2) % 4) if (c != t // 2 and t % 2 == holder) else None
    )
    summed = low.astype(WIDE) + across.astype(WIDE)
    if planes > 4:
        return lax.psum_scatter(summed.astype(LOW), "dp", scatter_dimension=1, tiled=True)
    relay = lambda c, z, t: (c, (z + 1) % planes, t) if (c == t // 2 and t % 2 == holder) else None
    take = lambda j: lax.dynamic_slice_in_dim(summed, (j % planes) * rows, rows, 1)
    running = take(lay.plane - 1)
    for step in range(1, planes):
        running = lay.route(running.astype(LOW), relay).astype(WIDE) + take(lay.plane - 1 - step)
    return running.astype(LOW)


def hand_back(lay, value, holder, section):
    same = lay.route(
        value[0], lambda c, z, t: (section, z, t) if (c == t // 2 and t % 2 == holder) else None
    )
    beside = lay.route(
        value[1], lambda c, z, t: (section, z, t ^ 1) if (c == t // 2 and t % 2 == holder) else None
    )
    return same.astype(WIDE) + beside.astype(WIDE)


def general_body(block_input, w_self, w_self_out, w_cross, w_up, w_down, norm_gains, lengths, task_mask, out_grad):
    lay = Layout()
    seqs, rows, width = block_input.shape[1:]
    slot = rows * lay.chips
    sec = lay.core
    item = lay.item

    def spread(value, first):
        pick = value[jnp.where(first, lay.chip % 2, 1 - lay.chip % 2)]
        flip = 0 if first else 1
        return lay.route(pick, lambda c, z, t: (t // 2, z, 2 * ((t % 2) ^ flip) + c))

    def merge_rows(mine, theirs):
        low_half = jnp.where(lay.core == 0, mine, theirs)
        high_half = jnp.where(lay.core == 0, theirs, mine)
        return jnp.concatenate([low_half[0], low_half[1], high_half[0], high_half[1]], axis=0)

    first = spread(block_input[0], True)
    second = spread(block_input[0], False)
    mine = jnp.where(item == 0, jnp.stack([first, second]), jnp.stack([second, first]))
    x_rows = merge_rows(mine, lay.other_core(mine)).astype(WIDE)

    picked = out_grad[lay.core]
    even = lay.route(picked, lambda c, z, t: (t // 2, z, 2 * c + 1) if t % 2 == 0 else None)
    odd = lay.route(picked, lambda c, z, t: (t // 2, z, 2 * c + 1) if t % 2 == 1 else None)
    mine = jnp.stack([even, odd])
    cotangent = merge_rows(mine, lay.other_core(mine))

    gains_here = norm_gains[0].astype(WIDE)
    gains = jnp.where(sec == lay.role, gains_here, lay.other_core(norm_gains[0]).astype(WIDE))

    depth = w_self.shape[1]
    wide = w_self.shape[3]
    self_block = pack_heads(
        {"q": w_self[0, :, 0], "k": w_self[0, :, 1], "v": w_self[0, :, 2], "o": w_self_out[0].T}
    )
    feed_block = jnp.concatenate([w_up[0], w_down[0].T], axis=1)
    cross_block = w_cross[0].reshape(depth, 2 * wide)

    def collect(block):
        same = lay.route(block, lambda c, z, t: (t // 2, z, t) if c == t % 2 else None)
        beside = lay.route(block, lambda c, z, t: (t // 2, z, t ^ 1) if c != t % 2 else None)
        return jnp.stack([same, beside])

    def collect_cross(block, section):
        same = lay.route(block, lambda c, z, t: (t // 2, z, t) if (c == section and t % 2 == 1) else None)
        beside = lay.route(block, lambda c, z, t: (t // 2, z, t ^ 1) if (c == section and t % 2 == 0) else None)
        return same, beside

    w_att = ring_gather(lay, collect(self_block))
    w_ffn = ring_gather(lay, collect(feed_block))
    memory_side = collect_cross(cross_block, 0)
    query_side = collect_cross(cross_block, 1)
    w_crs = ring_gather(
        lay,
        jnp.stack(
            [
                pack_heads({"q": q[:, :wide], "k": m[:, :wide], "v": m[:, wide:], "o": q[:, wide:]})
                for m, q in zip(memory_side, query_side)
            ]
        ),
    )
    hidden = w_up.shape[2]
    part = lambda w, name: jnp.concatenate([unpack_heads(w[0], name), unpack_heads(w[1], name)], axis=1)
    att = {n: part(w_att, n) for n in "qkvo"}
    crs = {n: part(w_crs, n) for n in "qkvo"}
    up = jnp.concatenate([w_ffn[0, :, :hidden], w_ffn[1, :, :hidden]], axis=1)
    down_t = jnp.concatenate([w_ffn[0, :, hidden:], w_ffn[1, :, hidden:]], axis=1)

    positions = jnp.arange(slot)
    own_length = jnp.where(lay.is_decoder, lengths[1, item], lengths[0, item])
    self_allowed = (positions[None, :] < own_length) & (
        (positions[None, :] <= positions[:, None]) | jnp.logical_not(lay.is_decoder)
    )
    cross_allowed = jnp.broadcast_to(
        ((positions < lengths[0, item]) & (task_mask[item] == 1))[None], (slot, slot)
    )

    def joined(partial):
        low = partial.astype(LOW)
        return low.astype(WIDE) + lay.other_core(low).astype(WIDE)

    normed0 = layer_norm(x_rows, gains[0]).astype(LOW)
    q, k, v = (mm(normed0, att[n]).astype(LOW) for n in "qkv")
    out_self, lse_self = attend(q, k, v, self_allowed)
    x_mid = x_rows + joined(mm_nt(out_self, att["o"]))
    normed1 = layer_norm(x_mid, gains[1]).astype(LOW)

    pre_enc = mm(normed1, up)
    act_enc, slope_enc = gelu_parts(pre_enc)
    act_enc = act_enc.astype(LOW)
    x_late_enc = x_mid + joined(mm_nt(act_enc, down_t))
    memory_enc = layer_norm(x_late_enc, gains[2]).astype(LOW)
    memory = lay.route(memory_enc, lambda c, z, t: (c, z, t ^ 1) if t % 2 == 0 else None)

    cq = mm(normed1, crs["q"]).astype(LOW)
    ck, cv = (mm(memory, crs[n]).astype(LOW) for n in "kv")
    out_cross, lse_cross = attend(cq, ck, cv, cross_allowed)
    x_late = x_mid + joined(mm_nt(out_cross, crs["o"]))
    normed2 = layer_norm(x_late, gains[2]).astype(LOW)
    pre_dec = mm(normed2, up)
    act_dec, slope_dec = gelu_parts(pre_dec)
    act_dec = act_dec.astype(LOW)
    result_dec = (x_late + joined(mm_nt(act_dec, down_t))).astype(LOW)

    d_out = cotangent.astype(WIDE)
    d_pre = (slope_dec * mm(cotangent, down_t)).astype(LOW)
    d_ffn_dec = jnp.concatenate([mm_tn(normed2, d_pre), mm_tn(cotangent, act_dec)], axis=1)
    d_late_norm, d_gain2_dec = norm_back(x_late, gains[2], joined(mm_nt(d_pre, up)))
    d_late = d_out + d_late_norm
    grad_late = d_late.astype(LOW)
    d_att = mm(grad_late, crs["o"]).astype(LOW)
    d_cq, d_ck, d_cv = attend_back(cq, ck, cv, lse_cross, d_att, cross_allowed)
    d_memory = joined(mm_nt(d_ck, crs["k"]) + mm_nt(d_cv, crs["v"]))
    d_crs = {
        "q": mm_tn(normed1, d_cq),
        "k": mm_tn(memory, d_ck),
        "v": mm_tn(memory, d_cv),
        "o": mm_tn(grad_late, out_cross),
    }
    d_mid_norm, d_gain1_dec = norm_back(x_mid, gains[1], joined(mm_nt(d_cq, crs["q"])))
    d_mid_dec = d_late + d_mid_norm

    d_memory = lay.route(d_memory.astype(LOW), lambda c, z, t: (c, z, t ^ 1) if t % 2 == 1 else None).astype(WIDE)
    d_late_enc, d_gain2_enc = norm_back(x_late_enc, gains[2], d_memory)
    grad_late_enc = d_late_enc.astype(LOW)
    d_pre = (slope_enc * mm(grad_late_enc, down_t)).astype(LOW)
    d_ffn_enc = jnp.concatenate([mm_tn(normed1, d_pre), mm_tn(grad_late_enc, act_enc)], axis=1)
    d_mid_norm, d_gain1_enc = norm_back(x_mid, gains[1], joined(mm_nt(d_pre, up)))
    d_mid_enc = d_late_enc + d_mid_norm

    d_mid = jnp.where(lay.is_decoder, d_mid_dec, d_mid_enc)
    grad_mid = d_mid.astype(LOW)
    d_att = mm(grad_mid, att["o"]).astype(LOW)
    d_q, d_k, d_v = attend_back(q, k, v, lse_self, d_att, self_allowed)
    d_norm = joined(mm_nt(d_q, att["q"]) + mm_nt(d_k, att["k"]) + mm_nt(d_v, att["v"]))
    d_att_w = {
        "q": mm_tn(normed0, d_q),
        "k": mm_tn(normed0, d_k),
        "v": mm_tn(normed0, d_v),
        "o": mm_tn(grad_mid, out_self),
    }
    d_first, d_gain0 = norm_back(x_rows, gains[0], d_norm)
    d_rows = d_mid + d_first

    half = 3 * HEAD

    def blocks(parts):
        return jnp.stack(
            [pack_heads({n: parts[n][:, half * b : half * (b + 1)] for n in parts}) for b in range(2)]
        )

    def feed_blocks(both):
        total = both.shape[1] // 2
        return jnp.stack(
            [
                jnp.concatenate(
                    [both[:, hidden * b : hidden * (b + 1)], both[:, total + hidden * b : total + hidden * (b + 1)]],
                    axis=1,
                )
                for b in range(2)
            ]
        )

    self_total = blocks(d_att_w)
    home_self = hand_back(lay, ring_scatter(lay, self_total, 0), 0, 0) + hand_back(
        lay, ring_scatter(lay, self_total, 1), 1, 1
    )
    home_feed = hand_back(lay, ring_scatter(lay, feed_blocks(d_ffn_enc), 0), 0, 0) + hand_back(
        lay, ring_scatter(lay, feed_blocks(d_ffn_dec), 1), 1, 1
    )
    cross_total = ring_scatter(lay, blocks(d_crs), 1)
    side = lambda names: jnp.stack(
        [jnp.concatenate([unpack_heads(cross_total[b], n) for n in names], axis=1) for b in range(2)]
    )
    home_cross = hand_back(lay, side("kv"), 1, 0) + hand_back(lay, side("qo"), 1, 1)

    g_self = jnp.stack([unpack_heads(home_self, n) for n in "qkv"], axis=1)[None]
    g_self_out = unpack_heads(home_self, "o").T[None]
    g_cross = home_cross.reshape(1, depth, 2, wide)
    g_up = home_feed[:, :hidden][None]
    g_down = home_feed[:, hidden:].T[None]

    gain2 = jnp.where(lay.is_decoder, d_gain2_dec, d_gain2_enc)
    gain1 = jnp.where(lay.is_decoder, d_gain1_dec, d_gain1_enc)
    gain_rows = jnp.stack([d_gain0, gain1, gain2])
    slots = jnp.stack(
        [
            jnp.where((lay.role == r) & (lay.core == 0), gain_rows, 0.0)
            for r in range(2)
        ]
    )
    gain_total = lax.psum(slots, AXES)[sec][None]

    def rows_home(value):
        mine = lax.dynamic_slice_in_dim(value, lay.core * 2 * rows, 2 * rows, 0).reshape(2, rows, width)
        a = lay.route(mine[item], lambda c, z, t: (t % 2, z, 2 * c + t // 2))
        b = lay.route(mine[1 - item], lambda c, z, t: (t % 2, z, 2 * c + 1 - t // 2))
        even = lay.chip % 2 == 0
        return jnp.where(even, jnp.stack([a, b]), jnp.stack([b, a]))[None]

    block_output = rows_home(jnp.where(lay.is_decoder, result_dec, memory_enc))
    input_grad = rows_home(d_rows.astype(LOW)).astype(WIDE)
    return (
        block_output,
        input_grad,
        g_self,
        g_self_out,
        g_cross,
        g_up,
        g_down,
        gain_total[:, :2],
        gain_total[:, 2],
    )


def body(block_input, w_self, w_self_out, w_cross, w_up, w_down, norm_gains, lengths, task_mask, out_grad):
    lay = Layout()
    seqs, rows, width = block_input.shape[1:]
    slot = rows * lay.chips
    sec = lay.core
    item = lay.item

    if lay.planes != 4:
        return general_body(
            block_input, w_self, w_self_out, w_cross, w_up, w_down, norm_gains, lengths, task_mask, out_grad
        )

    depth = w_self.shape[1]
    wide = w_self.shape[3]
    hidden = w_up.shape[2]
    self_block = pack_heads(
        {"q": w_self[0, :, 0], "k": w_self[0, :, 1], "v": w_self[0, :, 2], "o": w_self_out[0].T}
    )
    pair = {"q": w_cross[0, :, 0], "o": w_cross[0, :, 1], "k": w_cross[0, :, 0], "v": w_cross[0, :, 1]}
    pieces = [pair[n][:, HEAD * h : HEAD * (h + 1)] for n, h in ORDER]
    cross_block = jnp.where(
        sec == 1, jnp.concatenate(pieces[:6], axis=1), jnp.concatenate(pieces[6:], axis=1)
    )
    kept = block_call(
        lay.planes,
        slot,
        width,
        hidden,
        depth,
        (self_block, cross_block, w_up[0], w_down[0].T, block_input[0], out_grad, norm_gains[0], lengths, task_mask),
    )[:6]
    block_output, input_grad, g_up, g_down, g_qkv, g_out, g_cross, g_gain, g_last = widen_call(kept)
    return (
        block_output[None],
        input_grad[None],
        jnp.swapaxes(g_qkv, 0, 1)[None],
        g_out[None],
        g_cross[None],
        g_up[None],
        g_down.T[None],
        g_gain[None],
        g_last,
    )


def solution(mesh):
    placed = (
        P("section", "dp", "tensor", None),
        P("section", "dp", None, "tensor"),
        P("section", "tensor", "dp"),
        P("section", "dp", None, "tensor"),
        P("section", "dp", "tensor"),
        P("section", "tensor", "dp"),
        P("section", None, None),
        P(None, "dp"),
        P("dp", None),
        P("dp", "tensor", None),
    )
    return jax.shard_map(
        body,
        mesh=mesh,
        in_specs=placed,
        out_specs=(
            P("section", "dp", "tensor", None),
            P("section", "dp", "tensor", None),
            P("section", "dp", None, "tensor"),
            P("section", "tensor", "dp"),
            P("section", "dp", None, "tensor"),
            P("section", "dp", "tensor"),
            P("section", "tensor", "dp"),
            P("section", None, None),
            P("section", None),
        ),
        check_vma=False,
    )
```

```python
import functools

import jax
import jax.numpy as jnp
from jax import lax
from jax.experimental import pallas as pl
from jax.experimental.pallas import tpu as pltpu
from jax.sharding import PartitionSpec as P

HEAD = 64
TILE = 128
EPSILON = 1e-05
SCORE_SCALE = 0.125
NEG_FILL = -1000000000.0
AXES = ("section", "dp", "tensor")
LOW = jnp.bfloat16
WIDE = jnp.float32


class Layout:
    def __init__(self):
        self.cores = lax.axis_size("section")
        self.planes = lax.axis_size("dp")
        self.chips = lax.axis_size("tensor")
        self.core = lax.axis_index("section")
        self.plane = lax.axis_index("dp")
        self.chip = lax.axis_index("tensor")
        self.role = self.chip % 2
        self.item = self.chip // 2
        self.is_decoder = self.role == 1
        self.relays = self.core == self.item

    def route(self, value, target):
        pairs = []
        for core in range(self.cores):
            for plane in range(self.planes):
                for chip in range(self.chips):
                    to = target(core, plane, chip)
                    if to is None:
                        continue
                    source = (core * self.planes + plane) * self.chips + chip
                    goal = (to[0] * self.planes + to[1]) * self.chips + to[2]
                    pairs.append((source, goal))
        return lax.ppermute(value, AXES, pairs)

    def other_core(self, value):
        return self.route(value, lambda c, z, t: (1 - c, z, t))


def normalize(values):
    centred = values - jnp.mean(values, axis=-1, keepdims=True)
    spread = jnp.mean(centred * centred, axis=-1, keepdims=True)
    scale = lax.rsqrt(spread + EPSILON)
    return centred * scale, scale


def layer_norm(values, gain):
    return normalize(values)[0] * gain


def norm_back(values, gain, grad):
    normal, scale = normalize(values)
    scaled = grad * gain
    first = jnp.mean(scaled, axis=-1, keepdims=True)
    second = jnp.mean(scaled * normal, axis=-1, keepdims=True)
    return (scaled - first - normal * second) * scale, jnp.sum(grad * normal, axis=0)


ORDER = (("q", 0), ("q", 1), ("q", 2), ("o", 2), ("o", 0), ("o", 1), ("k", 0), ("k", 1), ("v", 0), ("v", 1), ("k", 2), ("v", 2))


def pack_heads(parts):
    return jnp.concatenate([parts[n][:, HEAD * h : HEAD * (h + 1)] for n, h in ORDER], axis=1)


def unpack_heads(block, name):
    where = {(n, h): i for i, (n, h) in enumerate(ORDER)}
    return jnp.concatenate(
        [block[:, HEAD * where[(name, h)] : HEAD * (where[(name, h)] + 1)] for h in range(3)], axis=1
    )


def mm(left, right):
    return jnp.dot(left, right, preferred_element_type=WIDE)


def mm_nt(left, right):
    return lax.dot_general(left, right, (((1,), (1,)), ((), ())), preferred_element_type=WIDE)


def mm_tn(left, right):
    return lax.dot_general(left, right, (((0,), (0,)), ((), ())), preferred_element_type=WIDE)


def split_heads(value):
    return value.reshape(value.shape[0], -1, HEAD)


def attend(q, k, v, allowed):
    scores = jnp.einsum("qhd,khd->hqk", split_heads(q), split_heads(k), preferred_element_type=WIDE) * SCORE_SCALE
    scores = jnp.where(allowed[None], scores, NEG_FILL)
    top = jnp.max(scores, axis=-1, keepdims=True)
    power = jnp.exp(scores - top)
    total = jnp.sum(power, axis=-1, keepdims=True)
    probs = (power / total).astype(LOW)
    out = jnp.einsum("hqk,khd->qhd", probs, split_heads(v), preferred_element_type=WIDE)
    return out.astype(LOW).reshape(q.shape), top + jnp.log(total)


def attend_back(q, k, v, log_sum, d_out, allowed):
    scores = jnp.einsum("qhd,khd->hqk", split_heads(q), split_heads(k), preferred_element_type=WIDE) * SCORE_SCALE
    scores = jnp.where(allowed[None], scores, NEG_FILL)
    probs = jnp.exp(scores - log_sum)
    d_probs = jnp.einsum("qhd,khd->hqk", split_heads(d_out), split_heads(v), preferred_element_type=WIDE)
    inner = jnp.sum(probs * d_probs, axis=-1, keepdims=True)
    d_scores = (probs * (d_probs - inner)).astype(LOW)
    d_v = jnp.einsum("hqk,qhd->khd", probs.astype(LOW), split_heads(d_out), preferred_element_type=WIDE)
    d_q = jnp.einsum("hqk,khd->qhd", d_scores, split_heads(k), preferred_element_type=WIDE) * SCORE_SCALE
    d_k = jnp.einsum("hqk,qhd->khd", d_scores, split_heads(q), preferred_element_type=WIDE) * SCORE_SCALE
    return tuple(g.astype(LOW).reshape(q.shape) for g in (d_q, d_k, d_v))


def gelu_parts(value):
    coef = 0.7978845608028654
    cube = 0.044715
    inner = coef * (value + cube * value * value * value)
    soft = jnp.tanh(inner)
    slope = 0.5 * (1.0 + soft) + 0.5 * value * (1.0 - soft * soft) * coef * (1.0 + 3.0 * cube * value * value)
    return 0.5 * value * (1.0 + soft), slope


MESH = pl.DeviceIdType.MESH
GROUPS = ("att", "crs", "up", "dn")
BLOCK = 256
VMEM_BYTES = 62 * 2**20


def lanes(shape):
    return lax.broadcasted_iota(jnp.int32, shape, len(shape) - 1)


def subs(shape):
    return lax.broadcasted_iota(jnp.int32, shape, 0)


def strip(i, size):
    return pl.ds(pl.multiple_of(i * size, size), size)


def head_place(h):
    two = (h == 2).astype(jnp.int32)
    one = (h >= 1).astype(jnp.int32)
    return two, 2 + 2 * two, 3 + two, 1 - two, HEAD * (one - two), HEAD * one


def each(count, step, name=None):
    def run(i, carry):
        step(i)
        return carry

    with jax.named_scope(name or step.__name__):
        lax.fori_loop(0, count, run, 0)


class Place:
    def __init__(self, planes):
        self.planes = planes
        self.c = lax.axis_index("section")
        self.z = lax.axis_index("dp")
        self.t = lax.axis_index("tensor")
        self.y = lax.div(self.t, 2)
        self.r = lax.rem(self.t, 2)
        self.twin = (1 - self.c, self.z, self.t)
        self.above = (self.c, lax.rem(self.z + 1, planes), self.t)
        self.below = (self.c, lax.rem(self.z + planes - 1, planes), self.t)
        self.across = (self.c, self.z, lax.rem(self.t + 2, 4))
        self.beside = (self.c, self.z, self.t + 1 - 2 * self.r)
        self.relays = self.c == self.y
        self.encodes = self.r == 0
        self.decodes = self.r == 1

    def meet(self):
        barrier = pltpu.get_barrier_semaphore()
        peers = [self.above, self.below]
        for dc in range(2):
            for dt in range(4):
                if dc or dt:
                    peers.append((lax.rem(self.c + dc, 2), self.z, lax.rem(self.t + dt, 4)))
        for peer in peers:
            pl.semaphore_signal(barrier, inc=1, device_id=peer, device_id_type=MESH)
        pl.semaphore_wait(barrier, len(peers))


def push(source, goal, sent, got, device):
    return pltpu.make_async_remote_copy(
        src_ref=source, dst_ref=goal, send_sem=sent, recv_sem=got, device_id=device, device_id_type=MESH
    )


def both(first, second):
    return jnp.logical_and(first, second)


def center(values):
    middle = values - jnp.mean(values, axis=-1, keepdims=True)
    scale = lax.rsqrt(jnp.mean(middle * middle, axis=-1, keepdims=True) + EPSILON)
    return middle * scale, scale


def attend_block(h, p, o, lse, lse_row, bias, kx, qx, vt, causal):
    count = p.shape[0]
    qt, kt, vtile, ot, qlo, vlo = head_place(h)
    lane = lanes((count, TILE))
    in_q = both(lane >= qlo, lane < qlo + HEAD)
    in_v = both(lane >= vlo, lane < vlo + HEAD)
    spare = HEAD - qlo
    kx[...] = jnp.where(lane == spare, bias[...], jnp.where(in_q, p[:, strip(kt, TILE)], jnp.zeros((), LOW)))
    vt[...] = jnp.where(in_v, p[:, strip(vtile, TILE)].astype(WIDE), 1.0).T.astype(LOW)
    qx[...] = jnp.where(
        in_q, p[:, strip(qt, TILE)].astype(WIDE) * SCORE_SCALE, jnp.where(lane == spare, 1.0, 0.0)
    ).astype(LOW)
    size = count // 2 if causal else count

    def queries(i):
        q = strip(i, size) if causal else pl.ds(0, count)
        scores = mm_nt(kx[...], qx[q, :])
        if causal:
            scores = jnp.where(subs(scores.shape) <= lanes(scores.shape) + i * size, scores, NEG_FILL)
        top = jnp.max(scores, axis=0, keepdims=True)
        power = jnp.exp(scores - top).astype(LOW)
        out = mm(vt[...], power)
        total = jnp.where(vlo == 0, out[HEAD : HEAD + 1, :], out[0:1, :])
        result = (out / total).T
        lane = lanes((size, TILE))
        in_v = both(lane >= vlo, lane < vlo + HEAD)
        o[q, strip(ot, TILE)] = jnp.where(in_v, result, o[q, strip(ot, TILE)].astype(WIDE)).astype(LOW)
        row = subs((8, size))
        lse[:, q] = jnp.where(row == lse_row, top + jnp.log(total), lse[:, q])

    if causal:
        each(count // size, queries)
    else:
        queries(0)


SUMS = ("ffn", "crs", "att")
DIRECT = ("att", "up")
ASIDE = (("up", 0), ("up", 1), ("dn", 0))


def split_three(value):
    high = value.astype(LOW).astype(WIDE)
    middle = (value - high).astype(LOW).astype(WIDE)
    return high, middle, value - high - middle


def attend_back_block(h, p, o, d_o, d_p, lse, lse_row, bias, kx, qx, vx, gx, kt_v, dk_v, dv_v, causal):
    count = p.shape[0]
    qt, kt, vtile, ot, qlo, vlo = head_place(h)
    lane = lanes((count, TILE))
    in_q = both(lane >= qlo, lane < qlo + HEAD)
    in_v = both(lane >= vlo, lane < vlo + HEAD)
    sq, sv = HEAD - qlo, HEAD - vlo
    keys = jnp.where(
        in_q, p[:, strip(kt, TILE)].astype(WIDE), jnp.where(both(lane > sq, lane < sq + 4), 1.0, 0.0)
    )
    keys = jnp.where(lane == sq, bias[...].astype(WIDE), keys)
    kx[...] = keys.astype(LOW)
    kt_v[...] = keys.T.astype(LOW)
    vx[...] = jnp.where(
        in_v, p[:, strip(vtile, TILE)].astype(WIDE), jnp.where(both(lane >= sv, lane < sv + 3), 1.0, 0.0)
    ).astype(LOW)
    own = jnp.sum(jnp.where(subs((8, count)) == lse_row, lse[...], 0.0), axis=0, keepdims=True)
    a, b, c = split_three(-jnp.broadcast_to(own, (TILE, count)).T)
    extra = jnp.where(
        lane == sq,
        1.0,
        jnp.where(lane == sq + 1, a, jnp.where(lane == sq + 2, b, jnp.where(lane == sq + 3, c, 0.0))),
    )
    qx[...] = jnp.where(in_q, p[:, strip(qt, TILE)].astype(WIDE) * SCORE_SCALE, extra).astype(LOW)
    grad = jnp.where(in_v, d_o[:, strip(ot, TILE)].astype(WIDE), 0.0)
    inner = jnp.sum(grad * o[:, strip(ot, TILE)].astype(WIDE), axis=-1, keepdims=True)
    a, b, c = split_three(-inner)
    gx[...] = (
        grad + jnp.where(lane == sv, a, jnp.where(lane == sv + 1, b, jnp.where(lane == sv + 2, c, 0.0)))
    ).astype(LOW)
    size = count // 2 if causal else count

    def place(q, tile_index, low, value):
        cut = strip(tile_index, TILE)
        lane = lanes(value.shape)
        inside = both(lane >= low, lane < low + HEAD)
        d_p[q, cut] = jnp.where(inside, value, d_p[q, cut].astype(WIDE)).astype(LOW)

    whole = pl.ds(0, count)
    if causal:
        dk_v[...] = jnp.zeros_like(dk_v)
        dv_v[...] = jnp.zeros_like(dv_v)

    def queries(i):
        q = strip(i, size) if causal else pl.ds(0, count)
        scores = mm_nt(kx[...], qx[q, :])
        if causal:
            scores = jnp.where(subs(scores.shape) <= lanes(scores.shape) + i * size, scores, NEG_FILL)
        probs = jnp.exp(scores)
        d_scores = (probs * mm_nt(vx[...], gx[q, :])).astype(LOW)
        d_v = mm(probs.astype(LOW), gx[q, :])
        d_k = mm(d_scores, qx[q, :])
        place(q, qt, qlo, mm(kt_v[...], d_scores).T * SCORE_SCALE)
        if causal:
            dk_v[...] += d_k
            dv_v[...] += d_v
        else:
            place(whole, kt, qlo, d_k)
            place(whole, vtile, vlo, d_v)

    if not causal:
        queries(0)
    else:
        each(count // size, queries)
        place(whole, kt, qlo, dk_v[...])
        place(whole, vtile, vlo, dv_v[...])


def block_kernel(
    planes, self_in, crs_in, up_in, dn_in, x_in, cot_in, gain_in, lengths, task_mask,
    block_out, grad_low, home_ffn, home_crs, home_att, gain_out,
    cot, first_k, x_k, second_k, late_k, memory_k, p_k, o_k, lse_k, pc_k, oc_k, lsec_k, act_k, grad_k, y3_k,
    dw_ffn, dw_crs, dw_att, yb_ffn, yb_crs, yb_att, zb_ffn, zb_crs, zb_att, via_att,
    att_v, crs_v, up_v, dn_v, a_v, b_v, o_v, do_v, mid_v, late_v, s_v, g_v, c_v, ta, tb, tc,
    send_v, recv_v, kx, qx, vx, gx, dk_v, dv_v, kt_v, lse_v, gain_v, gain_in_v, gain_buf, out_st, dw_st, sum_st,
    bias_self, bias_cross, res_ffn, res_crs, res_att,
    x_sem, x_sent, y0_sent, c_sem, zw_got, zw_sent, yw_got, yw_sent, side_got, side_sent,
    row_got, row_sent, fwd_sem, cot_got, gain_sem, copy_sem, ex_got, ex_sent, mem_got, mem_sent, mf_got, mf_sent,
    dm_got, dm_sent, df_got, df_sent, y_got, y_sent, z_got, z_sent, home_got, home_sent,
    blk_got, blk_sent, gr_got, gr_sent, gr_hop_got, gr_hop_sent, sum_sem, dw_sem, via_got, via_sent, hand_got, hand_sent,
):
    at = Place(planes)
    c, z, t, y, r = at.c, at.z, at.t, at.y, at.r
    rows = x_in.shape[1]
    slot = s_v.shape[0]
    tiles = slot // BLOCK
    depth = up_in.shape[0]
    side = crs_in.shape[1]
    relay = at.relays
    other = jnp.logical_not(relay)
    vmem = {"att": att_v, "crs": crs_v, "up": up_v, "dn": dn_v}
    shard = {"att": self_in, "up": up_in, "dn": dn_in}
    here = pl.ds(pl.multiple_of(z * depth, depth), depth)
    dw = {"ffn": dw_ffn, "crs": dw_crs, "att": dw_att}
    yb = {"ffn": yb_ffn, "crs": yb_crs, "att": yb_att}
    zb = {"ffn": zb_ffn, "crs": zb_crs, "att": zb_att}
    home = {"ffn": home_ffn, "crs": home_crs, "att": home_att}
    res = {"ffn": res_ffn, "crs": res_crs, "att": res_att}
    names = {}

    def copying(name, source, goal):
        index = names.setdefault(name, len(names))
        return pltpu.make_async_copy(source, goal, copy_sem.at[index])

    def half_of(core):
        return pl.ds(pl.multiple_of(core * 2 * rows, 2 * rows), 2 * rows)

    at.meet()

    relay_dev = (y, z, 2 * y + c)
    over_dev = (y, z, 2 * (1 - y) + c)
    stays = both(c == y, r == c)

    def launch(g):
        i = GROUPS.index(g)
        goal = vmem[g].at[r, here, :]

        @pl.when(stays)
        def _():
            pltpu.make_async_copy(shard[g], goal, x_sem.at[i, r]).start()

        @pl.when(jnp.logical_not(stays))
        def _():
            push(shard[g], goal, x_sent.at[i], x_sem.at[i, r], relay_dev).start()

    def launch_over(g):
        i = GROUPS.index(g)
        return push(shard[g], vmem[g].at[r, here, :], y0_sent.at[i], yw_got.at[i, 0, r], over_dev)

    crs_dev = (y, z, 2 * y + 1)
    crs_stays = both(c == y, r == 1)

    def crs_goal(block, section):
        return crs_v.at[block, here, pl.ds(pl.multiple_of((1 - section) * side, side), side)]

    def launch_crs():
        @pl.when(crs_stays)
        def _():
            pltpu.make_async_copy(crs_in, crs_goal(r, c), c_sem.at[r, c]).start()

        @pl.when(jnp.logical_not(crs_stays))
        def _():
            push(crs_in, crs_goal(r, c), x_sent.at[1], c_sem.at[r, c], crs_dev).start()

    row_goal = s_v.at[strip(t, rows), :]
    cot_goal = cot.at[strip(t, rows), :]

    def row_stays(s):
        return both(both(c == y, r == c), y == s)

    def launch_rows(s):
        dev = (y, z, 2 * s + c)

        @pl.when(row_stays(s))
        def _():
            pltpu.make_async_copy(x_in.at[s], row_goal, row_got.at[r]).start()

        @pl.when(jnp.logical_not(row_stays(s)))
        def _():
            push(x_in.at[s], row_goal, row_sent.at[s], row_got.at[r], dev).start()

    def launch_cot():
        dev = (y, z, 2 * c + 1)

        @pl.when(crs_stays)
        def _():
            pltpu.make_async_copy(cot_in.at[c], cot_goal, cot_got.at[r]).start()

        @pl.when(jnp.logical_not(crs_stays))
        def _():
            push(cot_in.at[c], cot_goal, row_sent.at[2], cot_got.at[r], dev).start()

    gain_copy = push(gain_in, gain_in_v.at[c], gain_sem.at[0], gain_sem.at[1], at.twin)
    gain_copy.start()
    launch("att")
    launch_over("att").start()
    launch_rows(0)
    launch_rows(1)
    launch("up")
    launch_over("up").start()
    launch_crs()
    launch("dn")
    launch_cot()

    place = subs((slot, TILE))
    seen = jnp.where(y == 0, task_mask[0:1, :], task_mask[1:2, :]) == 1
    seen = jnp.broadcast_to(jnp.where(seen, 1.0, 0.0), (TILE, slot)).T > 0.5
    bias_self[...] = jnp.where(place < lengths[r, y], 0.0, NEG_FILL).astype(LOW)
    bias_cross[...] = jnp.where(both(place < lengths[0, y], seen), 0.0, NEG_FILL).astype(LOW)

    def piece(g, k, b):
        j = lax.rem(z - k + planes, planes)
        return vmem[g].at[b, pl.ds(pl.multiple_of(j * depth, depth), depth), :]

    def ring(g, k, b):
        i = GROUPS.index(g)
        return push(
            piece(g, k - 1, b), piece(g, k - 1, b), zw_sent.at[i, k - 1, b], zw_got.at[i, k - 1, b], at.above
        )

    def ring_in(g, k, b):
        i = GROUPS.index(g)
        return push(piece(g, k, b), piece(g, k, b), zw_sent.at[i, k - 1, b], zw_got.at[i, k - 1, b], at.above)

    def cross_over(g, k, b):
        i = GROUPS.index(g)
        return push(piece(g, k, b), piece(g, k, b), yw_sent.at[i, k, b], yw_got.at[i, k, b], at.across)

    def arrive(g, k, b):
        if k:
            ring_in(g, k, b).wait_recv()
        elif g == "crs":
            for section in range(2):
                goal = crs_goal(b, section)
                push(goal, goal, x_sent.at[1], c_sem.at[b, section], at.twin).wait_recv()
        else:
            i = GROUPS.index(g)
            goal = vmem[g].at[b, here, :]
            push(goal, goal, x_sent.at[i], x_sem.at[i, b], at.twin).wait_recv()

    def passing(g, k, up=True, over=True):
        skips = [b for b in range(2) if k == 1 and (g, b) in ASIDE]

        def half(b):
            if up:
                with jax.named_scope("await_" + g + str(k)):
                    arrive(g, k, b)
                if k + 1 < planes:
                    ring(g, k + 1, b).start()
            if over and not (k == 0 and g in DIRECT) and len(skips) < 2:
                if skips:
                    pl.when(b != skips[0])(lambda: cross_over(g, k, b).start())
                else:
                    cross_over(g, k, b).start()

        def run():
            each(2, half, "pass_" + g)

        return run

    def schedule(order):
        events = []
        for n, g in enumerate(order):
            for k in range(planes):
                if k == 0 and n == 0:
                    events.append(passing(g, 0))
                elif k:
                    events.append(passing(g, k))
                if n + 1 < len(order):
                    if k == planes - 2:
                        events[-1] = chained(events[-1], passing(order[n + 1], 0, True, False))
                    if k == planes - 1:
                        events[-1] = chained(events[-1], passing(order[n + 1], 0, False, True))
        return events

    def chained(one, two):
        def run():
            one()
            two()

        return run

    enc_events = schedule(("att", "up", "dn"))
    dec_events = schedule(("att", "crs", "up", "dn"))

    def pump_enc(count):
        for _ in range(min(count, len(enc_events))):
            pl.when(both(relay, at.encodes))(enc_events.pop(0))

    def pump_dec(count):
        for _ in range(min(count, len(dec_events))):
            pl.when(both(relay, at.decodes))(dec_events.pop(0))

    def pump(count):
        pump_enc(count)
        pump_dec(count)

    def side_hop(g, b):
        i = GROUPS.index(g)
        return push(piece(g, 0, b), piece(g, 0, b), side_sent.at[i, b], side_got.at[i, b], at.above)

    def side_in(g, b):
        i = GROUPS.index(g)
        return push(piece(g, 1, b), piece(g, 1, b), side_sent.at[i, b], side_got.at[i, b], at.above)

    def pass_aside(g):
        @pl.when(other)
        def _():
            for b in range(2):
                cross_over(g, 0, b).wait_recv()
                if (g, b) in ASIDE:
                    side_hop(g, b).start()

    def settle(g):
        listens = both(other, at.decodes) if g == "crs" else other

        @pl.when(listens)
        @jax.named_scope("settle_" + g)
        def _():
            for k in range(planes):
                for b in range(2):
                    if k == 1 and (g, b) in ASIDE:
                        side_in(g, b).wait_recv()
                    elif k or g in ("att", "crs"):
                        cross_over(g, k, b).wait_recv()

    def exchange(e, i):
        q = strip(i, BLOCK)
        k = e % 2
        return push(send_v.at[k, q, :], recv_v.at[k, q, :], ex_sent.at[e, i], ex_got.at[e, i], at.twin)

    def joined(e, i):
        q = strip(i, BLOCK)
        exchange(e, i).wait_recv()
        return send_v[e % 2, q, :].astype(WIDE) + recv_v[e % 2, q, :].astype(WIDE)

    def sent(e):
        each(tiles, lambda i: exchange(e, i).wait_send())

    pump(3)
    for k in range(2):
        goal = s_v.at[strip(2 * c + k, rows), :]
        push(goal, goal, row_sent.at[0], row_got.at[k], at.twin).wait_recv()
    half, far_half = half_of(c), half_of(1 - c)
    rows_on = push(s_v.at[half, :], s_v.at[half, :], fwd_sem.at[0], fwd_sem.at[1], at.twin)
    rows_on.start()
    push(gain_in, gain_in_v.at[1 - c], gain_sem.at[0], gain_sem.at[1], at.twin).wait_recv()
    gain_here = pltpu.make_async_copy(gain_in, gain_in_v.at[c], gain_sem.at[2])
    gain_here.start()
    gain_here.wait()
    gains = gain_in_v[r].astype(WIDE)
    g0, g1, g2 = gains[0:1, :], gains[1:2, :], gains[2:3, :]
    gain_v[...] = jnp.zeros_like(gain_v)
    push(s_v.at[far_half, :], s_v.at[far_half, :], fwd_sem.at[0], fwd_sem.at[1], at.twin).wait_recv()
    x_put = copying("x", s_v, x_k)
    x_put.start()

    def enter(i):
        q = strip(i, BLOCK)
        c_v[q, :] = (center(s_v[q, :].astype(WIDE))[0] * g0).astype(LOW)

    each(tiles, enter)
    first_put = copying("first", c_v, first_k)
    first_put.start()
    pump(1)
    settle("att")

    def project(source, weights, part):
        def project_rows(n):
            b, q = lax.rem(n, 2), strip(lax.div(n, 2), BLOCK)
            if part != "kv":
                a_v[b, q, 0:256] = mm(source[q, :], weights[b, :, 0:256]).astype(LOW)
            if part != "q":
                a_v[b, q, 256:640] = mm(source[q, :], weights[b, :, 384:768]).astype(LOW)

        each(2 * tiles, project_rows)

    packed_v = a_v.at[:, :, 0:640]
    project(c_v, att_v, "all")
    pass_aside("up")
    p_put = copying("p", packed_v, p_k)
    p_put.start()
    o_v[...] = jnp.zeros_like(o_v)
    lse_v[...] = jnp.zeros_like(lse_v)
    pump(1)

    def attend_heads(bias, causal, hooks):
        def head_forward(n):
            b = lax.div(n, 3)
            attend_block(lax.rem(n, 3), a_v.at[b], o_v.at[b], lse_v, n, bias, kx, qx, kt_v, causal)
            for when, event in hooks:
                pl.when(both(n == when, relay))(event)

        each(6, head_forward)

    enc_hooks = [(2, enc_events.pop(0)), (5, enc_events.pop(0))]
    dec_hooks = [(2, dec_events.pop(0)), (4, dec_events.pop(0))]
    pl.when(at.encodes)(lambda: attend_heads(bias_self, False, enc_hooks))
    pl.when(at.decodes)(lambda: attend_heads(bias_self, True, dec_hooks))
    o_put, lse_put = copying("o", o_v, o_k), copying("lse", lse_v, lse_k)
    o_put.start()
    lse_put.start()

    def out_project(e, weights):
        def out_rows(i):
            q = strip(i, BLOCK)
            part = mm_nt(o_v[0, q, :], weights[0, :, 128:384]) + mm_nt(o_v[1, q, :], weights[1, :, 128:384])
            send_v[e % 2, q, :] = part.astype(LOW)
            exchange(e, i).start()

        each(tiles, out_rows)

    out_project(0, att_v)
    pump(1)
    x_put.wait()
    pass_aside("dn")
    rows_on.wait_send()

    def middle(i):
        q = strip(i, BLOCK)
        value = s_v[q, :].astype(WIDE) + joined(0, i)
        mid_v[q, :] = value
        s_v[q, :] = (center(value)[0] * g1).astype(LOW)

    each(tiles, middle)
    first_put.wait()
    p_put.wait()
    o_put.wait()
    lse_put.wait()

    def mem_send(i):
        q = pl.ds(pl.multiple_of((2 * c + i) * BLOCK, BLOCK), BLOCK)
        return push(g_v.at[q, :], g_v.at[q, :], mem_sent.at[i], mem_got.at[i], at.beside)

    def mem_forward(i, core):
        q = pl.ds(pl.multiple_of((2 * core + i) * BLOCK, BLOCK), BLOCK)
        return push(g_v.at[q, :], g_v.at[q, :], mf_sent.at[i], mf_got.at[i], at.twin)

    def row_home(k, source, goal, sent_by, got):
        dev = (r, z, 2 * c + k)
        keeps = both(both(c == r, y == c), r == k)
        return keeps, source, goal.at[y], sent_by.at[k], got.at[y], dev

    def go_home(*spec):
        keeps, source, goal, sent_by, got, dev = row_home(*spec)

        @pl.when(keeps)
        def _():
            pltpu.make_async_copy(source, goal, got).start()

        @pl.when(jnp.logical_not(keeps))
        def _():
            push(source, goal, sent_by, got, dev).start()

    def went_home(*spec):
        keeps, source, goal, sent_by, got, dev = row_home(*spec)

        @pl.when(jnp.logical_not(keeps))
        def _():
            push(source, goal, sent_by, got, dev).wait_send()

    def memory_home(k):
        return k, memory_k.at[strip(2 * c + k, rows), :], block_out, blk_sent, blk_got

    settle_up = lambda: settle("up")
    pl.when(at.encodes)(settle_up)

    @pl.when(at.encodes)
    def _():
        def up_rows(n):
            b, q = lax.rem(n, 2), strip(lax.div(n, 2), BLOCK)
            value, grade = gelu_parts(mm(s_v[q, :], up_v[b]))
            a_v[b, q, :] = value.astype(LOW)
            b_v[b, q, :] = grade.astype(LOW)

        each(2 * tiles, up_rows)

    pump_enc(9)

    @pl.when(at.encodes)
    def _():
        settle("dn")

        def down_rows(i):
            q = strip(i, BLOCK)
            part = mm_nt(a_v[0, q, :], dn_v[0]) + mm_nt(a_v[1, q, :], dn_v[1])
            send_v[1, q, :] = part.astype(LOW)
            exchange(1, i).start()

        each(tiles, down_rows)

        def finish(n):
            i = lax.rem(n + 2 * c, 4)
            q = strip(i, BLOCK)
            value = mid_v[q, :] + joined(1, i)
            late_v[q, :] = value
            g_v[q, :] = (center(value)[0] * g2).astype(LOW)

            @pl.when(n < 2)
            def _():
                mem_send(n).start()

        each(tiles, finish)
        keep = copying("memory", g_v, memory_k)
        keep.start()
        keep.wait()
        for k in range(2):
            go_home(*memory_home(k))
        sent(0)

    def norm_grad(values, gain, grad, gain_row, counted):
        normal, scale = center(values)
        scaled = grad * gain
        one = jnp.mean(scaled, axis=-1, keepdims=True)
        two = jnp.mean(scaled * normal, axis=-1, keepdims=True)
        total = jnp.sum(grad * normal, axis=0, keepdims=True)
        gain_v[gain_row : gain_row + 1, :] += jnp.where(counted, total, 0.0)
        return (scaled - one - normal * two) * scale

    def ours(i):
        return lax.div(i, 2) == c

    @pl.when(at.decodes)
    def _():
        second_put = copying("second", s_v, second_k)
        second_put.start()
        for k in range(2):
            goal = cot.at[strip(2 * c + k, rows), :]
            push(goal, goal, row_sent.at[2], cot_got.at[k], at.twin).wait_recv()
        cot_on = push(cot.at[half, :], cot.at[half, :], fwd_sem.at[2], fwd_sem.at[3], at.twin)
        cot_on.start()
        for _ in range(len(dec_events) - 3):
            pl.when(relay)(dec_events.pop(0))
        settle("crs")
        project(s_v, crs_v, "q")
        pl.when(relay)(dec_events.pop(0))
        pl.when(relay)(dec_events.pop(0))
        push(cot.at[far_half, :], cot.at[far_half, :], fwd_sem.at[2], fwd_sem.at[3], at.twin).wait_recv()
        cot_in_v = copying("cot", cot, c_v)
        cot_in_v.start()
        o_v[...] = jnp.zeros_like(o_v)
        lse_v[...] = jnp.zeros_like(lse_v)
        for i in range(2):
            mem_send(i).wait_recv()
            mem_forward(i, c).start()
        for i in range(2):
            mem_forward(i, 1 - c).wait_recv()
        project(g_v, crs_v, "kv")
        puts = [copying("pc", packed_v, pc_k), copying("memory", g_v, memory_k)]
        for copy in puts:
            copy.start()
        attend_heads(bias_cross, False, [(0, dec_events.pop(0))])
        puts += [copying("oc", o_v, oc_k), copying("lsec", lse_v, lsec_k)]
        for copy in puts[2:]:
            copy.start()
        out_project(1, crs_v)
        second_put.wait()

        def finish(i):
            q = strip(i, BLOCK)
            value = mid_v[q, :] + joined(1, i)
            late_v[q, :] = value
            s_v[q, :] = (center(value)[0] * g2).astype(LOW)

        each(tiles, finish)
        late_put = copying("late", late_v, late_k)
        late_put.start()
        settle("up")
        settle("dn")
        cot_in_v.wait()
        sent(0)
        for copy in puts:
            copy.wait()

        def feed_rows(i):
            q = strip(i, BLOCK)

            def feed_half(b):
                value, grade = gelu_parts(mm(s_v[q, :], up_v[b]))
                a_v[b, q, :] = value.astype(LOW)
                b_v[b, q, :] = (mm(c_v[q, :], dn_v[b]) * grade).astype(LOW)

            each(2, feed_half)
            part = mm_nt(b_v[0, q, :], up_v[0]) + mm_nt(b_v[1, q, :], up_v[1])
            send_v[0, q, :] = part.astype(LOW)
            exchange(2, i).start()

        each(tiles, feed_rows)
        copying("act", a_v, act_k).start()
        late_put.wait()
        cot_on.wait_send()
        each(2, lambda i: mem_forward(i, c).wait_send())

    def block_of(k):
        return lax.rem(z - 1 - k + 2 * planes, planes)

    def y_hop(g, k, b):
        i = SUMS.index(g)
        return push(dw[g].at[k, b], yb[g].at[k, b], y_sent.at[i, k, b], y_got.at[i, k, b], at.across)

    def z_hop(g, k, b):
        i = SUMS.index(g)
        return push(res[g].at[b], zb[g].at[k, b], z_sent.at[i, k, b], z_got.at[i, k, b], at.above)

    def via_hop(k):
        diagonal = (c, z, lax.rem(t + 2, 4) + 1 - 2 * r)
        return push(dw_att.at[k, 1], via_att.at[k], via_sent.at[k], via_got.at[k], diagonal)

    def hand_on(k):
        return push(via_att.at[k], yb_att.at[k, 1], hand_sent.at[k], hand_got.at[k], at.beside)

    def leave(g, k):
        @pl.when(other)
        def _():
            y_hop(g, k, 0).start()
            if g == "att":
                pl.when(at.decodes)(lambda: y_hop(g, k, 1).start())
                pl.when(at.encodes)(lambda: via_hop(k).start())
            else:
                y_hop(g, k, 1).start()

    def emit(g, compute):
        columns = dw[g].shape[3]

        def put(k, s):
            return pltpu.make_async_copy(dw_st.at[s, :, :, 0:columns], dw[g].at[k], dw_sem.at[s])

        def run(k):
            s = lax.rem(k, 2)
            j = block_of(k)
            compute(s, pl.ds(pl.multiple_of(j * depth, depth), depth))
            put(k, s).start()

            @pl.when(k >= 1)
            def _():
                put(k - 1, 1 - s).wait()
                leave(g, k - 1)

        each(planes, run, "emit_" + g)
        put(planes - 1, (planes - 1) % 2).wait()
        leave(g, planes - 1)

    def home_copy(g, b, section):
        i = SUMS.index(g)
        columns = dw[g].shape[3]
        source = res[g].at[b]
        if g == "crs":
            source = source.at[:, pl.ds((1 - section) * (columns // 2), columns // 2)]
        device = (section, z, 2 * y + b)
        keeps = both(c == section, r == b)
        return keeps, source, push(source, home[g], home_sent.at[i, b, section if g == "crs" else 0], home_got.at[i], device)

    def sections(g):
        return (0, 1) if g == "crs" else (r,)

    def sum_at(g, n):
        i = SUMS.index(g)
        columns = dw[g].shape[3]
        k, b = lax.div(n, 2), lax.rem(n, 2)

        def fetch(m, source):
            return pltpu.make_async_copy(source, sum_st.at[m, :, 0:columns], sum_sem.at[m])

        @pl.when(relay)
        @jax.named_scope("sum_" + g)
        def _():
            before = lax.max(k - 1, 0)
            if g == "att":
                detour = both(at.encodes, b == 1)
                pl.when(detour)(lambda: hand_on(k).wait_recv())
                pl.when(jnp.logical_not(detour))(lambda: y_hop(g, k, b).wait_recv())
            else:
                y_hop(g, k, b).wait_recv()
            fetch(0, dw[g].at[k, b]).start()
            fetch(1, yb[g].at[k, b]).start()

            @pl.when(k > 0)
            def _():
                z_hop(g, before, b).wait_recv()
                fetch(2, zb[g].at[before, b]).start()
                z_hop(g, before, b).wait_send()
                fetch(2, zb[g].at[before, b]).wait()

            fetch(0, dw[g].at[k, b]).wait()
            fetch(1, yb[g].at[k, b]).wait()
            share = depth // 4

            def add_rows(m):
                q = strip(m, share)
                total = sum_st[0, q, 0:columns].astype(WIDE) + sum_st[1, q, 0:columns].astype(WIDE)
                total = total + jnp.where(k > 0, sum_st[2, q, 0:columns].astype(WIDE), 0.0)
                res[g][b, q, :] = total.astype(LOW)

            each(4, add_rows)

            @pl.when(k + 1 < planes)
            def _():
                z_hop(g, k, b).start()

            @pl.when(k + 1 == planes)
            def _():
                for section in sections(g):
                    keeps, source, copy = home_copy(g, b, section)

                    @pl.when(keeps)
                    def _():
                        pltpu.make_async_copy(source, home[g], home_got.at[i]).start()

                    @pl.when(jnp.logical_not(keeps))
                    def _():
                        copy.start()

    def sums(g, first_step, count):
        each(count, lambda n: sum_at(g, first_step + n), "sums_" + g)

    def turn(source, goal):
        def run(i):
            q = strip(i, BLOCK)
            goal[:, q] = source[q, :].astype(WIDE).T.astype(LOW)

        each(tiles, run, "turn")

    def dm_hop(n, source):
        q = pl.ds(pl.multiple_of((2 * c + n) * BLOCK, BLOCK), BLOCK)
        return push(source.at[q, :], c_v.at[q, :], dm_sent.at[n], dm_got.at[n], at.beside)

    def df_hop(n, core):
        q = pl.ds(pl.multiple_of((2 * core + n) * BLOCK, BLOCK), BLOCK)
        return push(c_v.at[q, :], c_v.at[q, :], df_sent.at[n], df_got.at[n], at.twin)

    @pl.when(at.encodes)
    def _():
        turn(s_v, ta)

        def back_rows(m):
            n = lax.div(m, 2)
            own = lax.rem(m, 2) == 0
            i = jnp.where(own, 2 * c + n, 2 * (1 - c) + n)
            q = strip(i, BLOCK)

            @pl.when(own)
            def _():
                dm_hop(n, c_v).wait_recv()
                df_hop(n, c).start()

            @pl.when(jnp.logical_not(own))
            def _():
                df_hop(n, 1 - c).wait_recv()

            grad = norm_grad(late_v[q, :], g2, c_v[q, :].astype(WIDE), 2, ours(i))
            late_v[q, :] = grad
            low = grad.astype(LOW)
            part = None
            for b in range(2):
                d_pre = (mm(low, dn_v[b]) * b_v[b, q, :].astype(WIDE)).astype(LOW)
                b_v[b, q, :] = d_pre
                term = mm_nt(d_pre, up_v[b])
                part = term if part is None else part + term
            send_v[0, q, :] = part.astype(LOW)

            @pl.when(own)
            def _():
                df_hop(n, c).wait_send()

            c_v[q, :] = low
            exchange(2, i).start()

        each(tiles, back_rows)

    pl.when(at.decodes)(lambda: turn(s_v, ta))
    turn(c_v, tb)

    def ffn_block(s, j):
        def ffn_half(b):
            dw_st[s, b, :, 0:768] = mm(ta[j, :], b_v[b]).astype(LOW)
            dw_st[s, b, :, 768:1536] = mm(tb[j, :], a_v[b]).astype(LOW)

        each(2, ffn_half)

    emit("ffn", ffn_block)

    @pl.when(at.decodes)
    def _():
        copying("act", a_v, act_k).wait()
        packed = copying("pc", pc_k, packed_v)
        small = [copying("oc", oc_k, o_v), copying("lsec", lsec_k, lse_v), copying("second", second_k, s_v)]
        packed.start()
        for copy in small:
            copy.start()

        def late_rows(i):
            q = strip(i, BLOCK)
            grad = c_v[q, :].astype(WIDE) + norm_grad(late_v[q, :], g2, joined(2, i), 2, ours(i))
            late_v[q, :] = grad
            g_v[q, :] = grad.astype(LOW)

        each(tiles, late_rows)

        def cross_out(i):
            q = strip(i, BLOCK)
            for b in range(2):
                do_v[b, q, :] = mm(g_v[q, :], crs_v[b, :, 128:384]).astype(LOW)

        each(tiles, cross_out)
        for copy in small:
            copy.wait()
        packed.wait()
        b_v[...] = jnp.zeros_like(b_v)

        def cross_head(n):
            b = lax.div(n, 3)
            attend_back_block(
                lax.rem(n, 3), a_v.at[b], o_v.at[b], do_v.at[b], b_v.at[b], lse_v, n, bias_cross,
                kx, qx, vx, gx, kt_v, dk_v, dv_v, False,
            )

        each(6, cross_head)
        sent(1)

        def to_memory(q):
            return mm_nt(b_v[0, q, 256:640], crs_v[0, :, 384:768]) + mm_nt(b_v[1, q, 256:640], crs_v[1, :, 384:768])

        def far(n):
            i = 2 * (1 - c) + n
            q = strip(i, BLOCK)
            send_v[1, q, :] = to_memory(q).astype(LOW)
            exchange(3, i).start()

        each(2, far)

        def near(n):
            i = 2 * c + n
            q = strip(i, BLOCK)
            part = to_memory(q)
            exchange(3, i).wait_recv()
            send_v[1, q, :] = (part + recv_v[1, q, :].astype(WIDE)).astype(LOW)
            dm_hop(n, send_v.at[1]).start()

        each(2, near)

        def to_query(i):
            q = strip(i, BLOCK)
            part = mm_nt(b_v[0, q, 0:256], crs_v[0, :, 0:256]) + mm_nt(b_v[1, q, 0:256], crs_v[1, :, 0:256])
            send_v[0, q, :] = part.astype(LOW)
            exchange(4, i).start()

        sent(2)
        each(tiles, to_query)
        sums("ffn", 0, 2)
        turn(s_v, ta)
        stage_in = copying("memory", memory_k, s_v)
        stage_in.start()
        turn(g_v, tc)
        stage_in.wait()
        turn(s_v, tb)
        copying("first", first_k, s_v).start()

        def crs_block(s, j):
            def att_half(b):
                left = mm(ta[j, :], b_v[b, :, 0:256])
                out = mm(tc[j, :], o_v[b])
                dw_st[s, b, :, 0:128] = left[:, 0:128].astype(LOW)
                dw_st[s, b, :, 128:256] = (left[:, 128:256] + out[:, 0:128]).astype(LOW)
                dw_st[s, b, :, 256:384] = out[:, 128:256].astype(LOW)
                dw_st[s, b, :, 384:768] = mm(tb[j, :], b_v[b, :, 256:640]).astype(LOW)

            each(2, att_half)

        emit("crs", crs_block)
        sums("ffn", 2, 2)

        def below(i):
            q = strip(i, BLOCK)
            grad = late_v[q, :] + norm_grad(mid_v[q, :], g1, joined(4, i), 1, ours(i))
            late_v[q, :] = grad
            g_v[q, :] = grad.astype(LOW)

        each(tiles, below)
        copying("first", first_k, s_v).wait()

        def gone(n):
            exchange(3, 2 * (1 - c) + n).wait_send()
            dm_hop(n, send_v.at[1]).wait_send()

        each(2, gone)

    @pl.when(at.encodes)
    def _():
        copying("first", first_k, s_v).start()
        each(2, lambda i: mem_send(i).wait_send())

        def below(i):
            q = strip(i, BLOCK)
            grad = late_v[q, :] + norm_grad(mid_v[q, :], g1, joined(2, i), 1, ours(i))
            late_v[q, :] = grad
            g_v[q, :] = grad.astype(LOW)

        each(tiles, below)
        copying("first", first_k, s_v).wait()
        sent(1)

    packed = copying("p", p_k, packed_v)
    small = [copying("o", o_k, o_v), copying("lse", lse_k, lse_v)]
    packed.start()
    for copy in small:
        copy.start()

    def self_out(i):
        q = strip(i, BLOCK)
        for b in range(2):
            do_v[b, q, :] = mm(g_v[q, :], att_v[b, :, 128:384]).astype(LOW)

    each(tiles, self_out)
    b_v[...] = jnp.zeros_like(b_v)
    for copy in small:
        copy.wait()
    packed.wait()

    def self_heads(causal, hook):
        def self_head(n):
            b = lax.div(n, 3)
            attend_back_block(
                lax.rem(n, 3), a_v.at[b], o_v.at[b], do_v.at[b], b_v.at[b], lse_v, n, bias_self,
                kx, qx, vx, gx, kt_v, dk_v, dv_v, causal,
            )
            hook(n)

        each(6, self_head)

    def enc_hook(n):
        @pl.when(jnp.logical_and(n != 2, n != 5))
        def _():
            sum_at("ffn", n - lax.div(n, 3))

    def dec_hook(n):
        @pl.when(n < 4)
        def _():
            sum_at("ffn", 4 + n)

        @pl.when(n >= 4)
        def _():
            sum_at("crs", n - 4)

    pl.when(at.encodes)(lambda: self_heads(False, enc_hook))
    pl.when(at.decodes)(lambda: self_heads(True, dec_hook))

    def to_rows(q):
        part = None
        for b in range(2):
            term = mm_nt(b_v[b, q, 0:256], att_v[b, :, 0:256]) + mm_nt(b_v[b, q, 256:640], att_v[b, :, 384:768])
            part = term if part is None else part + term
        return part

    def far_rows(n):
        i = 2 * (1 - c) + n
        q = strip(i, BLOCK)
        send_v[1, q, :] = to_rows(q).astype(LOW)
        exchange(5, i).start()

    each(2, far_rows)
    pl.when(at.encodes)(lambda: sums("ffn", 4, 2))
    pl.when(at.decodes)(lambda: sums("crs", 2, 2))
    turn(s_v, ta)
    x_in_v = copying("x", x_k, s_v)
    x_in_v.start()
    turn(g_v, tc)

    def att_block(s, j):
        def att_half(b):
            left = mm(ta[j, :], b_v[b, :, 0:256])
            out = mm(tc[j, :], o_v[b])
            dw_st[s, b, :, 0:128] = left[:, 0:128].astype(LOW)
            dw_st[s, b, :, 128:256] = (left[:, 128:256] + out[:, 0:128]).astype(LOW)
            dw_st[s, b, :, 256:384] = out[:, 128:256].astype(LOW)
            dw_st[s, b, :, 384:768] = mm(ta[j, :], b_v[b, :, 256:640]).astype(LOW)

        each(2, att_half)

    emit("att", att_block)
    pl.when(at.decodes)(lambda: sums("crs", 4, 2))

    @pl.when(both(relay, at.decodes))
    @jax.named_scope("hand_on")
    def _():
        for k in range(planes):
            via_hop(k).wait_recv()
            hand_on(k).start()

    x_in_v.wait()

    def near_rows(n):
        i = 2 * c + n
        q = strip(i, BLOCK)
        part = to_rows(q)
        exchange(5, i).wait_recv()
        grad = part + recv_v[1, q, :].astype(WIDE)
        value = late_v[q, :] + norm_grad(s_v[q, :].astype(WIDE), g0, grad, 0, True)
        out_st[strip(n, BLOCK), :] = value.astype(LOW)

    each(2, near_rows)
    out_put = copying("out", out_st, grad_k)
    out_put.start()
    out_put.wait()

    def grad_home(k):
        return k, grad_k.at[strip(k, rows), :], grad_low, gr_sent, gr_got

    def rows_leave():
        for k in range(2):
            go_home(*grad_home(k))

    pl.when(relay)(rows_leave)

    def gain_hop(n, source, device):
        return push(source, gain_buf.at[n], gr_hop_sent.at[n], gr_hop_got.at[n], device)

    gain_buf[0] = gain_v[...]
    twin_hop = gain_hop(1, gain_buf.at[0], at.twin)
    twin_hop.start()
    twin_hop.wait()
    peer_hop = gain_hop(3, gain_buf.at[2], (1 - c, z, lax.rem(t + 2, 4)))
    last = 4 + planes

    @pl.when(relay)
    def _():
        gain_buf[2] = gain_buf[0] + gain_buf[1]
        peer_hop.start()

    def ring_hop(n):
        return gain_hop(5 + n, gain_buf.at[4 + n], at.above)

    def gain_step(n):
        @pl.when(relay)
        @jax.named_scope("gains")
        def _():
            if n == 0:
                peer_hop.wait()
                gain_buf[4] = gain_buf[2] + gain_buf[3]
            else:
                ring_hop(n - 1).wait()
            if n < planes - 1:
                ring_hop(n).start()
            else:
                total = None
                for j in range(planes):
                    held = gain_buf[jnp.where(z == j, 4, 5 + lax.rem(z - 1 - j + planes, planes))]
                    total = held if total is None else total + held
                gain_buf[last] = total
                for b in range(2):
                    keeps = both(c == r, r == b)

                    @pl.when(keeps)
                    def _():
                        pltpu.make_async_copy(gain_buf.at[last], gain_buf.at[last + 1], gr_hop_got.at[last + 1]).start()

                    @pl.when(jnp.logical_not(keeps))
                    def _():
                        final_hop(b).start()

    def final_hop(b):
        return push(
            gain_buf.at[last], gain_buf.at[last + 1], gr_hop_sent.at[last + b], gr_hop_got.at[last + 1],
            (r, z, 2 * y + b),
        )

    def y3_home(k):
        return k, y3_k.at[strip(k, rows), :], block_out, blk_sent, blk_got

    def out_leaves():
        for k in range(2):
            go_home(*y3_home(k))

    @pl.when(at.decodes)
    def _():
        sums("att", 0, 2)
        copies = [copying("act", act_k, a_v), copying("late", late_k, mid_v)]
        for copy in copies:
            copy.start()
        sent(4)
        for copy in copies:
            copy.wait()

        def to_out(q):
            return mm_nt(a_v[0, q, :], dn_v[0]) + mm_nt(a_v[1, q, :], dn_v[1])

        def far_out(n):
            i = 2 * (1 - c) + n
            q = strip(i, BLOCK)
            send_v[0, q, :] = to_out(q).astype(LOW)
            exchange(6, i).start()

        each(2, far_out)

        def near_out(n):
            i = 2 * c + n
            q = strip(i, BLOCK)
            part = to_out(q)
            exchange(6, i).wait_recv()
            out_st[strip(n, BLOCK), :] = (mid_v[q, :] + part + recv_v[0, q, :].astype(WIDE)).astype(LOW)

        each(2, near_out)
        y3_put = copying("out", out_st, y3_k)
        y3_put.start()
        y3_put.wait()
        pl.when(relay)(out_leaves)

    @pl.when(other)
    def _():
        for k in range(planes):
            y_hop("att", k, 0).wait_send()
            pl.when(at.decodes)(lambda: y_hop("att", k, 1).wait_send())
            pl.when(at.encodes)(lambda: via_hop(k).wait_send())
        rows_leave()
        pl.when(at.decodes)(out_leaves)

    @pl.when(at.encodes)
    def _():
        sums("att", 1, 1)
        sums("ffn", 6, 2)

    pl.when(at.decodes)(lambda: sums("crs", 6, 2))

    def last_sums(n):
        @pl.when(jnp.logical_or(both(at.encodes, n >= 1), n >= 2))
        def _():
            sum_at("att", n + jnp.where(at.encodes, 1 - 2 * lax.rem(n, 2), 0))

        for m in range(planes):
            pl.when(n == 2 * m)(functools.partial(gain_step, m))

    each(2 * planes, last_sums)

    with jax.named_scope("await_gains"):
        final = gain_buf.at[last + 1]
        push(gain_buf.at[last], final, gr_hop_sent.at[last], gr_hop_got.at[last + 1], at.twin).wait_recv()
    gains_home = copying("gains", final, gain_out)
    gains_home.start()
    with jax.named_scope("await_rows"):
        for n in range(2):
            for goal, got in ((block_out, blk_got), (grad_low, gr_got)):
                push(goal.at[n], goal.at[n], blk_sent.at[0], got.at[n], at.twin).wait_recv()
    for i, g in enumerate(SUMS):
        with jax.named_scope("await_home_" + g):
            push(home[g], home[g], home_sent.at[i, 0, 0], home_got.at[i], at.twin).wait_recv()
    gains_home.wait()
    for k in range(2):
        went_home(*grad_home(k))

    @pl.when(at.encodes)
    def _():
        for k in range(2):
            went_home(*memory_home(k))
        sent(2)

    @pl.when(at.decodes)
    def _():
        for k in range(2):
            went_home(*y3_home(k))
        each(2, lambda n: exchange(6, 2 * (1 - c) + n).wait_send())

    each(2, lambda n: exchange(5, 2 * (1 - c) + n).wait_send())

    @pl.when(relay)
    def _():
        for b in range(2):
            pl.when(jnp.logical_not(both(c == r, r == b)))(lambda: final_hop(b).wait_send())

    for g in SUMS:
        there = at.decodes if g == "crs" else jnp.logical_or(at.decodes, at.encodes)

        if g != "att":

            @pl.when(both(other, there))
            def _():
                for k in range(planes):
                    for b in range(2):
                        y_hop(g, k, b).wait_send()

        @pl.when(both(relay, there))
        def _():
            for b in range(2):
                for section in sections(g):
                    keeps, source, copy = home_copy(g, b, section)

                    @pl.when(jnp.logical_not(keeps))
                    def _():
                        copy.wait_send()

    @pl.when(both(relay, at.decodes))
    def _():
        for k in range(planes):
            hand_on(k).wait_send()

    gain_copy.wait_send()
    for g in DIRECT:
        launch_over(g).wait_send()

    @pl.when(jnp.logical_not(stays))
    def _():
        for g in ("att", "up", "dn"):
            push(shard[g], vmem[g].at[r, here, :], x_sent.at[GROUPS.index(g)], x_sem.at[0, 0], relay_dev).wait_send()

    @pl.when(jnp.logical_not(crs_stays))
    def _():
        push(crs_in, crs_goal(r, c), x_sent.at[1], c_sem.at[0, 0], crs_dev).wait_send()
        push(cot_in.at[c], cot_goal, row_sent.at[2], cot_got.at[r], at.twin).wait_send()

    for s in range(2):

        @pl.when(jnp.logical_not(row_stays(s)))
        def _():
            push(x_in.at[s], row_goal, row_sent.at[s], row_got.at[r], at.twin).wait_send()

    for g in GROUPS:
        member = both(relay, at.decodes) if g == "crs" else relay

        @pl.when(member)
        def _():
            for k in range(planes):
                for b in range(2):
                    if k:
                        ring(g, k, b).wait_send()
                    if (k or g not in DIRECT) and (k != 1 or (g, b) not in ASIDE):
                        cross_over(g, k, b).wait_send()

    @pl.when(other)
    def _():
        for g, b in ASIDE:
            side_hop(g, b).wait_send()


def block_call(planes, slot, width, hidden, depth, args):
    shape = jax.ShapeDtypeStruct
    rows = slot // 4
    square = (slot, width)
    wides = {"ffn": 2 * hidden, "crs": width, "att": width}
    packed, outs, logs, acts = (2, slot, 640), (2, slot, 256), (8, slot), (2, slot, hidden)
    out_shape = (
        [shape((2, rows, width), LOW)] * 2
        + [shape((depth, 2 * hidden), LOW), shape((depth, width // 2), LOW), shape((depth, width), LOW)]
        + [shape((8, width), WIDE)]
        + [shape(square, LOW)] * 4
        + [shape(square, WIDE), shape(square, LOW)]
        + [shape(packed, LOW), shape(outs, LOW), shape(logs, WIDE)] * 2
        + [shape(acts, LOW)]
        + [shape((2 * rows, width), LOW)] * 2
        + [shape((planes, 2, depth, wides[g]), LOW) for g in SUMS] * 3
        + [shape((planes, depth, width), LOW)]
    )
    dma = pltpu.SemaphoreType.DMA
    v = pltpu.VMEM
    groups = len(GROUPS)
    scratch = (
        [v((2, width, width), LOW)] * 2
        + [v((2, width, hidden), LOW)] * 2
        + [v(acts, LOW)] * 2
        + [v(outs, LOW)] * 2
        + [v(square, WIDE)] * 2
        + [v(square, LOW)] * 3
        + [v((width, slot), LOW)] * 3
        + [v((2,) + square, LOW)] * 2
        + [v((slot, TILE), LOW)] * 4
        + [v((slot, TILE), WIDE)] * 2
        + [v((TILE, slot), LOW), v(logs, WIDE), v((8, width), WIDE), v((2, 3, width), LOW)]
        + [v((planes + 6, 8, width), WIDE)]
        + [v((2 * rows, width), LOW), v((2, 2, depth, 2 * hidden), LOW), v((3, depth, 2 * hidden), LOW)]
        + [v((slot, TILE), LOW)] * 2
        + [v((2, depth, wides[g]), LOW) for g in SUMS]
        + [dma((groups, 2)), dma((groups,)), dma((groups,)), dma((2, 2))]
        + [dma((groups, planes, 2))] * 4
        + [dma((groups, 2))] * 2
        + [dma((2,)), dma((3,)), dma((4,)), dma((2,)), dma((3,)), dma((40,)), dma((7, 4)), dma((7, 4))]
        + [dma((2,))] * 8
        + [dma((3, planes, 2))] * 4
        + [dma((3,)), dma((3, 2, 2))]
        + [dma((2,))] * 4
        + [dma((planes + 6,))] * 2
        + [dma((3,)), dma((2,))]
        + [dma((planes,))] * 4
    )
    any_spec = pl.BlockSpec(memory_space=pl.ANY)
    vmem_spec = pl.BlockSpec(memory_space=pltpu.VMEM)
    return pl.pallas_call(
        functools.partial(block_kernel, planes),
        out_shape=out_shape,
        in_specs=[any_spec] * 6 + [vmem_spec, pl.BlockSpec(memory_space=pltpu.SMEM), vmem_spec],
        out_specs=[any_spec] * len(out_shape),
        scratch_shapes=scratch,
        compiler_params=pltpu.CompilerParams(collective_id=0, has_side_effects=True, vmem_limit_bytes=VMEM_BYTES),
    )(*args)


def widen_kernel(
    block_in, grad_in, ffn_in, crs_in, att_in, gain_in,
    block_out, grad_out, up_out, dn_out, qkv_out, out_out, crs_out, gain_out, last_out,
):
    c = lax.axis_index("section")
    hidden = up_out.shape[1]
    share, part = block_in.shape[1] // 4, ffn_in.shape[0] // 4

    def strips(i):
        q = strip(i, share)
        for n in range(2):
            block_out[n, q, :] = block_in[n, q, :]
            grad_out[n, q, :] = grad_in[n, q, :].astype(WIDE)
        q = strip(i, part)
        up_out[q, :] = ffn_in[q, 0:hidden].astype(WIDE)
        dn_out[q, :] = ffn_in[q, hidden : 2 * hidden].astype(WIDE)

    each(4, strips)
    tiles = [crs_in[:, TILE * n : TILE * (n + 1)].astype(WIDE) for n in range(3)]
    mixed = jnp.where(c == 1, tiles[1], tiles[2])
    crs_out[:, 0, 0:TILE] = tiles[0]
    crs_out[:, 0, TILE : TILE + HEAD] = mixed[:, 0:HEAD]
    crs_out[:, 1, 0:TILE] = jnp.where(c == 1, tiles[2], tiles[1])
    crs_out[:, 1, TILE : TILE + HEAD] = pltpu.roll(mixed, HEAD, 1)[:, 0:HEAD]
    q_tile, q_o, o_tile, k_tile, v_tile, k_v = (att_in[:, TILE * n : TILE * (n + 1)].astype(WIDE) for n in range(6))
    for n, (whole, rest) in enumerate(((q_tile, q_o), (k_tile, k_v), (v_tile, pltpu.roll(k_v, HEAD, 1)))):
        qkv_out[n, :, 0:TILE] = whole
        qkv_out[n, :, TILE : TILE + HEAD] = rest[:, 0:HEAD]
    out_out[0:TILE, :] = o_tile.T
    out_out[TILE : TILE + HEAD, :] = pltpu.roll(q_o, HEAD, 1).T[0:HEAD, :]
    gain_out[...] = gain_in[0:2, :]
    last_out[...] = gain_in[2:3, :]


def widen_call(kept):
    shape = jax.ShapeDtypeStruct
    rows, width = kept[0].shape[1:]
    depth, hidden = kept[2].shape[0], kept[2].shape[1] // 2
    wide = width // 4
    return pl.pallas_call(
        widen_kernel,
        out_shape=[
            shape((2, rows, width), LOW), shape((2, rows, width), WIDE), shape((depth, hidden), WIDE),
            shape((depth, hidden), WIDE), shape((3, depth, wide), WIDE), shape((wide, depth), WIDE),
            shape((depth, 2, wide), WIDE), shape((2, width), WIDE), shape((1, width), WIDE),
        ],
    )(*kept)


def ring_gather(lay, shard):
    planes = lay.planes
    rows = shard.shape[1]
    if planes > 4:
        piece = lax.all_gather(shard, "dp", axis=1, tiled=True)
        across = lay.route(piece, lambda c, z, t: (c, z, (t + 2) % 4) if c == t // 2 else None)
        return jnp.where(lay.relays, piece, across)
    relay = lambda c, z, t: (c, (z + 1) % planes, t) if c == t // 2 else None
    whole = jnp.zeros((shard.shape[0], planes * rows, shard.shape[2]), shard.dtype)
    piece = shard
    for step in range(planes):
        across = lay.route(piece, lambda c, z, t: (c, z, (t + 2) % 4) if c == t // 2 else None)
        chosen = jnp.where(lay.relays, piece, across)
        whole = lax.dynamic_update_slice(whole, chosen, (0, ((lay.plane - step) % planes) * rows, 0))
        if step + 1 < planes:
            piece = lay.route(piece, relay)
    return whole


def ring_scatter(lay, total, holder):
    planes = lay.planes
    rows = total.shape[1] // planes
    low = total.astype(LOW)
    across = lay.route(
        low, lambda c, z, t: (c, z, (t + 2) % 4) if (c != t // 2 and t % 2 == holder) else None
    )
    summed = low.astype(WIDE) + across.astype(WIDE)
    if planes > 4:
        return lax.psum_scatter(summed.astype(LOW), "dp", scatter_dimension=1, tiled=True)
    relay = lambda c, z, t: (c, (z + 1) % planes, t) if (c == t // 2 and t % 2 == holder) else None
    take = lambda j: lax.dynamic_slice_in_dim(summed, (j % planes) * rows, rows, 1)
    running = take(lay.plane - 1)
    for step in range(1, planes):
        running = lay.route(running.astype(LOW), relay).astype(WIDE) + take(lay.plane - 1 - step)
    return running.astype(LOW)


def hand_back(lay, value, holder, section):
    same = lay.route(
        value[0], lambda c, z, t: (section, z, t) if (c == t // 2 and t % 2 == holder) else None
    )
    beside = lay.route(
        value[1], lambda c, z, t: (section, z, t ^ 1) if (c == t // 2 and t % 2 == holder) else None
    )
    return same.astype(WIDE) + beside.astype(WIDE)


def general_body(block_input, w_self, w_self_out, w_cross, w_up, w_down, norm_gains, lengths, task_mask, out_grad):
    lay = Layout()
    seqs, rows, width = block_input.shape[1:]
    slot = rows * lay.chips
    sec = lay.core
    item = lay.item

    def spread(value, first):
        pick = value[jnp.where(first, lay.chip % 2, 1 - lay.chip % 2)]
        flip = 0 if first else 1
        return lay.route(pick, lambda c, z, t: (t // 2, z, 2 * ((t % 2) ^ flip) + c))

    def merge_rows(mine, theirs):
        low_half = jnp.where(lay.core == 0, mine, theirs)
        high_half = jnp.where(lay.core == 0, theirs, mine)
        return jnp.concatenate([low_half[0], low_half[1], high_half[0], high_half[1]], axis=0)

    first = spread(block_input[0], True)
    second = spread(block_input[0], False)
    mine = jnp.where(item == 0, jnp.stack([first, second]), jnp.stack([second, first]))
    x_rows = merge_rows(mine, lay.other_core(mine)).astype(WIDE)

    picked = out_grad[lay.core]
    even = lay.route(picked, lambda c, z, t: (t // 2, z, 2 * c + 1) if t % 2 == 0 else None)
    odd = lay.route(picked, lambda c, z, t: (t // 2, z, 2 * c + 1) if t % 2 == 1 else None)
    mine = jnp.stack([even, odd])
    cotangent = merge_rows(mine, lay.other_core(mine))

    gains_here = norm_gains[0].astype(WIDE)
    gains = jnp.where(sec == lay.role, gains_here, lay.other_core(norm_gains[0]).astype(WIDE))

    depth = w_self.shape[1]
    wide = w_self.shape[3]
    self_block = pack_heads(
        {"q": w_self[0, :, 0], "k": w_self[0, :, 1], "v": w_self[0, :, 2], "o": w_self_out[0].T}
    )
    feed_block = jnp.concatenate([w_up[0], w_down[0].T], axis=1)
    cross_block = w_cross[0].reshape(depth, 2 * wide)

    def collect(block):
        same = lay.route(block, lambda c, z, t: (t // 2, z, t) if c == t % 2 else None)
        beside = lay.route(block, lambda c, z, t: (t // 2, z, t ^ 1) if c != t % 2 else None)
        return jnp.stack([same, beside])

    def collect_cross(block, section):
        same = lay.route(block, lambda c, z, t: (t // 2, z, t) if (c == section and t % 2 == 1) else None)
        beside = lay.route(block, lambda c, z, t: (t // 2, z, t ^ 1) if (c == section and t % 2 == 0) else None)
        return same, beside

    w_att = ring_gather(lay, collect(self_block))
    w_ffn = ring_gather(lay, collect(feed_block))
    memory_side = collect_cross(cross_block, 0)
    query_side = collect_cross(cross_block, 1)
    w_crs = ring_gather(
        lay,
        jnp.stack(
            [
                pack_heads({"q": q[:, :wide], "k": m[:, :wide], "v": m[:, wide:], "o": q[:, wide:]})
                for m, q in zip(memory_side, query_side)
            ]
        ),
    )
    hidden = w_up.shape[2]
    part = lambda w, name: jnp.concatenate([unpack_heads(w[0], name), unpack_heads(w[1], name)], axis=1)
    att = {n: part(w_att, n) for n in "qkvo"}
    crs = {n: part(w_crs, n) for n in "qkvo"}
    up = jnp.concatenate([w_ffn[0, :, :hidden], w_ffn[1, :, :hidden]], axis=1)
    down_t = jnp.concatenate([w_ffn[0, :, hidden:], w_ffn[1, :, hidden:]], axis=1)

    positions = jnp.arange(slot)
    own_length = jnp.where(lay.is_decoder, lengths[1, item], lengths[0, item])
    self_allowed = (positions[None, :] < own_length) & (
        (positions[None, :] <= positions[:, None]) | jnp.logical_not(lay.is_decoder)
    )
    cross_allowed = jnp.broadcast_to(
        ((positions < lengths[0, item]) & (task_mask[item] == 1))[None], (slot, slot)
    )

    def joined(partial):
        low = partial.astype(LOW)
        return low.astype(WIDE) + lay.other_core(low).astype(WIDE)

    normed0 = layer_norm(x_rows, gains[0]).astype(LOW)
    q, k, v = (mm(normed0, att[n]).astype(LOW) for n in "qkv")
    out_self, lse_self = attend(q, k, v, self_allowed)
    x_mid = x_rows + joined(mm_nt(out_self, att["o"]))
    normed1 = layer_norm(x_mid, gains[1]).astype(LOW)

    pre_enc = mm(normed1, up)
    act_enc, slope_enc = gelu_parts(pre_enc)
    act_enc = act_enc.astype(LOW)
    x_late_enc = x_mid + joined(mm_nt(act_enc, down_t))
    memory_enc = layer_norm(x_late_enc, gains[2]).astype(LOW)
    memory = lay.route(memory_enc, lambda c, z, t: (c, z, t ^ 1) if t % 2 == 0 else None)

    cq = mm(normed1, crs["q"]).astype(LOW)
    ck, cv = (mm(memory, crs[n]).astype(LOW) for n in "kv")
    out_cross, lse_cross = attend(cq, ck, cv, cross_allowed)
    x_late = x_mid + joined(mm_nt(out_cross, crs["o"]))
    normed2 = layer_norm(x_late, gains[2]).astype(LOW)
    pre_dec = mm(normed2, up)
    act_dec, slope_dec = gelu_parts(pre_dec)
    act_dec = act_dec.astype(LOW)
    result_dec = (x_late + joined(mm_nt(act_dec, down_t))).astype(LOW)

    d_out = cotangent.astype(WIDE)
    d_pre = (slope_dec * mm(cotangent, down_t)).astype(LOW)
    d_ffn_dec = jnp.concatenate([mm_tn(normed2, d_pre), mm_tn(cotangent, act_dec)], axis=1)
    d_late_norm, d_gain2_dec = norm_back(x_late, gains[2], joined(mm_nt(d_pre, up)))
    d_late = d_out + d_late_norm
    grad_late = d_late.astype(LOW)
    d_att = mm(grad_late, crs["o"]).astype(LOW)
    d_cq, d_ck, d_cv = attend_back(cq, ck, cv, lse_cross, d_att, cross_allowed)
    d_memory = joined(mm_nt(d_ck, crs["k"]) + mm_nt(d_cv, crs["v"]))
    d_crs = {
        "q": mm_tn(normed1, d_cq),
        "k": mm_tn(memory, d_ck),
        "v": mm_tn(memory, d_cv),
        "o": mm_tn(grad_late, out_cross),
    }
    d_mid_norm, d_gain1_dec = norm_back(x_mid, gains[1], joined(mm_nt(d_cq, crs["q"])))
    d_mid_dec = d_late + d_mid_norm

    d_memory = lay.route(d_memory.astype(LOW), lambda c, z, t: (c, z, t ^ 1) if t % 2 == 1 else None).astype(WIDE)
    d_late_enc, d_gain2_enc = norm_back(x_late_enc, gains[2], d_memory)
    grad_late_enc = d_late_enc.astype(LOW)
    d_pre = (slope_enc * mm(grad_late_enc, down_t)).astype(LOW)
    d_ffn_enc = jnp.concatenate([mm_tn(normed1, d_pre), mm_tn(grad_late_enc, act_enc)], axis=1)
    d_mid_norm, d_gain1_enc = norm_back(x_mid, gains[1], joined(mm_nt(d_pre, up)))
    d_mid_enc = d_late_enc + d_mid_norm

    d_mid = jnp.where(lay.is_decoder, d_mid_dec, d_mid_enc)
    grad_mid = d_mid.astype(LOW)
    d_att = mm(grad_mid, att["o"]).astype(LOW)
    d_q, d_k, d_v = attend_back(q, k, v, lse_self, d_att, self_allowed)
    d_norm = joined(mm_nt(d_q, att["q"]) + mm_nt(d_k, att["k"]) + mm_nt(d_v, att["v"]))
    d_att_w = {
        "q": mm_tn(normed0, d_q),
        "k": mm_tn(normed0, d_k),
        "v": mm_tn(normed0, d_v),
        "o": mm_tn(grad_mid, out_self),
    }
    d_first, d_gain0 = norm_back(x_rows, gains[0], d_norm)
    d_rows = d_mid + d_first

    half = 3 * HEAD

    def blocks(parts):
        return jnp.stack(
            [pack_heads({n: parts[n][:, half * b : half * (b + 1)] for n in parts}) for b in range(2)]
        )

    def feed_blocks(both):
        total = both.shape[1] // 2
        return jnp.stack(
            [
                jnp.concatenate(
                    [both[:, hidden * b : hidden * (b + 1)], both[:, total + hidden * b : total + hidden * (b + 1)]],
                    axis=1,
                )
                for b in range(2)
            ]
        )

    self_total = blocks(d_att_w)
    home_self = hand_back(lay, ring_scatter(lay, self_total, 0), 0, 0) + hand_back(
        lay, ring_scatter(lay, self_total, 1), 1, 1
    )
    home_feed = hand_back(lay, ring_scatter(lay, feed_blocks(d_ffn_enc), 0), 0, 0) + hand_back(
        lay, ring_scatter(lay, feed_blocks(d_ffn_dec), 1), 1, 1
    )
    cross_total = ring_scatter(lay, blocks(d_crs), 1)
    side = lambda names: jnp.stack(
        [jnp.concatenate([unpack_heads(cross_total[b], n) for n in names], axis=1) for b in range(2)]
    )
    home_cross = hand_back(lay, side("kv"), 1, 0) + hand_back(lay, side("qo"), 1, 1)

    g_self = jnp.stack([unpack_heads(home_self, n) for n in "qkv"], axis=1)[None]
    g_self_out = unpack_heads(home_self, "o").T[None]
    g_cross = home_cross.reshape(1, depth, 2, wide)
    g_up = home_feed[:, :hidden][None]
    g_down = home_feed[:, hidden:].T[None]

    gain2 = jnp.where(lay.is_decoder, d_gain2_dec, d_gain2_enc)
    gain1 = jnp.where(lay.is_decoder, d_gain1_dec, d_gain1_enc)
    gain_rows = jnp.stack([d_gain0, gain1, gain2])
    slots = jnp.stack(
        [
            jnp.where((lay.role == r) & (lay.core == 0), gain_rows, 0.0)
            for r in range(2)
        ]
    )
    gain_total = lax.psum(slots, AXES)[sec][None]

    def rows_home(value):
        mine = lax.dynamic_slice_in_dim(value, lay.core * 2 * rows, 2 * rows, 0).reshape(2, rows, width)
        a = lay.route(mine[item], lambda c, z, t: (t % 2, z, 2 * c + t // 2))
        b = lay.route(mine[1 - item], lambda c, z, t: (t % 2, z, 2 * c + 1 - t // 2))
        even = lay.chip % 2 == 0
        return jnp.where(even, jnp.stack([a, b]), jnp.stack([b, a]))[None]

    block_output = rows_home(jnp.where(lay.is_decoder, result_dec, memory_enc))
    input_grad = rows_home(d_rows.astype(LOW)).astype(WIDE)
    return (
        block_output,
        input_grad,
        g_self,
        g_self_out,
        g_cross,
        g_up,
        g_down,
        gain_total[:, :2],
        gain_total[:, 2],
    )


def body(block_input, w_self, w_self_out, w_cross, w_up, w_down, norm_gains, lengths, task_mask, out_grad):
    lay = Layout()
    seqs, rows, width = block_input.shape[1:]
    slot = rows * lay.chips
    sec = lay.core
    item = lay.item

    if lay.planes != 4:
        return general_body(
            block_input, w_self, w_self_out, w_cross, w_up, w_down, norm_gains, lengths, task_mask, out_grad
        )

    depth = w_self.shape[1]
    wide = w_self.shape[3]
    hidden = w_up.shape[2]
    self_block = pack_heads(
        {"q": w_self[0, :, 0], "k": w_self[0, :, 1], "v": w_self[0, :, 2], "o": w_self_out[0].T}
    )
    pair = {"q": w_cross[0, :, 0], "o": w_cross[0, :, 1], "k": w_cross[0, :, 0], "v": w_cross[0, :, 1]}
    pieces = [pair[n][:, HEAD * h : HEAD * (h + 1)] for n, h in ORDER]
    cross_block = jnp.where(
        sec == 1, jnp.concatenate(pieces[:6], axis=1), jnp.concatenate(pieces[6:], axis=1)
    )
    kept = block_call(
        lay.planes,
        slot,
        width,
        hidden,
        depth,
        (self_block, cross_block, w_up[0], w_down[0].T, block_input[0], out_grad, norm_gains[0], lengths, task_mask),
    )[:6]
    block_output, input_grad, g_up, g_down, g_qkv, g_out, g_cross, g_gain, g_last = widen_call(kept)
    return (
        block_output[None],
        input_grad[None],
        jnp.swapaxes(g_qkv, 0, 1)[None],
        g_out[None],
        g_cross[None],
        g_up[None],
        g_down.T[None],
        g_gain[None],
        g_last,
    )


def solution(mesh):
    placed = (
        P("section", "dp", "tensor", None),
        P("section", "dp", None, "tensor"),
        P("section", "tensor", "dp"),
        P("section", "dp", None, "tensor"),
        P("section", "dp", "tensor"),
        P("section", "tensor", "dp"),
        P("section", None, None),
        P(None, "dp"),
        P("dp", None),
        P("dp", "tensor", None),
    )
    return jax.shard_map(
        body,
        mesh=mesh,
        in_specs=placed,
        out_specs=(
            P("section", "dp", "tensor", None),
            P("section", "dp", "tensor", None),
            P("section", "dp", None, "tensor"),
            P("section", "tensor", "dp"),
            P("section", "dp", None, "tensor"),
            P("section", "dp", "tensor"),
            P("section", "tensor", "dp"),
            P("section", None, None),
            P("section", None),
        ),
        check_vma=False,
    )
```

```python
import functools

import jax
import jax.numpy as jnp
from jax import lax
from jax.experimental import pallas as pl
from jax.experimental.pallas import tpu as pltpu
from jax.sharding import PartitionSpec as P

HEAD = 64
TILE = 128
EPSILON = 1e-05
SCORE_SCALE = 0.125
NEG_FILL = -1000000000.0
AXES = ("section", "dp", "tensor")
LOW = jnp.bfloat16
WIDE = jnp.float32


class Layout:
    def __init__(self):
        self.cores = lax.axis_size("section")
        self.planes = lax.axis_size("dp")
        self.chips = lax.axis_size("tensor")
        self.core = lax.axis_index("section")
        self.plane = lax.axis_index("dp")
        self.chip = lax.axis_index("tensor")
        self.role = self.chip % 2
        self.item = self.chip // 2
        self.is_decoder = self.role == 1
        self.relays = self.core == self.item

    def route(self, value, target):
        pairs = []
        for core in range(self.cores):
            for plane in range(self.planes):
                for chip in range(self.chips):
                    to = target(core, plane, chip)
                    if to is None:
                        continue
                    source = (core * self.planes + plane) * self.chips + chip
                    goal = (to[0] * self.planes + to[1]) * self.chips + to[2]
                    pairs.append((source, goal))
        return lax.ppermute(value, AXES, pairs)

    def other_core(self, value):
        return self.route(value, lambda c, z, t: (1 - c, z, t))


def normalize(values):
    centred = values - jnp.mean(values, axis=-1, keepdims=True)
    spread = jnp.mean(centred * centred, axis=-1, keepdims=True)
    scale = lax.rsqrt(spread + EPSILON)
    return centred * scale, scale


def layer_norm(values, gain):
    return normalize(values)[0] * gain


def norm_back(values, gain, grad):
    normal, scale = normalize(values)
    scaled = grad * gain
    first = jnp.mean(scaled, axis=-1, keepdims=True)
    second = jnp.mean(scaled * normal, axis=-1, keepdims=True)
    return (scaled - first - normal * second) * scale, jnp.sum(grad * normal, axis=0)


ORDER = (("q", 0), ("q", 1), ("q", 2), ("o", 2), ("o", 0), ("o", 1), ("k", 0), ("k", 1), ("v", 0), ("v", 1), ("k", 2), ("v", 2))


def pack_heads(parts):
    return jnp.concatenate([parts[n][:, HEAD * h : HEAD * (h + 1)] for n, h in ORDER], axis=1)


def unpack_heads(block, name):
    where = {(n, h): i for i, (n, h) in enumerate(ORDER)}
    return jnp.concatenate(
        [block[:, HEAD * where[(name, h)] : HEAD * (where[(name, h)] + 1)] for h in range(3)], axis=1
    )


def mm(left, right):
    return jnp.dot(left, right, preferred_element_type=WIDE)


def mm_nt(left, right):
    return lax.dot_general(left, right, (((1,), (1,)), ((), ())), preferred_element_type=WIDE)


def mm_tn(left, right):
    return lax.dot_general(left, right, (((0,), (0,)), ((), ())), preferred_element_type=WIDE)


def split_heads(value):
    return value.reshape(value.shape[0], -1, HEAD)


def attend(q, k, v, allowed):
    scores = jnp.einsum("qhd,khd->hqk", split_heads(q), split_heads(k), preferred_element_type=WIDE) * SCORE_SCALE
    scores = jnp.where(allowed[None], scores, NEG_FILL)
    top = jnp.max(scores, axis=-1, keepdims=True)
    power = jnp.exp(scores - top)
    total = jnp.sum(power, axis=-1, keepdims=True)
    probs = (power / total).astype(LOW)
    out = jnp.einsum("hqk,khd->qhd", probs, split_heads(v), preferred_element_type=WIDE)
    return out.astype(LOW).reshape(q.shape), top + jnp.log(total)


def attend_back(q, k, v, log_sum, d_out, allowed):
    scores = jnp.einsum("qhd,khd->hqk", split_heads(q), split_heads(k), preferred_element_type=WIDE) * SCORE_SCALE
    scores = jnp.where(allowed[None], scores, NEG_FILL)
    probs = jnp.exp(scores - log_sum)
    d_probs = jnp.einsum("qhd,khd->hqk", split_heads(d_out), split_heads(v), preferred_element_type=WIDE)
    inner = jnp.sum(probs * d_probs, axis=-1, keepdims=True)
    d_scores = (probs * (d_probs - inner)).astype(LOW)
    d_v = jnp.einsum("hqk,qhd->khd", probs.astype(LOW), split_heads(d_out), preferred_element_type=WIDE)
    d_q = jnp.einsum("hqk,khd->qhd", d_scores, split_heads(k), preferred_element_type=WIDE) * SCORE_SCALE
    d_k = jnp.einsum("hqk,qhd->khd", d_scores, split_heads(q), preferred_element_type=WIDE) * SCORE_SCALE
    return tuple(g.astype(LOW).reshape(q.shape) for g in (d_q, d_k, d_v))


def gelu_parts(value):
    coef = 0.7978845608028654
    cube = 0.044715
    inner = coef * (value + cube * value * value * value)
    soft = jnp.tanh(inner)
    slope = 0.5 * (1.0 + soft) + 0.5 * value * (1.0 - soft * soft) * coef * (1.0 + 3.0 * cube * value * value)
    return 0.5 * value * (1.0 + soft), slope


MESH = pl.DeviceIdType.MESH
GROUPS = ("att", "crs", "up", "dn")
BLOCK = 256
VMEM_BYTES = 62 * 2**20


def lanes(shape):
    return lax.broadcasted_iota(jnp.int32, shape, len(shape) - 1)


def subs(shape):
    return lax.broadcasted_iota(jnp.int32, shape, 0)


def strip(i, size):
    return pl.ds(pl.multiple_of(i * size, size), size)


def head_place(h):
    two = (h == 2).astype(jnp.int32)
    one = (h >= 1).astype(jnp.int32)
    return two, 2 + 2 * two, 3 + two, 1 - two, HEAD * (one - two), HEAD * one


def each(count, step, name=None):
    def run(i, carry):
        step(i)
        return carry

    with jax.named_scope(name or step.__name__):
        lax.fori_loop(0, count, run, 0)


class Place:
    def __init__(self, planes):
        self.planes = planes
        self.c = lax.axis_index("section")
        self.z = lax.axis_index("dp")
        self.t = lax.axis_index("tensor")
        self.y = lax.div(self.t, 2)
        self.r = lax.rem(self.t, 2)
        self.twin = (1 - self.c, self.z, self.t)
        self.above = (self.c, lax.rem(self.z + 1, planes), self.t)
        self.below = (self.c, lax.rem(self.z + planes - 1, planes), self.t)
        self.across = (self.c, self.z, lax.rem(self.t + 2, 4))
        self.beside = (self.c, self.z, self.t + 1 - 2 * self.r)
        self.relays = self.c == self.y
        self.encodes = self.r == 0
        self.decodes = self.r == 1

    def meet(self):
        barrier = pltpu.get_barrier_semaphore()
        peers = [self.above, self.below]
        for dc in range(2):
            for dt in range(4):
                if dc or dt:
                    peers.append((lax.rem(self.c + dc, 2), self.z, lax.rem(self.t + dt, 4)))
        for peer in peers:
            pl.semaphore_signal(barrier, inc=1, device_id=peer, device_id_type=MESH)
        pl.semaphore_wait(barrier, len(peers))


def push(source, goal, sent, got, device):
    return pltpu.make_async_remote_copy(
        src_ref=source, dst_ref=goal, send_sem=sent, recv_sem=got, device_id=device, device_id_type=MESH
    )


def both(first, second):
    return jnp.logical_and(first, second)


def center(values):
    middle = values - jnp.mean(values, axis=-1, keepdims=True)
    scale = lax.rsqrt(jnp.mean(middle * middle, axis=-1, keepdims=True) + EPSILON)
    return middle * scale, scale


def attend_block(h, p, o, lse, lse_row, bias, kx, qx, vt, causal):
    count = p.shape[0]
    qt, kt, vtile, ot, qlo, vlo = head_place(h)
    lane = lanes((count, TILE))
    in_q = both(lane >= qlo, lane < qlo + HEAD)
    in_v = both(lane >= vlo, lane < vlo + HEAD)
    spare = HEAD - qlo
    kx[...] = jnp.where(lane == spare, bias[...], jnp.where(in_q, p[:, strip(kt, TILE)], jnp.zeros((), LOW)))
    vt[...] = jnp.where(in_v, p[:, strip(vtile, TILE)].astype(WIDE), 1.0).T.astype(LOW)
    qx[...] = jnp.where(
        in_q, p[:, strip(qt, TILE)].astype(WIDE) * SCORE_SCALE, jnp.where(lane == spare, 1.0, 0.0)
    ).astype(LOW)
    size = count // 2 if causal else count

    def queries(i):
        q = strip(i, size) if causal else pl.ds(0, count)
        scores = mm_nt(kx[...], qx[q, :])
        if causal:
            scores = jnp.where(subs(scores.shape) <= lanes(scores.shape) + i * size, scores, NEG_FILL)
        top = jnp.max(scores, axis=0, keepdims=True)
        power = jnp.exp(scores - top).astype(LOW)
        out = mm(vt[...], power)
        total = jnp.where(vlo == 0, out[HEAD : HEAD + 1, :], out[0:1, :])
        result = (out / total).T
        lane = lanes((size, TILE))
        in_v = both(lane >= vlo, lane < vlo + HEAD)
        o[q, strip(ot, TILE)] = jnp.where(in_v, result, o[q, strip(ot, TILE)].astype(WIDE)).astype(LOW)
        row = subs((8, size))
        lse[:, q] = jnp.where(row == lse_row, top + jnp.log(total), lse[:, q])

    if causal:
        each(count // size, queries)
    else:
        queries(0)


SUMS = ("ffn", "crs", "att")
DIRECT = ("att", "up")
ASIDE = (("up", 0), ("up", 1), ("dn", 0), ("dn", 1))


def split_three(value):
    high = value.astype(LOW).astype(WIDE)
    middle = (value - high).astype(LOW).astype(WIDE)
    return high, middle, value - high - middle


def attend_back_block(h, p, o, d_o, d_p, lse, lse_row, bias, kx, qx, vx, gx, kt_v, dk_v, dv_v, causal):
    count = p.shape[0]
    qt, kt, vtile, ot, qlo, vlo = head_place(h)
    lane = lanes((count, TILE))
    in_q = both(lane >= qlo, lane < qlo + HEAD)
    in_v = both(lane >= vlo, lane < vlo + HEAD)
    sq, sv = HEAD - qlo, HEAD - vlo
    keys = jnp.where(
        in_q, p[:, strip(kt, TILE)].astype(WIDE), jnp.where(both(lane > sq, lane < sq + 4), 1.0, 0.0)
    )
    keys = jnp.where(lane == sq, bias[...].astype(WIDE), keys)
    kx[...] = keys.astype(LOW)
    kt_v[...] = keys.T.astype(LOW)
    vx[...] = jnp.where(
        in_v, p[:, strip(vtile, TILE)].astype(WIDE), jnp.where(both(lane >= sv, lane < sv + 3), 1.0, 0.0)
    ).astype(LOW)
    own = jnp.sum(jnp.where(subs((8, count)) == lse_row, lse[...], 0.0), axis=0, keepdims=True)
    a, b, c = split_three(-jnp.broadcast_to(own, (TILE, count)).T)
    extra = jnp.where(
        lane == sq,
        1.0,
        jnp.where(lane == sq + 1, a, jnp.where(lane == sq + 2, b, jnp.where(lane == sq + 3, c, 0.0))),
    )
    qx[...] = jnp.where(in_q, p[:, strip(qt, TILE)].astype(WIDE) * SCORE_SCALE, extra).astype(LOW)
    grad = jnp.where(in_v, d_o[:, strip(ot, TILE)].astype(WIDE), 0.0)
    inner = jnp.sum(grad * o[:, strip(ot, TILE)].astype(WIDE), axis=-1, keepdims=True)
    a, b, c = split_three(-inner)
    gx[...] = (
        grad + jnp.where(lane == sv, a, jnp.where(lane == sv + 1, b, jnp.where(lane == sv + 2, c, 0.0)))
    ).astype(LOW)
    size = count // 2 if causal else count

    def place(q, tile_index, low, value):
        cut = strip(tile_index, TILE)
        lane = lanes(value.shape)
        inside = both(lane >= low, lane < low + HEAD)
        d_p[q, cut] = jnp.where(inside, value, d_p[q, cut].astype(WIDE)).astype(LOW)

    whole = pl.ds(0, count)
    if causal:
        dk_v[...] = jnp.zeros_like(dk_v)
        dv_v[...] = jnp.zeros_like(dv_v)

    def queries(i):
        q = strip(i, size) if causal else pl.ds(0, count)
        scores = mm_nt(kx[...], qx[q, :])
        if causal:
            scores = jnp.where(subs(scores.shape) <= lanes(scores.shape) + i * size, scores, NEG_FILL)
        probs = jnp.exp(scores)
        d_scores = (probs * mm_nt(vx[...], gx[q, :])).astype(LOW)
        d_v = mm(probs.astype(LOW), gx[q, :])
        d_k = mm(d_scores, qx[q, :])
        place(q, qt, qlo, mm(kt_v[...], d_scores).T * SCORE_SCALE)
        if causal:
            dk_v[...] += d_k
            dv_v[...] += d_v
        else:
            place(whole, kt, qlo, d_k)
            place(whole, vtile, vlo, d_v)

    if not causal:
        queries(0)
    else:
        each(count // size, queries)
        place(whole, kt, qlo, dk_v[...])
        place(whole, vtile, vlo, dv_v[...])


def block_kernel(
    planes, self_in, crs_in, up_in, dn_in, x_in, cot_in, gain_in, lengths, task_mask,
    block_out, grad_low, home_ffn, home_crs, home_att, gain_out,
    cot, first_k, x_k, second_k, late_k, memory_k, p_k, o_k, lse_k, pc_k, oc_k, lsec_k, act_k, grad_k, y3_k,
    dw_ffn, dw_crs, dw_att, yb_ffn, yb_crs, yb_att, zb_ffn, zb_crs, zb_att, via_att,
    att_v, crs_v, up_v, dn_v, a_v, b_v, o_v, do_v, mid_v, late_v, s_v, g_v, c_v, ta, tb, tc,
    send_v, recv_v, kx, qx, vx, gx, dk_v, dv_v, kt_v, lse_v, gain_v, gain_in_v, gain_buf, out_st, dw_st, sum_st,
    bias_self, bias_cross, res_ffn, res_crs, res_att,
    x_sem, x_sent, y0_sent, c_sem, zw_got, zw_sent, yw_got, yw_sent, side_got, side_sent,
    row_got, row_sent, fwd_sem, cot_got, gain_sem, copy_sem, ex_got, ex_sent, mem_got, mem_sent, mf_got, mf_sent,
    dm_got, dm_sent, df_got, df_sent, y_got, y_sent, z_got, z_sent, home_got, home_sent,
    blk_got, blk_sent, gr_got, gr_sent, gr_hop_got, gr_hop_sent, sum_sem, dw_sem, via_got, via_sent, hand_got, hand_sent,
):
    at = Place(planes)
    c, z, t, y, r = at.c, at.z, at.t, at.y, at.r
    rows = x_in.shape[1]
    slot = s_v.shape[0]
    tiles = slot // BLOCK
    depth = up_in.shape[0]
    side = crs_in.shape[1]
    relay = at.relays
    other = jnp.logical_not(relay)
    vmem = {"att": att_v, "crs": crs_v, "up": up_v, "dn": dn_v}
    shard = {"att": self_in, "up": up_in, "dn": dn_in}
    here = pl.ds(pl.multiple_of(z * depth, depth), depth)
    dw = {"ffn": dw_ffn, "crs": dw_crs, "att": dw_att}
    yb = {"ffn": yb_ffn, "crs": yb_crs, "att": yb_att}
    zb = {"ffn": zb_ffn, "crs": zb_crs, "att": zb_att}
    home = {"ffn": home_ffn, "crs": home_crs, "att": home_att}
    res = {"ffn": res_ffn, "crs": res_crs, "att": res_att}
    names = {}

    def copying(name, source, goal):
        index = names.setdefault(name, len(names))
        return pltpu.make_async_copy(source, goal, copy_sem.at[index])

    def half_of(core):
        return pl.ds(pl.multiple_of(core * 2 * rows, 2 * rows), 2 * rows)

    at.meet()

    relay_dev = (y, z, 2 * y + c)
    over_dev = (y, z, 2 * (1 - y) + c)
    stays = both(c == y, r == c)

    def launch(g):
        i = GROUPS.index(g)
        goal = vmem[g].at[r, here, :]

        @pl.when(stays)
        def _():
            pltpu.make_async_copy(shard[g], goal, x_sem.at[i, r]).start()

        @pl.when(jnp.logical_not(stays))
        def _():
            push(shard[g], goal, x_sent.at[i], x_sem.at[i, r], relay_dev).start()

    def launch_over(g):
        i = GROUPS.index(g)
        return push(shard[g], vmem[g].at[r, here, :], y0_sent.at[i], yw_got.at[i, 0, r], over_dev)

    crs_dev = (y, z, 2 * y + 1)
    crs_stays = both(c == y, r == 1)

    def crs_goal(block, section):
        return crs_v.at[block, here, pl.ds(pl.multiple_of((1 - section) * side, side), side)]

    def launch_crs():
        @pl.when(crs_stays)
        def _():
            pltpu.make_async_copy(crs_in, crs_goal(r, c), c_sem.at[r, c]).start()

        @pl.when(jnp.logical_not(crs_stays))
        def _():
            push(crs_in, crs_goal(r, c), x_sent.at[1], c_sem.at[r, c], crs_dev).start()

    row_goal = s_v.at[strip(t, rows), :]
    cot_goal = cot.at[strip(t, rows), :]

    def row_stays(s):
        return both(both(c == y, r == c), y == s)

    def launch_rows(s):
        dev = (y, z, 2 * s + c)

        @pl.when(row_stays(s))
        def _():
            pltpu.make_async_copy(x_in.at[s], row_goal, row_got.at[r]).start()

        @pl.when(jnp.logical_not(row_stays(s)))
        def _():
            push(x_in.at[s], row_goal, row_sent.at[s], row_got.at[r], dev).start()

    def launch_cot():
        dev = (y, z, 2 * c + 1)

        @pl.when(crs_stays)
        def _():
            pltpu.make_async_copy(cot_in.at[c], cot_goal, cot_got.at[r]).start()

        @pl.when(jnp.logical_not(crs_stays))
        def _():
            push(cot_in.at[c], cot_goal, row_sent.at[2], cot_got.at[r], dev).start()

    gain_copy = push(gain_in, gain_in_v.at[c], gain_sem.at[0], gain_sem.at[1], at.twin)
    gain_copy.start()
    launch("att")
    launch_over("att").start()
    launch_rows(0)
    launch_rows(1)
    launch("up")
    launch_over("up").start()
    launch_crs()
    launch("dn")
    launch_cot()

    place = subs((slot, TILE))
    seen = jnp.where(y == 0, task_mask[0:1, :], task_mask[1:2, :]) == 1
    seen = jnp.broadcast_to(jnp.where(seen, 1.0, 0.0), (TILE, slot)).T > 0.5
    bias_self[...] = jnp.where(place < lengths[r, y], 0.0, NEG_FILL).astype(LOW)
    bias_cross[...] = jnp.where(both(place < lengths[0, y], seen), 0.0, NEG_FILL).astype(LOW)

    def piece(g, k, b):
        j = lax.rem(z - k + planes, planes)
        return vmem[g].at[b, pl.ds(pl.multiple_of(j * depth, depth), depth), :]

    def ring(g, k, b):
        i = GROUPS.index(g)
        return push(
            piece(g, k - 1, b), piece(g, k - 1, b), zw_sent.at[i, k - 1, b], zw_got.at[i, k - 1, b], at.above
        )

    def ring_in(g, k, b):
        i = GROUPS.index(g)
        return push(piece(g, k, b), piece(g, k, b), zw_sent.at[i, k - 1, b], zw_got.at[i, k - 1, b], at.above)

    def cross_over(g, k, b):
        i = GROUPS.index(g)
        return push(piece(g, k, b), piece(g, k, b), yw_sent.at[i, k, b], yw_got.at[i, k, b], at.across)

    def arrive(g, k, b):
        if k:
            ring_in(g, k, b).wait_recv()
        elif g == "crs":
            for section in range(2):
                goal = crs_goal(b, section)
                push(goal, goal, x_sent.at[1], c_sem.at[b, section], at.twin).wait_recv()
        else:
            i = GROUPS.index(g)
            goal = vmem[g].at[b, here, :]
            push(goal, goal, x_sent.at[i], x_sem.at[i, b], at.twin).wait_recv()

    def passing(g, k, up=True, over=True):
        skips = [b for b in range(2) if k == 1 and (g, b) in ASIDE]

        def half(b):
            if up:
                with jax.named_scope("await_" + g + str(k)):
                    arrive(g, k, b)
                if k + 1 < planes:
                    ring(g, k + 1, b).start()
            if over and not (k == 0 and g in DIRECT) and len(skips) < 2:
                if skips:
                    pl.when(b != skips[0])(lambda: cross_over(g, k, b).start())
                else:
                    cross_over(g, k, b).start()

        def run():
            each(2, half, "pass_" + g)

        return run

    def schedule(order):
        events = []
        for n, g in enumerate(order):
            for k in range(planes):
                if k == 0 and n == 0:
                    events.append(passing(g, 0))
                elif k:
                    events.append(passing(g, k))
                if n + 1 < len(order):
                    if k == planes - 2:
                        events[-1] = chained(events[-1], passing(order[n + 1], 0, True, False))
                    if k == planes - 1:
                        events[-1] = chained(events[-1], passing(order[n + 1], 0, False, True))
        return events

    def chained(one, two):
        def run():
            one()
            two()

        return run

    enc_events = schedule(("att", "up", "dn"))
    dec_events = schedule(("att", "crs", "up", "dn"))

    def pump_enc(count):
        for _ in range(min(count, len(enc_events))):
            pl.when(both(relay, at.encodes))(enc_events.pop(0))

    def pump_dec(count):
        for _ in range(min(count, len(dec_events))):
            pl.when(both(relay, at.decodes))(dec_events.pop(0))

    def pump(count):
        pump_enc(count)
        pump_dec(count)

    def side_hop(g, b):
        i = GROUPS.index(g)
        return push(piece(g, 0, b), piece(g, 0, b), side_sent.at[i, b], side_got.at[i, b], at.above)

    def side_in(g, b):
        i = GROUPS.index(g)
        return push(piece(g, 1, b), piece(g, 1, b), side_sent.at[i, b], side_got.at[i, b], at.above)

    def pass_aside(g):
        @pl.when(other)
        def _():
            for b in range(2):
                cross_over(g, 0, b).wait_recv()
                if (g, b) in ASIDE:
                    side_hop(g, b).start()

    def settle(g):
        listens = both(other, at.decodes) if g == "crs" else other

        @pl.when(listens)
        @jax.named_scope("settle_" + g)
        def _():
            for k in range(planes):
                for b in range(2):
                    if k == 1 and (g, b) in ASIDE:
                        side_in(g, b).wait_recv()
                    elif k or g in ("att", "crs"):
                        cross_over(g, k, b).wait_recv()

    def exchange(e, i):
        q = strip(i, BLOCK)
        k = e % 2
        return push(send_v.at[k, q, :], recv_v.at[k, q, :], ex_sent.at[e, i], ex_got.at[e, i], at.twin)

    def joined(e, i):
        q = strip(i, BLOCK)
        exchange(e, i).wait_recv()
        return send_v[e % 2, q, :].astype(WIDE) + recv_v[e % 2, q, :].astype(WIDE)

    def sent(e):
        each(tiles, lambda i: exchange(e, i).wait_send())

    pump(3)
    for k in range(2):
        goal = s_v.at[strip(2 * c + k, rows), :]
        push(goal, goal, row_sent.at[0], row_got.at[k], at.twin).wait_recv()
    half, far_half = half_of(c), half_of(1 - c)
    rows_on = push(s_v.at[half, :], s_v.at[half, :], fwd_sem.at[0], fwd_sem.at[1], at.twin)
    rows_on.start()
    push(gain_in, gain_in_v.at[1 - c], gain_sem.at[0], gain_sem.at[1], at.twin).wait_recv()
    gain_here = pltpu.make_async_copy(gain_in, gain_in_v.at[c], gain_sem.at[2])
    gain_here.start()
    gain_here.wait()
    gains = gain_in_v[r].astype(WIDE)
    g0, g1, g2 = gains[0:1, :], gains[1:2, :], gains[2:3, :]
    gain_v[...] = jnp.zeros_like(gain_v)
    push(s_v.at[far_half, :], s_v.at[far_half, :], fwd_sem.at[0], fwd_sem.at[1], at.twin).wait_recv()
    x_put = copying("x", s_v, x_k)
    x_put.start()

    def enter(i):
        q = strip(i, BLOCK)
        c_v[q, :] = (center(s_v[q, :].astype(WIDE))[0] * g0).astype(LOW)

    each(tiles, enter)
    first_put = copying("first", c_v, first_k)
    first_put.start()
    pump(1)
    settle("att")

    def project(source, weights, part):
        def project_rows(n):
            b, q = lax.rem(n, 2), strip(lax.div(n, 2), BLOCK)
            if part != "kv":
                a_v[b, q, 0:256] = mm(source[q, :], weights[b, :, 0:256]).astype(LOW)
            if part != "q":
                a_v[b, q, 256:640] = mm(source[q, :], weights[b, :, 384:768]).astype(LOW)

        each(2 * tiles, project_rows)

    packed_v = a_v.at[:, :, 0:640]
    project(c_v, att_v, "all")
    pass_aside("up")
    p_put = copying("p", packed_v, p_k)
    p_put.start()
    o_v[...] = jnp.zeros_like(o_v)
    lse_v[...] = jnp.zeros_like(lse_v)
    pump(1)

    def attend_heads(bias, causal, hooks):
        def head_forward(n):
            b = lax.div(n, 3)
            attend_block(lax.rem(n, 3), a_v.at[b], o_v.at[b], lse_v, n, bias, kx, qx, kt_v, causal)
            for when, event in hooks:
                pl.when(both(n == when, relay))(event)

        each(6, head_forward)

    enc_hooks = [(2, enc_events.pop(0)), (5, enc_events.pop(0))]
    dec_hooks = [(2, dec_events.pop(0)), (4, dec_events.pop(0))]
    pl.when(at.encodes)(lambda: attend_heads(bias_self, False, enc_hooks))
    pl.when(at.decodes)(lambda: attend_heads(bias_self, True, dec_hooks))
    o_put, lse_put = copying("o", o_v, o_k), copying("lse", lse_v, lse_k)
    o_put.start()
    lse_put.start()

    def out_project(e, weights):
        def out_rows(i):
            q = strip(i, BLOCK)
            part = mm_nt(o_v[0, q, :], weights[0, :, 128:384]) + mm_nt(o_v[1, q, :], weights[1, :, 128:384])
            send_v[e % 2, q, :] = part.astype(LOW)
            exchange(e, i).start()

        each(tiles, out_rows)

    out_project(0, att_v)
    pump(1)
    x_put.wait()
    pass_aside("dn")
    rows_on.wait_send()

    def middle(i):
        q = strip(i, BLOCK)
        value = s_v[q, :].astype(WIDE) + joined(0, i)
        mid_v[q, :] = value
        s_v[q, :] = (center(value)[0] * g1).astype(LOW)

    each(tiles, middle)
    first_put.wait()
    p_put.wait()
    o_put.wait()
    lse_put.wait()

    def mem_send(i):
        q = pl.ds(pl.multiple_of((2 * c + i) * BLOCK, BLOCK), BLOCK)
        return push(g_v.at[q, :], g_v.at[q, :], mem_sent.at[i], mem_got.at[i], at.beside)

    def mem_forward(i, core):
        q = pl.ds(pl.multiple_of((2 * core + i) * BLOCK, BLOCK), BLOCK)
        return push(g_v.at[q, :], g_v.at[q, :], mf_sent.at[i], mf_got.at[i], at.twin)

    def row_home(k, source, goal, sent_by, got):
        dev = (r, z, 2 * c + k)
        keeps = both(both(c == r, y == c), r == k)
        return keeps, source, goal.at[y], sent_by.at[k], got.at[y], dev

    def go_home(*spec):
        keeps, source, goal, sent_by, got, dev = row_home(*spec)

        @pl.when(keeps)
        def _():
            pltpu.make_async_copy(source, goal, got).start()

        @pl.when(jnp.logical_not(keeps))
        def _():
            push(source, goal, sent_by, got, dev).start()

    def went_home(*spec):
        keeps, source, goal, sent_by, got, dev = row_home(*spec)

        @pl.when(jnp.logical_not(keeps))
        def _():
            push(source, goal, sent_by, got, dev).wait_send()

    def memory_home(k):
        return k, memory_k.at[strip(2 * c + k, rows), :], block_out, blk_sent, blk_got

    settle_up = lambda: settle("up")
    pl.when(at.encodes)(settle_up)

    @pl.when(at.encodes)
    def _():
        def up_rows(n):
            b, q = lax.rem(n, 2), strip(lax.div(n, 2), BLOCK)
            value, grade = gelu_parts(mm(s_v[q, :], up_v[b]))
            a_v[b, q, :] = value.astype(LOW)
            b_v[b, q, :] = grade.astype(LOW)

        each(2 * tiles, up_rows)

    pump_enc(9)

    @pl.when(at.encodes)
    def _():
        settle("dn")

        def down_rows(i):
            q = strip(i, BLOCK)
            part = mm_nt(a_v[0, q, :], dn_v[0]) + mm_nt(a_v[1, q, :], dn_v[1])
            send_v[1, q, :] = part.astype(LOW)
            exchange(1, i).start()

        each(tiles, down_rows)

        def finish(n):
            i = lax.rem(n + 2 * c, 4)
            q = strip(i, BLOCK)
            value = mid_v[q, :] + joined(1, i)
            late_v[q, :] = value
            g_v[q, :] = (center(value)[0] * g2).astype(LOW)

            @pl.when(n < 2)
            def _():
                mem_send(n).start()

        each(tiles, finish)
        keep = copying("memory", g_v, memory_k)
        keep.start()
        keep.wait()
        for k in range(2):
            go_home(*memory_home(k))
        sent(0)

    def norm_grad(values, gain, grad, gain_row, counted):
        normal, scale = center(values)
        scaled = grad * gain
        one = jnp.mean(scaled, axis=-1, keepdims=True)
        two = jnp.mean(scaled * normal, axis=-1, keepdims=True)
        total = jnp.sum(grad * normal, axis=0, keepdims=True)
        gain_v[gain_row : gain_row + 1, :] += jnp.where(counted, total, 0.0)
        return (scaled - one - normal * two) * scale

    def ours(i):
        return lax.div(i, 2) == c

    @pl.when(at.decodes)
    def _():
        second_put = copying("second", s_v, second_k)
        second_put.start()
        for k in range(2):
            goal = cot.at[strip(2 * c + k, rows), :]
            push(goal, goal, row_sent.at[2], cot_got.at[k], at.twin).wait_recv()
        cot_on = push(cot.at[half, :], cot.at[half, :], fwd_sem.at[2], fwd_sem.at[3], at.twin)
        cot_on.start()
        for _ in range(len(dec_events) - 3):
            pl.when(relay)(dec_events.pop(0))
        settle("crs")
        project(s_v, crs_v, "q")
        pl.when(relay)(dec_events.pop(0))
        pl.when(relay)(dec_events.pop(0))
        push(cot.at[far_half, :], cot.at[far_half, :], fwd_sem.at[2], fwd_sem.at[3], at.twin).wait_recv()
        cot_in_v = copying("cot", cot, c_v)
        cot_in_v.start()
        o_v[...] = jnp.zeros_like(o_v)
        lse_v[...] = jnp.zeros_like(lse_v)
        for i in range(2):
            mem_send(i).wait_recv()
            mem_forward(i, c).start()
        for i in range(2):
            mem_forward(i, 1 - c).wait_recv()
        project(g_v, crs_v, "kv")
        puts = [copying("pc", packed_v, pc_k), copying("memory", g_v, memory_k)]
        for copy in puts:
            copy.start()
        attend_heads(bias_cross, False, [(0, dec_events.pop(0))])
        puts += [copying("oc", o_v, oc_k), copying("lsec", lse_v, lsec_k)]
        for copy in puts[2:]:
            copy.start()
        out_project(1, crs_v)
        second_put.wait()

        def finish(i):
            q = strip(i, BLOCK)
            value = mid_v[q, :] + joined(1, i)
            late_v[q, :] = value
            s_v[q, :] = (center(value)[0] * g2).astype(LOW)

        each(tiles, finish)
        late_put = copying("late", late_v, late_k)
        late_put.start()
        settle("up")
        settle("dn")
        cot_in_v.wait()
        sent(0)
        for copy in puts:
            copy.wait()

        def feed_rows(i):
            q = strip(i, BLOCK)

            def feed_half(b):
                value, grade = gelu_parts(mm(s_v[q, :], up_v[b]))
                a_v[b, q, :] = value.astype(LOW)
                b_v[b, q, :] = (mm(c_v[q, :], dn_v[b]) * grade).astype(LOW)

            each(2, feed_half)
            part = mm_nt(b_v[0, q, :], up_v[0]) + mm_nt(b_v[1, q, :], up_v[1])
            send_v[0, q, :] = part.astype(LOW)
            exchange(2, i).start()

        each(tiles, feed_rows)
        copying("act", a_v, act_k).start()
        late_put.wait()
        cot_on.wait_send()
        each(2, lambda i: mem_forward(i, c).wait_send())

    def block_of(k):
        return lax.rem(z - 1 - k + 2 * planes, planes)

    def y_hop(g, k, b):
        i = SUMS.index(g)
        return push(dw[g].at[k, b], yb[g].at[k, b], y_sent.at[i, k, b], y_got.at[i, k, b], at.across)

    def z_hop(g, k, b):
        i = SUMS.index(g)
        return push(res[g].at[b], zb[g].at[k, b], z_sent.at[i, k, b], z_got.at[i, k, b], at.above)

    def via_hop(k):
        diagonal = (c, z, lax.rem(t + 2, 4) + 1 - 2 * r)
        return push(dw_att.at[k, 1], via_att.at[k], via_sent.at[k], via_got.at[k], diagonal)

    def hand_on(k):
        return push(via_att.at[k], yb_att.at[k, 1], hand_sent.at[k], hand_got.at[k], at.beside)

    def leave(g, k):
        @pl.when(other)
        def _():
            y_hop(g, k, 0).start()
            if g == "att":
                pl.when(at.decodes)(lambda: y_hop(g, k, 1).start())
                pl.when(at.encodes)(lambda: via_hop(k).start())
            else:
                y_hop(g, k, 1).start()

    def emit(g, compute):
        columns = dw[g].shape[3]

        def put(k, s):
            return pltpu.make_async_copy(dw_st.at[s, :, :, 0:columns], dw[g].at[k], dw_sem.at[s])

        def run(k):
            s = lax.rem(k, 2)
            j = block_of(k)
            compute(s, pl.ds(pl.multiple_of(j * depth, depth), depth))
            put(k, s).start()

            @pl.when(k >= 1)
            def _():
                put(k - 1, 1 - s).wait()
                leave(g, k - 1)

        each(planes, run, "emit_" + g)
        put(planes - 1, (planes - 1) % 2).wait()
        leave(g, planes - 1)

    def home_copy(g, b, section):
        i = SUMS.index(g)
        columns = dw[g].shape[3]
        source = res[g].at[b]
        if g == "crs":
            source = source.at[:, pl.ds((1 - section) * (columns // 2), columns // 2)]
        device = (section, z, 2 * y + b)
        keeps = both(c == section, r == b)
        return keeps, source, push(source, home[g], home_sent.at[i, b, section if g == "crs" else 0], home_got.at[i], device)

    def sections(g):
        return (0, 1) if g == "crs" else (r,)

    def sum_at(g, n):
        i = SUMS.index(g)
        columns = dw[g].shape[3]
        k, b = lax.div(n, 2), lax.rem(n, 2)

        def fetch(m, source):
            return pltpu.make_async_copy(source, sum_st.at[m, :, 0:columns], sum_sem.at[m])

        @pl.when(relay)
        @jax.named_scope("sum_" + g)
        def _():
            before = lax.max(k - 1, 0)
            if g == "att":
                detour = both(at.encodes, b == 1)
                pl.when(detour)(lambda: hand_on(k).wait_recv())
                pl.when(jnp.logical_not(detour))(lambda: y_hop(g, k, b).wait_recv())
            else:
                y_hop(g, k, b).wait_recv()
            fetch(0, dw[g].at[k, b]).start()
            fetch(1, yb[g].at[k, b]).start()

            @pl.when(k > 0)
            def _():
                z_hop(g, before, b).wait_recv()
                fetch(2, zb[g].at[before, b]).start()
                z_hop(g, before, b).wait_send()
                fetch(2, zb[g].at[before, b]).wait()

            fetch(0, dw[g].at[k, b]).wait()
            fetch(1, yb[g].at[k, b]).wait()
            share = depth // 4

            def add_rows(m):
                q = strip(m, share)
                total = sum_st[0, q, 0:columns].astype(WIDE) + sum_st[1, q, 0:columns].astype(WIDE)
                total = total + jnp.where(k > 0, sum_st[2, q, 0:columns].astype(WIDE), 0.0)
                res[g][b, q, :] = total.astype(LOW)

            each(4, add_rows)

            @pl.when(k + 1 < planes)
            def _():
                z_hop(g, k, b).start()

            @pl.when(k + 1 == planes)
            def _():
                for section in sections(g):
                    keeps, source, copy = home_copy(g, b, section)

                    @pl.when(keeps)
                    def _():
                        pltpu.make_async_copy(source, home[g], home_got.at[i]).start()

                    @pl.when(jnp.logical_not(keeps))
                    def _():
                        copy.start()

    def sums(g, first_step, count):
        each(count, lambda n: sum_at(g, first_step + n), "sums_" + g)

    def turn(source, goal):
        def run(i):
            q = strip(i, BLOCK)
            goal[:, q] = source[q, :].astype(WIDE).T.astype(LOW)

        each(tiles, run, "turn")

    def dm_hop(n, source):
        q = pl.ds(pl.multiple_of((2 * c + n) * BLOCK, BLOCK), BLOCK)
        return push(source.at[q, :], c_v.at[q, :], dm_sent.at[n], dm_got.at[n], at.beside)

    def df_hop(n, core):
        q = pl.ds(pl.multiple_of((2 * core + n) * BLOCK, BLOCK), BLOCK)
        return push(c_v.at[q, :], c_v.at[q, :], df_sent.at[n], df_got.at[n], at.twin)

    @pl.when(at.encodes)
    def _():
        turn(s_v, ta)

        def back_rows(m):
            n = lax.div(m, 2)
            own = lax.rem(m, 2) == 0
            i = jnp.where(own, 2 * c + n, 2 * (1 - c) + n)
            q = strip(i, BLOCK)

            @pl.when(own)
            def _():
                dm_hop(n, c_v).wait_recv()
                df_hop(n, c).start()

            @pl.when(jnp.logical_not(own))
            def _():
                df_hop(n, 1 - c).wait_recv()

            grad = norm_grad(late_v[q, :], g2, c_v[q, :].astype(WIDE), 2, ours(i))
            late_v[q, :] = grad
            low = grad.astype(LOW)
            part = None
            for b in range(2):
                d_pre = (mm(low, dn_v[b]) * b_v[b, q, :].astype(WIDE)).astype(LOW)
                b_v[b, q, :] = d_pre
                term = mm_nt(d_pre, up_v[b])
                part = term if part is None else part + term
            send_v[0, q, :] = part.astype(LOW)

            @pl.when(own)
            def _():
                df_hop(n, c).wait_send()

            c_v[q, :] = low
            exchange(2, i).start()

        each(tiles, back_rows)

    pl.when(at.decodes)(lambda: turn(s_v, ta))
    turn(c_v, tb)

    def ffn_block(s, j):
        def ffn_half(b):
            dw_st[s, b, :, 0:768] = mm(ta[j, :], b_v[b]).astype(LOW)
            dw_st[s, b, :, 768:1536] = mm(tb[j, :], a_v[b]).astype(LOW)

        each(2, ffn_half)

    emit("ffn", ffn_block)

    @pl.when(at.decodes)
    def _():
        copying("act", a_v, act_k).wait()
        packed = copying("pc", pc_k, packed_v)
        small = [copying("oc", oc_k, o_v), copying("lsec", lsec_k, lse_v), copying("second", second_k, s_v)]
        packed.start()
        for copy in small:
            copy.start()

        def late_rows(i):
            q = strip(i, BLOCK)
            grad = c_v[q, :].astype(WIDE) + norm_grad(late_v[q, :], g2, joined(2, i), 2, ours(i))
            late_v[q, :] = grad
            g_v[q, :] = grad.astype(LOW)

        each(tiles, late_rows)

        def cross_out(i):
            q = strip(i, BLOCK)
            for b in range(2):
                do_v[b, q, :] = mm(g_v[q, :], crs_v[b, :, 128:384]).astype(LOW)

        each(tiles, cross_out)
        for copy in small:
            copy.wait()
        packed.wait()
        b_v[...] = jnp.zeros_like(b_v)

        def cross_head(n):
            b = lax.div(n, 3)
            attend_back_block(
                lax.rem(n, 3), a_v.at[b], o_v.at[b], do_v.at[b], b_v.at[b], lse_v, n, bias_cross,
                kx, qx, vx, gx, kt_v, dk_v, dv_v, False,
            )

        each(6, cross_head)
        sent(1)

        def to_memory(q):
            return mm_nt(b_v[0, q, 256:640], crs_v[0, :, 384:768]) + mm_nt(b_v[1, q, 256:640], crs_v[1, :, 384:768])

        def far(n):
            i = 2 * (1 - c) + n
            q = strip(i, BLOCK)
            send_v[1, q, :] = to_memory(q).astype(LOW)
            exchange(3, i).start()

        each(2, far)

        def near(n):
            i = 2 * c + n
            q = strip(i, BLOCK)
            part = to_memory(q)
            exchange(3, i).wait_recv()
            send_v[1, q, :] = (part + recv_v[1, q, :].astype(WIDE)).astype(LOW)
            dm_hop(n, send_v.at[1]).start()

        each(2, near)

        def to_query(i):
            q = strip(i, BLOCK)
            part = mm_nt(b_v[0, q, 0:256], crs_v[0, :, 0:256]) + mm_nt(b_v[1, q, 0:256], crs_v[1, :, 0:256])
            send_v[0, q, :] = part.astype(LOW)
            exchange(4, i).start()

        sent(2)
        each(tiles, to_query)
        sums("ffn", 0, 2)
        turn(s_v, ta)
        stage_in = copying("memory", memory_k, s_v)
        stage_in.start()
        turn(g_v, tc)
        stage_in.wait()
        turn(s_v, tb)
        copying("first", first_k, s_v).start()

        def crs_block(s, j):
            def att_half(b):
                left = mm(ta[j, :], b_v[b, :, 0:256])
                out = mm(tc[j, :], o_v[b])
                dw_st[s, b, :, 0:128] = left[:, 0:128].astype(LOW)
                dw_st[s, b, :, 128:256] = (left[:, 128:256] + out[:, 0:128]).astype(LOW)
                dw_st[s, b, :, 256:384] = out[:, 128:256].astype(LOW)
                dw_st[s, b, :, 384:768] = mm(tb[j, :], b_v[b, :, 256:640]).astype(LOW)

            each(2, att_half)

        emit("crs", crs_block)
        sums("ffn", 2, 2)

        def below(i):
            q = strip(i, BLOCK)
            grad = late_v[q, :] + norm_grad(mid_v[q, :], g1, joined(4, i), 1, ours(i))
            late_v[q, :] = grad
            g_v[q, :] = grad.astype(LOW)

        each(tiles, below)
        copying("first", first_k, s_v).wait()

        def gone(n):
            exchange(3, 2 * (1 - c) + n).wait_send()
            dm_hop(n, send_v.at[1]).wait_send()

        each(2, gone)

    @pl.when(at.encodes)
    def _():
        copying("first", first_k, s_v).start()
        each(2, lambda i: mem_send(i).wait_send())

        def below(i):
            q = strip(i, BLOCK)
            grad = late_v[q, :] + norm_grad(mid_v[q, :], g1, joined(2, i), 1, ours(i))
            late_v[q, :] = grad
            g_v[q, :] = grad.astype(LOW)

        each(tiles, below)
        copying("first", first_k, s_v).wait()
        sent(1)

    packed = copying("p", p_k, packed_v)
    small = [copying("o", o_k, o_v), copying("lse", lse_k, lse_v)]
    packed.start()
    for copy in small:
        copy.start()

    def self_out(i):
        q = strip(i, BLOCK)
        for b in range(2):
            do_v[b, q, :] = mm(g_v[q, :], att_v[b, :, 128:384]).astype(LOW)

    each(tiles, self_out)
    b_v[...] = jnp.zeros_like(b_v)
    for copy in small:
        copy.wait()
    packed.wait()

    def self_heads(causal, hook):
        def self_head(n):
            b = lax.div(n, 3)
            attend_back_block(
                lax.rem(n, 3), a_v.at[b], o_v.at[b], do_v.at[b], b_v.at[b], lse_v, n, bias_self,
                kx, qx, vx, gx, kt_v, dk_v, dv_v, causal,
            )
            hook(n)

        each(6, self_head)

    def enc_hook(n):
        @pl.when(jnp.logical_and(n != 2, n != 5))
        def _():
            sum_at("ffn", n - lax.div(n, 3))

    def dec_hook(n):
        @pl.when(n < 4)
        def _():
            sum_at("ffn", 4 + n)

        @pl.when(n >= 4)
        def _():
            sum_at("crs", n - 4)

    pl.when(at.encodes)(lambda: self_heads(False, enc_hook))
    pl.when(at.decodes)(lambda: self_heads(True, dec_hook))

    def to_rows(q):
        part = None
        for b in range(2):
            term = mm_nt(b_v[b, q, 0:256], att_v[b, :, 0:256]) + mm_nt(b_v[b, q, 256:640], att_v[b, :, 384:768])
            part = term if part is None else part + term
        return part

    def far_rows(n):
        i = 2 * (1 - c) + n
        q = strip(i, BLOCK)
        send_v[1, q, :] = to_rows(q).astype(LOW)
        exchange(5, i).start()

    each(2, far_rows)
    pl.when(at.encodes)(lambda: sums("ffn", 4, 2))
    pl.when(at.decodes)(lambda: sums("crs", 2, 2))
    turn(s_v, ta)
    x_in_v = copying("x", x_k, s_v)
    x_in_v.start()
    turn(g_v, tc)

    def att_block(s, j):
        def att_half(b):
            left = mm(ta[j, :], b_v[b, :, 0:256])
            out = mm(tc[j, :], o_v[b])
            dw_st[s, b, :, 0:128] = left[:, 0:128].astype(LOW)
            dw_st[s, b, :, 128:256] = (left[:, 128:256] + out[:, 0:128]).astype(LOW)
            dw_st[s, b, :, 256:384] = out[:, 128:256].astype(LOW)
            dw_st[s, b, :, 384:768] = mm(ta[j, :], b_v[b, :, 256:640]).astype(LOW)

        each(2, att_half)

    emit("att", att_block)
    pl.when(at.decodes)(lambda: sums("crs", 4, 2))

    @pl.when(both(relay, at.decodes))
    @jax.named_scope("hand_on")
    def _():
        for k in range(planes):
            via_hop(k).wait_recv()
            hand_on(k).start()

    x_in_v.wait()

    def near_rows(n):
        i = 2 * c + n
        q = strip(i, BLOCK)
        part = to_rows(q)
        exchange(5, i).wait_recv()
        grad = part + recv_v[1, q, :].astype(WIDE)
        value = late_v[q, :] + norm_grad(s_v[q, :].astype(WIDE), g0, grad, 0, True)
        out_st[strip(n, BLOCK), :] = value.astype(LOW)

    each(2, near_rows)
    out_put = copying("out", out_st, grad_k)
    out_put.start()
    out_put.wait()

    def grad_home(k):
        return k, grad_k.at[strip(k, rows), :], grad_low, gr_sent, gr_got

    def rows_leave():
        for k in range(2):
            go_home(*grad_home(k))

    pl.when(relay)(rows_leave)

    def gain_hop(n, source, device):
        return push(source, gain_buf.at[n], gr_hop_sent.at[n], gr_hop_got.at[n], device)

    gain_buf[0] = gain_v[...]
    twin_hop = gain_hop(1, gain_buf.at[0], at.twin)
    twin_hop.start()
    twin_hop.wait()
    peer_hop = gain_hop(3, gain_buf.at[2], (1 - c, z, lax.rem(t + 2, 4)))
    last = 4 + planes

    @pl.when(relay)
    def _():
        gain_buf[2] = gain_buf[0] + gain_buf[1]
        peer_hop.start()

    def ring_hop(n):
        return gain_hop(5 + n, gain_buf.at[4 + n], at.above)

    def gain_step(n):
        @pl.when(relay)
        @jax.named_scope("gains")
        def _():
            if n == 0:
                peer_hop.wait()
                gain_buf[4] = gain_buf[2] + gain_buf[3]
            else:
                ring_hop(n - 1).wait()
            if n < planes - 1:
                ring_hop(n).start()
            else:
                total = None
                for j in range(planes):
                    held = gain_buf[jnp.where(z == j, 4, 5 + lax.rem(z - 1 - j + planes, planes))]
                    total = held if total is None else total + held
                gain_buf[last] = total
                for b in range(2):
                    keeps = both(c == r, r == b)

                    @pl.when(keeps)
                    def _():
                        pltpu.make_async_copy(gain_buf.at[last], gain_buf.at[last + 1], gr_hop_got.at[last + 1]).start()

                    @pl.when(jnp.logical_not(keeps))
                    def _():
                        final_hop(b).start()

    def final_hop(b):
        return push(
            gain_buf.at[last], gain_buf.at[last + 1], gr_hop_sent.at[last + b], gr_hop_got.at[last + 1],
            (r, z, 2 * y + b),
        )

    def y3_home(k):
        return k, y3_k.at[strip(k, rows), :], block_out, blk_sent, blk_got

    def out_leaves():
        for k in range(2):
            go_home(*y3_home(k))

    @pl.when(at.decodes)
    def _():
        sums("att", 0, 2)
        copies = [copying("act", act_k, a_v), copying("late", late_k, mid_v)]
        for copy in copies:
            copy.start()
        sent(4)
        for copy in copies:
            copy.wait()

        def to_out(q):
            return mm_nt(a_v[0, q, :], dn_v[0]) + mm_nt(a_v[1, q, :], dn_v[1])

        def far_out(n):
            i = 2 * (1 - c) + n
            q = strip(i, BLOCK)
            send_v[0, q, :] = to_out(q).astype(LOW)
            exchange(6, i).start()

        each(2, far_out)

        def near_out(n):
            i = 2 * c + n
            q = strip(i, BLOCK)
            part = to_out(q)
            exchange(6, i).wait_recv()
            out_st[strip(n, BLOCK), :] = (mid_v[q, :] + part + recv_v[0, q, :].astype(WIDE)).astype(LOW)

        each(2, near_out)
        y3_put = copying("out", out_st, y3_k)
        y3_put.start()
        y3_put.wait()
        pl.when(relay)(out_leaves)

    @pl.when(other)
    def _():
        for k in range(planes):
            y_hop("att", k, 0).wait_send()
            pl.when(at.decodes)(lambda: y_hop("att", k, 1).wait_send())
            pl.when(at.encodes)(lambda: via_hop(k).wait_send())
        rows_leave()
        pl.when(at.decodes)(out_leaves)

    @pl.when(at.encodes)
    def _():
        sums("att", 1, 1)
        sums("ffn", 6, 2)

    pl.when(at.decodes)(lambda: sums("crs", 6, 2))

    def last_sums(n):
        @pl.when(jnp.logical_or(both(at.encodes, n >= 1), n >= 2))
        def _():
            sum_at("att", n + jnp.where(at.encodes, 1 - 2 * lax.rem(n, 2), 0))

        for m in range(planes):
            pl.when(n == 2 * m)(functools.partial(gain_step, m))

    each(2 * planes, last_sums)

    with jax.named_scope("await_gains"):
        final = gain_buf.at[last + 1]
        push(gain_buf.at[last], final, gr_hop_sent.at[last], gr_hop_got.at[last + 1], at.twin).wait_recv()
    gains_home = copying("gains", final, gain_out)
    gains_home.start()
    with jax.named_scope("await_rows"):
        for n in range(2):
            for goal, got in ((block_out, blk_got), (grad_low, gr_got)):
                push(goal.at[n], goal.at[n], blk_sent.at[0], got.at[n], at.twin).wait_recv()
    for i, g in enumerate(SUMS):
        with jax.named_scope("await_home_" + g):
            push(home[g], home[g], home_sent.at[i, 0, 0], home_got.at[i], at.twin).wait_recv()
    gains_home.wait()
    for k in range(2):
        went_home(*grad_home(k))

    @pl.when(at.encodes)
    def _():
        for k in range(2):
            went_home(*memory_home(k))
        sent(2)

    @pl.when(at.decodes)
    def _():
        for k in range(2):
            went_home(*y3_home(k))
        each(2, lambda n: exchange(6, 2 * (1 - c) + n).wait_send())

    each(2, lambda n: exchange(5, 2 * (1 - c) + n).wait_send())

    @pl.when(relay)
    def _():
        for b in range(2):
            pl.when(jnp.logical_not(both(c == r, r == b)))(lambda: final_hop(b).wait_send())

    for g in SUMS:
        there = at.decodes if g == "crs" else jnp.logical_or(at.decodes, at.encodes)

        if g != "att":

            @pl.when(both(other, there))
            def _():
                for k in range(planes):
                    for b in range(2):
                        y_hop(g, k, b).wait_send()

        @pl.when(both(relay, there))
        def _():
            for b in range(2):
                for section in sections(g):
                    keeps, source, copy = home_copy(g, b, section)

                    @pl.when(jnp.logical_not(keeps))
                    def _():
                        copy.wait_send()

    @pl.when(both(relay, at.decodes))
    def _():
        for k in range(planes):
            hand_on(k).wait_send()

    gain_copy.wait_send()
    for g in DIRECT:
        launch_over(g).wait_send()

    @pl.when(jnp.logical_not(stays))
    def _():
        for g in ("att", "up", "dn"):
            push(shard[g], vmem[g].at[r, here, :], x_sent.at[GROUPS.index(g)], x_sem.at[0, 0], relay_dev).wait_send()

    @pl.when(jnp.logical_not(crs_stays))
    def _():
        push(crs_in, crs_goal(r, c), x_sent.at[1], c_sem.at[0, 0], crs_dev).wait_send()
        push(cot_in.at[c], cot_goal, row_sent.at[2], cot_got.at[r], at.twin).wait_send()

    for s in range(2):

        @pl.when(jnp.logical_not(row_stays(s)))
        def _():
            push(x_in.at[s], row_goal, row_sent.at[s], row_got.at[r], at.twin).wait_send()

    for g in GROUPS:
        member = both(relay, at.decodes) if g == "crs" else relay

        @pl.when(member)
        def _():
            for k in range(planes):
                for b in range(2):
                    if k:
                        ring(g, k, b).wait_send()
                    if (k or g not in DIRECT) and (k != 1 or (g, b) not in ASIDE):
                        cross_over(g, k, b).wait_send()

    @pl.when(other)
    def _():
        for g, b in ASIDE:
            side_hop(g, b).wait_send()


def block_call(planes, slot, width, hidden, depth, args):
    shape = jax.ShapeDtypeStruct
    rows = slot // 4
    square = (slot, width)
    wides = {"ffn": 2 * hidden, "crs": width, "att": width}
    packed, outs, logs, acts = (2, slot, 640), (2, slot, 256), (8, slot), (2, slot, hidden)
    out_shape = (
        [shape((2, rows, width), LOW)] * 2
        + [shape((depth, 2 * hidden), LOW), shape((depth, width // 2), LOW), shape((depth, width), LOW)]
        + [shape((8, width), WIDE)]
        + [shape(square, LOW)] * 4
        + [shape(square, WIDE), shape(square, LOW)]
        + [shape(packed, LOW), shape(outs, LOW), shape(logs, WIDE)] * 2
        + [shape(acts, LOW)]
        + [shape((2 * rows, width), LOW)] * 2
        + [shape((planes, 2, depth, wides[g]), LOW) for g in SUMS] * 3
        + [shape((planes, depth, width), LOW)]
    )
    dma = pltpu.SemaphoreType.DMA
    v = pltpu.VMEM
    groups = len(GROUPS)
    scratch = (
        [v((2, width, width), LOW)] * 2
        + [v((2, width, hidden), LOW)] * 2
        + [v(acts, LOW)] * 2
        + [v(outs, LOW)] * 2
        + [v(square, WIDE)] * 2
        + [v(square, LOW)] * 3
        + [v((width, slot), LOW)] * 3
        + [v((2,) + square, LOW)] * 2
        + [v((slot, TILE), LOW)] * 4
        + [v((slot, TILE), WIDE)] * 2
        + [v((TILE, slot), LOW), v(logs, WIDE), v((8, width), WIDE), v((2, 3, width), LOW)]
        + [v((planes + 6, 8, width), WIDE)]
        + [v((2 * rows, width), LOW), v((2, 2, depth, 2 * hidden), LOW), v((3, depth, 2 * hidden), LOW)]
        + [v((slot, TILE), LOW)] * 2
        + [v((2, depth, wides[g]), LOW) for g in SUMS]
        + [dma((groups, 2)), dma((groups,)), dma((groups,)), dma((2, 2))]
        + [dma((groups, planes, 2))] * 4
        + [dma((groups, 2))] * 2
        + [dma((2,)), dma((3,)), dma((4,)), dma((2,)), dma((3,)), dma((40,)), dma((7, 4)), dma((7, 4))]
        + [dma((2,))] * 8
        + [dma((3, planes, 2))] * 4
        + [dma((3,)), dma((3, 2, 2))]
        + [dma((2,))] * 4
        + [dma((planes + 6,))] * 2
        + [dma((3,)), dma((2,))]
        + [dma((planes,))] * 4
    )
    any_spec = pl.BlockSpec(memory_space=pl.ANY)
    vmem_spec = pl.BlockSpec(memory_space=pltpu.VMEM)
    return pl.pallas_call(
        functools.partial(block_kernel, planes),
        out_shape=out_shape,
        in_specs=[any_spec] * 6 + [vmem_spec, pl.BlockSpec(memory_space=pltpu.SMEM), vmem_spec],
        out_specs=[any_spec] * len(out_shape),
        scratch_shapes=scratch,
        compiler_params=pltpu.CompilerParams(collective_id=0, has_side_effects=True, vmem_limit_bytes=VMEM_BYTES),
    )(*args)


def widen_kernel(
    block_in, grad_in, ffn_in, crs_in, att_in, gain_in,
    block_out, grad_out, up_out, dn_out, qkv_out, out_out, crs_out, gain_out, last_out,
):
    c = lax.axis_index("section")
    hidden = up_out.shape[1]
    share, part = block_in.shape[1] // 4, ffn_in.shape[0] // 4

    def strips(i):
        q = strip(i, share)
        for n in range(2):
            block_out[n, q, :] = block_in[n, q, :]
            grad_out[n, q, :] = grad_in[n, q, :].astype(WIDE)
        q = strip(i, part)
        up_out[q, :] = ffn_in[q, 0:hidden].astype(WIDE)
        dn_out[q, :] = ffn_in[q, hidden : 2 * hidden].astype(WIDE)

    each(4, strips)
    tiles = [crs_in[:, TILE * n : TILE * (n + 1)].astype(WIDE) for n in range(3)]
    mixed = jnp.where(c == 1, tiles[1], tiles[2])
    crs_out[:, 0, 0:TILE] = tiles[0]
    crs_out[:, 0, TILE : TILE + HEAD] = mixed[:, 0:HEAD]
    crs_out[:, 1, 0:TILE] = jnp.where(c == 1, tiles[2], tiles[1])
    crs_out[:, 1, TILE : TILE + HEAD] = pltpu.roll(mixed, HEAD, 1)[:, 0:HEAD]
    q_tile, q_o, o_tile, k_tile, v_tile, k_v = (att_in[:, TILE * n : TILE * (n + 1)].astype(WIDE) for n in range(6))
    for n, (whole, rest) in enumerate(((q_tile, q_o), (k_tile, k_v), (v_tile, pltpu.roll(k_v, HEAD, 1)))):
        qkv_out[n, :, 0:TILE] = whole
        qkv_out[n, :, TILE : TILE + HEAD] = rest[:, 0:HEAD]
    out_out[0:TILE, :] = o_tile.T
    out_out[TILE : TILE + HEAD, :] = pltpu.roll(q_o, HEAD, 1).T[0:HEAD, :]
    gain_out[...] = gain_in[0:2, :]
    last_out[...] = gain_in[2:3, :]


def widen_call(kept):
    shape = jax.ShapeDtypeStruct
    rows, width = kept[0].shape[1:]
    depth, hidden = kept[2].shape[0], kept[2].shape[1] // 2
    wide = width // 4
    return pl.pallas_call(
        widen_kernel,
        out_shape=[
            shape((2, rows, width), LOW), shape((2, rows, width), WIDE), shape((depth, hidden), WIDE),
            shape((depth, hidden), WIDE), shape((3, depth, wide), WIDE), shape((wide, depth), WIDE),
            shape((depth, 2, wide), WIDE), shape((2, width), WIDE), shape((1, width), WIDE),
        ],
    )(*kept)


def ring_gather(lay, shard):
    planes = lay.planes
    rows = shard.shape[1]
    if planes > 4:
        piece = lax.all_gather(shard, "dp", axis=1, tiled=True)
        across = lay.route(piece, lambda c, z, t: (c, z, (t + 2) % 4) if c == t // 2 else None)
        return jnp.where(lay.relays, piece, across)
    relay = lambda c, z, t: (c, (z + 1) % planes, t) if c == t // 2 else None
    whole = jnp.zeros((shard.shape[0], planes * rows, shard.shape[2]), shard.dtype)
    piece = shard
    for step in range(planes):
        across = lay.route(piece, lambda c, z, t: (c, z, (t + 2) % 4) if c == t // 2 else None)
        chosen = jnp.where(lay.relays, piece, across)
        whole = lax.dynamic_update_slice(whole, chosen, (0, ((lay.plane - step) % planes) * rows, 0))
        if step + 1 < planes:
            piece = lay.route(piece, relay)
    return whole


def ring_scatter(lay, total, holder):
    planes = lay.planes
    rows = total.shape[1] // planes
    low = total.astype(LOW)
    across = lay.route(
        low, lambda c, z, t: (c, z, (t + 2) % 4) if (c != t // 2 and t % 2 == holder) else None
    )
    summed = low.astype(WIDE) + across.astype(WIDE)
    if planes > 4:
        return lax.psum_scatter(summed.astype(LOW), "dp", scatter_dimension=1, tiled=True)
    relay = lambda c, z, t: (c, (z + 1) % planes, t) if (c == t // 2 and t % 2 == holder) else None
    take = lambda j: lax.dynamic_slice_in_dim(summed, (j % planes) * rows, rows, 1)
    running = take(lay.plane - 1)
    for step in range(1, planes):
        running = lay.route(running.astype(LOW), relay).astype(WIDE) + take(lay.plane - 1 - step)
    return running.astype(LOW)


def hand_back(lay, value, holder, section):
    same = lay.route(
        value[0], lambda c, z, t: (section, z, t) if (c == t // 2 and t % 2 == holder) else None
    )
    beside = lay.route(
        value[1], lambda c, z, t: (section, z, t ^ 1) if (c == t // 2 and t % 2 == holder) else None
    )
    return same.astype(WIDE) + beside.astype(WIDE)


def general_body(block_input, w_self, w_self_out, w_cross, w_up, w_down, norm_gains, lengths, task_mask, out_grad):
    lay = Layout()
    seqs, rows, width = block_input.shape[1:]
    slot = rows * lay.chips
    sec = lay.core
    item = lay.item

    def spread(value, first):
        pick = value[jnp.where(first, lay.chip % 2, 1 - lay.chip % 2)]
        flip = 0 if first else 1
        return lay.route(pick, lambda c, z, t: (t // 2, z, 2 * ((t % 2) ^ flip) + c))

    def merge_rows(mine, theirs):
        low_half = jnp.where(lay.core == 0, mine, theirs)
        high_half = jnp.where(lay.core == 0, theirs, mine)
        return jnp.concatenate([low_half[0], low_half[1], high_half[0], high_half[1]], axis=0)

    first = spread(block_input[0], True)
    second = spread(block_input[0], False)
    mine = jnp.where(item == 0, jnp.stack([first, second]), jnp.stack([second, first]))
    x_rows = merge_rows(mine, lay.other_core(mine)).astype(WIDE)

    picked = out_grad[lay.core]
    even = lay.route(picked, lambda c, z, t: (t // 2, z, 2 * c + 1) if t % 2 == 0 else None)
    odd = lay.route(picked, lambda c, z, t: (t // 2, z, 2 * c + 1) if t % 2 == 1 else None)
    mine = jnp.stack([even, odd])
    cotangent = merge_rows(mine, lay.other_core(mine))

    gains_here = norm_gains[0].astype(WIDE)
    gains = jnp.where(sec == lay.role, gains_here, lay.other_core(norm_gains[0]).astype(WIDE))

    depth = w_self.shape[1]
    wide = w_self.shape[3]
    self_block = pack_heads(
        {"q": w_self[0, :, 0], "k": w_self[0, :, 1], "v": w_self[0, :, 2], "o": w_self_out[0].T}
    )
    feed_block = jnp.concatenate([w_up[0], w_down[0].T], axis=1)
    cross_block = w_cross[0].reshape(depth, 2 * wide)

    def collect(block):
        same = lay.route(block, lambda c, z, t: (t // 2, z, t) if c == t % 2 else None)
        beside = lay.route(block, lambda c, z, t: (t // 2, z, t ^ 1) if c != t % 2 else None)
        return jnp.stack([same, beside])

    def collect_cross(block, section):
        same = lay.route(block, lambda c, z, t: (t // 2, z, t) if (c == section and t % 2 == 1) else None)
        beside = lay.route(block, lambda c, z, t: (t // 2, z, t ^ 1) if (c == section and t % 2 == 0) else None)
        return same, beside

    w_att = ring_gather(lay, collect(self_block))
    w_ffn = ring_gather(lay, collect(feed_block))
    memory_side = collect_cross(cross_block, 0)
    query_side = collect_cross(cross_block, 1)
    w_crs = ring_gather(
        lay,
        jnp.stack(
            [
                pack_heads({"q": q[:, :wide], "k": m[:, :wide], "v": m[:, wide:], "o": q[:, wide:]})
                for m, q in zip(memory_side, query_side)
            ]
        ),
    )
    hidden = w_up.shape[2]
    part = lambda w, name: jnp.concatenate([unpack_heads(w[0], name), unpack_heads(w[1], name)], axis=1)
    att = {n: part(w_att, n) for n in "qkvo"}
    crs = {n: part(w_crs, n) for n in "qkvo"}
    up = jnp.concatenate([w_ffn[0, :, :hidden], w_ffn[1, :, :hidden]], axis=1)
    down_t = jnp.concatenate([w_ffn[0, :, hidden:], w_ffn[1, :, hidden:]], axis=1)

    positions = jnp.arange(slot)
    own_length = jnp.where(lay.is_decoder, lengths[1, item], lengths[0, item])
    self_allowed = (positions[None, :] < own_length) & (
        (positions[None, :] <= positions[:, None]) | jnp.logical_not(lay.is_decoder)
    )
    cross_allowed = jnp.broadcast_to(
        ((positions < lengths[0, item]) & (task_mask[item] == 1))[None], (slot, slot)
    )

    def joined(partial):
        low = partial.astype(LOW)
        return low.astype(WIDE) + lay.other_core(low).astype(WIDE)

    normed0 = layer_norm(x_rows, gains[0]).astype(LOW)
    q, k, v = (mm(normed0, att[n]).astype(LOW) for n in "qkv")
    out_self, lse_self = attend(q, k, v, self_allowed)
    x_mid = x_rows + joined(mm_nt(out_self, att["o"]))
    normed1 = layer_norm(x_mid, gains[1]).astype(LOW)

    pre_enc = mm(normed1, up)
    act_enc, slope_enc = gelu_parts(pre_enc)
    act_enc = act_enc.astype(LOW)
    x_late_enc = x_mid + joined(mm_nt(act_enc, down_t))
    memory_enc = layer_norm(x_late_enc, gains[2]).astype(LOW)
    memory = lay.route(memory_enc, lambda c, z, t: (c, z, t ^ 1) if t % 2 == 0 else None)

    cq = mm(normed1, crs["q"]).astype(LOW)
    ck, cv = (mm(memory, crs[n]).astype(LOW) for n in "kv")
    out_cross, lse_cross = attend(cq, ck, cv, cross_allowed)
    x_late = x_mid + joined(mm_nt(out_cross, crs["o"]))
    normed2 = layer_norm(x_late, gains[2]).astype(LOW)
    pre_dec = mm(normed2, up)
    act_dec, slope_dec = gelu_parts(pre_dec)
    act_dec = act_dec.astype(LOW)
    result_dec = (x_late + joined(mm_nt(act_dec, down_t))).astype(LOW)

    d_out = cotangent.astype(WIDE)
    d_pre = (slope_dec * mm(cotangent, down_t)).astype(LOW)
    d_ffn_dec = jnp.concatenate([mm_tn(normed2, d_pre), mm_tn(cotangent, act_dec)], axis=1)
    d_late_norm, d_gain2_dec = norm_back(x_late, gains[2], joined(mm_nt(d_pre, up)))
    d_late = d_out + d_late_norm
    grad_late = d_late.astype(LOW)
    d_att = mm(grad_late, crs["o"]).astype(LOW)
    d_cq, d_ck, d_cv = attend_back(cq, ck, cv, lse_cross, d_att, cross_allowed)
    d_memory = joined(mm_nt(d_ck, crs["k"]) + mm_nt(d_cv, crs["v"]))
    d_crs = {
        "q": mm_tn(normed1, d_cq),
        "k": mm_tn(memory, d_ck),
        "v": mm_tn(memory, d_cv),
        "o": mm_tn(grad_late, out_cross),
    }
    d_mid_norm, d_gain1_dec = norm_back(x_mid, gains[1], joined(mm_nt(d_cq, crs["q"])))
    d_mid_dec = d_late + d_mid_norm

    d_memory = lay.route(d_memory.astype(LOW), lambda c, z, t: (c, z, t ^ 1) if t % 2 == 1 else None).astype(WIDE)
    d_late_enc, d_gain2_enc = norm_back(x_late_enc, gains[2], d_memory)
    grad_late_enc = d_late_enc.astype(LOW)
    d_pre = (slope_enc * mm(grad_late_enc, down_t)).astype(LOW)
    d_ffn_enc = jnp.concatenate([mm_tn(normed1, d_pre), mm_tn(grad_late_enc, act_enc)], axis=1)
    d_mid_norm, d_gain1_enc = norm_back(x_mid, gains[1], joined(mm_nt(d_pre, up)))
    d_mid_enc = d_late_enc + d_mid_norm

    d_mid = jnp.where(lay.is_decoder, d_mid_dec, d_mid_enc)
    grad_mid = d_mid.astype(LOW)
    d_att = mm(grad_mid, att["o"]).astype(LOW)
    d_q, d_k, d_v = attend_back(q, k, v, lse_self, d_att, self_allowed)
    d_norm = joined(mm_nt(d_q, att["q"]) + mm_nt(d_k, att["k"]) + mm_nt(d_v, att["v"]))
    d_att_w = {
        "q": mm_tn(normed0, d_q),
        "k": mm_tn(normed0, d_k),
        "v": mm_tn(normed0, d_v),
        "o": mm_tn(grad_mid, out_self),
    }
    d_first, d_gain0 = norm_back(x_rows, gains[0], d_norm)
    d_rows = d_mid + d_first

    half = 3 * HEAD

    def blocks(parts):
        return jnp.stack(
            [pack_heads({n: parts[n][:, half * b : half * (b + 1)] for n in parts}) for b in range(2)]
        )

    def feed_blocks(both):
        total = both.shape[1] // 2
        return jnp.stack(
            [
                jnp.concatenate(
                    [both[:, hidden * b : hidden * (b + 1)], both[:, total + hidden * b : total + hidden * (b + 1)]],
                    axis=1,
                )
                for b in range(2)
            ]
        )

    self_total = blocks(d_att_w)
    home_self = hand_back(lay, ring_scatter(lay, self_total, 0), 0, 0) + hand_back(
        lay, ring_scatter(lay, self_total, 1), 1, 1
    )
    home_feed = hand_back(lay, ring_scatter(lay, feed_blocks(d_ffn_enc), 0), 0, 0) + hand_back(
        lay, ring_scatter(lay, feed_blocks(d_ffn_dec), 1), 1, 1
    )
    cross_total = ring_scatter(lay, blocks(d_crs), 1)
    side = lambda names: jnp.stack(
        [jnp.concatenate([unpack_heads(cross_total[b], n) for n in names], axis=1) for b in range(2)]
    )
    home_cross = hand_back(lay, side("kv"), 1, 0) + hand_back(lay, side("qo"), 1, 1)

    g_self = jnp.stack([unpack_heads(home_self, n) for n in "qkv"], axis=1)[None]
    g_self_out = unpack_heads(home_self, "o").T[None]
    g_cross = home_cross.reshape(1, depth, 2, wide)
    g_up = home_feed[:, :hidden][None]
    g_down = home_feed[:, hidden:].T[None]

    gain2 = jnp.where(lay.is_decoder, d_gain2_dec, d_gain2_enc)
    gain1 = jnp.where(lay.is_decoder, d_gain1_dec, d_gain1_enc)
    gain_rows = jnp.stack([d_gain0, gain1, gain2])
    slots = jnp.stack(
        [
            jnp.where((lay.role == r) & (lay.core == 0), gain_rows, 0.0)
            for r in range(2)
        ]
    )
    gain_total = lax.psum(slots, AXES)[sec][None]

    def rows_home(value):
        mine = lax.dynamic_slice_in_dim(value, lay.core * 2 * rows, 2 * rows, 0).reshape(2, rows, width)
        a = lay.route(mine[item], lambda c, z, t: (t % 2, z, 2 * c + t // 2))
        b = lay.route(mine[1 - item], lambda c, z, t: (t % 2, z, 2 * c + 1 - t // 2))
        even = lay.chip % 2 == 0
        return jnp.where(even, jnp.stack([a, b]), jnp.stack([b, a]))[None]

    block_output = rows_home(jnp.where(lay.is_decoder, result_dec, memory_enc))
    input_grad = rows_home(d_rows.astype(LOW)).astype(WIDE)
    return (
        block_output,
        input_grad,
        g_self,
        g_self_out,
        g_cross,
        g_up,
        g_down,
        gain_total[:, :2],
        gain_total[:, 2],
    )


def body(block_input, w_self, w_self_out, w_cross, w_up, w_down, norm_gains, lengths, task_mask, out_grad):
    lay = Layout()
    seqs, rows, width = block_input.shape[1:]
    slot = rows * lay.chips
    sec = lay.core
    item = lay.item

    if lay.planes != 4:
        return general_body(
            block_input, w_self, w_self_out, w_cross, w_up, w_down, norm_gains, lengths, task_mask, out_grad
        )

    depth = w_self.shape[1]
    wide = w_self.shape[3]
    hidden = w_up.shape[2]
    self_block = pack_heads(
        {"q": w_self[0, :, 0], "k": w_self[0, :, 1], "v": w_self[0, :, 2], "o": w_self_out[0].T}
    )
    pair = {"q": w_cross[0, :, 0], "o": w_cross[0, :, 1], "k": w_cross[0, :, 0], "v": w_cross[0, :, 1]}
    pieces = [pair[n][:, HEAD * h : HEAD * (h + 1)] for n, h in ORDER]
    cross_block = jnp.where(
        sec == 1, jnp.concatenate(pieces[:6], axis=1), jnp.concatenate(pieces[6:], axis=1)
    )
    kept = block_call(
        lay.planes,
        slot,
        width,
        hidden,
        depth,
        (self_block, cross_block, w_up[0], w_down[0].T, block_input[0], out_grad, norm_gains[0], lengths, task_mask),
    )[:6]
    block_output, input_grad, g_up, g_down, g_qkv, g_out, g_cross, g_gain, g_last = widen_call(kept)
    return (
        block_output[None],
        input_grad[None],
        jnp.swapaxes(g_qkv, 0, 1)[None],
        g_out[None],
        g_cross[None],
        g_up[None],
        g_down.T[None],
        g_gain[None],
        g_last,
    )


def solution(mesh):
    placed = (
        P("section", "dp", "tensor", None),
        P("section", "dp", None, "tensor"),
        P("section", "tensor", "dp"),
        P("section", "dp", None, "tensor"),
        P("section", "dp", "tensor"),
        P("section", "tensor", "dp"),
        P("section", None, None),
        P(None, "dp"),
        P("dp", None),
        P("dp", "tensor", None),
    )
    return jax.shard_map(
        body,
        mesh=mesh,
        in_specs=placed,
        out_specs=(
            P("section", "dp", "tensor", None),
            P("section", "dp", "tensor", None),
            P("section", "dp", None, "tensor"),
            P("section", "tensor", "dp"),
            P("section", "dp", None, "tensor"),
            P("section", "dp", "tensor"),
            P("section", "tensor", "dp"),
            P("section", None, None),
            P("section", None),
        ),
        check_vma=False,
    )
```
